32 devices in a mesh: dp: 8 (over z, y), enc: 4 (over x, core).
Axes of the slice: x: 2, y: 2, z: 4, core: 2. Of those that a mesh axis runs over, the one named last changes fastest.
Arguments:
- text_embed: bfloat16 [12288, 768], P(('dp', 'enc'))
- region_features: bfloat16 [8192, 2048], P(('dp', 'enc')), may hold values from -6 to 6
- boxes: bfloat16 [4, 8192], P(None, ('dp', 'enc')), may hold values from 0 to 1
- caption_image: int32 [96], P(('dp', 'enc')), may hold values from 0 to 1, as said below
- caption_lengths: int32 [96], P(('dp', 'enc')), may hold values from 1 to 128, as said below
- region_counts: int32 [64], P(('dp', 'enc')), may hold values from 32 to 128, as said below
- region_target: int32 [32, 256], P(('dp', 'enc')), may hold values from 0 to 255, each once within a row
- region_source: int32 [32, 256], P(('dp', 'enc')), may hold values from 0 to 255, as said below
- w_visual: bfloat16 [2048, 768], replicated, may hold values from -0.125 to 0.125
- w_box: bfloat16 [768, 4], replicated, may hold values from -3 to 3
- visual_bias: float32 [768], replicated, may hold values from -3 to 3
- visual_gain: float32 [768], replicated, may hold values from 0.5 to 1.5
- visual_shift: float32 [768], replicated, may hold values from -2 to 2
- w_qkv: bfloat16 [768, 2304], replicated, may hold values from -0.21875 to 0.21875
- qv_bias: float32 [1536], replicated, may hold values from -2 to 2
- w_out: bfloat16 [768, 768], replicated, may hold values from -2.5 to 2.5
- out_bias: float32 [768], replicated, may hold values from -2 to 2
- attn_gain: float32 [768], replicated, may hold values from 0.5 to 1.5
- attn_shift: float32 [768], replicated, may hold values from -2 to 2
- w_up: bfloat16 [768, 3072], replicated, may hold values from -0.21875 to 0.21875
- up_bias: float32 [3072], replicated, may hold values from -2 to 2
- w_down: bfloat16 [3072, 768], replicated, may hold values from -0.15625 to 0.15625
- down_bias: float32 [768], replicated, may hold values from -2 to 2
- ffn_gain: float32 [768], replicated, may hold values from 0.5 to 1.5
- ffn_shift: float32 [768], replicated, may hold values from -2 to 2
- out_grad: bfloat16 [24576, 768], P(('dp', 'enc')), may hold values from -6 to 6
Outputs:
- out_rows: bfloat16 [24576, 768], P(('dp', 'enc'))
- text_grad: float32 [12288, 768], P(('dp', 'enc'))
- feature_grad: float32 [8192, 2048], P(('dp', 'enc'))
- box_grad: float32 [4, 8192], P(None, ('dp', 'enc'))
- rms_values: float32 [3], replicated
- w_visual_grad: float32 [2048, 768], P('dp')
- w_box_grad: float32 [768, 4], P('dp')
- visual_bias_grad: float32 [768], P('dp')
- visual_gain_grad: float32 [768], P('dp')
- visual_shift_grad: float32 [768], P('dp')
- w_qkv_grad: float32 [768, 2304], P('dp')
- qv_bias_grad: float32 [1536], P('dp')
- w_out_grad: float32 [768, 768], P('dp')
- out_bias_grad: float32 [768], P('dp')
- attn_gain_grad: float32 [768], P('dp')
- attn_shift_grad: float32 [768], P('dp')
- w_up_grad: float32 [768, 3072], P('dp')
- up_bias_grad: float32 [3072], P('dp')
- w_down_grad: float32 [3072, 768], P('dp')
- down_bias_grad: float32 [768], P('dp')
- ffn_gain_grad: float32 [768], P('dp')
- ffn_shift_grad: float32 [768], P('dp')
The draws below stay inside these ranges and needn't reach their ends.
Inputs may be any that keep to these rules, and one draw needn't show every extreme that they name: `caption_image`: among the 3 captions of one device each local image number appears once or twice. `caption_lengths`: the largest length 128 is reached in every draw. `region_counts`: the largest count 128 is reached in every draw. Row s is a permutation; region row r of device s goes to device region_target[s, r] // 8 at place region_target[s, r] % 8 of that device's message. Row d is a permutation; region_source[d, t] % 8 == t % 8, the 8 slots of each aligned block of 8 slots share one source device region_source[d, t] // 8, and each source device serves exactly one block of a row.
All inputs are finite; a program needn't handle non-finite values.
Results may differ from the reference program's by a relative error of at most 0.018.
Values may be sent and summed in bfloat16 or wider, within the bound.
No kernel may reach another device: no remote copies, remote signals or barrier semaphores. Data moves between devices by JAX's collectives and lax.ppermute only.
A program may use at most 256 MiB of HBM per device.

```python
import jax
import jax.numpy as jnp
from jax import lax

D = 768
HEADS = 12
HEAD = 64
FF = 3072
FEAT = 2048
TXT = 128
REG = 128
IMG_DEV = 2
SEQ = 256
CAPT_DEV = 3
REG_DEV = 256
NODES = 32
IMAGES = 64
CAPTIONS = 96
TEXT_TOK = 12288
ROWS = 8192
CAP = 8


def draw_text_embed(key, part):
    row_ids = jnp.arange(TEXT_TOK, dtype=jnp.float32)
    scaling = 0.4 * (1.0 + 5.0 * row_ids / TEXT_TOK)
    values = jax.random.normal(key, (TEXT_TOK, D), jnp.float32)
    return (values * scaling[:, None]).astype(jnp.bfloat16)


def shuffled_captions(subkey):
    return jax.random.permutation(subkey, CAPT_DEV)


def draw_caption_image(key, part):
    subkeys = jax.random.split(jax.random.fold_in(key, 3), NODES)
    order = jax.vmap(shuffled_captions)(subkeys)
    return (order % IMG_DEV).reshape(-1).astype(jnp.int32)


def draw_caption_lengths(key, part):
    first = jax.random.fold_in(key, 5)
    device_ids = jnp.arange(CAPTIONS, dtype=jnp.int32) // CAPT_DEV
    upper_end = jnp.maximum(TXT // 4 + (TXT - TXT // 4) * (device_ids + 1) // NODES, 1)
    values = jax.random.randint(first, (CAPTIONS,), 1, upper_end + 1)
    return values.at[CAPTIONS - 1].set(TXT).astype(jnp.int32)


def draw_region_counts(key, part):
    first = jax.random.fold_in(key, 7)
    device_ids = jnp.arange(IMAGES, dtype=jnp.int32) // IMG_DEV
    upper_end = REG // 4 + (REG - REG // 4) * (device_ids + 1) // NODES
    values = jax.random.randint(first, (IMAGES,), REG // 4, upper_end + 1)
    return values.at[IMAGES - 1].set(REG).astype(jnp.int32)


def source_blocks(subkey):
    senders = jax.random.permutation(subkey, NODES)
    slots = jnp.arange(REG_DEV, dtype=jnp.int32)
    return senders[slots // CAP] * CAP + slots % CAP


def draw_region_source(key, part):
    subkeys = jax.random.split(jax.random.fold_in(key, 11), NODES)
    return jax.vmap(source_blocks)(subkeys).astype(jnp.int32)


def shard_levels(own_key, shape, shards, smallest, largest):
    level, own = 1.0, jax.random.fold_in(own_key, 6)
    for dim, blocks in shards:
        steps = jnp.exp(jax.random.uniform(jax.random.fold_in(own, dim), (blocks,), jnp.float32, smallest / len(shards), largest / len(shards)))
        level = level * jnp.repeat(steps, shape[dim] // blocks).reshape([-1 if axis == dim else 1 for axis in range(len(shape))])
    return level


def bell_draw(own_key, dims, scale, reach, cuts=(), kind=jnp.bfloat16):
    array = scale * jax.random.normal(own_key, dims, jnp.float32)
    if cuts:
        array = array * shard_levels(own_key, dims, cuts, -0.22, 0.18)
    return jnp.clip(array, -reach, reach).astype(kind)


def setup_inputs(seed: int = 0) -> dict:
    seeds = jax.random.split(jax.random.key(seed), 27)
    return {
        "text_embed": draw_text_embed(jax.random.fold_in(seeds[26], 71), 0),
        "region_features": bell_draw(seeds[1], (ROWS, FEAT), 1.0, 6.0, ((0, 32),)),
        "boxes": jnp.clip(1.0 * jax.random.uniform(seeds[2], (4, ROWS), jnp.float32) ** shard_levels(seeds[2], (4, ROWS), ((1, 32),), -0.2, 0.2), 0.0, 1.0).astype(jnp.bfloat16),
        "caption_image": draw_caption_image(jax.random.fold_in(seeds[26], 71), 0),
        "caption_lengths": draw_caption_lengths(jax.random.fold_in(seeds[26], 71), 0),
        "region_counts": draw_region_counts(jax.random.fold_in(seeds[26], 71), 0),
        "region_target": jax.vmap(lambda own: jax.random.permutation(own, REG_DEV))(jax.random.split(seeds[6], NODES)).reshape((NODES, REG_DEV)).astype(jnp.int32),
        "region_source": draw_region_source(jax.random.fold_in(seeds[26], 71), 0),
        "w_visual": bell_draw(seeds[8], (FEAT, D), FEAT ** -0.5, 0.125),
        "w_box": bell_draw(seeds[9], (D, 4), 4 ** -0.5, 3.0),
        "visual_bias": bell_draw(seeds[10], (D,), 0.5, 3.0, (), jnp.float32),
        "visual_gain": jnp.clip(1.0 + 0.1 * jax.random.normal(seeds[11], (D,), jnp.float32), 0.5, 1.5),
        "visual_shift": bell_draw(seeds[12], (D,), 0.3, 2.0, (), jnp.float32),
        "w_qkv": bell_draw(seeds[13], (D, 3 * D), D ** -0.5, 0.21875),
        "qv_bias": bell_draw(seeds[14], (2 * D,), 0.3, 2.0, (), jnp.float32),
        "w_out": bell_draw(seeds[15], (D, D), (max(D // 144, 1)) ** -0.5, 2.5),
        "out_bias": bell_draw(seeds[16], (D,), 0.3, 2.0, (), jnp.float32),
        "attn_gain": jnp.clip(1.0 + 0.1 * jax.random.normal(seeds[17], (D,), jnp.float32), 0.5, 1.5),
        "attn_shift": bell_draw(seeds[18], (D,), 0.3, 2.0, (), jnp.float32),
        "w_up": bell_draw(seeds[19], (D, FF), D ** -0.5, 0.21875),
        "up_bias": bell_draw(seeds[20], (FF,), 0.3, 2.0, (), jnp.float32),
        "w_down": bell_draw(seeds[21], (FF, D), (FF // 2) ** -0.5, 0.15625),
        "down_bias": bell_draw(seeds[22], (D,), 0.3, 2.0, (), jnp.float32),
        "ffn_gain": jnp.clip(1.0 + 0.1 * jax.random.normal(seeds[23], (D,), jnp.float32), 0.5, 1.5),
        "ffn_shift": bell_draw(seeds[24], (D,), 0.3, 2.0, (), jnp.float32),
        "out_grad": bell_draw(seeds[25], (CAPTIONS * SEQ, D), 1.0, 6.0, ((0, 32),)),
    }


@jax.custom_vjp
def low(v):
    return lax.optimization_barrier(v.astype(jnp.bfloat16)).astype(jnp.float32)

@jax.custom_vjp
def low_back(v):
    return v

def low_keep(v):
    return (low(v), None)

def low_pass(kept, grad):
    return (grad,)

def back_keep(v):
    return (v, None)

def back_low(kept, grad):
    return (low(grad),)
low.defvjp(low_keep, low_pass)
low_back.defvjp(back_keep, back_low)
epsilon = 1e-12

def matmul(left, right):
    return jnp.dot(left, right, precision=lax.Precision.HIGHEST, preferred_element_type=jnp.float32)

def layer_norm(values, gain, shift):
    centre = values - lax.optimization_barrier(jnp.mean(values, -1, keepdims=True))
    spread = lax.optimization_barrier(jnp.mean(centre * centre, -1, keepdims=True))
    return centre * lax.rsqrt(spread + epsilon) * gain + shift

def gather_rows(region_target, region_source):
    node_ids = jnp.arange(NODES, dtype=jnp.int32)
    senders = (region_source // CAP).astype(jnp.int32)
    places = (region_source % CAP).astype(jnp.int32)
    message_index = (node_ids[:, None] * CAP + places).astype(jnp.int32)
    row_ids = jnp.broadcast_to(jnp.arange(REG_DEV, dtype=jnp.int32)[None, :], (NODES, REG_DEV))
    inverse = jnp.zeros((NODES, REG_DEV), jnp.int32).at[node_ids[:, None], region_target].set(row_ids)
    taken = inverse[senders, message_index]
    return (senders * REG_DEV + taken).reshape(-1).astype(jnp.int32)

def reference(text_embed, region_features, boxes, caption_image, caption_lengths, region_counts, region_target, region_source, w_visual, w_box, visual_bias, visual_gain, visual_shift, w_qkv, qv_bias, w_out, out_bias, attn_gain, attn_shift, w_up, up_bias, w_down, down_bias, ffn_gain, ffn_shift, out_grad):
    gather_index = gather_rows(region_target, region_source)
    params = tuple((p.astype(jnp.float32) for p in (w_visual, w_box, visual_bias, visual_gain, visual_shift, w_qkv, qv_bias, w_out, out_bias, attn_gain, attn_shift, w_up, up_bias, w_down, down_bias, ffn_gain, ffn_shift)))
    image_local = caption_image.reshape(NODES, CAPT_DEV)
    lengths_node = caption_lengths.reshape(NODES, CAPT_DEV)
    counts_node = region_counts.reshape(NODES, IMG_DEV)
    width = D

    def forward(weights, text_rows, features, box_rows):
        wv, wb, vbias, vgain, vshift, wqkv, qvb, wout, obias, again, ashift, wup, ubias, wdown, dbias, fgain, fshift = weights
        pre = matmul(features, wv) + matmul(box_rows.T, wb.T) + vbias
        pre = low_back(pre)
        region = low_back(low(layer_norm(pre, vgain, vshift)))
        images = region[gather_index].reshape(NODES, IMG_DEV, REG, width)
        texts = text_rows.reshape(NODES, CAPT_DEV, TXT, width)

        def one_node(inputs):
            text_node, image_node, choose, lengths, counts = inputs
            select = (choose[:, None] == jnp.arange(IMG_DEV, dtype=jnp.int32)[None, :]).astype(jnp.float32)
            cap_regions = jnp.einsum('cm,mrd->crd', select, image_node, precision=lax.Precision.HIGHEST)
            seq_rows = jnp.concatenate([text_node, cap_regions], 1)
            region_count = lax.optimization_barrier(jnp.sum(jnp.where(choose[:, None] == jnp.arange(IMG_DEV, dtype=jnp.int32)[None, :], counts[None, :], 0), 1))
            place = jnp.arange(SEQ, dtype=jnp.int32)[None, :]
            valid_slot = jnp.where(place < TXT, place < lengths[:, None], place - TXT < region_count[:, None])
            flat = seq_rows.reshape(CAPT_DEV * SEQ, width)
            qkv = matmul(flat, wqkv)
            query = low_back(low(qkv[:, :width] + qvb[:width])).reshape(CAPT_DEV, SEQ, HEADS, HEAD)
            keyed = low_back(low(qkv[:, width:2 * width])).reshape(CAPT_DEV, SEQ, HEADS, HEAD)
            valued = low_back(low(qkv[:, 2 * width:] + qvb[width:])).reshape(CAPT_DEV, SEQ, HEADS, HEAD)
            scores = jnp.einsum('cqhe,ckhe->chqk', query, keyed, precision=lax.Precision.HIGHEST) * 0.125
            scores = low_back(scores)
            masked = jnp.where(valid_slot[:, None, None, :], scores, -1e+30)
            probs = low(jax.nn.softmax(masked, -1))
            context = jnp.einsum('chqk,ckhe->cqhe', probs, valued, precision=lax.Precision.HIGHEST)
            context = low_back(low(context)).reshape(CAPT_DEV * SEQ, width)
            attn = low_back(matmul(context, wout) + obias)
            hidden = layer_norm(flat + attn, again, ashift)
            upper = low_back(matmul(low(hidden), wup) + ubias)
            act = low(jax.nn.gelu(upper, approximate=False))
            ffn = low_back(matmul(act, wdown) + dbias)
            final = layer_norm(hidden + ffn, fgain, fshift)
            row_mask = valid_slot.reshape(-1, 1).astype(jnp.float32)
            stats = jnp.stack([jnp.sum(row_mask * flat * flat), jnp.sum(row_mask * attn * attn), jnp.sum(row_mask * ffn * ffn), jnp.sum(row_mask) + 0.0 * jnp.sum(flat[0, :1])])
            return (final * row_mask, stats)
        outs, stats = lax.map(jax.checkpoint(one_node), (texts, images, image_local, lengths_node, counts_node))
        return (outs.reshape(CAPTIONS * SEQ, width), lax.optimization_barrier(jnp.sum(stats, 0)))
    out_value, pullback, stats = jax.vjp(forward, params, text_embed.astype(jnp.float32), region_features.astype(jnp.float32), boxes.astype(jnp.float32), has_aux=True)
    param_grads, text_grad, feature_grad, box_grad = pullback(out_grad.astype(jnp.float32))
    rms_values = jnp.sqrt(stats[:3] / (stats[3] * width))
    return (out_value.astype(jnp.bfloat16), text_grad, feature_grad, box_grad, rms_values, param_grads[0], param_grads[1], param_grads[2], param_grads[3], param_grads[4], param_grads[5], param_grads[6], param_grads[7], param_grads[8], param_grads[9], param_grads[10], param_grads[11], param_grads[12], param_grads[13], param_grads[14], param_grads[15], param_grads[16])
```

```python
import jax
import jax.numpy as jnp
from jax import lax
from jax.sharding import PartitionSpec as P

HEADS = 12
HEAD = 64


epsilon = 1e-12
inv_sqrt_two = 0.7071067811865476
inv_sqrt_tau = 0.3989422804014327


def layer_norm(values, gain, shift):
    centre = values - jnp.mean(values, -1, keepdims=True)
    spread = jnp.mean(centre * centre, -1, keepdims=True)
    inv_std = lax.rsqrt(spread + epsilon)
    normed = centre * inv_std
    return (normed * gain + shift, normed, inv_std)


def norm_back(grad, normed, inv_std, gain):
    scaled = grad * gain
    return inv_std * (
        scaled
        - jnp.mean(scaled, -1, keepdims=True)
        - normed * jnp.mean(scaled * normed, -1, keepdims=True)
    )


def col_sum(values):
    return jnp.sum(values.astype(jnp.float32), 0)


def on_device(
    text_embed,
    region_features,
    boxes,
    caption_image,
    caption_lengths,
    region_counts,
    region_target,
    region_source,
    w_visual,
    w_box,
    visual_bias,
    visual_gain,
    visual_shift,
    w_qkv,
    qv_bias,
    w_out,
    out_bias,
    attn_gain,
    attn_shift,
    w_up,
    up_bias,
    w_down,
    down_bias,
    ffn_gain,
    ffn_shift,
    out_grad,
):
    f32 = jnp.float32
    bf16 = jnp.bfloat16
    width = text_embed.shape[1]
    captions = caption_image.shape[0]
    images = region_counts.shape[0]
    region_dev = region_target.shape[1]
    regions = region_dev // images
    text_len = text_embed.shape[0] // captions
    seq_len = text_len + regions
    row_count = captions * seq_len
    flat_target = region_target[0]
    flat_source = region_source[0]
    region_pre = (
        jnp.dot(region_features, w_visual, preferred_element_type=f32)
        + jnp.dot(boxes.T, w_box.T, preferred_element_type=f32)
        + visual_bias
    )
    region_norm, vis_normed, vis_inv = layer_norm(region_pre, visual_gain, visual_shift)
    region_low = region_norm.astype(bf16)
    message = jnp.zeros_like(region_low).at[flat_target].set(region_low)
    arrived = lax.all_to_all(message, ("dp", "enc"), split_axis=0, concat_axis=0, tiled=True)
    local_regions = arrived[flat_source].reshape(images, regions, width)
    image_ids = jnp.arange(images, dtype=jnp.int32)
    select = caption_image[:, None] == image_ids[None, :]
    caption_regions = jnp.einsum(
        "cm,mrd->crd", select.astype(bf16), local_regions, preferred_element_type=f32
    ).astype(bf16)
    seq_rows = jnp.concatenate([text_embed.reshape(captions, text_len, width), caption_regions], 1)
    region_count = jnp.sum(jnp.where(select, region_counts[None, :], 0), 1)
    place = jnp.arange(seq_len, dtype=jnp.int32)[None, :]
    valid_slot = jnp.where(
        place < text_len, place < caption_lengths[:, None], place - text_len < region_count[:, None]
    )
    flat = seq_rows.reshape(row_count, width)
    flat_wide = flat.astype(f32)
    qkv = jnp.dot(flat, w_qkv, preferred_element_type=f32)
    query_low = (
        (qkv[:, :width] + qv_bias[:width]).astype(bf16).reshape(captions, seq_len, HEADS, HEAD)
    )
    key_low = qkv[:, width : 2 * width].astype(bf16).reshape(captions, seq_len, HEADS, HEAD)
    value_low = (
        (qkv[:, 2 * width :] + qv_bias[width:]).astype(bf16).reshape(captions, seq_len, HEADS, HEAD)
    )
    key_mask = valid_slot[:, None, None, :]

    def masked_scores():
        scores = (
            jnp.einsum("cqhe,ckhe->chqk", query_low, key_low, preferred_element_type=f32) * 0.125
        )
        return jnp.where(key_mask, scores, -1e30)

    masked = masked_scores()
    top = jnp.max(masked, -1, keepdims=True)
    log_total = top + jnp.log(jnp.sum(jnp.exp(masked - top), -1, keepdims=True))
    probs_low = jnp.exp(masked - log_total).astype(bf16)
    context_low = (
        jnp.einsum("chqk,ckhe->cqhe", probs_low, value_low, preferred_element_type=f32)
        .astype(bf16)
        .reshape(row_count, width)
    )
    attn_out = jnp.dot(context_low, w_out, preferred_element_type=f32) + out_bias
    hidden, attn_normed, attn_inv = layer_norm(flat_wide + attn_out, attn_gain, attn_shift)
    hidden_low = hidden.astype(bf16)
    upper = jnp.dot(hidden_low, w_up, preferred_element_type=f32) + up_bias
    act_low = jax.nn.gelu(upper, approximate=False).astype(bf16)
    ffn_out = jnp.dot(act_low, w_down, preferred_element_type=f32) + down_bias
    final, ffn_normed, ffn_inv = layer_norm(hidden + ffn_out, ffn_gain, ffn_shift)
    row_mask = valid_slot.reshape(-1, 1).astype(f32)
    out_rows = (final * row_mask).astype(bf16)
    stats = jnp.stack(
        [
            jnp.sum(row_mask * flat_wide * flat_wide),
            jnp.sum(row_mask * attn_out * attn_out),
            jnp.sum(row_mask * ffn_out * ffn_out),
            jnp.sum(row_mask),
        ]
    )
    out_cot = out_grad.astype(f32) * row_mask
    g_ffn_gain = jnp.sum(out_cot * ffn_normed, 0)
    g_ffn_shift = jnp.sum(out_cot, 0)
    d_second = norm_back(out_cot, ffn_normed, ffn_inv, ffn_gain)
    d_ffn_low = d_second.astype(bf16)
    g_down_bias = col_sum(d_ffn_low)
    g_w_down = jnp.einsum("rf,rd->fd", act_low, d_ffn_low, preferred_element_type=f32)
    d_act = jnp.einsum("rd,fd->rf", d_ffn_low, w_down, preferred_element_type=f32)
    slope = (
        0.5 * (1.0 + jax.scipy.special.erf(upper * inv_sqrt_two))
        + upper * jnp.exp(-0.5 * upper * upper) * inv_sqrt_tau
    )
    d_upper_low = (d_act * slope).astype(bf16)
    g_up_bias = col_sum(d_upper_low)
    g_w_up = jnp.einsum("rd,rf->df", hidden_low, d_upper_low, preferred_element_type=f32)
    d_hidden = d_second + jnp.einsum("rf,df->rd", d_upper_low, w_up, preferred_element_type=f32)
    g_attn_gain = jnp.sum(d_hidden * attn_normed, 0)
    g_attn_shift = jnp.sum(d_hidden, 0)
    d_resid = norm_back(d_hidden, attn_normed, attn_inv, attn_gain)
    d_attn_low = d_resid.astype(bf16)
    g_out_bias = col_sum(d_attn_low)
    g_w_out = jnp.einsum("rd,re->de", context_low, d_attn_low, preferred_element_type=f32)
    d_context_low = (
        jnp.einsum("re,de->rd", d_attn_low, w_out, preferred_element_type=f32)
        .astype(bf16)
        .reshape(captions, seq_len, HEADS, HEAD)
    )
    probs_again = jnp.exp(masked_scores() - log_total)
    d_probs = jnp.einsum("cqhe,ckhe->chqk", d_context_low, value_low, preferred_element_type=f32)
    inner = jnp.sum(d_probs * probs_again, -1, keepdims=True)
    d_scores_low = (probs_again * (d_probs - inner)).astype(bf16)
    d_query = (
        (jnp.einsum("chqk,ckhe->cqhe", d_scores_low, key_low, preferred_element_type=f32) * 0.125)
        .astype(bf16)
        .reshape(row_count, width)
    )
    d_key = (
        (jnp.einsum("chqk,cqhe->ckhe", d_scores_low, query_low, preferred_element_type=f32) * 0.125)
        .astype(bf16)
        .reshape(row_count, width)
    )
    d_value = (
        jnp.einsum("chqk,cqhe->ckhe", probs_low, d_context_low, preferred_element_type=f32)
        .astype(bf16)
        .reshape(row_count, width)
    )
    d_qkv = jnp.concatenate([d_query, d_key, d_value], 1)
    g_qv_bias = jnp.concatenate([col_sum(d_query), col_sum(d_value)], 0)
    g_w_qkv = jnp.einsum("rd,rk->dk", flat, d_qkv, preferred_element_type=f32)
    d_flat = jnp.einsum("rk,dk->rd", d_qkv, w_qkv, preferred_element_type=f32) + d_resid
    d_seq = d_flat.reshape(captions, seq_len, width)
    text_grad = d_seq[:, :text_len].reshape(captions * text_len, width)
    d_images = jnp.einsum(
        "cm,crd->mrd", select.astype(f32), d_seq[:, text_len:], precision=lax.Precision.HIGHEST
    )
    d_image_low = d_images.reshape(region_dev, width).astype(bf16)
    back_message = jnp.zeros_like(d_image_low).at[flat_source].set(d_image_low)
    returned = lax.all_to_all(back_message, ("dp", "enc"), split_axis=0, concat_axis=0, tiled=True)
    d_region = returned[flat_target].astype(f32)
    g_visual_shift = jnp.sum(d_region, 0)
    g_visual_gain = jnp.sum(d_region * vis_normed, 0)
    d_pre_low = norm_back(d_region, vis_normed, vis_inv, visual_gain).astype(bf16)
    g_visual_bias = col_sum(d_pre_low)
    g_w_visual = jnp.einsum("rf,rd->fd", region_features, d_pre_low, preferred_element_type=f32)
    feature_grad = jnp.einsum("rd,fd->rf", d_pre_low, w_visual, preferred_element_type=f32)
    g_w_box = jnp.einsum("rd,br->db", d_pre_low, boxes, preferred_element_type=f32)
    box_grad = jnp.einsum("rd,db->br", d_pre_low, w_box, preferred_element_type=f32)
    groups = lax.axis_size("dp")
    low = lambda t: t.astype(bf16)

    def cols(whole):
        return whole.reshape(groups, -1)

    smalls = jnp.concatenate(
        [
            cols(g_visual_bias),
            cols(g_visual_gain),
            cols(g_visual_shift),
            cols(g_out_bias),
            cols(g_attn_gain),
            cols(g_attn_shift),
            cols(g_down_bias),
            cols(g_ffn_gain),
            cols(g_ffn_shift),
            cols(g_qv_bias),
            cols(g_up_bias),
            cols(g_w_box),
        ],
        1,
    )
    quarter = smalls.shape[1] // 4
    smalls = smalls.reshape(groups, 4, quarter)
    smalls = jnp.concatenate([smalls, jnp.broadcast_to(stats, (groups, 4, 4))], 2)
    smalls = jnp.pad(smalls, ((0, 0), (0, 0), (0, 8 * (width // 2) - quarter - 4)))
    smalls = smalls.reshape(groups, 2, 2, 8, width // 2).transpose(0, 1, 3, 2, 4)
    smalls = smalls.reshape(groups, 2, 8, width)

    vis_rows = g_w_visual.shape[0] // groups // 2
    vis = low(g_w_visual).reshape(groups, 2, vis_rows, width)
    vis = jnp.concatenate([vis, low(smalls)], 2).reshape(-1, width)
    down = low(g_w_down)
    up = low(g_w_up)
    qkvo = jnp.concatenate([low(g_w_qkv), low(g_w_out)], 1)
    down = reduce_tall(down, 0)
    up = reduce_wide(up, 1)
    qkvo = reduce_wide(qkvo, 0)
    vis = reduce_tall(vis, 1)
    vis = vis.reshape(2, vis_rows + 8, width)
    share_vis = vis[:, :vis_rows].reshape(-1, width)
    tail = vis[:, vis_rows:].reshape(2, 8, 2, width // 2).transpose(0, 2, 1, 3)
    tail = tail.reshape(4, 4 * width)
    total = tail[0, quarter : quarter + 4]
    rms_values = jnp.sqrt(total[:3] / (total[3] * width))
    tail = tail[:, :quarter].reshape(-1)
    small = []
    at = 0
    for size in [width // groups] * 9 + [2 * width // groups, 4 * width // groups, 4 * width // groups]:
        small.append(tail[at : at + size])
        at += size
    return (
        out_rows,
        text_grad,
        feature_grad,
        box_grad,
        rms_values,
        share_vis,
        small[11].reshape(-1, 4),
        small[0],
        small[1],
        small[2],
        qkvo[:, : 3 * width],
        small[9],
        qkvo[:, 3 * width :],
        small[3],
        small[4],
        small[5],
        up,
        small[10],
        down,
        small[6],
        small[7],
        small[8],
    )


def device_bit(bit):
    me = lax.axis_index("dp") * lax.axis_size("enc") + lax.axis_index("enc")
    return lax.rem(me // bit, 2)


def swap(values, bit):
    count = lax.axis_size("dp") * lax.axis_size("enc")
    return lax.ppermute(values, ("dp", "enc"), [(i, i ^ bit) for i in range(count)])


def halve(values, bit, axis):
    mine = device_bit(bit)
    size = values.shape[axis] // 2
    sent = lax.dynamic_slice_in_dim(values, (1 - mine) * size, size, axis)
    kept = lax.dynamic_slice_in_dim(values, mine * size, size, axis)
    return kept + swap(sent, bit)


def halve_lead(values, bit, axis):
    mine = device_bit(bit)
    sent = lax.dynamic_index_in_dim(values, 1 - mine, axis, keepdims=False)
    kept = lax.dynamic_index_in_dim(values, mine, axis, keepdims=False)
    return kept + swap(sent, bit)


def double(values, bit, axis):
    mine = device_bit(bit)
    other = swap(values, bit)
    low_half = jnp.where(mine == 0, values, other)
    high_half = jnp.where(mine == 0, other, values)
    return jnp.concatenate([low_half, high_half], axis)


def reduce_tall(values, first):
    groups = lax.axis_size("dp")
    bits = groups.bit_length() - 1
    rows = values.shape[0] // groups // 2
    values = halve(values, 1, 1)
    width = values.shape[1]
    values = values.reshape((2,) * (bits + 1) + (rows, width))
    if first == 0:
        values = halve_lead(values, 2, bits)
        values = halve_lead(values, 4, bits - 1)
    else:
        values = halve_lead(values, 4, bits - 1)
        values = halve_lead(values, 2, bits - 1)
    for b in range(1, bits):
        values = halve_lead(values, 4 << b, bits - 1 - b)
    values = double(values, 2, 0)
    return double(values, 1, 1).astype(jnp.float32)


def reduce_wide(values, first):
    groups = lax.axis_size("dp")
    bits = groups.bit_length() - 1
    rows = values.shape[0] // groups
    values = halve(values, 1, 1)

    def by_row(values, b):
        shape = values.shape
        values = values.reshape((2,) * (bits - b) + (rows, shape[-1]))
        return halve_lead(values, 4 << b, bits - 1 - b)

    if first == 0:
        values = halve(values, 2, 1)
        values = by_row(values, 0)
    else:
        values = by_row(values, 0)
        values = halve(values, 2, values.ndim - 1)
    for b in range(1, bits):
        values = by_row(values, b)
    values = double(values, 2, 1)
    return double(values, 1, 1).astype(jnp.float32)


def solution(mesh):
    return jax.shard_map(
        on_device,
        mesh=mesh,
        in_specs=(
            P(("dp", "enc"), None),
            P(("dp", "enc"), None),
            P(None, ("dp", "enc")),
            P(("dp", "enc")),
            P(("dp", "enc")),
            P(("dp", "enc")),
            P(("dp", "enc"), None),
            P(("dp", "enc"), None),
            P(),
            P(),
            P(),
            P(),
            P(),
            P(),
            P(),
            P(),
            P(),
            P(),
            P(),
            P(),
            P(),
            P(),
            P(),
            P(),
            P(),
            P(("dp", "enc"), None),
        ),
        out_specs=(
            P(("dp", "enc"), None),
            P(("dp", "enc"), None),
            P(("dp", "enc"), None),
            P(None, ("dp", "enc")),
            P(),
            P("dp", None),
            P("dp", None),
            P("dp"),
            P("dp"),
            P("dp"),
            P("dp", None),
            P("dp"),
            P("dp", None),
            P("dp"),
            P("dp"),
            P("dp"),
            P("dp", None),
            P("dp"),
            P("dp", None),
            P("dp"),
            P("dp"),
            P("dp"),
        ),
        check_vma=False,
    )
```

```python
import jax
import jax.numpy as jnp
from jax import lax
from jax.experimental import pallas as pl
from jax.experimental.pallas import tpu as pltpu
from jax.sharding import PartitionSpec as P

HEADS = 12
HEAD = 64
epsilon = 1e-12
inv_sqrt_two = 0.7071067811865476
inv_sqrt_tau = 0.3989422804014327
f32 = jnp.float32
bf16 = jnp.bfloat16
NN = (((1,), (0,)), ((), ()))
NT = (((1,), (1,)), ((), ()))
TN = (((0,), (0,)), ((), ()))


def mm(a, b, dims=NN):
    return lax.dot_general(a, b, dims, preferred_element_type=f32)


def params(limit=56):
    return pltpu.CompilerParams(
        dimension_semantics=("arbitrary",), vmem_limit_bytes=limit << 20
    )


def whole(shape):
    return pl.BlockSpec(shape, lambda i, *s: (0,) * len(shape), pipeline_mode=pl.Buffered(1))


def shape(dims, kind=f32):
    return jax.ShapeDtypeStruct(dims, kind)


def norm_parts(values):
    centre = values - jnp.mean(values, -1, keepdims=True)
    inv_std = lax.rsqrt(jnp.mean(centre * centre, -1, keepdims=True) + epsilon)
    return centre * inv_std, inv_std


def norm_back(grad, normed, inv_std, gain):
    scaled = grad * gain
    return inv_std * (
        scaled
        - jnp.mean(scaled, -1, keepdims=True)
        - normed * jnp.mean(scaled * normed, -1, keepdims=True)
    )


def row_sum(values):
    return jnp.sum(values, 0, keepdims=True)


def one_hot(index_row, count):
    rows = lax.broadcasted_iota(jnp.int32, (count, index_row.shape[1]), 0)
    return jnp.where(rows == index_row, 1.0, 0.0).astype(bf16)


def region_forward(features, boxes, target, w_visual, w_box_t, bias, gain, shift):
    rows, feat = features.shape
    width = w_visual.shape[1]
    steps = 4
    part = feat // steps

    def kernel(f_ref, box_ref, t_ref, wv_ref, wb_ref, b_ref, g_ref, s_ref, m_ref, n_ref, i_ref, acc):
        step = pl.program_id(0)
        partial = mm(f_ref[...], wv_ref[...])

        @pl.when(step == 0)
        def _():
            acc[...] = partial + (mm(box_ref[...], wb_ref[...], TN) + b_ref[...])

        @pl.when(step > 0)
        def _():
            acc[...] += partial

        @pl.when(step == steps - 1)
        def _():
            normed, inv = norm_parts(acc[...])
            n_ref[...] = normed
            i_ref[...] = jnp.broadcast_to(inv, i_ref.shape)
            low = (normed * g_ref[...] + s_ref[...]).astype(bf16)
            m_ref[...] = mm(one_hot(t_ref[...], rows), low).astype(bf16)

    return pl.pallas_call(
        kernel,
        grid=(steps,),
        in_specs=[
            pl.BlockSpec((rows, part), lambda i: (0, i)),
            whole(boxes.shape),
            whole((1, rows)),
            pl.BlockSpec((part, width), lambda i: (i, 0)),
            whole(w_box_t.shape),
            whole((1, width)),
            whole((1, width)),
            whole((1, width)),
        ],
        out_specs=[whole((rows, width)), whole((rows, width)), whole((rows, 128))],
        out_shape=[shape((rows, width), bf16), shape((rows, width)), shape((rows, 128))],
        scratch_shapes=[pltpu.VMEM((rows, width), f32)],
        compiler_params=params(24),
        name="region_forward",
    )(features, boxes, target, w_visual, w_box_t, bias, gain, shift)


def text_qkv(text, w_qkv, qv_bias):
    rows, width = text.shape

    def kernel(t_ref, w_ref, b_ref, o_ref):
        step = pl.program_id(0)
        bias = b_ref[...] * jnp.where(step == 1, 0.0, 1.0)
        o_ref[...] = (mm(t_ref[...], w_ref[...]) + bias).astype(bf16)

    return pl.pallas_call(
        kernel,
        grid=(3,),
        in_specs=[
            whole((rows, width)),
            pl.BlockSpec((width, width), lambda i: (0, i)),
            pl.BlockSpec((1, width), lambda i: (0, i // 2)),
        ],
        out_specs=pl.BlockSpec((rows, width), lambda i: (0, i)),
        out_shape=shape((rows, 3 * width), bf16),
        compiler_params=params(24),
        name="text_qkv",
    )(text, w_qkv, qv_bias)


def forward(
    scalars, text, text_low, arrived, source, out_grad, w_qkv, qv_bias, w_out, out_bias,
    attn_gain, attn_shift, w_up, up_bias, w_down, down_bias, ffn_gain, ffn_shift, dims,
):
    captions, images = dims
    width = text.shape[1]
    text_len = text.shape[0] // captions
    slots = arrived.shape[0]
    regions = slots // images
    seq = text_len + regions
    rows = captions * seq
    ff = w_up.shape[1]
    half = width // 2
    parts = 4
    part = ff // parts
    grid = captions + 2 * parts

    def kernel(
        sc_ref, t_ref, tq_ref, a_ref, src_ref, og_ref, wq_hbm, qvb_ref, wo_hbm, ob_ref, ag_ref, as_ref,
        wu_hbm, ub_ref, wd_hbm, db_ref, fg_ref, fs_ref,
        out_ref, x_ref, qkv_ref, probs_ref, ctx_ref, an_ref, ai_ref, hid_ref, slope_ref, ds_ref, df_ref,
        sums_ref, send_ref, keep_ref,
        regs, rqkv, act_all, dffn_all, wq, wo, wu, wd, sems,
    ):
        step = pl.program_id(0)

        places = [(wq_hbm, wq), (wo_hbm, wo), (wu_hbm, wu), (wd_hbm, wd)]

        def copy(at):
            return pltpu.make_async_copy(*places[at], sems.at[at])

        @pl.when(step == 0)
        def _():
            for at in range(len(places)):
                copy(at).start()
            sums_ref[...] = jnp.zeros_like(sums_ref)
            local = mm(one_hot(src_ref[...], slots), a_ref[...], TN).astype(bf16)
            regs[...] = local
            copy(0).wait()
            for part_id in range(3):
                at = slice(part_id * width, (part_id + 1) * width)
                got = mm(local, wq[:, at])
                if part_id == 0:
                    got = got + qvb_ref[:, :width]
                if part_id == 2:
                    got = got + qvb_ref[:, width:]
                rqkv[:, at] = got.astype(bf16)

        @pl.when(step < captions)
        def _():
            image = sc_ref[step]
            length = sc_ref[captions + step]
            count = sc_ref[2 * captions + image]
            at = pl.ds(pl.multiple_of(image * regions, regions), regions)
            x_ref[:text_len, :] = t_ref[...]
            x_ref[text_len:, :] = regs[at, :]
            qkv_ref[:text_len, :] = tq_ref[...]
            qkv_ref[text_len:, :] = rqkv[at, :]
            lane = lax.broadcasted_iota(jnp.int32, (1, seq), 1)
            key_end = jnp.where(lane < text_len, length, text_len + count)
            key_bias = jnp.where(lane < key_end, 0.0, -1e30)
            place = lax.broadcasted_iota(jnp.int32, (seq, 1), 0)
            row_end = jnp.where(place < text_len, length, text_len + count)
            row_mask = jnp.where(place < row_end, 1.0, 0.0)
            pair_lane = lax.broadcasted_iota(jnp.int32, (1, 2 * HEAD), 1)
            first = pair_lane < HEAD
            scale = [
                jnp.where(first, 0.125, 0.0).astype(bf16),
                jnp.where(first, 0.0, 0.125).astype(bf16),
            ]
            for pair in range(HEADS // 2):
                lo = pair * 2 * HEAD
                q = qkv_ref[:, lo : lo + 2 * HEAD]
                k = qkv_ref[:, width + lo : width + lo + 2 * HEAD]
                v = qkv_ref[:, 2 * width + lo : 2 * width + lo + 2 * HEAD]
                outs = []
                for one in range(2):
                    scores = mm(q * scale[one], k, NT) + key_bias
                    top = jnp.max(scores, -1, keepdims=True)
                    raised = jnp.exp(scores - top)
                    total = jnp.sum(raised, -1, keepdims=True)
                    low = (raised * (1.0 / total)).astype(bf16)
                    probs_ref[2 * pair + one] = low
                    outs.append(mm(low, v))
                ctx_ref[:, lo : lo + 2 * HEAD] = jnp.where(first, outs[0], outs[1]).astype(bf16)

            @pl.when(step == 0)
            def _():
                copy(1).wait()

            x_wide = x_ref[...].astype(f32)
            attn_out = mm(ctx_ref[...], wo[...]) + ob_ref[...]
            normed, inv = norm_parts(x_wide + attn_out)
            an_ref[...] = normed
            ai_ref[...] = jnp.broadcast_to(inv, ai_ref.shape)
            hidden = normed * ag_ref[...] + as_ref[...]
            hidden_low = hidden.astype(bf16)
            hid_ref[...] = hidden_low

            @pl.when(step == 0)
            def _():
                copy(2).wait()

            here = pl.ds(pl.multiple_of(step * seq, seq), seq)
            for piece in range(parts):
                at = slice(piece * part, (piece + 1) * part)
                upper = mm(hidden_low, wu[:, at]) + ub_ref[:, at]
                phi = 0.5 * (1.0 + lax.erf(upper * inv_sqrt_two))
                act_all[here, at] = (upper * phi).astype(bf16)
                slope = phi + upper * jnp.exp(-0.5 * upper * upper) * inv_sqrt_tau
                slope_ref[:, at] = slope.astype(bf16)

            @pl.when(step == 0)
            def _():
                copy(3).wait()

            ffn_out = mm(act_all[here, :], wd[...]) + db_ref[...]
            ffn_normed, ffn_inv = norm_parts(hidden + ffn_out)
            out_ref[...] = ((ffn_normed * fg_ref[...] + fs_ref[...]) * row_mask).astype(bf16)
            cot = og_ref[...].astype(f32) * row_mask
            second = norm_back(cot, ffn_normed, ffn_inv, fg_ref[...])
            ds_ref[...] = second
            low = second.astype(bf16)
            df_ref[...] = low
            dffn_all[here, :] = low
            for at, value in enumerate(
                (
                    cot * ffn_normed,
                    cot,
                    low.astype(f32),
                    row_mask * x_wide * x_wide,
                    row_mask * attn_out * attn_out,
                    row_mask * ffn_out * ffn_out,
                    jnp.broadcast_to(row_mask, (seq, width)),
                )
            ):
                sums_ref[at : at + 1, :] += row_sum(value)

        def gradient(to_ref, piece, side):
            cols = pl.ds(pl.multiple_of(side * half, half), half)
            acts = pl.ds(pl.multiple_of(piece * part, part), part)
            to_ref[...] = mm(act_all[:, acts], dffn_all[:, cols], TN).astype(bf16)

        core = sc_ref[2 * captions + images]

        @pl.when((step >= captions) & (step < captions + parts))
        def _():
            gradient(send_ref, step - captions, 1 - core)

        @pl.when(step >= captions + parts)
        def _():
            gradient(keep_ref, step - captions - parts, core)

    def rowwise(size, cols):
        return pl.BlockSpec((size, cols), lambda i, s: (jnp.minimum(i, captions - 1), 0))

    anywhere = pl.BlockSpec(memory_space=pl.ANY)
    return pl.pallas_call(
        kernel,
        grid_spec=pltpu.PrefetchScalarGridSpec(
            num_scalar_prefetch=1,
            grid=(grid,),
            in_specs=[
                rowwise(text_len, width),
                rowwise(text_len, 3 * width),
                whole((slots, width)),
                whole((1, slots)),
                rowwise(seq, width),
                anywhere,
                whole((1, 2 * width)),
                anywhere,
                whole((1, width)),
                whole((1, width)),
                whole((1, width)),
                anywhere,
                whole((1, ff)),
                anywhere,
                whole((1, width)),
                whole((1, width)),
                whole((1, width)),
            ],
            out_specs=[
                rowwise(seq, width),
                rowwise(seq, width),
                rowwise(seq, 3 * width),
                pl.BlockSpec((HEADS, seq, seq), lambda i, s: (jnp.minimum(i, captions - 1), 0, 0)),
                rowwise(seq, width),
                rowwise(seq, width),
                rowwise(seq, 128),
                rowwise(seq, width),
                rowwise(seq, ff),
                rowwise(seq, width),
                rowwise(seq, width),
                whole((8, width)),
                pl.BlockSpec((part, half), lambda i, s: (jnp.clip(i - captions, 0, parts - 1), 0)),
                pl.BlockSpec((part, half), lambda i, s: (jnp.clip(i - captions - parts, 0, parts - 1), 0)),
            ],
            scratch_shapes=[
                pltpu.VMEM((slots, width), bf16),
                pltpu.VMEM((slots, 3 * width), bf16),
                pltpu.VMEM((rows, ff), bf16),
                pltpu.VMEM((rows, width), bf16),
                pltpu.VMEM(w_qkv.shape, bf16),
                pltpu.VMEM(w_out.shape, bf16),
                pltpu.VMEM(w_up.shape, bf16),
                pltpu.VMEM(w_down.shape, bf16),
                pltpu.SemaphoreType.DMA((4,)),
            ],
        ),
        out_shape=[
            shape((rows, width), bf16),
            shape((rows, width), bf16),
            shape((rows, 3 * width), bf16),
            shape((captions * HEADS, seq, seq), bf16),
            shape((rows, width), bf16),
            shape((rows, width)),
            shape((rows, 128)),
            shape((rows, width), bf16),
            shape((rows, ff), bf16),
            shape((rows, width)),
            shape((rows, width), bf16),
            shape((8, width)),
            shape((ff, half), bf16),
            shape((ff, half), bf16),
        ],
        compiler_params=params(60),
        name="forward",
    )(
        scalars, text, text_low, arrived, source, out_grad, w_qkv, qv_bias, w_out, out_bias,
        attn_gain, attn_shift, w_up, up_bias, w_down, down_bias, ffn_gain, ffn_shift,
    )


def ffn_backward(core, d_ffn, d_second, slope, hidden_low, attn_normed, attn_inv, w_down, w_up, attn_gain, captions):
    rows, width = d_ffn.shape
    seq = rows // captions
    ff = w_up.shape[1]
    parts = 4
    part = ff // parts
    cols = ff // (2 * parts)

    def kernel(
        c_ref, df_ref, ds_ref, sl_ref, hid_ref, an_ref, ai_ref, wd_hbm, wu_hbm, ag_ref,
        dr_ref, da_ref, sums_ref, up_ref, send_ref, keep_ref, dup, wd, wu, sems,
    ):
        step = pl.program_id(0)

        places = [(wd_hbm, wd), (wu_hbm, wu)]

        def copy(at):
            return pltpu.make_async_copy(*places[at], sems.at[at])

        @pl.when(step == 0)
        def _():
            for at in range(len(places)):
                copy(at).start()
            sums_ref[...] = jnp.zeros_like(sums_ref)
            up_ref[...] = jnp.zeros_like(up_ref)
            copy(0).wait()

        @pl.when(step < captions)
        def _():
            here = pl.ds(pl.multiple_of(step * seq, seq), seq)
            d_low = df_ref[...]
            for piece in range(parts):
                at = slice(piece * part, (piece + 1) * part)
                d_act = mm(d_low, wd[at, :], NT)
                low = (d_act * sl_ref[:, at].astype(f32)).astype(bf16)
                dup[here, at] = low
                up_ref[0:1, at] += row_sum(low.astype(f32))

            @pl.when(step == 0)
            def _():
                copy(1).wait()

            d_hidden = ds_ref[...] + mm(dup[here, :], wu[...], NT)
            normed = an_ref[...]
            resid = norm_back(d_hidden, normed, ai_ref[:, 0:1], ag_ref[...])
            dr_ref[...] = resid
            low = resid.astype(bf16)
            da_ref[...] = low
            sums_ref[0:1, :] += row_sum(d_hidden * normed)
            sums_ref[1:2, :] += row_sum(d_hidden)
            sums_ref[2:3, :] += row_sum(low.astype(f32))

        def gradient(to_ref, piece, side):
            at = pl.ds(pl.multiple_of(side * (ff // 2) + piece * cols, 128), cols)
            to_ref[...] = mm(hid_ref[...], dup[:, at], TN).astype(bf16)

        @pl.when((step >= captions) & (step < captions + parts))
        def _():
            gradient(send_ref, step - captions, 1 - c_ref[0])

        @pl.when(step >= captions + parts)
        def _():
            gradient(keep_ref, step - captions - parts, c_ref[0])

    def rowwise(cols):
        return pl.BlockSpec((seq, cols), lambda i, s: (jnp.minimum(i, captions - 1), 0))

    anywhere = pl.BlockSpec(memory_space=pl.ANY)
    return pl.pallas_call(
        kernel,
        grid_spec=pltpu.PrefetchScalarGridSpec(
            num_scalar_prefetch=1,
            grid=(captions + 2 * parts,),
            in_specs=[
                rowwise(width),
                rowwise(width),
                rowwise(ff),
                whole((rows, width)),
                rowwise(width),
                rowwise(128),
                anywhere,
                anywhere,
                whole((1, width)),
            ],
            out_specs=[
                rowwise(width),
                rowwise(width),
                whole((8, width)),
                whole((8, ff)),
                pl.BlockSpec((width, cols), lambda i, s: (0, jnp.clip(i - captions, 0, parts - 1))),
                pl.BlockSpec((width, cols), lambda i, s: (0, jnp.clip(i - captions - parts, 0, parts - 1))),
            ],
            scratch_shapes=[
                pltpu.VMEM((rows, ff), bf16),
                pltpu.VMEM(w_down.shape, bf16),
                pltpu.VMEM(w_up.shape, bf16),
                pltpu.SemaphoreType.DMA((2,)),
            ],
        ),
        out_shape=[
            shape((rows, width)),
            shape((rows, width), bf16),
            shape((8, width)),
            shape((8, ff)),
            shape((width, ff // 2), bf16),
            shape((width, ff // 2), bf16),
        ],
        compiler_params=params(56),
        name="ffn_backward",
    )(core, d_ffn, d_second, slope, hidden_low, attn_normed, attn_inv, w_down, w_up, attn_gain)


def attention_backward(scalars, d_attn, d_resid, probs, qkv, source, w_out, w_qkv, dims):
    captions, images = dims
    rows, width = d_attn.shape
    seq = rows // captions
    slots = source.shape[1]
    regions = slots // images
    text_len = seq - regions

    def kernel(
        sc_ref, da_ref, dr_ref, p_ref, qkv_ref, src_ref, wo_ref, wq_hbm,
        dqkv_ref, text_ref, back_ref, sums_ref, d_img, wq, sem,
    ):
        step = pl.program_id(0)

        def copy():
            return pltpu.make_async_copy(wq_hbm, wq, sem)

        @pl.when(step == 0)
        def _():
            copy().start()
            sums_ref[...] = jnp.zeros_like(sums_ref)
            d_img[...] = jnp.zeros_like(d_img)

        d_ctx = mm(da_ref[...], wo_ref[...], NT).astype(bf16)
        first = lax.broadcasted_iota(jnp.int32, (1, 2 * HEAD), 1) < HEAD
        masks = [jnp.where(first, 1.0, 0.0).astype(bf16), jnp.where(first, 0.0, 1.0).astype(bf16)]
        for pair in range(HEADS // 2):
            lo = pair * 2 * HEAD
            q = qkv_ref[:, lo : lo + 2 * HEAD]
            k = qkv_ref[:, width + lo : width + lo + 2 * HEAD]
            v = qkv_ref[:, 2 * width + lo : 2 * width + lo + 2 * HEAD]
            d_c = d_ctx[:, lo : lo + 2 * HEAD]
            got = []
            for one in range(2):
                low = p_ref[2 * pair + one]
                d_probs = mm(d_c * masks[one], v, NT)
                wide = low.astype(f32)
                both = wide * d_probs
                inner = jnp.sum(both, -1, keepdims=True)
                d_scores = (both - wide * inner).astype(bf16)
                got.append(
                    (mm(d_scores, k) * 0.125, mm(d_scores, q, TN) * 0.125, mm(low, d_c, TN))
                )
            for at in range(3):
                dqkv_ref[:, at * width + lo : at * width + lo + 2 * HEAD] = jnp.where(
                    first, got[0][at], got[1][at]
                ).astype(bf16)

        @pl.when(step == 0)
        def _():
            copy().wait()

        sums_ref[0:1, :] += row_sum(dqkv_ref[:, :width].astype(f32))
        sums_ref[1:2, :] += row_sum(dqkv_ref[:, 2 * width :].astype(f32))
        d_x = mm(dqkv_ref[...], wq[...], NT) + dr_ref[...]
        text_ref[...] = d_x[:text_len]
        at = pl.ds(pl.multiple_of(sc_ref[step] * regions, regions), regions)
        d_img[at, :] += d_x[text_len:]

        @pl.when(step == captions - 1)
        def _():
            back_ref[...] = mm(one_hot(src_ref[...], slots), d_img[...].astype(bf16)).astype(bf16)

    def rowwise(size, cols):
        return pl.BlockSpec((size, cols), lambda i, s: (i, 0))

    return pl.pallas_call(
        kernel,
        grid_spec=pltpu.PrefetchScalarGridSpec(
            num_scalar_prefetch=1,
            grid=(captions,),
            in_specs=[
                rowwise(seq, width),
                rowwise(seq, width),
                pl.BlockSpec((HEADS, seq, seq), lambda i, s: (i, 0, 0)),
                rowwise(seq, 3 * width),
                whole((1, slots)),
                whole(w_out.shape),
                pl.BlockSpec(memory_space=pl.ANY),
            ],
            out_specs=[
                rowwise(seq, 3 * width),
                rowwise(text_len, width),
                whole((slots, width)),
                whole((8, width)),
            ],
            scratch_shapes=[
                pltpu.VMEM((slots, width), f32),
                pltpu.VMEM(w_qkv.shape, bf16),
                pltpu.SemaphoreType.DMA,
            ],
        ),
        out_shape=[
            shape((rows, 3 * width), bf16),
            shape((captions * text_len, width)),
            shape((slots, width), bf16),
            shape((8, width)),
        ],
        compiler_params=params(48),
        name="attention_backward",
    )(scalars, d_attn, d_resid, probs, qkv, source, w_out, w_qkv)


def qkvo_gradient(core, x, d_qkv, context, d_attn):
    rows, width = x.shape
    cols = width // 2

    def kernel(c_ref, x_ref, dq_ref, ctx_ref, da_ref, send_ref, keep_ref):
        step = pl.program_id(0)
        core_bit = c_ref[0]

        def gradient(to_ref, piece, side):
            block = side * 4 + piece

            @pl.when(block < 6)
            def _():
                to_ref[...] = mm(x_ref[...], dq_ref[...], TN).astype(bf16)

            @pl.when(block >= 6)
            def _():
                to_ref[...] = mm(ctx_ref[...], da_ref[...], TN).astype(bf16)

        @pl.when(step < 4)
        def _():
            gradient(send_ref, step, 1 - core_bit)

        @pl.when(step >= 4)
        def _():
            gradient(keep_ref, step - 4, core_bit)

    def block(i, s):
        return jnp.where(i < 4, (1 - s[0]) * 4 + i, s[0] * 4 + i - 4)

    return pl.pallas_call(
        kernel,
        grid_spec=pltpu.PrefetchScalarGridSpec(
            num_scalar_prefetch=1,
            grid=(8,),
            in_specs=[
                whole((rows, width)),
                pl.BlockSpec((rows, cols), lambda i, s: (0, jnp.minimum(block(i, s), 5))),
                whole((rows, width)),
                pl.BlockSpec((rows, cols), lambda i, s: (0, jnp.maximum(block(i, s) - 6, 0))),
            ],
            out_specs=[
                pl.BlockSpec((width, cols), lambda i, s: (0, jnp.clip(i, 0, 3))),
                pl.BlockSpec((width, cols), lambda i, s: (0, jnp.clip(i - 4, 0, 3))),
            ],
        ),
        out_shape=[shape((width, 2 * width), bf16), shape((width, 2 * width), bf16)],
        compiler_params=params(40),
        name="qkvo_gradient",
    )(core, x, d_qkv, context, d_attn)


def region_backward(core, returned, target, normed, inv, gain, features, boxes, w_visual, w_box_t):
    rows, width = returned.shape
    feat = features.shape[1]
    half = width // 2
    parts = 4
    part = feat // parts
    box = boxes.shape[0]

    def kernel(
        c_ref, r_ref, t_ref, n_ref, i_ref, g_ref, f_ref, box_ref, wv_ref, wb_ref,
        send_ref, keep_ref, fg_ref, bg_ref, sums_ref, dpre,
    ):
        step = pl.program_id(0)

        @pl.when(step == 0)
        def _():
            d_region = mm(one_hot(t_ref[...], rows), r_ref[...], TN)
            normed = n_ref[...]
            low = norm_back(d_region, normed, i_ref[:, 0:1], g_ref[...]).astype(bf16)
            dpre[...] = low
            sums_ref[0:1, :] = row_sum(low.astype(f32))
            sums_ref[1:2, :] = row_sum(d_region * normed)
            sums_ref[2:3, :] = row_sum(d_region)
            sums_ref[3 : 3 + box, :] = mm(box_ref[...], low)
            bg_ref[...] = mm(wb_ref[...], low, NT)

        def gradient(to_ref, side):
            at = pl.ds(pl.multiple_of(side * half, half), half)
            to_ref[...] = mm(f_ref[...], dpre[:, at], TN).astype(bf16)

        @pl.when(step < parts)
        def _():
            gradient(send_ref, 1 - c_ref[0])

        @pl.when(step >= parts)
        def _():
            gradient(keep_ref, c_ref[0])
            fg_ref[...] = mm(dpre[...], wv_ref[...], NT)

    return pl.pallas_call(
        kernel,
        grid_spec=pltpu.PrefetchScalarGridSpec(
            num_scalar_prefetch=1,
            grid=(2 * parts,),
            in_specs=[
                whole((rows, width)),
                whole((1, rows)),
                whole((rows, width)),
                whole((rows, 128)),
                whole((1, width)),
                pl.BlockSpec((rows, part), lambda i, s: (0, lax.rem(i, parts))),
                whole(boxes.shape),
                pl.BlockSpec((part, width), lambda i, s: (jnp.maximum(i - parts, 0), 0)),
                whole(w_box_t.shape),
            ],
            out_specs=[
                pl.BlockSpec((part, half), lambda i, s: (jnp.clip(i, 0, parts - 1), 0)),
                pl.BlockSpec((part, half), lambda i, s: (jnp.clip(i - parts, 0, parts - 1), 0)),
                pl.BlockSpec((rows, part), lambda i, s: (0, jnp.maximum(i - parts, 0))),
                whole((box, rows)),
                whole((8, width)),
            ],
            scratch_shapes=[pltpu.VMEM((rows, width), bf16)],
        ),
        out_shape=[
            shape((feat, half), bf16),
            shape((feat, half), bf16),
            shape((rows, feat)),
            shape((box, rows)),
            shape((8, width)),
        ],
        compiler_params=params(24),
        name="region_backward",
    )(core, returned, target, normed, inv, gain, features, boxes, w_visual, w_box_t)


def device_bit(bit):
    me = lax.axis_index("dp") * lax.axis_size("enc") + lax.axis_index("enc")
    return lax.rem(me // bit, 2)


def swap(values, bit):
    count = lax.axis_size("dp") * lax.axis_size("enc")
    return lax.ppermute(values, ("dp", "enc"), [(i, i ^ bit) for i in range(count)])


def halve(values, bit, axis):
    mine = device_bit(bit)
    size = values.shape[axis] // 2
    sent = lax.dynamic_slice_in_dim(values, (1 - mine) * size, size, axis)
    kept = lax.dynamic_slice_in_dim(values, mine * size, size, axis)
    return kept + swap(sent, bit)


def halve_lead(values, bit, axis):
    mine = device_bit(bit)
    sent = lax.dynamic_index_in_dim(values, 1 - mine, axis, keepdims=False)
    kept = lax.dynamic_index_in_dim(values, mine, axis, keepdims=False)
    return kept + swap(sent, bit)


def double(values, bit, axis):
    mine = device_bit(bit)
    other = swap(values, bit)
    low_half = jnp.where(mine == 0, values, other)
    high_half = jnp.where(mine == 0, other, values)
    return jnp.concatenate([low_half, high_half], axis)


def reduce_tall(sent, kept, first):
    groups = lax.axis_size("dp")
    bits = groups.bit_length() - 1
    values = kept + swap(sent, 1)
    rows = values.shape[0] // groups // 2
    values = values.reshape((2,) * (bits + 1) + (rows, values.shape[1]))
    if first == 0:
        values = halve_lead(values, 2, bits)
        values = halve_lead(values, 4, bits - 1)
    else:
        values = halve_lead(values, 4, bits - 1)
        values = halve_lead(values, 2, bits - 1)
    for b in range(1, bits):
        values = halve_lead(values, 4 << b, bits - 1 - b)
    values = double(values, 2, 0)
    return double(values, 1, 1).astype(f32)


def reduce_wide(sent, kept, first):
    groups = lax.axis_size("dp")
    bits = groups.bit_length() - 1
    values = kept + swap(sent, 1)
    rows = values.shape[0] // groups

    def by_row(values, b):
        values = values.reshape((2,) * (bits - b) + (rows, values.shape[-1]))
        return halve_lead(values, 4 << b, bits - 1 - b)

    if first == 0:
        values = halve(values, 2, 1)
        values = by_row(values, 0)
    else:
        values = by_row(values, 0)
        values = halve(values, 2, values.ndim - 1)
    for b in range(1, bits):
        values = by_row(values, b)
    values = double(values, 2, 1)
    return double(values, 1, 1).astype(f32)


def all_sum(values):
    bit = 1
    while bit < lax.axis_size("dp") * lax.axis_size("enc"):
        values = values + swap(values, bit)
        bit *= 2
    return values


def on_device(
    text_embed,
    region_features,
    boxes,
    caption_image,
    caption_lengths,
    region_counts,
    region_target,
    region_source,
    w_visual,
    w_box,
    visual_bias,
    visual_gain,
    visual_shift,
    w_qkv,
    qv_bias,
    w_out,
    out_bias,
    attn_gain,
    attn_shift,
    w_up,
    up_bias,
    w_down,
    down_bias,
    ffn_gain,
    ffn_shift,
    out_grad,
):
    width = text_embed.shape[1]
    captions = caption_image.shape[0]
    images = region_counts.shape[0]
    dims = (captions, images)
    axes = ("dp", "enc")
    core = device_bit(1).astype(jnp.int32).reshape(1)
    scalars = jnp.concatenate([caption_image, caption_lengths, region_counts, core])
    w_box_t = w_box.T
    row = lambda v: v.reshape(1, -1)

    message, vis_normed, vis_inv = region_forward(
        region_features, boxes, region_target, w_visual, w_box_t,
        row(visual_bias), row(visual_gain), row(visual_shift),
    )
    arrived = lax.all_to_all(message, axes, split_axis=0, concat_axis=0, tiled=True)
    text_low = text_qkv(text_embed, w_qkv, row(qv_bias))
    (
        out_rows, x, qkv, probs, context, attn_normed, attn_inv, hidden_low, slope, d_second, d_ffn,
        sums_forward, down_sent, down_kept,
    ) = forward(
        scalars, text_embed, text_low, arrived, region_source, out_grad, w_qkv, row(qv_bias), w_out,
        row(out_bias), row(attn_gain), row(attn_shift), w_up, row(up_bias), w_down, row(down_bias),
        row(ffn_gain), row(ffn_shift), dims,
    )
    d_resid, d_attn, sums_ffn, sums_up, up_sent, up_kept = ffn_backward(
        core, d_ffn, d_second, slope, hidden_low, attn_normed, attn_inv, w_down, w_up, row(attn_gain), captions
    )
    d_qkv, text_grad, back_message, sums_attn = attention_backward(
        scalars, d_attn, d_resid, probs, qkv, region_source, w_out, w_qkv, dims
    )
    returned = lax.all_to_all(back_message, axes, split_axis=0, concat_axis=0, tiled=True)
    qkvo_sent, qkvo_kept = qkvo_gradient(core, x, d_qkv, context, d_attn)
    vis_sent, vis_kept, feature_grad, box_grad, sums_vis = region_backward(
        core, returned, region_target, vis_normed, vis_inv, row(visual_gain), region_features, boxes, w_visual, w_box_t
    )
    down = reduce_tall(down_sent, down_kept, 0)
    up = reduce_wide(up_sent, up_kept, 1)
    qkvo = reduce_wide(qkvo_sent, qkvo_kept, 0)
    share_vis = reduce_tall(vis_sent, vis_kept, 1)
    smalls = jnp.concatenate(
        [sums_forward, sums_ffn, sums_up[0].reshape(-1, width), sums_attn[:2], sums_vis], 0
    )
    smalls = all_sum(smalls)
    sums = jnp.sum(smalls[3:7], 1)
    rms_values = jnp.sqrt(sums[:3] / sums[3])
    groups = lax.axis_size("dp")
    position = lax.axis_index("dp")

    def share(values, axis=0):
        size = values.shape[axis] // groups
        return lax.dynamic_slice_in_dim(values, position * size, size, axis)

    base = 16 + w_up.shape[1] // width
    return (
        out_rows,
        text_grad,
        feature_grad,
        box_grad,
        rms_values,
        share_vis,
        share(smalls[base + 5 : base + 9], 1).T,
        share(smalls[base + 2]),
        share(smalls[base + 3]),
        share(smalls[base + 4]),
        qkvo[:, : 3 * width],
        share(smalls[base : base + 2].reshape(-1)),
        qkvo[:, 3 * width :],
        share(smalls[10]),
        share(smalls[8]),
        share(smalls[9]),
        up,
        share(smalls[16:base].reshape(-1)),
        down,
        share(smalls[2]),
        share(smalls[0]),
        share(smalls[1]),
    )


def solution(mesh):
    return jax.shard_map(
        on_device,
        mesh=mesh,
        in_specs=(
            P(("dp", "enc"), None),
            P(("dp", "enc"), None),
            P(None, ("dp", "enc")),
            P(("dp", "enc")),
            P(("dp", "enc")),
            P(("dp", "enc")),
            P(("dp", "enc"), None),
            P(("dp", "enc"), None),
            P(),
            P(),
            P(),
            P(),
            P(),
            P(),
            P(),
            P(),
            P(),
            P(),
            P(),
            P(),
            P(),
            P(),
            P(),
            P(),
            P(),
            P(("dp", "enc"), None),
        ),
        out_specs=(
            P(("dp", "enc"), None),
            P(("dp", "enc"), None),
            P(("dp", "enc"), None),
            P(None, ("dp", "enc")),
            P(),
            P("dp", None),
            P("dp", None),
            P("dp"),
            P("dp"),
            P("dp"),
            P("dp", None),
            P("dp"),
            P("dp", None),
            P("dp"),
            P("dp"),
            P("dp"),
            P("dp", None),
            P("dp"),
            P("dp", None),
            P("dp"),
            P("dp"),
            P("dp"),
        ),
        check_vma=False,
    )
```

```python
import jax
import jax.numpy as jnp
from jax import lax
from jax.experimental import pallas as pl
from jax.experimental.pallas import tpu as pltpu
from jax.sharding import PartitionSpec as P

HEADS = 12
HEAD = 64
epsilon = 1e-12
inv_sqrt_two = 0.7071067811865476
inv_sqrt_tau = 0.3989422804014327
f32 = jnp.float32
bf16 = jnp.bfloat16
NN = (((1,), (0,)), ((), ()))
NT = (((1,), (1,)), ((), ()))
TN = (((0,), (0,)), ((), ()))


def mm(a, b, dims=NN):
    return lax.dot_general(a, b, dims, preferred_element_type=f32)


def params(limit=56):
    return pltpu.CompilerParams(
        dimension_semantics=("arbitrary",), vmem_limit_bytes=limit << 20
    )


def whole(shape):
    return pl.BlockSpec(shape, lambda i, *s: (0,) * len(shape), pipeline_mode=pl.Buffered(1))


def vec(size):
    return pl.BlockSpec((size,), lambda i, *s: (0,))


def shape(dims, kind=f32):
    return jax.ShapeDtypeStruct(dims, kind)


def norm_parts(values):
    centre = values - jnp.mean(values, -1, keepdims=True)
    inv_std = lax.rsqrt(jnp.mean(centre * centre, -1, keepdims=True) + epsilon)
    return centre * inv_std, inv_std


def norm_back(grad, normed, inv_std, gain):
    scaled = grad * gain
    return inv_std * (
        scaled
        - jnp.mean(scaled, -1, keepdims=True)
        - normed * jnp.mean(scaled * normed, -1, keepdims=True)
    )


def row_sum(values):
    return jnp.sum(values, 0, keepdims=True)


def one_hot(index_row, count):
    rows = lax.broadcasted_iota(jnp.int32, (count, index_row.shape[1]), 0)
    return jnp.where(rows == index_row, 1.0, 0.0).astype(bf16)


def region_forward(features, boxes, target, w_visual, w_box_t, bias, gain, shift):
    rows, feat = features.shape
    width = w_visual.shape[1]
    steps = 4
    part = feat // steps

    def kernel(f_ref, box_ref, t_ref, wv_ref, wb_ref, b_ref, g_ref, s_ref, m_ref, n_ref, i_ref, acc):
        step = pl.program_id(0)
        partial = mm(f_ref[...], wv_ref[...])

        @pl.when(step == 0)
        def _():
            acc[...] = partial + (mm(box_ref[...], wb_ref[...], TN) + b_ref[...])

        @pl.when(step > 0)
        def _():
            acc[...] += partial

        @pl.when(step == steps - 1)
        def _():
            normed, inv = norm_parts(acc[...])
            n_ref[...] = normed
            i_ref[...] = jnp.broadcast_to(inv, i_ref.shape)
            low = (normed * g_ref[...] + s_ref[...]).astype(bf16)
            m_ref[...] = mm(one_hot(t_ref[...], rows), low).astype(bf16)

    return pl.pallas_call(
        kernel,
        grid=(steps,),
        in_specs=[
            pl.BlockSpec((rows, part), lambda i: (0, i)),
            whole(boxes.shape),
            whole((1, rows)),
            pl.BlockSpec((part, width), lambda i: (i, 0)),
            whole(w_box_t.shape),
            vec(width),
            vec(width),
            vec(width),
        ],
        out_specs=[whole((rows, width)), whole((rows, width)), whole((rows, 128))],
        out_shape=[shape((rows, width), bf16), shape((rows, width)), shape((rows, 128))],
        scratch_shapes=[pltpu.VMEM((rows, width), f32)],
        compiler_params=params(24),
        name="region_forward",
    )(features, boxes, target, w_visual, w_box_t, bias, gain, shift)


def text_qkv(text, w_qkv, qv_bias):
    rows, width = text.shape

    def kernel(t_ref, w_ref, b_ref, o_ref):
        step = pl.program_id(0)
        bias = b_ref[...] * jnp.where(step == 1, 0.0, 1.0)
        o_ref[...] = (mm(t_ref[...], w_ref[...]) + bias).astype(bf16)

    return pl.pallas_call(
        kernel,
        grid=(3,),
        in_specs=[
            whole((rows, width)),
            pl.BlockSpec((width, width), lambda i: (0, i)),
            pl.BlockSpec((1, width), lambda i: (0, i // 2)),
        ],
        out_specs=pl.BlockSpec((rows, width), lambda i: (0, i)),
        out_shape=shape((rows, 3 * width), bf16),
        compiler_params=params(24),
        name="text_qkv",
    )(text, w_qkv, qv_bias)


def forward(
    scalars, text, text_low, arrived, source, out_grad, w_qkv, qv_bias, w_out, out_bias,
    attn_gain, attn_shift, w_up, up_bias, w_down, down_bias, ffn_gain, ffn_shift, dims,
):
    captions, images = dims
    width = text.shape[1]
    text_len = text.shape[0] // captions
    slots = arrived.shape[0]
    regions = slots // images
    seq = text_len + regions
    rows = captions * seq
    ff = w_up.shape[1]
    half = width // 2
    parts = 4
    part = ff // parts
    grid = captions + parts

    def kernel(
        sc_ref, t_ref, tq_ref, a_ref, src_ref, og_ref, wq, qvb_ref, wo, ob_ref, ag_ref, as_ref,
        wu_hbm, ub_ref, wd_hbm, db_ref, fg_ref, fs_ref,
        out_ref, x_ref, qkv_ref, probs_ref, ctx_ref, an_ref, ai_ref, hid_ref, slope_ref, ds_ref, df_ref,
        sums_ref, send_ref, keep_ref,
        regs, rqkv, act_all, dffn_all, wu, wd, sems,
    ):
        step = pl.program_id(0)

        places = [(wu_hbm, wu), (wd_hbm, wd)]

        def copy(at):
            return pltpu.make_async_copy(*places[at], sems.at[at])

        @pl.when(step == 0)
        def _():
            for at in range(len(places)):
                copy(at).start()
            sums_ref[...] = jnp.zeros_like(sums_ref)
            local = mm(one_hot(src_ref[...], slots), a_ref[...], TN).astype(bf16)
            regs[...] = local
            for part_id in range(3):
                at = slice(part_id * width, (part_id + 1) * width)
                got = mm(local, wq[:, at])
                if part_id == 0:
                    got = got + qvb_ref[:, :width]
                if part_id == 2:
                    got = got + qvb_ref[:, width:]
                rqkv[:, at] = got.astype(bf16)

        @pl.when(step < captions)
        def _():
            image = sc_ref[step]
            length = sc_ref[captions + step]
            count = sc_ref[2 * captions + image]
            at = pl.ds(pl.multiple_of(image * regions, regions), regions)
            x_ref[:text_len, :] = t_ref[...]
            x_ref[text_len:, :] = regs[at, :]
            qkv_ref[:text_len, :] = tq_ref[...]
            qkv_ref[text_len:, :] = rqkv[at, :]
            place = lax.broadcasted_iota(jnp.int32, (seq, 1), 0)
            row_end = jnp.where(place < text_len, length, text_len + count)
            row_mask = jnp.where(place < row_end, 1.0, 0.0)
            key_bias = jnp.where(place < row_end, 0.0, -1e30)
            first = lax.broadcasted_iota(jnp.int32, (1, 2 * HEAD), 1) < HEAD
            scale = [
                jnp.where(first, 0.125, 0.0).astype(bf16),
                jnp.where(first, 0.0, 0.125).astype(bf16),
            ]
            for pair in range(HEADS // 2):
                lo = pair * 2 * HEAD
                q = qkv_ref[:, lo : lo + 2 * HEAD]
                k = qkv_ref[:, width + lo : width + lo + 2 * HEAD]
                v = qkv_ref[:, 2 * width + lo : 2 * width + lo + 2 * HEAD]
                scores = mm(k, jnp.concatenate([q * scale[0], q * scale[1]], 0), NT) + key_bias
                raised = jnp.exp(scores - jnp.max(scores, 0, keepdims=True))
                low = (raised * (1.0 / jnp.sum(raised, 0, keepdims=True))).astype(bf16)
                probs_ref[pair] = low
                outs = mm(low, v, TN)
                ctx_ref[:, lo : lo + 2 * HEAD] = jnp.where(first, outs[:seq], outs[seq:]).astype(bf16)

            x_wide = x_ref[...].astype(f32)
            attn_out = mm(ctx_ref[...], wo[...]) + ob_ref[...]
            normed, inv = norm_parts(x_wide + attn_out)
            an_ref[...] = normed
            ai_ref[...] = jnp.broadcast_to(inv, ai_ref.shape)
            hidden = normed * ag_ref[...] + as_ref[...]
            hidden_low = hidden.astype(bf16)
            hid_ref[...] = hidden_low

            @pl.when(step == 0)
            def _():
                copy(0).wait()

            here = pl.ds(pl.multiple_of(step * seq, seq), seq)
            for piece in range(parts):
                at = slice(piece * part, (piece + 1) * part)
                upper = mm(hidden_low, wu[:, at]) + ub_ref[:, at]
                phi = 0.5 * (1.0 + lax.erf(upper * inv_sqrt_two))
                act_all[here, at] = (upper * phi).astype(bf16)
                slope = phi + upper * jnp.exp(-0.5 * upper * upper) * inv_sqrt_tau
                slope_ref[:, at] = slope.astype(bf16)

            @pl.when(step == 0)
            def _():
                copy(1).wait()

            ffn_out = mm(act_all[here, :], wd[...]) + db_ref[...]
            ffn_normed, ffn_inv = norm_parts(hidden + ffn_out)
            out_ref[...] = ((ffn_normed * fg_ref[...] + fs_ref[...]) * row_mask).astype(bf16)
            cot = og_ref[...].astype(f32) * row_mask
            second = norm_back(cot, ffn_normed, ffn_inv, fg_ref[...])
            ds_ref[...] = second
            low = second.astype(bf16)
            df_ref[...] = low
            dffn_all[here, :] = low
            for at, value in enumerate(
                (
                    cot * ffn_normed,
                    cot,
                    low.astype(f32),
                    row_mask * x_wide * x_wide,
                    row_mask * attn_out * attn_out,
                    row_mask * ffn_out * ffn_out,
                    jnp.broadcast_to(row_mask, (seq, width)),
                )
            ):
                sums_ref[at : at + 1, :] += row_sum(value)

        @pl.when(step >= captions)
        def _():
            acts = pl.ds(pl.multiple_of((step - captions) * part, part), part)
            got = mm(act_all[:, acts], dffn_all[...], TN)
            mine = sc_ref[2 * captions + images] == 0
            send_ref[...] = jnp.where(mine, got[:, half:], got[:, :half]).astype(bf16)
            keep_ref[...] = jnp.where(mine, got[:, :half], got[:, half:]).astype(bf16)

    def rowwise(size, cols):
        return pl.BlockSpec((size, cols), lambda i, s: (jnp.minimum(i, captions - 1), 0))

    anywhere = pl.BlockSpec(memory_space=pl.ANY)
    return pl.pallas_call(
        kernel,
        grid_spec=pltpu.PrefetchScalarGridSpec(
            num_scalar_prefetch=1,
            grid=(grid,),
            in_specs=[
                rowwise(text_len, width),
                rowwise(text_len, 3 * width),
                whole((slots, width)),
                whole((1, slots)),
                rowwise(seq, width),
                whole(w_qkv.shape),
                whole((1, 2 * width)),
                whole(w_out.shape),
                vec(width),
                vec(width),
                vec(width),
                anywhere,
                whole((1, ff)),
                anywhere,
                vec(width),
                vec(width),
                vec(width),
            ],
            out_specs=[
                rowwise(seq, width),
                rowwise(seq, width),
                rowwise(seq, 3 * width),
                pl.BlockSpec(
                    (HEADS // 2, seq, 2 * seq), lambda i, s: (jnp.minimum(i, captions - 1), 0, 0)
                ),
                rowwise(seq, width),
                rowwise(seq, width),
                rowwise(seq, 128),
                rowwise(seq, width),
                rowwise(seq, ff),
                rowwise(seq, width),
                rowwise(seq, width),
                whole((8, width)),
                pl.BlockSpec((part, half), lambda i, s: (jnp.maximum(i - captions, 0), 0)),
                pl.BlockSpec((part, half), lambda i, s: (jnp.maximum(i - captions, 0), 0)),
            ],
            scratch_shapes=[
                pltpu.VMEM((slots, width), bf16),
                pltpu.VMEM((slots, 3 * width), bf16),
                pltpu.VMEM((rows, ff), bf16),
                pltpu.VMEM((rows, width), bf16),
                pltpu.VMEM(w_up.shape, bf16),
                pltpu.VMEM(w_down.shape, bf16),
                pltpu.SemaphoreType.DMA((2,)),
            ],
        ),
        out_shape=[
            shape((rows, width), bf16),
            shape((rows, width), bf16),
            shape((rows, 3 * width), bf16),
            shape((captions * HEADS // 2, seq, 2 * seq), bf16),
            shape((rows, width), bf16),
            shape((rows, width)),
            shape((rows, 128)),
            shape((rows, width), bf16),
            shape((rows, ff), bf16),
            shape((rows, width)),
            shape((rows, width), bf16),
            shape((8, width)),
            shape((ff, half), bf16),
            shape((ff, half), bf16),
        ],
        compiler_params=params(50),
        name="forward",
    )(
        scalars, text, text_low, arrived, source, out_grad, w_qkv, qv_bias, w_out, out_bias,
        attn_gain, attn_shift, w_up, up_bias, w_down, down_bias, ffn_gain, ffn_shift,
    )


def ffn_backward(d_ffn, d_second, slope, attn_normed, attn_inv, w_down, w_up, attn_gain, captions):
    rows, width = d_ffn.shape
    seq = rows // captions
    ff = w_up.shape[1]
    parts = 4
    part = ff // parts

    def kernel(
        df_ref, ds_ref, sl_ref, an_ref, ai_ref, wd_hbm, wu_hbm, ag_ref,
        dup_ref, dr_ref, da_ref, sums_ref, up_ref, wd, wu, sems,
    ):
        step = pl.program_id(0)
        places = [(wd_hbm, wd), (wu_hbm, wu)]

        def copy(at):
            return pltpu.make_async_copy(*places[at], sems.at[at])

        @pl.when(step == 0)
        def _():
            copy(0).start()
            sums_ref[...] = jnp.zeros_like(sums_ref)
            up_ref[...] = jnp.zeros_like(up_ref)
            copy(0).wait()
            copy(1).start()

        d_low = df_ref[...]
        for piece in range(parts):
            at = slice(piece * part, (piece + 1) * part)
            d_act = mm(d_low, wd[at, :], NT)
            wide = d_act * sl_ref[:, at].astype(f32)
            low = wide.astype(bf16)
            dup_ref[:, at] = low
            up_ref[0:1, at] += row_sum(low.astype(f32))

        @pl.when(step == 0)
        def _():
            copy(1).wait()

        d_hidden = ds_ref[...] + mm(dup_ref[...], wu[...], NT)
        normed = an_ref[...]
        resid = norm_back(d_hidden, normed, ai_ref[:, 0:1], ag_ref[...])
        dr_ref[...] = resid
        low = resid.astype(bf16)
        da_ref[...] = low
        sums_ref[0:1, :] += row_sum(d_hidden * normed)
        sums_ref[1:2, :] += row_sum(d_hidden)
        sums_ref[2:3, :] += row_sum(low.astype(f32))

    def rowwise(cols):
        return pl.BlockSpec((seq, cols), lambda i: (i, 0))

    anywhere = pl.BlockSpec(memory_space=pl.ANY)
    return pl.pallas_call(
        kernel,
        grid=(captions,),
        in_specs=[
            rowwise(width),
            rowwise(width),
            rowwise(ff),
            rowwise(width),
            rowwise(128),
            anywhere,
            anywhere,
            vec(width),
        ],
        out_specs=[
            rowwise(ff),
            rowwise(width),
            rowwise(width),
            whole((8, width)),
            whole((8, ff)),
        ],
        scratch_shapes=[
            pltpu.VMEM(w_down.shape, bf16),
            pltpu.VMEM(w_up.shape, bf16),
            pltpu.SemaphoreType.DMA((2,)),
        ],
        out_shape=[
            shape((rows, ff), bf16),
            shape((rows, width)),
            shape((rows, width), bf16),
            shape((8, width)),
            shape((8, ff)),
        ],
        compiler_params=params(36),
        cost_estimate=pl.CostEstimate(flops=4 * rows * width * ff, bytes_accessed=20 << 20, transcendentals=0),
        name="ffn_backward",
    )(d_ffn, d_second, slope, attn_normed, attn_inv, w_down, w_up, attn_gain)


def up_gradient(core, hidden_low, d_upper):
    rows, width = hidden_low.shape

    def kernel(c_ref, h_ref, d_ref, send_ref, keep_ref):
        step = pl.program_id(0)
        got = mm(h_ref[...], d_ref[...], TN).astype(bf16)

        @pl.when(step < 2)
        def _():
            send_ref[...] = got

        @pl.when(step >= 2)
        def _():
            keep_ref[...] = got

    return pl.pallas_call(
        kernel,
        grid_spec=pltpu.PrefetchScalarGridSpec(
            num_scalar_prefetch=1,
            grid=(4,),
            in_specs=[
                whole((rows, width)),
                pl.BlockSpec((rows, width), lambda i, s: (0, lax.rem(i + 2 * (1 - s[0]), 4))),
            ],
            out_specs=[
                pl.BlockSpec((width, width), lambda i, s: (0, jnp.minimum(i, 1))),
                pl.BlockSpec((width, width), lambda i, s: (0, jnp.maximum(i - 2, 0))),
            ],
        ),
        out_shape=[shape((width, 2 * width), bf16), shape((width, 2 * width), bf16)],
        compiler_params=params(24),
        cost_estimate=pl.CostEstimate(flops=8 * rows * width * width, bytes_accessed=10 << 20, transcendentals=0),
        name="up_gradient",
    )(core, hidden_low, d_upper)


def attention_backward(scalars, d_attn, d_resid, probs, qkv, source, w_out, w_qkv, dims):
    captions, images = dims
    rows, width = d_attn.shape
    seq = rows // captions
    slots = source.shape[1]
    regions = slots // images
    text_len = seq - regions

    def kernel(
        sc_ref, da_ref, dr_ref, p_ref, qkv_ref, src_ref, wo_ref, wq_hbm,
        dqkv_ref, text_ref, back_ref, sums_ref, d_img, wq, sem,
    ):
        step = pl.program_id(0)

        def copy():
            return pltpu.make_async_copy(wq_hbm, wq, sem)

        @pl.when(step == 0)
        def _():
            copy().start()
            sums_ref[...] = jnp.zeros_like(sums_ref)
            d_img[...] = jnp.zeros_like(d_img)

        d_ctx = mm(da_ref[...], wo_ref[...], NT).astype(bf16)
        first = lax.broadcasted_iota(jnp.int32, (1, 2 * HEAD), 1) < HEAD
        masks = [jnp.where(first, 1.0, 0.0).astype(bf16), jnp.where(first, 0.0, 1.0).astype(bf16)]
        for pair in range(HEADS // 2):
            lo = pair * 2 * HEAD
            q = qkv_ref[:, lo : lo + 2 * HEAD]
            k = qkv_ref[:, width + lo : width + lo + 2 * HEAD]
            v = qkv_ref[:, 2 * width + lo : 2 * width + lo + 2 * HEAD]
            d_c = d_ctx[:, lo : lo + 2 * HEAD]
            both_c = jnp.concatenate([d_c * masks[0], d_c * masks[1]], 0)
            both_q = jnp.concatenate([q * masks[0], q * masks[1]], 0)
            low = p_ref[pair]
            d_probs = mm(v, both_c, NT)
            wide = low.astype(f32)
            both = wide * d_probs
            inner = jnp.sum(both, 0, keepdims=True)
            d_scores = (both - wide * inner).astype(bf16)
            d_q = mm(d_scores, k, TN) * 0.125
            dqkv_ref[:, lo : lo + 2 * HEAD] = jnp.where(first, d_q[:seq], d_q[seq:]).astype(bf16)
            dqkv_ref[:, width + lo : width + lo + 2 * HEAD] = (mm(d_scores, both_q) * 0.125).astype(bf16)
            dqkv_ref[:, 2 * width + lo : 2 * width + lo + 2 * HEAD] = mm(low, both_c).astype(bf16)

        @pl.when(step == 0)
        def _():
            copy().wait()

        sums_ref[0:1, :] += row_sum(dqkv_ref[:, :width].astype(f32))
        sums_ref[1:2, :] += row_sum(dqkv_ref[:, 2 * width :].astype(f32))
        d_x = mm(dqkv_ref[...], wq[...], NT) + dr_ref[...]
        text_ref[...] = d_x[:text_len]
        at = pl.ds(pl.multiple_of(sc_ref[step] * regions, regions), regions)
        d_img[at, :] += d_x[text_len:]

        @pl.when(step == captions - 1)
        def _():
            back_ref[...] = mm(one_hot(src_ref[...], slots), d_img[...].astype(bf16)).astype(bf16)

    def rowwise(size, cols):
        return pl.BlockSpec((size, cols), lambda i, s: (i, 0))

    return pl.pallas_call(
        kernel,
        grid_spec=pltpu.PrefetchScalarGridSpec(
            num_scalar_prefetch=1,
            grid=(captions,),
            in_specs=[
                rowwise(seq, width),
                rowwise(seq, width),
                pl.BlockSpec((HEADS // 2, seq, 2 * seq), lambda i, s: (i, 0, 0)),
                rowwise(seq, 3 * width),
                whole((1, slots)),
                whole(w_out.shape),
                pl.BlockSpec(memory_space=pl.ANY),
            ],
            out_specs=[
                rowwise(seq, 3 * width),
                rowwise(text_len, width),
                whole((slots, width)),
                whole((8, width)),
            ],
            scratch_shapes=[
                pltpu.VMEM((slots, width), f32),
                pltpu.VMEM(w_qkv.shape, bf16),
                pltpu.SemaphoreType.DMA,
            ],
        ),
        out_shape=[
            shape((rows, 3 * width), bf16),
            shape((captions * text_len, width)),
            shape((slots, width), bf16),
            shape((8, width)),
        ],
        compiler_params=params(36),
        cost_estimate=pl.CostEstimate(flops=12 << 30, bytes_accessed=20 << 20, transcendentals=0),
        name="attention_backward",
    )(scalars, d_attn, d_resid, probs, qkv, source, w_out, w_qkv)


def qkvo_gradient(core, x, d_qkv, context, d_attn):
    rows, width = x.shape

    def block(i, s):
        return lax.rem(i + 2 * (1 - s[0]), 4)

    def kernel(c_ref, x_ref, dq_ref, ctx_ref, da_ref, send_ref, keep_ref):
        step = pl.program_id(0)
        last = lax.rem(step + 2 * (1 - c_ref[0]), 4) == 3

        def gradient(to_ref):
            @pl.when(jnp.logical_not(last))
            def _():
                to_ref[...] = mm(x_ref[...], dq_ref[...], TN).astype(bf16)

            @pl.when(last)
            def _():
                to_ref[...] = mm(ctx_ref[...], da_ref[...], TN).astype(bf16)

        @pl.when(step < 2)
        def _():
            gradient(send_ref)

        @pl.when(step >= 2)
        def _():
            gradient(keep_ref)

    return pl.pallas_call(
        kernel,
        grid_spec=pltpu.PrefetchScalarGridSpec(
            num_scalar_prefetch=1,
            grid=(4,),
            in_specs=[
                whole((rows, width)),
                pl.BlockSpec((rows, width), lambda i, s: (0, jnp.minimum(block(i, s), 2))),
                whole((rows, width)),
                whole((rows, width)),
            ],
            out_specs=[
                pl.BlockSpec((width, width), lambda i, s: (0, jnp.minimum(i, 1))),
                pl.BlockSpec((width, width), lambda i, s: (0, jnp.maximum(i - 2, 0))),
            ],
        ),
        out_shape=[shape((width, 2 * width), bf16), shape((width, 2 * width), bf16)],
        compiler_params=params(24),
        cost_estimate=pl.CostEstimate(flops=8 * rows * width * width, bytes_accessed=12 << 20, transcendentals=0),
        name="qkvo_gradient",
    )(core, x, d_qkv, context, d_attn)


def region_backward(
    core, returned, target, normed, inv, gain, features, boxes, w_visual, w_box_t,
    sums_forward, sums_ffn, sums_up, sums_attn, groups,
):
    rows, width = returned.shape
    feat = features.shape[1]
    half = width // 2
    steps = 4
    part = feat // steps
    quarter = feat // groups // 4
    tall = quarter + 8
    per_step = groups // steps
    box = boxes.shape[0]
    share = width // groups
    ff_share = sums_up.shape[1] // groups

    def kernel(
        c_ref, r_ref, t_ref, n_ref, i_ref, g_ref, f_ref, box_ref, wv_ref, wb_ref, sf_ref, sn_ref, su_ref, sa_ref,
        send_ref, keep_ref, fg_ref, bg_ref, dpre, small,
    ):
        step = pl.program_id(0)

        @pl.when(step == 0)
        def _():
            d_region = mm(one_hot(t_ref[...], rows), r_ref[...], TN)
            normed = n_ref[...]
            low = norm_back(d_region, normed, i_ref[:, 0:1], g_ref[...]).astype(bf16)
            dpre[...] = low
            bg_ref[...] = mm(wb_ref[...], low, NT)
            boxes_grad = mm(box_ref[...], low)
            vectors = [
                row_sum(low.astype(f32)),
                row_sum(d_region * normed),
                row_sum(d_region),
                sf_ref[0:1, :],
                sf_ref[1:2, :],
                sf_ref[2:3, :],
                sn_ref[0:1, :],
                sn_ref[1:2, :],
                sn_ref[2:3, :],
            ] + [boxes_grad[at : at + 1] for at in range(box)]
            small[...] = jnp.zeros_like(small)
            lane = lax.broadcasted_iota(jnp.int32, (1, half), 1)
            stats = jnp.zeros((1, half), f32)
            for at in range(4):
                total = jnp.sum(sf_ref[3 + at : 4 + at, :], 1, keepdims=True)
                stats = jnp.where(lane == at, total, stats)
            for group in range(groups):
                small[group, 0:1, 0:ff_share] = su_ref[0:1, group * ff_share : (group + 1) * ff_share]
                for side in range(2):
                    first = group * 2 * share
                    flat = jnp.concatenate([sa_ref[0:1, :], sa_ref[1:2, :]], 1)
                    small[group, 1:2, 0 : 2 * share] = flat[:, first : first + 2 * share]
                for at, value in enumerate(vectors):
                    row, col = (1, 2) if at == 0 else (2 + (at - 1) // 3, (at - 1) % 3)
                    small[group, row : row + 1, 128 * col : 128 * col + share] = value[
                        :, group * share : (group + 1) * share
                    ]
                small[group, 6:7, :] = stats

        got = mm(f_ref[...], dpre[...], TN)
        mine = c_ref[0] == 0
        for to_ref, low_half in ((send_ref, jnp.logical_not(mine)), (keep_ref, mine)):
            chosen = jnp.where(low_half, got[:, :half], got[:, half:]).astype(bf16)
            for group in range(per_step):
                for bit in range(2):
                    for piece in range(2):
                        at = ((group * 2 + bit) * 2 + piece) * quarter
                        to_ref[group, bit, piece, :quarter, :] = chosen[at : at + quarter]
                        if piece == 0:
                            to_ref[group, bit, piece, quarter:, :] = small[step * per_step + group].astype(bf16)
                        else:
                            to_ref[group, bit, piece, quarter:, :] = jnp.zeros((8, half), bf16)
        fg_ref[...] = mm(dpre[...], wv_ref[...], NT)

    out = pl.BlockSpec((per_step, 2, 2, tall, half), lambda i, s: (i, 0, 0, 0, 0))
    return pl.pallas_call(
        kernel,
        grid_spec=pltpu.PrefetchScalarGridSpec(
            num_scalar_prefetch=1,
            grid=(steps,),
            in_specs=[
                whole((rows, width)),
                whole((1, rows)),
                whole((rows, width)),
                whole((rows, 128)),
                vec(width),
                pl.BlockSpec((rows, part), lambda i, s: (0, i)),
                whole(boxes.shape),
                pl.BlockSpec((part, width), lambda i, s: (i, 0)),
                whole(w_box_t.shape),
                whole(sums_forward.shape),
                whole(sums_ffn.shape),
                whole(sums_up.shape),
                whole(sums_attn.shape),
            ],
            out_specs=[out, out, pl.BlockSpec((rows, part), lambda i, s: (0, i)), whole((box, rows))],
            scratch_shapes=[pltpu.VMEM((rows, width), bf16), pltpu.VMEM((groups, 8, half), f32)],
        ),
        out_shape=[
            shape((groups, 2, 2, tall, half), bf16),
            shape((groups, 2, 2, tall, half), bf16),
            shape((rows, feat)),
            shape((box, rows)),
        ],
        compiler_params=params(24),
        cost_estimate=pl.CostEstimate(flops=5 << 30, bytes_accessed=12 << 20, transcendentals=0),
        name="region_backward",
    )(
        core, returned, target, normed, inv, gain, features, boxes, w_visual, w_box_t,
        sums_forward, sums_ffn, sums_up, sums_attn,
    )


def device_number():
    return lax.axis_index("dp") * lax.axis_size("enc") + lax.axis_index("enc")


def swap(values, bit):
    count = lax.axis_size("dp") * lax.axis_size("enc")
    return lax.ppermute(values, ("dp", "enc"), [(i, i ^ bit) for i in range(count)])


def add(a, b):
    return (a.astype(f32) + b.astype(f32)).astype(bf16)


def scalar_call(kernel, bits, ins, in_specs, outs, out_specs, grid, limit, name):
    return pl.pallas_call(
        kernel,
        grid_spec=pltpu.PrefetchScalarGridSpec(
            num_scalar_prefetch=1, grid=(grid,), in_specs=in_specs, out_specs=out_specs
        ),
        out_shape=outs,
        compiler_params=params(limit),
        cost_estimate=pl.CostEstimate(
            flops=1 << 20, bytes_accessed=2 * sum(v.size * v.dtype.itemsize for v in ins), transcendentals=0
        ),
        name=name,
    )(bits, *ins)


def first_split(bits, kept, got, groups):
    tall = kept.ndim == 5
    high = groups // 2
    if tall:
        rows, cols = kept.shape[3:]
        view = (high, 2, 2, 2, rows, cols)
        block = (1, 2, 2, 2, rows, cols)
    else:
        rows, cols = kept.shape[0] // groups, kept.shape[1] // 4
        view = (high, 2, rows, 4 * cols)
        block = (1, 2, rows, 4 * cols)

    def kernel(b_ref, k_ref, r_ref, a_send, a_keep, b_send, b_keep):
        bit2, bit4 = b_ref[1], b_ref[2]

        def total(y, x, piece):
            if tall:
                return add(k_ref[0, y, x, piece], r_ref[0, y, x, piece])
            at = pl.ds(pl.multiple_of((2 * x + piece) * cols, 128), cols)
            return add(k_ref[0, y, :, at], r_ref[0, y, :, at])

        for other in range(2):
            a_send[0, other] = total(other, 1 - bit2, 0)
            a_keep[0, other] = total(other, bit2, 0)
            b_send[0, other] = total(1 - bit4, other, 1)
            b_keep[0, other] = total(bit4, other, 1)

    spec = pl.BlockSpec(block, lambda i, s: (i,) + (0,) * (len(block) - 1))
    out = pl.BlockSpec((1, 2, rows, cols), lambda i, s: (i, 0, 0, 0))
    return scalar_call(
        kernel, bits, (kept.reshape(view), got.reshape(view)), [spec, spec],
        [shape((high, 2, rows, cols), bf16)] * 4, [out] * 4, high, 16, "first_split",
    )


def second_split(bits, a_kept, a_got, b_kept, b_got):
    high, _, rows, cols = a_kept.shape

    def kernel(b_ref, ak, ar, bk, br, a_send, a_keep, b_send, b_keep):
        bit2, bit4 = b_ref[1], b_ref[2]
        a_send[0] = add(ak[0, 1 - bit4], ar[0, 1 - bit4])
        a_keep[0] = add(ak[0, bit4], ar[0, bit4])
        b_send[0] = add(bk[0, 1 - bit2], br[0, 1 - bit2])
        b_keep[0] = add(bk[0, bit2], br[0, bit2])

    spec = pl.BlockSpec((1, 2, rows, cols), lambda i, s: (i, 0, 0, 0))
    out = pl.BlockSpec((1, rows, cols), lambda i, s: (i, 0, 0))
    return scalar_call(
        kernel, bits, (a_kept, a_got, b_kept, b_got), [spec] * 4,
        [shape((high, rows, cols), bf16)] * 4, [out] * 4, high, 16, "second_split",
    )


def join_split(bits, pairs):
    high, _, cols = pairs[0][0].shape
    sizes = [kept.shape[1] for kept, _ in pairs]

    def kernel(b_ref, *refs):
        bit = b_ref[3]
        send, keep = refs[-2:]
        at = 0
        for n, size in enumerate(sizes):
            kept, got = refs[2 * n : 2 * n + 2]
            send[0, at : at + size] = add(kept[1 - bit], got[1 - bit])
            keep[0, at : at + size] = add(kept[bit], got[bit])
            at += size

    ins = [value for pair in pairs for value in pair]
    specs = [pl.BlockSpec((2, v.shape[1], cols), lambda i, s: (i, 0, 0)) for v in ins]
    out = pl.BlockSpec((1, sum(sizes), cols), lambda i, s: (i, 0, 0))
    return scalar_call(
        kernel, bits, ins, specs, [shape((high // 2, sum(sizes), cols), bf16)] * 2, [out] * 2,
        high // 2, 16, "join_split",
    )


def late_split(bits, kept, got, which):
    high, rows, cols = kept.shape

    def kernel(b_ref, k_ref, r_ref, send, keep):
        bit = b_ref[which]
        send[0] = add(k_ref[1 - bit], r_ref[1 - bit])
        keep[0] = add(k_ref[bit], r_ref[bit])

    spec = pl.BlockSpec((2, rows, cols), lambda i, s: (i, 0, 0))
    out = pl.BlockSpec((1, rows, cols), lambda i, s: (i, 0, 0))
    return scalar_call(
        kernel, bits, (kept, got), [spec] * 2, [shape((high // 2, rows, cols), bf16)] * 2, [out] * 2,
        high // 2, 16, "late_split",
    )


def start_halving(bits, sent, kept, groups):
    got = swap(sent, 1)
    a_send, a_keep, b_send, b_keep = first_split(bits, kept, got, groups)
    return a_send, a_keep, b_send, b_keep


def next_halving(bits, halves):
    a_send, a_keep, b_send, b_keep = halves
    return second_split(bits, a_keep, swap(a_send, 2), b_keep, swap(b_send, 4))


def finish_halving(bits, chunks, groups):
    pairs = []
    for a_send, a_keep, b_send, b_keep in chunks:
        pairs += [(a_keep, swap(a_send, 4)), (b_keep, swap(b_send, 2))]
    send, keep = join_split(bits, pairs)
    bit, which = 8, 3
    while send.shape[0] > 1:
        bit, which = 2 * bit, which + 1
        send, keep = late_split(bits, keep, swap(send, bit // 2), which)
    mine = (keep + swap(send, bit))[0]
    over_core = swap(mine, 1)
    over_x = swap(mine, 2)
    return mine, over_x, over_core, swap(over_x, 1)


def pick(b_ref, pieces, core, x):
    mine, over_x, over_core, over_both = pieces
    same_x = b_ref[1] == x
    return jnp.where(
        b_ref[0] == core, jnp.where(same_x, mine, over_x), jnp.where(same_x, over_core, over_both)
    ).astype(f32)


def finish_ffn(bits, pieces):
    rows, cols = pieces[0].shape
    part = rows // 4

    def kernel(b_ref, p0, p1, p2, p3, down_ref, up_ref):
        for core in range(2):
            for x in range(2):
                got = pick(b_ref, (p0[...], p1[...], p2[...], p3[...]), core, x)
                down_ref[2 * x * part : 2 * (x + 1) * part, core * cols : (core + 1) * cols] = got[: 2 * part]
                for piece in range(2):
                    at = ((core * 2 + x) * 2 + piece) * cols
                    up_ref[:, at : at + cols] = got[(2 + piece) * part : (3 + piece) * part]

    outs = [shape((4 * part, 2 * cols)), shape((part, 8 * cols))]
    return scalar_call(
        kernel, bits, pieces, [whole((rows, cols))] * 4, outs, [whole(o.shape) for o in outs], 1, 24, "finish_ffn"
    )


def finish_rest(bits, pieces, part, tall, ff_share, share, box):
    rows, cols = pieces[0].shape
    quarter = tall - 8
    sizes = [share] * 9 + [2 * share, ff_share]

    def kernel(b_ref, p0, p1, p2, p3, qkv_ref, o_ref, vis_ref, box_ref, rms_ref, *small_refs):
        for core in range(2):
            for x in range(2):
                got = pick(b_ref, (p0[...], p1[...], p2[...], p3[...]), core, x)
                for piece in range(2):
                    block = got[piece * part : (piece + 1) * part]
                    at = ((core * 2 + x) * 2 + piece) * cols
                    if core * 2 + x < 3:
                        qkv_ref[:, at : at + cols] = block
                    else:
                        o_ref[:, piece * cols : (piece + 1) * cols] = block
                    low = 2 * part + piece * tall
                    vis_ref[(2 * x + piece) * quarter : (2 * x + piece + 1) * quarter, core * cols : (core + 1) * cols] = got[
                        low : low + quarter
                    ]
        low = 2 * part + quarter
        small = p0[low : low + 8, :].astype(f32)
        for at in range(9):
            row, col = (1, 2) if at == 0 else (2 + (at - 1) // 3, (at - 1) % 3)
            small_refs[at][...] = small[row, 128 * col : 128 * col + share]
        small_refs[9][...] = small[1, 0 : 2 * share]
        small_refs[10][...] = small[0, 0:ff_share]
        lines = []
        for at in range(9, 9 + box):
            row, col = 2 + (at - 1) // 3, (at - 1) % 3
            lines.append(small[row : row + 1, 128 * col : 128 * (col + 1)])
        lines += [jnp.zeros((1, 128), f32)] * (8 - box)
        box_ref[...] = jnp.concatenate(lines, 0).T[:share, :box]
        stats = small[6:7, 0:128]
        rms_ref[...] = jnp.sqrt(stats / stats[:, 3:4])

    outs = [
        shape((part, 6 * cols)),
        shape((part, 2 * cols)),
        shape((4 * quarter, 2 * cols)),
        shape((share, box)),
        shape((1, 128)),
    ] + [shape((size,)) for size in sizes]
    specs = [whole(o.shape) for o in outs[:5]] + [vec(size) for size in sizes]
    return scalar_call(
        kernel, bits, pieces, [whole((rows, cols))] * 4, outs, specs, 1, 24, "finish_rest"
    )


def gate(value, *others):
    return lax.optimization_barrier((value, *others))[0]


def on_device(
    text_embed,
    region_features,
    boxes,
    caption_image,
    caption_lengths,
    region_counts,
    region_target,
    region_source,
    w_visual,
    w_box,
    visual_bias,
    visual_gain,
    visual_shift,
    w_qkv,
    qv_bias,
    w_out,
    out_bias,
    attn_gain,
    attn_shift,
    w_up,
    up_bias,
    w_down,
    down_bias,
    ffn_gain,
    ffn_shift,
    out_grad,
):
    width = text_embed.shape[1]
    captions = caption_image.shape[0]
    images = region_counts.shape[0]
    dims = (captions, images)
    axes = ("dp", "enc")
    groups = lax.axis_size("dp")
    count = groups * lax.axis_size("enc")
    me = device_number().astype(jnp.int32)
    bits = jnp.stack([(me >> at) & 1 for at in range(count.bit_length() - 1)])
    core = bits[:1]
    scalars = jnp.concatenate([caption_image, caption_lengths, region_counts, core])
    w_box_t = w_box.T
    row = lambda v: v.reshape(1, -1)
    qv_row = row(qv_bias)

    message, vis_normed, vis_inv = region_forward(
        region_features, boxes, region_target, w_visual, w_box_t, visual_bias, visual_gain, visual_shift
    )
    arrived = lax.all_to_all(message, axes, split_axis=0, concat_axis=0, tiled=True)
    text_low = text_qkv(text_embed, w_qkv, qv_row)
    (
        out_rows, x, qkv, probs, context, attn_normed, attn_inv, hidden_low, slope, d_second, d_ffn,
        sums_forward, down_sent, down_kept,
    ) = forward(
        scalars, text_embed, text_low, arrived, region_source, out_grad, w_qkv, qv_row, w_out,
        out_bias, attn_gain, attn_shift, w_up, row(up_bias), w_down, down_bias, ffn_gain, ffn_shift, dims,
    )
    d_upper, d_resid, d_attn, sums_ffn, sums_up = ffn_backward(
        d_ffn, d_second, slope, attn_normed, attn_inv, w_down, w_up, attn_gain, captions
    )
    down_view = (groups, 2, 2, w_down.shape[0] // groups // 4, width // 2)
    down = start_halving(bits, down_sent.reshape(down_view), down_kept.reshape(down_view), groups)
    up_sent, up_kept = up_gradient(gate(core, *down), hidden_low, d_upper)
    d_qkv, text_grad, back_message, sums_attn = attention_backward(
        gate(scalars, up_kept), d_attn, d_resid, probs, qkv, region_source, w_out, w_qkv, dims
    )
    returned = lax.all_to_all(back_message, axes, split_axis=0, concat_axis=0, tiled=True)
    up = start_halving(bits, up_sent, up_kept, groups)
    down = next_halving(bits, down)
    qkvo_sent, qkvo_kept = qkvo_gradient(gate(core, *down, *up), x, d_qkv, context, d_attn)
    vis_sent, vis_kept, feature_grad, box_grad = region_backward(
        gate(core, qkvo_kept), returned, region_target, vis_normed, vis_inv, visual_gain, region_features, boxes,
        w_visual, w_box_t, sums_forward, sums_ffn, sums_up, sums_attn, groups,
    )
    qkvo = start_halving(bits, qkvo_sent, qkvo_kept, groups)
    vis = start_halving(bits, vis_sent, vis_kept, groups)
    up = next_halving(bits, up)
    ffn_pieces = finish_halving(bits, (down, up), groups)
    qkvo = next_halving(bits, qkvo)
    vis = next_halving(bits, vis)
    rest_pieces = finish_halving(bits, (qkvo, vis), groups)
    g_down, g_up = finish_ffn(bits, ffn_pieces)
    share = width // groups
    g_qkv, g_out, g_visual, g_box, rms, *small = finish_rest(
        bits, rest_pieces, share, w_visual.shape[0] // groups // 4 + 8, w_up.shape[1] // groups, share, boxes.shape[0]
    )
    return (
        out_rows,
        text_grad,
        feature_grad,
        box_grad,
        rms[0, :3],
        g_visual,
        g_box,
        small[0],
        small[1],
        small[2],
        g_qkv,
        small[9],
        g_out,
        small[8],
        small[6],
        small[7],
        g_up,
        small[10],
        g_down,
        small[5],
        small[3],
        small[4],
    )


def solution(mesh):
    return jax.shard_map(
        on_device,
        mesh=mesh,
        in_specs=(
            P(("dp", "enc"), None),
            P(("dp", "enc"), None),
            P(None, ("dp", "enc")),
            P(("dp", "enc")),
            P(("dp", "enc")),
            P(("dp", "enc")),
            P(("dp", "enc"), None),
            P(("dp", "enc"), None),
            P(),
            P(),
            P(),
            P(),
            P(),
            P(),
            P(),
            P(),
            P(),
            P(),
            P(),
            P(),
            P(),
            P(),
            P(),
            P(),
            P(),
            P(("dp", "enc"), None),
        ),
        out_specs=(
            P(("dp", "enc"), None),
            P(("dp", "enc"), None),
            P(("dp", "enc"), None),
            P(None, ("dp", "enc")),
            P(),
            P("dp", None),
            P("dp", None),
            P("dp"),
            P("dp"),
            P("dp"),
            P("dp", None),
            P("dp"),
            P("dp", None),
            P("dp"),
            P("dp"),
            P("dp"),
            P("dp", None),
            P("dp"),
            P("dp", None),
            P("dp"),
            P("dp"),
            P("dp"),
        ),
        check_vma=False,
    )
```

```python
import jax
import jax.numpy as jnp
from jax import lax
from jax.experimental import pallas as pl
from jax.experimental.pallas import tpu as pltpu
from jax.sharding import PartitionSpec as P

HEADS = 12
UNROLL = 2
HEAD = 64
epsilon = 1e-12
inv_sqrt_two = 0.7071067811865476
inv_sqrt_tau = 0.3989422804014327
f32 = jnp.float32
bf16 = jnp.bfloat16
NN = (((1,), (0,)), ((), ()))
NT = (((1,), (1,)), ((), ()))
TN = (((0,), (0,)), ((), ()))


def mm(a, b, dims=NN):
    return lax.dot_general(a, b, dims, preferred_element_type=f32)


def cost(us):
    return pl.CostEstimate(flops=int(us * 1e9), bytes_accessed=1 << 20, transcendentals=0)


def params(limit=56):
    return pltpu.CompilerParams(
        dimension_semantics=("arbitrary",), vmem_limit_bytes=limit << 20
    )


def whole(shape):
    return pl.BlockSpec(shape, lambda i, *s: (0,) * len(shape), pipeline_mode=pl.Buffered(1))


def vec(size):
    return pl.BlockSpec((size,), lambda i, *s: (0,))


VMEM = pl.BlockSpec(memory_space=pltpu.VMEM)


def far(value):
    return pltpu.with_memory_space_constraint(value, pltpu.HBM)


def apart(dims, kind=f32):
    return pltpu.HBM(dims, kind)


def near(dims, kind=f32):
    return pltpu.VMEM(dims, kind)


def shape(dims, kind=f32):
    return jax.ShapeDtypeStruct(dims, kind)


def norm_parts(values):
    centre = values - jnp.mean(values, -1, keepdims=True)
    inv_std = lax.rsqrt(jnp.mean(centre * centre, -1, keepdims=True) + epsilon)
    return centre * inv_std, inv_std


def norm_back(grad, normed, inv_std, gain):
    scaled = grad * gain
    return inv_std * (
        scaled
        - jnp.mean(scaled, -1, keepdims=True)
        - normed * jnp.mean(scaled * normed, -1, keepdims=True)
    )


def row_sum(values):
    return jnp.sum(values, 0, keepdims=True)


def one_hot(index_row, count):
    rows = lax.broadcasted_iota(jnp.int32, (count, index_row.shape[1]), 0)
    return jnp.where(rows == index_row, 1.0, 0.0).astype(bf16)


def region_forward(features, boxes, target, w_visual, w_box_t, bias, gain, shift):
    rows, feat = features.shape
    width = w_visual.shape[1]
    steps = 4
    part = feat // steps

    def kernel(f_ref, box_ref, t_ref, wv_ref, wb_ref, b_ref, g_ref, s_ref, m_ref, n_ref, i_ref, acc):
        step = pl.program_id(0)
        partial = mm(f_ref[...], wv_ref[...])

        @pl.when(step == 0)
        def _():
            acc[...] = partial + (mm(box_ref[...], wb_ref[...], TN) + b_ref[...])

        @pl.when(step > 0)
        def _():
            acc[...] += partial

        @pl.when(step == steps - 1)
        def _():
            normed, inv = norm_parts(acc[...])
            n_ref[...] = normed
            i_ref[...] = jnp.broadcast_to(inv, i_ref.shape)
            low = (normed * g_ref[...] + s_ref[...]).astype(bf16)
            m_ref[...] = mm(one_hot(t_ref[...], rows), low).astype(bf16)

    return pl.pallas_call(
        kernel,
        grid=(steps,),
        in_specs=[
            pl.BlockSpec((rows, part), lambda i: (0, i)),
            whole(boxes.shape),
            whole((1, rows)),
            pl.BlockSpec((part, width), lambda i: (i, 0)),
            whole(w_box_t.shape),
            vec(width),
            vec(width),
            vec(width),
        ],
        out_specs=[VMEM, whole((rows, width)), whole((rows, 128))],
        out_shape=[near((rows, width), bf16), apart((rows, width)), apart((rows, 128))],
        scratch_shapes=[pltpu.VMEM((rows, width), f32)],
        compiler_params=params(24),
        cost_estimate=cost(3),
        name="region_forward",
    )(far(features), far(boxes), far(target), far(w_visual), w_box_t, far(bias), far(gain), far(shift))


def text_qkv(text, w_qkv, qv_bias):
    rows, width = text.shape

    def kernel(t_ref, w_ref, b_ref, o_ref):
        step = pl.program_id(0)
        bias = b_ref[...] * jnp.where(step == 1, 0.0, 1.0)
        o_ref[...] = (mm(t_ref[...], w_ref[...]) + bias).astype(bf16)

    return pl.pallas_call(
        kernel,
        grid=(3,),
        in_specs=[
            whole((rows, width)),
            pl.BlockSpec((width, width), lambda i: (0, i)),
            pl.BlockSpec((1, width), lambda i: (0, i // 2)),
        ],
        out_specs=pl.BlockSpec((rows, width), lambda i: (0, i)),
        out_shape=apart((rows, 3 * width), bf16),
        compiler_params=params(12),
        cost_estimate=cost(3),
        name="text_qkv",
    )(far(text), far(w_qkv), qv_bias)


def forward(
    scalars, text, text_low, arrived, source, out_grad, w_qkv, qv_bias, w_out, out_bias,
    attn_gain, attn_shift, w_up, up_bias, w_down, down_bias, ffn_gain, ffn_shift, dims,
):
    captions, images = dims
    width = text.shape[1]
    text_len = text.shape[0] // captions
    slots = arrived.shape[0]
    regions = slots // images
    seq = text_len + regions
    rows = captions * seq
    ff = w_up.shape[1]
    half = width // 2
    parts = 4
    part = ff // parts
    grid = captions + parts

    def kernel(
        sc_ref, t_ref, tq_ref, a_ref, src_ref, og_ref, wq_far, qvb_ref, wo_far, ob_ref, ag_ref, as_ref,
        wu_far, ub_ref, wd_far, db_ref, fg_ref, fs_ref,
        out_ref, x_ref, qkv_ref, probs_ref, ctx_ref, an_ref, ai_ref, hid_ref, slope_ref, ds_ref, df_ref,
        sums_ref, wu, wd, send_ref, keep_ref,
        regs, rqkv, act_all, wq, wo, sems,
    ):
        step = pl.program_id(0)

        def third(at):
            cols = slice(at * width, (at + 1) * width)
            return pltpu.make_async_copy(wq_far.at[:, cols], wq.at[:, cols], sems.at[at])

        def load(at):
            source, target = ((wo_far, wo), (wu_far, wu), (wd_far, wd))[at]
            return pltpu.make_async_copy(source, target, sems.at[3 + at])

        @pl.when(step == 0)
        def _():
            for at in range(3):
                third(at).start()
            load(0).start()
            sums_ref[...] = jnp.zeros_like(sums_ref)
            local = mm(one_hot(src_ref[...], slots), a_ref[...], TN).astype(bf16)
            regs[...] = local
            for part_id in range(3):
                at = slice(part_id * width, (part_id + 1) * width)
                third(part_id).wait()
                if part_id == 2:
                    load(1).start()
                    load(2).start()
                got = mm(local, wq[:, at])
                if part_id == 0:
                    got = got + qvb_ref[:, :width]
                if part_id == 2:
                    got = got + qvb_ref[:, width:]
                rqkv[:, at] = got.astype(bf16)

        @pl.when(step < captions)
        def _():
            image = sc_ref[8 + step]
            length = sc_ref[8 + captions + step]
            count = sc_ref[8 + 2 * captions + image]
            at = pl.ds(pl.multiple_of(image * regions, regions), regions)
            here = pl.ds(pl.multiple_of(step * seq, seq), seq)
            x_ref[:text_len, :] = t_ref[...]
            x_ref[text_len:, :] = regs[at, :]
            qkv_ref[:text_len, :] = tq_ref[...]
            qkv_ref[text_len:, :] = rqkv[at, :]
            place = lax.broadcasted_iota(jnp.int32, (seq, 1), 0)
            row_end = jnp.where(place < text_len, length, text_len + count)
            row_mask = jnp.where(place < row_end, 1.0, 0.0)
            key_bias = jnp.where(place < row_end, 0.0, -1e30)
            first = lax.broadcasted_iota(jnp.int32, (1, 2 * HEAD), 1) < HEAD
            scale = [
                jnp.where(first, 0.125, 0.0).astype(bf16),
                jnp.where(first, 0.0, 0.125).astype(bf16),
            ]
            def pair_forward(pair, carry):
                def cols(base):
                    return pl.ds(pl.multiple_of(base + pair * 2 * HEAD, 2 * HEAD), 2 * HEAD)

                q = qkv_ref[:, cols(0)]
                k = qkv_ref[:, cols(width)]
                v = qkv_ref[:, cols(2 * width)]
                scores = mm(k, jnp.concatenate([q * scale[0], q * scale[1]], 0), NT) + key_bias
                raised = jnp.exp(scores - jnp.max(scores, 0, keepdims=True))
                low = (raised * (1.0 / jnp.sum(raised, 0, keepdims=True))).astype(bf16)
                probs_ref[pair] = low
                outs = mm(low, v, TN)
                ctx_ref[:, cols(0)] = jnp.where(first, outs[:seq], outs[seq:]).astype(bf16)
                return carry

            lax.fori_loop(0, HEADS // 2, pair_forward, 0, unroll=UNROLL)

            @pl.when(step == 0)
            def _():
                load(0).wait()

            x_wide = x_ref[...].astype(f32)
            attn_out = mm(ctx_ref[...], wo[...]) + ob_ref[...]
            normed, inv = norm_parts(x_wide + attn_out)
            an_ref[here, :] = normed
            ai_ref[here, :] = jnp.broadcast_to(inv, (seq, 128))
            hidden = normed * ag_ref[...] + as_ref[...]
            hidden_low = hidden.astype(bf16)
            hid_ref[here, :] = hidden_low

            @pl.when(step == 0)
            def _():
                load(1).wait()

            for piece in range(parts):
                at = slice(piece * part, (piece + 1) * part)
                upper = mm(hidden_low, wu[:, at]) + ub_ref[:, at]
                phi = 0.5 * (1.0 + lax.erf(upper * inv_sqrt_two))
                act_all[here, at] = (upper * phi).astype(bf16)
                slope = phi + upper * jnp.exp(-0.5 * upper * upper) * inv_sqrt_tau
                slope_ref[here, at] = slope.astype(bf16)

            @pl.when(step == 0)
            def _():
                load(2).wait()

            ffn_out = mm(act_all[here, :], wd[...]) + db_ref[...]
            ffn_normed, ffn_inv = norm_parts(hidden + ffn_out)
            out_ref[...] = ((ffn_normed * fg_ref[...] + fs_ref[...]) * row_mask).astype(bf16)
            cot = og_ref[...].astype(f32) * row_mask
            second = norm_back(cot, ffn_normed, ffn_inv, fg_ref[...])
            ds_ref[here, :] = second
            low = second.astype(bf16)
            df_ref[here, :] = low
            for at, value in enumerate(
                (
                    cot * ffn_normed,
                    cot,
                    low.astype(f32),
                    row_mask * x_wide * x_wide,
                    row_mask * attn_out * attn_out,
                    row_mask * ffn_out * ffn_out,
                    jnp.broadcast_to(row_mask, (seq, width)),
                )
            ):
                sums_ref[at : at + 1, :] += row_sum(value)

        @pl.when(step >= captions)
        def _():
            acts = pl.ds(pl.multiple_of((step - captions) * part, part), part)
            got = mm(act_all[:, acts], df_ref[...], TN)
            mine = sc_ref[0] == 0
            send_ref[...] = jnp.where(mine, got[:, half:], got[:, :half]).astype(bf16)
            keep_ref[...] = jnp.where(mine, got[:, :half], got[:, half:]).astype(bf16)

    def rowwise(size, cols):
        return pl.BlockSpec((size, cols), lambda i, s: (jnp.minimum(i, captions - 1), 0))

    anywhere = pl.BlockSpec(memory_space=pl.ANY)
    return pl.pallas_call(
        kernel,
        grid_spec=pltpu.PrefetchScalarGridSpec(
            num_scalar_prefetch=1,
            grid=(grid,),
            in_specs=[
                rowwise(text_len, width),
                rowwise(text_len, 3 * width),
                whole((slots, width)),
                whole((1, slots)),
                rowwise(seq, width),
                anywhere,
                whole((1, 2 * width)),
                anywhere,
                vec(width),
                vec(width),
                vec(width),
                anywhere,
                whole((1, ff)),
                anywhere,
                vec(width),
                vec(width),
                vec(width),
            ],
            out_specs=[rowwise(seq, width), rowwise(seq, width), rowwise(seq, 3 * width)]
            + [pl.BlockSpec((HEADS // 2, seq, 2 * seq), lambda i, s: (jnp.minimum(i, captions - 1), 0, 0))]
            + [rowwise(seq, width)]
            + [VMEM] * 9
            + [pl.BlockSpec((part, half), lambda i, s: (jnp.maximum(i - captions, 0), 0))] * 2,
            scratch_shapes=[
                pltpu.VMEM((slots, width), bf16),
                pltpu.VMEM((slots, 3 * width), bf16),
                pltpu.VMEM((rows, ff), bf16),
                pltpu.VMEM(w_qkv.shape, bf16),
                pltpu.VMEM(w_out.shape, bf16),
                pltpu.SemaphoreType.DMA((6,)),
            ],
        ),
        out_shape=[
            apart((rows, width), bf16),
            apart((rows, width), bf16),
            apart((rows, 3 * width), bf16),
            apart((captions * HEADS // 2, seq, 2 * seq), bf16),
            apart((rows, width), bf16),
            near((rows, width)),
            near((rows, 128)),
            near((rows, width), bf16),
            near((rows, ff), bf16),
            near((rows, width)),
            near((rows, width), bf16),
            near((8, width)),
            near(w_up.shape, bf16),
            near(w_down.shape, bf16),
            apart((ff, half), bf16),
            apart((ff, half), bf16),
        ],
        compiler_params=params(33),
        cost_estimate=cost(30),
        name="forward",
    )(
        scalars,
        *(
            far(v)
            for v in (
                text, text_low, arrived, source, out_grad, w_qkv, qv_bias, w_out, out_bias,
                attn_gain, attn_shift, w_up, up_bias, w_down, down_bias, ffn_gain, ffn_shift,
            )
        ),
    )


def ffn_backward(core, d_ffn, d_second, slope, attn_normed, attn_inv, w_down, w_up, attn_gain, seq, hold, first, size, begun):
    rows, width = d_ffn.shape
    ff = w_up.shape[1]
    parts = 4
    part = ff // parts

    def kernel(c_ref, df_ref, ds_ref, sl_ref, an_ref, ai_ref, wd, wu, ag_ref, *rest):
        dup_ref, dr_ref, da_ref, sums_ref, up_ref = rest[len(begun) + len(hold) :]
        step = pl.program_id(0)

        @pl.when(step == 0)
        def _():
            if begun:
                sums_ref[...] = rest[3][...]
                up_ref[...] = rest[4][...]
            else:
                sums_ref[...] = jnp.zeros_like(sums_ref)
                up_ref[...] = jnp.zeros_like(up_ref)

        here = pl.ds(pl.multiple_of((first + step) * seq, seq), seq)
        d_low = df_ref[here, :]
        for piece in range(parts):
            at = slice(piece * part, (piece + 1) * part)
            d_act = mm(d_low, wd[at, :], NT)
            low = (d_act * sl_ref[here, at].astype(f32)).astype(bf16)
            dup_ref[here, at] = low
            up_ref[0:1, at] += row_sum(low.astype(f32))
        d_hidden = ds_ref[here, :] + mm(dup_ref[here, :], wu[...], NT)
        normed = an_ref[here, :]
        resid = norm_back(d_hidden, normed, ai_ref[here, 0:1], ag_ref[...])
        dr_ref[here, :] = resid
        low = resid.astype(bf16)
        da_ref[here, :] = low
        sums_ref[0:1, :] += row_sum(d_hidden * normed)
        sums_ref[1:2, :] += row_sum(d_hidden)
        sums_ref[2:3, :] += row_sum(low.astype(f32))

    return pl.pallas_call(
        kernel,
        grid_spec=pltpu.PrefetchScalarGridSpec(
            num_scalar_prefetch=1,
            grid=(size,),
            in_specs=[VMEM] * 7
            + [vec(width)]
            + [VMEM] * len(begun)
            + [VMEM] * len(hold),
            out_specs=[VMEM] * 5,
        ),
        out_shape=[
            near((rows, ff), bf16),
            near((rows, width)),
            near((rows, width), bf16),
            near((8, width)),
            near((8, ff)),
        ],
        input_output_aliases={9: 0, 10: 1, 11: 2} if begun else {},
        compiler_params=params(6),
        cost_estimate=cost(4 * size),
        name="ffn_backward",
    )(core, d_ffn, d_second, slope, attn_normed, attn_inv, w_down, w_up, attn_gain, *begun, *hold)


def up_gradient(core, hidden_low, d_upper):
    rows, width = hidden_low.shape

    def kernel(c_ref, h_ref, d_ref, send_ref, keep_ref):
        step = pl.program_id(0)
        here = pl.ds(pl.multiple_of(step * width, width), width)
        for to_ref, side in ((send_ref, 1 - c_ref[0]), (keep_ref, c_ref[0])):
            cols = pl.ds(pl.multiple_of((2 * side + step) * width, width), width)
            to_ref[:, here] = mm(h_ref[...], d_ref[:, cols], TN).astype(bf16)

    return pl.pallas_call(
        kernel,
        grid_spec=pltpu.PrefetchScalarGridSpec(
            num_scalar_prefetch=1, grid=(2,), in_specs=[VMEM, VMEM], out_specs=[VMEM, VMEM]
        ),
        out_shape=[near((width, 2 * width), bf16)] * 2,
        compiler_params=params(6),
        cost_estimate=cost(0.1),
        name="up_gradient",
    )(core, hidden_low, d_upper)


def attention_backward(scalars, d_attn, d_resid, probs, qkv, source, w_out, w_qkv, dims, first_caption, size, begun):
    captions, images = dims
    rows, width = d_attn.shape
    seq = rows // captions
    slots = source.shape[1]
    regions = slots // images
    text_len = seq - regions
    last = first_caption + size == captions

    def kernel(
        sc_ref, da_ref, dr_ref, p_ref, qkv_ref, src_ref, wo_ref, wq, *rest,
    ):
        begun_refs = rest[: len(begun)]
        dqkv_ref, text_ref, back_ref, sums_ref, d_img, d_ctx_ref = rest[len(begun) :]
        step = pl.program_id(0)
        here = pl.ds(pl.multiple_of((first_caption + step) * seq, seq), seq)

        @pl.when(step == 0)
        def _():
            if begun:
                sums_ref[...] = begun_refs[3][...]
                d_img[...] = begun_refs[2][...]
            else:
                sums_ref[...] = jnp.zeros_like(sums_ref)
                d_img[...] = jnp.zeros_like(d_img)

        d_ctx_ref[...] = mm(da_ref[here, :], wo_ref[...], NT).astype(bf16)
        first = lax.broadcasted_iota(jnp.int32, (1, 2 * HEAD), 1) < HEAD
        masks = [jnp.where(first, 1.0, 0.0).astype(bf16), jnp.where(first, 0.0, 1.0).astype(bf16)]
        def pair_backward(pair, carry):
            def cols(base):
                return pl.ds(pl.multiple_of(base + pair * 2 * HEAD, 2 * HEAD), 2 * HEAD)

            q = qkv_ref[here, cols(0)]
            k = qkv_ref[here, cols(width)]
            v = qkv_ref[here, cols(2 * width)]
            d_c = d_ctx_ref[:, cols(0)]
            both_c = jnp.concatenate([d_c * masks[0], d_c * masks[1]], 0)
            both_q = jnp.concatenate([q * masks[0], q * masks[1]], 0)
            low = p_ref[(first_caption + step) * (HEADS // 2) + pair]
            d_probs = mm(v, both_c, NT)
            wide = low.astype(f32)
            both = wide * d_probs
            inner = jnp.sum(both, 0, keepdims=True)
            d_scores = (both - wide * inner).astype(bf16)
            d_q = mm(d_scores, k, TN) * 0.125
            dqkv_ref[here, cols(0)] = jnp.where(first, d_q[:seq], d_q[seq:]).astype(bf16)
            dqkv_ref[here, cols(width)] = (mm(d_scores, both_q) * 0.125).astype(bf16)
            dqkv_ref[here, cols(2 * width)] = mm(low, both_c).astype(bf16)
            return carry

        lax.fori_loop(0, HEADS // 2, pair_backward, 0, unroll=UNROLL)

        sums_ref[0:1, :] += row_sum(dqkv_ref[here, :width].astype(f32))
        sums_ref[1:2, :] += row_sum(dqkv_ref[here, 2 * width :].astype(f32))
        d_x = mm(dqkv_ref[here, :], wq[...], NT) + dr_ref[here, :]
        text_ref[...] = d_x[:text_len]
        at = pl.ds(pl.multiple_of(sc_ref[8 + first_caption + step] * regions, regions), regions)
        d_img[at, :] += d_x[text_len:]

        @pl.when(step == size - 1)
        def _():
            if last:
                back_ref[...] = mm(one_hot(src_ref[...], slots), d_img[...].astype(bf16)).astype(bf16)
            else:
                back_ref[...] = d_img[...]

    return pl.pallas_call(
        kernel,
        grid_spec=pltpu.PrefetchScalarGridSpec(
            num_scalar_prefetch=1,
            grid=(size,),
            in_specs=[VMEM] * 4
            + [whole((1, slots)), VMEM, VMEM]
            + ([VMEM, pl.BlockSpec(memory_space=pl.ANY)] + [VMEM, VMEM] if begun else []),
            out_specs=[
                VMEM,
                pl.BlockSpec((text_len, width), lambda i, s: (i + first_caption, 0)),
                VMEM,
                VMEM,
            ],
            scratch_shapes=[
                pltpu.VMEM((slots, width), f32),
                pltpu.VMEM((seq, width), bf16),
            ],
        ),
        out_shape=[
            near((rows, 3 * width), bf16),
            pltpu.HBM((captions * text_len, width), f32),
            near((slots, width), bf16 if last else f32),
            near((8, width)),
        ],
        input_output_aliases={8: 0, 9: 1} if begun else {},
        compiler_params=params(11),
        cost_estimate=cost(5 * size),
        name="attention_backward",
    )(scalars, d_attn, d_resid, probs, qkv, source, w_out, w_qkv, *begun)


def qkvo_gradient(core, x, d_qkv, context, d_attn):
    rows, width = x.shape

    def kernel(c_ref, x_ref, dq_ref, ctx_ref, da_ref, send_ref, keep_ref):
        step = pl.program_id(0)
        block = lax.rem(step + 2 * (1 - c_ref[0]), 4)
        cols = pl.ds(pl.multiple_of(jnp.minimum(block, 2) * width, width), width)

        def gradient(to_ref):
            @pl.when(block < 3)
            def _():
                to_ref[...] = mm(x_ref[...], dq_ref[:, cols], TN).astype(bf16)

            @pl.when(block == 3)
            def _():
                to_ref[...] = mm(ctx_ref[...], da_ref[...], TN).astype(bf16)

        @pl.when(step < 2)
        def _():
            gradient(send_ref)

        @pl.when(step >= 2)
        def _():
            gradient(keep_ref)

    return pl.pallas_call(
        kernel,
        grid_spec=pltpu.PrefetchScalarGridSpec(
            num_scalar_prefetch=1,
            grid=(4,),
            in_specs=[VMEM] * 4,
            out_specs=[
                pl.BlockSpec((width, width), lambda i, s: (0, jnp.minimum(i, 1))),
                pl.BlockSpec((width, width), lambda i, s: (0, jnp.maximum(i - 2, 0))),
            ],
        ),
        out_shape=[apart((width, 2 * width), bf16)] * 2,
        compiler_params=params(11),
        cost_estimate=cost(5),
        name="qkvo_gradient",
    )(core, x, d_qkv, context, d_attn)


def region_backward(
    core, returned, target, normed, inv, gain, features, boxes, w_visual, w_box_t,
    sums_forward, sums_ffn, sums_up, sums_attn, groups,
):
    rows, width = returned.shape
    feat = features.shape[1]
    half = width // 2
    steps = 4
    part = feat // steps
    quarter = feat // groups // 4
    tall = quarter + 8
    per_step = groups // steps
    box = boxes.shape[0]
    share = width // groups
    ff_share = sums_up.shape[1] // groups

    def kernel(
        c_ref, r_ref, t_ref, n_ref, i_ref, g_ref, f_ref, box_ref, wv_ref, wb_ref, sf_ref, sn_ref, su_ref, sa_ref,
        send_ref, keep_ref, fg_ref, bg_ref, dpre, small,
    ):
        step = pl.program_id(0)

        @pl.when(step == 0)
        def _():
            d_region = mm(one_hot(t_ref[...], rows), r_ref[...], TN)
            normed = n_ref[...]
            low = norm_back(d_region, normed, i_ref[:, 0:1], g_ref[...]).astype(bf16)
            dpre[...] = low
            bg_ref[...] = mm(wb_ref[...], low, NT)
            boxes_grad = mm(box_ref[...], low)
            vectors = [
                row_sum(low.astype(f32)),
                row_sum(d_region * normed),
                row_sum(d_region),
                sf_ref[0:1, :],
                sf_ref[1:2, :],
                sf_ref[2:3, :],
                sn_ref[0:1, :],
                sn_ref[1:2, :],
                sn_ref[2:3, :],
            ] + [boxes_grad[at : at + 1] for at in range(box)]
            small[...] = jnp.zeros_like(small)
            lane = lax.broadcasted_iota(jnp.int32, (1, half), 1)
            stats = jnp.zeros((1, half), f32)
            for at in range(4):
                total = jnp.sum(sf_ref[3 + at : 4 + at, :], 1, keepdims=True)
                stats = jnp.where(lane == at, total, stats)
            for group in range(groups):
                small[group, 0:1, 0:ff_share] = su_ref[0:1, group * ff_share : (group + 1) * ff_share]
                for side in range(2):
                    first = group * 2 * share
                    flat = jnp.concatenate([sa_ref[0:1, :], sa_ref[1:2, :]], 1)
                    small[group, 1:2, 0 : 2 * share] = flat[:, first : first + 2 * share]
                for at, value in enumerate(vectors):
                    row, col = (1, 2) if at == 0 else (2 + (at - 1) // 3, (at - 1) % 3)
                    small[group, row : row + 1, 128 * col : 128 * col + share] = value[
                        :, group * share : (group + 1) * share
                    ]
                small[group, 6:7, :] = stats

        got = mm(f_ref[...], dpre[...], TN)
        mine = c_ref[0] == 0
        for to_ref, low_half in ((send_ref, jnp.logical_not(mine)), (keep_ref, mine)):
            chosen = jnp.where(low_half, got[:, :half], got[:, half:]).astype(bf16)
            for group in range(per_step):
                for bit in range(2):
                    for piece in range(2):
                        at = ((group * 2 + bit) * 2 + piece) * quarter
                        to_ref[group, bit, piece, :quarter, :] = chosen[at : at + quarter]
                        if piece == 0:
                            to_ref[group, bit, piece, quarter:, :] = small[step * per_step + group].astype(bf16)
                        else:
                            to_ref[group, bit, piece, quarter:, :] = jnp.zeros((8, half), bf16)
        fg_ref[...] = mm(dpre[...], wv_ref[...], NT)

    out = pl.BlockSpec((per_step, 2, 2, tall, half), lambda i, s: (i, 0, 0, 0, 0))
    return pl.pallas_call(
        kernel,
        grid_spec=pltpu.PrefetchScalarGridSpec(
            num_scalar_prefetch=1,
            grid=(steps,),
            in_specs=[
                whole((rows, width)),
                whole((1, rows)),
                whole((rows, width)),
                whole((rows, 128)),
                vec(width),
                pl.BlockSpec((rows, part), lambda i, s: (0, i)),
                whole(boxes.shape),
                pl.BlockSpec((part, width), lambda i, s: (i, 0)),
                whole(w_box_t.shape),
                whole(sums_forward.shape),
                whole(sums_ffn.shape),
                whole(sums_up.shape),
                whole(sums_attn.shape),
            ],
            out_specs=[out, out, pl.BlockSpec((rows, part), lambda i, s: (0, i)), whole((box, rows))],
            scratch_shapes=[pltpu.VMEM((rows, width), bf16), pltpu.VMEM((groups, 8, half), f32)],
        ),
        out_shape=[
            pltpu.HBM((groups, 2, 2, tall, half), bf16),
            pltpu.HBM((groups, 2, 2, tall, half), bf16),
            pltpu.HBM((rows, feat), f32),
            shape((box, rows)),
        ],
        compiler_params=params(20),
        cost_estimate=cost(6),
        name="region_backward",
    )(
        core, returned, far(target), far(normed), far(inv), far(gain), far(features), far(boxes), far(w_visual),
        w_box_t, sums_forward, sums_ffn, sums_up, sums_attn,
    )


def device_number():
    return lax.axis_index("dp") * lax.axis_size("enc") + lax.axis_index("enc")


def swap(values, bit):
    count = lax.axis_size("dp") * lax.axis_size("enc")
    return lax.ppermute(values, ("dp", "enc"), [(i, i ^ bit) for i in range(count)])


def add(a, b):
    return (a.astype(f32) + b.astype(f32)).astype(bf16)


def scalar_call(kernel, bits, ins, in_specs, outs, out_specs, grid, limit, name, last=False, place=near):
    outs = outs if last else [place(o.shape, o.dtype) for o in outs]
    return pl.pallas_call(
        kernel,
        grid_spec=pltpu.PrefetchScalarGridSpec(
            num_scalar_prefetch=1, grid=(grid,), in_specs=in_specs, out_specs=out_specs
        ),
        out_shape=outs,
        compiler_params=params(limit),
        cost_estimate=cost(1),
        name=name,
    )(bits, *ins)


def first_split(bits, kept, got, groups, place=near):
    tall = kept.ndim == 5
    high = groups // 2
    if tall:
        rows, cols = kept.shape[3:]
        view = (high, 2, 2, 2, rows, cols)
        block = (1, 2, 2, 2, rows, cols)
    else:
        rows, cols = kept.shape[0] // groups, kept.shape[1] // 4
        view = (high, 2, rows, 4 * cols)
        block = (1, 2, rows, 4 * cols)

    def kernel(b_ref, k_ref, r_ref, a_send, a_keep, b_send, b_keep):
        bit2, bit4 = b_ref[1], b_ref[2]

        def total(y, x, piece):
            if tall:
                return add(k_ref[0, y, x, piece], r_ref[0, y, x, piece])
            at = pl.ds(pl.multiple_of((2 * x + piece) * cols, 128), cols)
            return add(k_ref[0, y, :, at], r_ref[0, y, :, at])

        for other in range(2):
            a_send[0, other] = total(other, 1 - bit2, 0)
            a_keep[0, other] = total(other, bit2, 0)
            b_send[0, other] = total(1 - bit4, other, 1)
            b_keep[0, other] = total(bit4, other, 1)

    spec = pl.BlockSpec(block, lambda i, s: (i,) + (0,) * (len(block) - 1))
    out = pl.BlockSpec((1, 2, rows, cols), lambda i, s: (i, 0, 0, 0))
    return scalar_call(
        kernel, bits, (kept.reshape(view), got.reshape(view)), [spec, spec],
        [shape((high, 2, rows, cols), bf16)] * 4, [out] * 4, high, 6, "first_split", place=place,
    )


def second_split(bits, a_kept, a_got, b_kept, b_got):
    high, _, rows, cols = a_kept.shape

    def kernel(b_ref, ak, ar, bk, br, a_send, a_keep, b_send, b_keep):
        bit2, bit4 = b_ref[1], b_ref[2]
        a_send[0] = add(ak[0, 1 - bit4], ar[0, 1 - bit4])
        a_keep[0] = add(ak[0, bit4], ar[0, bit4])
        b_send[0] = add(bk[0, 1 - bit2], br[0, 1 - bit2])
        b_keep[0] = add(bk[0, bit2], br[0, bit2])

    spec = pl.BlockSpec((1, 2, rows, cols), lambda i, s: (i, 0, 0, 0))
    out = pl.BlockSpec((1, rows, cols), lambda i, s: (i, 0, 0))
    return scalar_call(
        kernel, bits, (a_kept, a_got, b_kept, b_got), [spec] * 4,
        [shape((high, rows, cols), bf16)] * 4, [out] * 4, high, 6, "second_split",
    )


def join_split(bits, pairs, place=near):
    high, _, cols = pairs[0][0].shape
    sizes = [kept.shape[1] for kept, _ in pairs]

    def kernel(b_ref, *refs):
        bit = b_ref[3]
        send, keep = refs[-2:]
        at = 0
        for n, size in enumerate(sizes):
            kept, got = refs[2 * n : 2 * n + 2]
            send[0, at : at + size] = add(kept[1 - bit], got[1 - bit])
            keep[0, at : at + size] = add(kept[bit], got[bit])
            at += size

    ins = [value for pair in pairs for value in pair]
    specs = [pl.BlockSpec((2, v.shape[1], cols), lambda i, s: (i, 0, 0)) for v in ins]
    out = pl.BlockSpec((1, sum(sizes), cols), lambda i, s: (i, 0, 0))
    return scalar_call(
        kernel, bits, ins, specs, [shape((high // 2, sum(sizes), cols), bf16)] * 2, [out] * 2,
        high // 2, 6, "join_split", place=place,
    )


def late_split(bits, kept, got, which):
    high, rows, cols = kept.shape

    def kernel(b_ref, k_ref, r_ref, send, keep):
        bit = b_ref[which]
        send[0] = add(k_ref[1 - bit], r_ref[1 - bit])
        keep[0] = add(k_ref[bit], r_ref[bit])

    spec = pl.BlockSpec((2, rows, cols), lambda i, s: (i, 0, 0))
    out = pl.BlockSpec((1, rows, cols), lambda i, s: (i, 0, 0))
    return scalar_call(
        kernel, bits, (kept, got), [spec] * 2, [shape((high // 2, rows, cols), bf16)] * 2, [out] * 2,
        high // 2, 6, "late_split",
    )


def over_two(halves):
    return swap(halves[0], 2), halves[1], swap(halves[2], 4), halves[3]


def over_other_two(halves):
    return swap(halves[0], 4), halves[1], swap(halves[2], 2), halves[3]


def second(bits, moved):
    return second_split(bits, moved[1], moved[0], moved[3], moved[2])


def join(bits, *moved, place=near):
    pairs = []
    for one in moved:
        pairs += [(one[1], one[0]), (one[3], one[2])]
    return join_split(bits, pairs, place)


def after_all(*trees):
    leaves, tree = jax.tree.flatten(trees)
    return jax.tree.unflatten(tree, lax.optimization_barrier(leaves))


def late_first(bits, kept, got):
    if kept.shape[0] == 1:
        return (kept + got,)
    return late_split(bits, kept, got, 4)


def late_move(halves):
    return swap(halves[0], 16) if len(halves) > 1 else None


def late_rest(bits, halves, moved):
    bit, which = 16, 5
    while len(halves) > 1:
        if halves[1].shape[0] == 1:
            halves = (halves[1] + moved,)
        else:
            halves = late_split(bits, halves[1], moved, which)
            bit, which = 2 * bit, which + 1
            moved = swap(halves[0], bit)
    return halves[0][0]


def spread(mine):
    over_x = swap(mine, 2)
    return mine, over_x, swap(mine, 1), swap(over_x, 1)


def pick(b_ref, pieces, core, x):
    mine, over_x, over_core, over_both = pieces
    same_x = b_ref[1] == x
    return jnp.where(
        b_ref[0] == core, jnp.where(same_x, mine, over_x), jnp.where(same_x, over_core, over_both)
    ).astype(f32)


def finish_down(bits, pieces):
    rows, cols = pieces[0].shape

    def kernel(b_ref, p0, p1, p2, p3, down_ref):
        for core in range(2):
            for x in range(2):
                got = pick(b_ref, (p0[...], p1[...], p2[...], p3[...]), core, x)
                down_ref[x * rows : (x + 1) * rows, core * cols : (core + 1) * cols] = got

    outs = [shape((2 * rows, 2 * cols))]
    return scalar_call(
        kernel, bits, pieces, [whole((rows, cols))] * 4, outs, [whole(o.shape) for o in outs], 1, 8, "finish_down", True
    )[0]


def finish_wide(bits, pieces, sizes):
    rows, cols = pieces[0].shape
    part = rows // 2

    def kernel(b_ref, p0, p1, p2, p3, *out_refs):
        for core in range(2):
            for x in range(2):
                got = pick(b_ref, (p0[...], p1[...], p2[...], p3[...]), core, x)
                for piece in range(2):
                    at = ((core * 2 + x) * 2 + piece) * cols
                    for out_ref, size in zip(out_refs, sizes):
                        if 0 <= at < size:
                            out_ref[:, at : at + cols] = got[piece * part : (piece + 1) * part]
                        at -= size

    outs = [shape((part, size)) for size in sizes]
    return scalar_call(
        kernel, bits, pieces, [whole((rows, cols))] * 4, outs, [whole(o.shape) for o in outs], 1, 8, "finish_wide", True
    )


def finish_visual(bits, pieces, ff_share, share, box):
    rows, cols = pieces[0].shape
    tall = rows // 2
    quarter = tall - 8
    sizes = [share] * 9 + [2 * share, ff_share]

    def kernel(b_ref, p0, p1, p2, p3, vis_ref, box_ref, rms_ref, *small_refs):
        for core in range(2):
            for x in range(2):
                got = pick(b_ref, (p0[...], p1[...], p2[...], p3[...]), core, x)
                for piece in range(2):
                    low = piece * tall
                    vis_ref[(2 * x + piece) * quarter : (2 * x + piece + 1) * quarter, core * cols : (core + 1) * cols] = got[
                        low : low + quarter
                    ]
        small = p0[quarter : quarter + 8, :].astype(f32)
        for at in range(9):
            row, col = (1, 2) if at == 0 else (2 + (at - 1) // 3, (at - 1) % 3)
            small_refs[at][...] = small[row, 128 * col : 128 * col + share]
        small_refs[9][...] = small[1, 0 : 2 * share]
        small_refs[10][...] = small[0, 0:ff_share]
        for at in range(9, 9 + box):
            row, col = 2 + (at - 1) // 3, (at - 1) % 3
            box_ref[at - 9 : at - 8, :] = small[row : row + 1, 128 * col : 128 * col + share]
        stats = small[6, 0:128]
        total = jnp.sum(small[6:7, 3:4])
        rms_ref[...] = jnp.sqrt(stats / total)[:3]

    outs = [shape((4 * quarter, 2 * cols)), shape((box, share)), shape((3,))] + [shape((size,)) for size in sizes]
    specs = [whole(o.shape) for o in outs[:2]] + [vec(3)] + [vec(size) for size in sizes]
    return scalar_call(
        kernel, bits, pieces, [whole((rows, cols))] * 4, outs, specs, 1, 8, "finish_visual", True
    )


def gate(value, *others):
    return lax.optimization_barrier((value, *others))[0]


def on_device(
    text_embed,
    region_features,
    boxes,
    caption_image,
    caption_lengths,
    region_counts,
    region_target,
    region_source,
    w_visual,
    w_box,
    visual_bias,
    visual_gain,
    visual_shift,
    w_qkv,
    qv_bias,
    w_out,
    out_bias,
    attn_gain,
    attn_shift,
    w_up,
    up_bias,
    w_down,
    down_bias,
    ffn_gain,
    ffn_shift,
    out_grad,
):
    width = text_embed.shape[1]
    captions = caption_image.shape[0]
    images = region_counts.shape[0]
    dims = (captions, images)
    axes = ("dp", "enc")
    groups = lax.axis_size("dp")
    count = groups * lax.axis_size("enc")
    me = device_number().astype(jnp.int32)
    places = lax.iota(jnp.int32, 8)
    scalars = jnp.concatenate([(me >> places) & 1, caption_image, caption_lengths, region_counts])
    w_box_t = w_box.T
    row = lambda v: v.reshape(1, -1)
    qv_row = row(qv_bias)

    message, vis_normed, vis_inv = region_forward(
        region_features, boxes, region_target, w_visual, w_box_t, visual_bias, visual_gain, visual_shift
    )
    arrived = lax.all_to_all(message, axes, split_axis=0, concat_axis=0, tiled=True)
    text_low = text_qkv(text_embed, w_qkv, qv_row)
    (
        out_rows, x, qkv, probs, context, attn_normed, attn_inv, hidden_low, slope, d_second, d_ffn,
        sums_forward, w_up_near, w_down_near, down_sent, down_kept,
    ) = forward(
        scalars, text_embed, text_low, arrived, region_source, out_grad, w_qkv, qv_row, w_out,
        out_bias, attn_gain, attn_shift, w_up, row(up_bias), w_down, down_bias, ffn_gain, ffn_shift, dims,
    )
    seq = x.shape[0] // captions
    rest = captions - 1
    bits = core = scalars
    hold = ()
    ffn_ins = (d_ffn, d_second, slope, attn_normed, attn_inv, w_down_near, w_up_near, attn_gain, seq, hold)
    down_view = (groups, 2, 2, w_down.shape[0] // groups // 4, width // 2)
    down_sent, down_kept = down_sent.reshape(down_view), down_kept.reshape(down_view)

    moved = swap(down_sent, 1)
    begun = ffn_backward(core, *ffn_ins, 0, 1, ())

    moved, begun, sc = after_all(moved, begun, scalars)
    down = first_split(sc, down_kept, moved, groups)
    down, begun, sc = after_all(down, begun, sc)
    moved = over_two(down)
    d_upper, d_resid, d_attn, sums_ffn, sums_up = ffn_backward(sc, *ffn_ins, 1, rest, tuple(begun))
    up_sent, up_kept = up_gradient(sc, hidden_low, gate(d_upper, d_attn))

    moved, up_sent, up_kept, d_attn, sc = after_all(moved, up_sent, up_kept, d_attn, sc)
    down = second(sc, moved)
    down, up_sent, up_kept, sc = after_all(down, up_sent, up_kept, sc)
    moved = over_other_two(down), swap(up_sent, 1)
    att_ins = (d_attn, d_resid, probs, qkv, region_source, w_out, w_qkv, dims)
    begun = attention_backward(sc, *att_ins, 0, 1, ())

    moved, up_kept, begun, sc = after_all(moved, up_kept, begun, sc)
    up = first_split(sc, up_kept, moved[1], groups)
    down = join(sc, moved[0])
    down, up, begun, sc = after_all(down, up, begun, sc)
    moved = over_two(up), swap(down[0], 8)
    d_qkv, text_grad, back_message, sums_attn = attention_backward(sc, *att_ins, 1, rest, tuple(begun))

    moved, down, d_qkv, back_message, sc = after_all(moved, down, d_qkv, back_message, sc)
    up = second(sc, moved[0])
    down = late_first(sc, down[1], moved[1])
    up, down, sc = after_all(up, down, sc)
    moved = over_other_two(up), late_move(down)
    qkvo_sent, qkvo_kept = qkvo_gradient(sc, x, d_qkv, context, d_attn)

    moved, down, qkvo_sent, qkvo_kept, back_message, sc = after_all(
        moved, down, qkvo_sent, qkvo_kept, back_message, sc
    )
    up = join(sc, moved[0], place=apart)
    down = late_rest(sc, down, moved[1])
    up, down, qkvo_sent, qkvo_kept, back_message, sc = after_all(up, down, qkvo_sent, qkvo_kept, back_message, sc)
    returned = lax.all_to_all(back_message, axes, split_axis=0, concat_axis=0, tiled=True)
    qkvo = first_split(sc, qkvo_kept, swap(qkvo_sent, 1), groups, apart)
    up_moved = swap(up[0], 8)
    down = spread(down)

    qkvo_moved = over_two(qkvo)
    returned, sc = after_all(returned, gate(sc, *qkvo))
    vis_sent, vis_kept, feature_grad, box_grad = region_backward(
        sc, returned, region_target, vis_normed, vis_inv, visual_gain,
        region_features, boxes, w_visual, w_box_t, sums_forward, sums_ffn, sums_up, sums_attn, groups,
    )

    up_moved, qkvo_moved, vis_sent, vis_kept, sc = after_all(up_moved, qkvo_moved, vis_sent, vis_kept, sc)
    up = late_first(sc, up[1], up_moved)
    qkvo = second(sc, qkvo_moved)
    up, qkvo, vis_sent, sc = after_all(up, qkvo, vis_sent, sc)
    vis_moved = swap(vis_sent, 1)
    qkvo_moved = over_other_two(qkvo)
    up_moved = late_move(up)
    vis = first_split(sc, vis_kept, vis_moved, groups)
    vis_moved = over_two(vis)
    g_down = finish_down(gate(sc, *vis), down)
    sc = gate(sc, g_down)
    qkvo = join(sc, qkvo_moved)
    qkvo_moved = swap(qkvo[0], 8)
    up = spread(late_rest(sc, up, up_moved))
    vis = second(sc, vis_moved)
    vis_moved = over_other_two(vis)
    qkvo = late_first(sc, qkvo[1], qkvo_moved)
    qkvo_moved = late_move(qkvo)
    vis = join(sc, vis_moved)
    vis_moved = swap(vis[0], 8)
    (g_up,) = finish_wide(gate(sc, *vis), up, (4 * width,))
    sc = gate(sc, g_up)
    qkvo = spread(late_rest(sc, qkvo, qkvo_moved))
    vis = late_first(sc, vis[1], vis_moved)
    vis_moved = late_move(vis)
    g_qkv, g_out = finish_wide(gate(sc, *vis), qkvo, (3 * width, width))
    vis = late_rest(gate(sc, g_qkv), vis, vis_moved)
    vis = spread(gate(vis, g_qkv))
    g_visual, g_box_t, rms_values, *small = finish_visual(
        sc, vis, w_up.shape[1] // groups, width // groups, boxes.shape[0]
    )
    return (
        out_rows,
        text_grad,
        feature_grad,
        box_grad,
        rms_values,
        g_visual,
        g_box_t.T,
        small[0],
        small[1],
        small[2],
        g_qkv,
        small[9],
        g_out,
        small[8],
        small[6],
        small[7],
        g_up,
        small[10],
        g_down,
        small[5],
        small[3],
        small[4],
    )


def solution(mesh):
    return jax.shard_map(
        on_device,
        mesh=mesh,
        in_specs=(
            P(("dp", "enc"), None),
            P(("dp", "enc"), None),
            P(None, ("dp", "enc")),
            P(("dp", "enc")),
            P(("dp", "enc")),
            P(("dp", "enc")),
            P(("dp", "enc"), None),
            P(("dp", "enc"), None),
            P(),
            P(),
            P(),
            P(),
            P(),
            P(),
            P(),
            P(),
            P(),
            P(),
            P(),
            P(),
            P(),
            P(),
            P(),
            P(),
            P(),
            P(("dp", "enc"), None),
        ),
        out_specs=(
            P(("dp", "enc"), None),
            P(("dp", "enc"), None),
            P(("dp", "enc"), None),
            P(None, ("dp", "enc")),
            P(),
            P("dp", None),
            P("dp", None),
            P("dp"),
            P("dp"),
            P("dp"),
            P("dp", None),
            P("dp"),
            P("dp", None),
            P("dp"),
            P("dp"),
            P("dp"),
            P("dp", None),
            P("dp"),
            P("dp", None),
            P("dp"),
            P("dp"),
            P("dp"),
        ),
        check_vma=False,
    )
```

```python
import jax
import jax.numpy as jnp
from jax import lax
from jax.experimental import pallas as pl
from jax.experimental.pallas import tpu as pltpu
from jax.sharding import PartitionSpec as P

HEADS = 12
UNROLL = 2
HEAD = 64
epsilon = 1e-12
inv_sqrt_two = 0.7071067811865476
inv_sqrt_tau = 0.3989422804014327
f32 = jnp.float32
bf16 = jnp.bfloat16
NN = (((1,), (0,)), ((), ()))
NT = (((1,), (1,)), ((), ()))
TN = (((0,), (0,)), ((), ()))


def mm(a, b, dims=NN):
    return lax.dot_general(a, b, dims, preferred_element_type=f32)


def cost(us):
    return pl.CostEstimate(flops=int(us * 1e9), bytes_accessed=1 << 20, transcendentals=0)


def params(limit=56):
    return pltpu.CompilerParams(
        dimension_semantics=("arbitrary",), vmem_limit_bytes=limit << 20
    )


def whole(shape):
    return pl.BlockSpec(shape, lambda i, *s: (0,) * len(shape), pipeline_mode=pl.Buffered(1))


def vec(size):
    return pl.BlockSpec((size,), lambda i, *s: (0,))


VMEM = pl.BlockSpec(memory_space=pltpu.VMEM)


def far(value):
    return pltpu.with_memory_space_constraint(value, pltpu.HBM)


def apart(dims, kind=f32):
    return pltpu.HBM(dims, kind)


def near(dims, kind=f32):
    return pltpu.VMEM(dims, kind)


def shape(dims, kind=f32):
    return jax.ShapeDtypeStruct(dims, kind)


def norm_parts(values):
    centre = values - jnp.mean(values, -1, keepdims=True)
    inv_std = lax.rsqrt(jnp.mean(centre * centre, -1, keepdims=True) + epsilon)
    return centre * inv_std, inv_std


def norm_back(grad, normed, inv_std, gain):
    scaled = grad * gain
    return inv_std * (
        scaled
        - jnp.mean(scaled, -1, keepdims=True)
        - normed * jnp.mean(scaled * normed, -1, keepdims=True)
    )


def row_sum(values):
    return jnp.sum(values, 0, keepdims=True)


def one_hot(index_row, count):
    rows = lax.broadcasted_iota(jnp.int32, (count, index_row.shape[1]), 0)
    return jnp.where(rows == index_row, 1.0, 0.0).astype(bf16)


def region_forward(features, boxes, target, w_visual, w_box_t, bias, gain, shift):
    rows, feat = features.shape
    width = w_visual.shape[1]
    steps = 4
    part = feat // steps

    def kernel(f_ref, box_ref, t_ref, wv_ref, wb_ref, b_ref, g_ref, s_ref, m_ref, n_ref, i_ref, acc):
        step = pl.program_id(0)
        partial = mm(f_ref[...], wv_ref[...])

        @pl.when(step == 0)
        def _():
            acc[...] = partial + (mm(box_ref[...], wb_ref[...], TN) + b_ref[...])

        @pl.when(step > 0)
        def _():
            acc[...] += partial

        @pl.when(step == steps - 1)
        def _():
            normed, inv = norm_parts(acc[...])
            n_ref[...] = normed
            i_ref[...] = jnp.broadcast_to(inv, i_ref.shape)
            low = (normed * g_ref[...] + s_ref[...]).astype(bf16)
            m_ref[...] = mm(one_hot(t_ref[...], rows), low).astype(bf16)

    return pl.pallas_call(
        kernel,
        grid=(steps,),
        in_specs=[
            pl.BlockSpec((rows, part), lambda i: (0, i)),
            whole(boxes.shape),
            whole((1, rows)),
            pl.BlockSpec((part, width), lambda i: (i, 0)),
            whole(w_box_t.shape),
            vec(width),
            vec(width),
            vec(width),
        ],
        out_specs=[VMEM, whole((rows, width)), whole((rows, 128))],
        out_shape=[near((rows, width), bf16), apart((rows, width)), apart((rows, 128))],
        scratch_shapes=[pltpu.VMEM((rows, width), f32)],
        compiler_params=params(24),
        cost_estimate=cost(3),
        name="region_forward",
    )(far(features), far(boxes), far(target), far(w_visual), w_box_t, far(bias), far(gain), far(shift))


def text_qkv(text, w_qkv, qv_bias):
    rows, width = text.shape

    def kernel(t_ref, w_ref, b_ref, o_ref):
        step = pl.program_id(0)
        bias = b_ref[...] * jnp.where(step == 1, 0.0, 1.0)
        o_ref[...] = (mm(t_ref[...], w_ref[...]) + bias).astype(bf16)

    return pl.pallas_call(
        kernel,
        grid=(3,),
        in_specs=[
            whole((rows, width)),
            pl.BlockSpec((width, width), lambda i: (0, i)),
            pl.BlockSpec((1, width), lambda i: (0, i // 2)),
        ],
        out_specs=pl.BlockSpec((rows, width), lambda i: (0, i)),
        out_shape=apart((rows, 3 * width), bf16),
        compiler_params=params(12),
        cost_estimate=cost(3),
        name="text_qkv",
    )(far(text), far(w_qkv), qv_bias)


def forward(
    scalars, text, text_low, arrived, source, out_grad, w_qkv, qv_bias, w_out, out_bias,
    attn_gain, attn_shift, w_up, up_bias, w_down, down_bias, ffn_gain, ffn_shift, dims,
):
    captions, images = dims
    width = text.shape[1]
    text_len = text.shape[0] // captions
    slots = arrived.shape[0]
    regions = slots // images
    seq = text_len + regions
    rows = captions * seq
    ff = w_up.shape[1]
    half = width // 2
    parts = 4
    part = ff // parts
    grid = captions + parts

    def kernel(
        sc_ref, t_ref, tq_ref, a_ref, src_ref, og_ref, wq_far, qvb_ref, wo_far, ob_ref, ag_ref, as_ref,
        wu_far, ub_ref, wd_far, db_ref, fg_ref, fs_ref,
        out_ref, x_ref, qkv_ref, probs_ref, ctx_ref, an_ref, ai_ref, hid_ref, slope_ref, ds_ref, df_ref,
        sums_ref, wu, wd, send_ref, keep_ref,
        regs, rqkv, act_all, wq, wo, sems,
    ):
        step = pl.program_id(0)

        def third(at):
            cols = slice(at * width, (at + 1) * width)
            return pltpu.make_async_copy(wq_far.at[:, cols], wq.at[:, cols], sems.at[at])

        def load(at):
            source, target = ((wo_far, wo), (wu_far, wu), (wd_far, wd))[at]
            return pltpu.make_async_copy(source, target, sems.at[3 + at])

        @pl.when(step == 0)
        def _():
            for at in range(3):
                third(at).start()
            load(0).start()
            sums_ref[...] = jnp.zeros_like(sums_ref)
            local = mm(one_hot(src_ref[...], slots), a_ref[...], TN).astype(bf16)
            regs[...] = local
            for part_id in range(3):
                at = slice(part_id * width, (part_id + 1) * width)
                third(part_id).wait()
                if part_id == 2:
                    load(1).start()
                    load(2).start()
                got = mm(local, wq[:, at])
                if part_id == 0:
                    got = got + qvb_ref[:, :width]
                if part_id == 2:
                    got = got + qvb_ref[:, width:]
                rqkv[:, at] = got.astype(bf16)

        @pl.when(step < captions)
        def _():
            image = sc_ref[8 + step]
            length = sc_ref[8 + captions + step]
            count = sc_ref[8 + 2 * captions + image]
            at = pl.ds(pl.multiple_of(image * regions, regions), regions)
            here = pl.ds(pl.multiple_of(step * seq, seq), seq)
            x_ref[:text_len, :] = t_ref[...]
            x_ref[text_len:, :] = regs[at, :]
            qkv_ref[:text_len, :] = tq_ref[...]
            qkv_ref[text_len:, :] = rqkv[at, :]
            place = lax.broadcasted_iota(jnp.int32, (seq, 1), 0)
            row_end = jnp.where(place < text_len, length, text_len + count)
            row_mask = jnp.where(place < row_end, 1.0, 0.0)
            key_bias = jnp.where(place < row_end, 0.0, -1e30)
            first = lax.broadcasted_iota(jnp.int32, (1, 2 * HEAD), 1) < HEAD
            scale = [
                jnp.where(first, 0.125, 0.0).astype(bf16),
                jnp.where(first, 0.0, 0.125).astype(bf16),
            ]
            def pair_forward(pair, carry):
                def cols(base):
                    return pl.ds(pl.multiple_of(base + pair * 2 * HEAD, 2 * HEAD), 2 * HEAD)

                q = qkv_ref[:, cols(0)]
                k = qkv_ref[:, cols(width)]
                v = qkv_ref[:, cols(2 * width)]
                scores = mm(k, jnp.concatenate([q * scale[0], q * scale[1]], 0), NT) + key_bias
                raised = jnp.exp(scores - jnp.max(scores, 0, keepdims=True))
                low = (raised * (1.0 / jnp.sum(raised, 0, keepdims=True))).astype(bf16)
                probs_ref[pair] = low
                outs = mm(low, v, TN)
                ctx_ref[:, cols(0)] = jnp.where(first, outs[:seq], outs[seq:]).astype(bf16)
                return carry

            lax.fori_loop(0, HEADS // 2, pair_forward, 0, unroll=3)

            @pl.when(step == 0)
            def _():
                load(0).wait()

            x_wide = x_ref[...].astype(f32)
            attn_out = mm(ctx_ref[...], wo[...]) + ob_ref[...]
            normed, inv = norm_parts(x_wide + attn_out)
            an_ref[here, :] = normed
            ai_ref[here, :] = jnp.broadcast_to(inv, (seq, 128))
            hidden = normed * ag_ref[...] + as_ref[...]
            hidden_low = hidden.astype(bf16)
            hid_ref[here, :] = hidden_low

            @pl.when(step == 0)
            def _():
                load(1).wait()

            for piece in range(parts):
                at = slice(piece * part, (piece + 1) * part)
                upper = mm(hidden_low, wu[:, at]) + ub_ref[:, at]
                phi = 0.5 * (1.0 + lax.erf(upper * inv_sqrt_two))
                act_all[here, at] = (upper * phi).astype(bf16)
                slope = phi + upper * jnp.exp(-0.5 * upper * upper) * inv_sqrt_tau
                slope_ref[here, at] = slope.astype(bf16)

            @pl.when(step == 0)
            def _():
                load(2).wait()

            ffn_out = mm(act_all[here, :], wd[...]) + db_ref[...]
            ffn_normed, ffn_inv = norm_parts(hidden + ffn_out)
            out_ref[...] = ((ffn_normed * fg_ref[...] + fs_ref[...]) * row_mask).astype(bf16)
            cot = og_ref[...].astype(f32) * row_mask
            second = norm_back(cot, ffn_normed, ffn_inv, fg_ref[...])
            ds_ref[here, :] = second
            low = second.astype(bf16)
            df_ref[here, :] = low
            for at, value in enumerate(
                (
                    cot * ffn_normed,
                    cot,
                    low.astype(f32),
                    row_mask * x_wide * x_wide,
                    row_mask * attn_out * attn_out,
                    row_mask * ffn_out * ffn_out,
                    jnp.broadcast_to(row_mask, (seq, width)),
                )
            ):
                sums_ref[at : at + 1, :] += row_sum(value)

        @pl.when(step >= captions)
        def _():
            acts = pl.ds(pl.multiple_of((step - captions) * part, part), part)
            got = mm(act_all[:, acts], df_ref[...], TN)
            mine = sc_ref[0] == 0
            send_ref[...] = jnp.where(mine, got[:, half:], got[:, :half]).astype(bf16)
            keep_ref[...] = jnp.where(mine, got[:, :half], got[:, half:]).astype(bf16)

    def rowwise(size, cols):
        return pl.BlockSpec((size, cols), lambda i, s: (jnp.minimum(i, captions - 1), 0))

    anywhere = pl.BlockSpec(memory_space=pl.ANY)
    return pl.pallas_call(
        kernel,
        grid_spec=pltpu.PrefetchScalarGridSpec(
            num_scalar_prefetch=1,
            grid=(grid,),
            in_specs=[
                rowwise(text_len, width),
                rowwise(text_len, 3 * width),
                whole((slots, width)),
                whole((1, slots)),
                rowwise(seq, width),
                anywhere,
                whole((1, 2 * width)),
                anywhere,
                vec(width),
                vec(width),
                vec(width),
                anywhere,
                whole((1, ff)),
                anywhere,
                vec(width),
                vec(width),
                vec(width),
            ],
            out_specs=[rowwise(seq, width), rowwise(seq, width), rowwise(seq, 3 * width)]
            + [pl.BlockSpec((HEADS // 2, seq, 2 * seq), lambda i, s: (jnp.minimum(i, captions - 1), 0, 0))]
            + [rowwise(seq, width)]
            + [VMEM] * 9
            + [pl.BlockSpec((part, half), lambda i, s: (jnp.maximum(i - captions, 0), 0))] * 2,
            scratch_shapes=[
                pltpu.VMEM((slots, width), bf16),
                pltpu.VMEM((slots, 3 * width), bf16),
                pltpu.VMEM((rows, ff), bf16),
                pltpu.VMEM(w_qkv.shape, bf16),
                pltpu.VMEM(w_out.shape, bf16),
                pltpu.SemaphoreType.DMA((6,)),
            ],
        ),
        out_shape=[
            apart((rows, width), bf16),
            apart((rows, width), bf16),
            apart((rows, 3 * width), bf16),
            apart((captions * HEADS // 2, seq, 2 * seq), bf16),
            apart((rows, width), bf16),
            near((rows, width)),
            near((rows, 128)),
            near((rows, width), bf16),
            near((rows, ff), bf16),
            near((rows, width)),
            near((rows, width), bf16),
            near((8, width)),
            near(w_up.shape, bf16),
            near(w_down.shape, bf16),
            apart((ff, half), bf16),
            apart((ff, half), bf16),
        ],
        compiler_params=params(33),
        cost_estimate=cost(30),
        name="forward",
    )(
        scalars,
        *(
            far(v)
            for v in (
                text, text_low, arrived, source, out_grad, w_qkv, qv_bias, w_out, out_bias,
                attn_gain, attn_shift, w_up, up_bias, w_down, down_bias, ffn_gain, ffn_shift,
            )
        ),
    )


def ffn_backward(core, d_ffn, d_second, slope, attn_normed, attn_inv, w_down, w_up, attn_gain, seq, hold, first, size, begun):
    rows, width = d_ffn.shape
    ff = w_up.shape[1]
    parts = 4
    part = ff // parts

    def kernel(c_ref, df_ref, ds_ref, sl_ref, an_ref, ai_ref, wd, wu, ag_ref, *rest):
        dup_ref, dr_ref, da_ref, sums_ref, up_ref = rest[len(begun) + len(hold) :]
        step = pl.program_id(0)

        @pl.when(step == 0)
        def _():
            if begun:
                sums_ref[...] = rest[3][...]
                up_ref[...] = rest[4][...]
            else:
                sums_ref[...] = jnp.zeros_like(sums_ref)
                up_ref[...] = jnp.zeros_like(up_ref)

        here = pl.ds(pl.multiple_of((first + step) * seq, seq), seq)
        d_low = df_ref[here, :]
        for piece in range(parts):
            at = slice(piece * part, (piece + 1) * part)
            d_act = mm(d_low, wd[at, :], NT)
            low = (d_act * sl_ref[here, at].astype(f32)).astype(bf16)
            dup_ref[here, at] = low
            up_ref[0:1, at] += row_sum(low.astype(f32))
        d_hidden = ds_ref[here, :] + mm(dup_ref[here, :], wu[...], NT)
        normed = an_ref[here, :]
        resid = norm_back(d_hidden, normed, ai_ref[here, 0:1], ag_ref[...])
        dr_ref[here, :] = resid
        low = resid.astype(bf16)
        da_ref[here, :] = low
        sums_ref[0:1, :] += row_sum(d_hidden * normed)
        sums_ref[1:2, :] += row_sum(d_hidden)
        sums_ref[2:3, :] += row_sum(low.astype(f32))

    return pl.pallas_call(
        kernel,
        grid_spec=pltpu.PrefetchScalarGridSpec(
            num_scalar_prefetch=1,
            grid=(size,),
            in_specs=[VMEM] * 7
            + [vec(width)]
            + [VMEM] * len(begun)
            + [VMEM] * len(hold),
            out_specs=[VMEM] * 5,
        ),
        out_shape=[
            near((rows, ff), bf16),
            near((rows, width)),
            near((rows, width), bf16),
            near((8, width)),
            near((8, ff)),
        ],
        input_output_aliases={9: 0, 10: 1, 11: 2} if begun else {},
        compiler_params=params(6),
        cost_estimate=cost(4 * size),
        name="ffn_backward",
    )(core, d_ffn, d_second, slope, attn_normed, attn_inv, w_down, w_up, attn_gain, *begun, *hold)


def up_gradient(core, hidden_low, d_upper):
    rows, width = hidden_low.shape

    def kernel(c_ref, h_ref, d_ref, send_ref, keep_ref):
        step = pl.program_id(0)
        here = pl.ds(pl.multiple_of(step * width, width), width)
        for to_ref, side in ((send_ref, 1 - c_ref[0]), (keep_ref, c_ref[0])):
            cols = pl.ds(pl.multiple_of((2 * side + step) * width, width), width)
            to_ref[:, here] = mm(h_ref[...], d_ref[:, cols], TN).astype(bf16)

    return pl.pallas_call(
        kernel,
        grid_spec=pltpu.PrefetchScalarGridSpec(
            num_scalar_prefetch=1, grid=(2,), in_specs=[VMEM, VMEM], out_specs=[VMEM, VMEM]
        ),
        out_shape=[near((width, 2 * width), bf16)] * 2,
        compiler_params=params(6),
        cost_estimate=cost(0.1),
        name="up_gradient",
    )(core, hidden_low, d_upper)


def attention_backward(scalars, d_attn, d_resid, probs, qkv, source, w_out, w_qkv, dims, first_caption, size, begun):
    captions, images = dims
    rows, width = d_attn.shape
    seq = rows // captions
    slots = source.shape[1]
    regions = slots // images
    text_len = seq - regions
    last = first_caption + size == captions

    def kernel(
        sc_ref, da_ref, dr_ref, p_ref, qkv_ref, src_ref, wo_ref, wq, *rest,
    ):
        begun_refs = rest[: len(begun)]
        dqkv_ref, text_ref, back_ref, sums_ref, d_img, d_ctx_ref = rest[len(begun) :]
        step = pl.program_id(0)
        here = pl.ds(pl.multiple_of((first_caption + step) * seq, seq), seq)

        @pl.when(step == 0)
        def _():
            if begun:
                sums_ref[...] = begun_refs[3][...]
                d_img[...] = begun_refs[2][...]
            else:
                sums_ref[...] = jnp.zeros_like(sums_ref)
                d_img[...] = jnp.zeros_like(d_img)

        d_ctx_ref[...] = mm(da_ref[here, :], wo_ref[...], NT).astype(bf16)
        first = lax.broadcasted_iota(jnp.int32, (1, 2 * HEAD), 1) < HEAD
        masks = [jnp.where(first, 1.0, 0.0).astype(bf16), jnp.where(first, 0.0, 1.0).astype(bf16)]
        def pair_backward(pair, carry):
            def cols(base):
                return pl.ds(pl.multiple_of(base + pair * 2 * HEAD, 2 * HEAD), 2 * HEAD)

            q = qkv_ref[here, cols(0)]
            k = qkv_ref[here, cols(width)]
            v = qkv_ref[here, cols(2 * width)]
            d_c = d_ctx_ref[:, cols(0)]
            both_c = jnp.concatenate([d_c * masks[0], d_c * masks[1]], 0)
            both_q = jnp.concatenate([q * masks[0], q * masks[1]], 0)
            low = p_ref[(first_caption + step) * (HEADS // 2) + pair]
            d_probs = mm(v, both_c, NT)
            wide = low.astype(f32)
            both = wide * d_probs
            inner = jnp.sum(both, 0, keepdims=True)
            d_scores = (both - wide * inner).astype(bf16)
            d_q = mm(d_scores, k, TN) * 0.125
            dqkv_ref[here, cols(0)] = jnp.where(first, d_q[:seq], d_q[seq:]).astype(bf16)
            dqkv_ref[here, cols(width)] = (mm(d_scores, both_q) * 0.125).astype(bf16)
            dqkv_ref[here, cols(2 * width)] = mm(low, both_c).astype(bf16)
            return carry

        lax.fori_loop(0, HEADS // 2, pair_backward, 0, unroll=UNROLL)

        sums_ref[0:1, :] += row_sum(dqkv_ref[here, :width].astype(f32))
        sums_ref[1:2, :] += row_sum(dqkv_ref[here, 2 * width :].astype(f32))
        d_x = mm(dqkv_ref[here, :], wq[...], NT) + dr_ref[here, :]
        text_ref[...] = d_x[:text_len]
        at = pl.ds(pl.multiple_of(sc_ref[8 + first_caption + step] * regions, regions), regions)
        d_img[at, :] += d_x[text_len:]

        @pl.when(step == size - 1)
        def _():
            if last:
                back_ref[...] = mm(one_hot(src_ref[...], slots), d_img[...].astype(bf16)).astype(bf16)
            else:
                back_ref[...] = d_img[...]

    return pl.pallas_call(
        kernel,
        grid_spec=pltpu.PrefetchScalarGridSpec(
            num_scalar_prefetch=1,
            grid=(size,),
            in_specs=[VMEM] * 4
            + [whole((1, slots)), VMEM, VMEM]
            + ([VMEM, pl.BlockSpec(memory_space=pl.ANY)] + [VMEM, VMEM] if begun else []),
            out_specs=[
                VMEM,
                pl.BlockSpec((text_len, width), lambda i, s: (i + first_caption, 0)),
                VMEM,
                VMEM,
            ],
            scratch_shapes=[
                pltpu.VMEM((slots, width), f32),
                pltpu.VMEM((seq, width), bf16),
            ],
        ),
        out_shape=[
            near((rows, 3 * width), bf16),
            pltpu.HBM((captions * text_len, width), f32),
            near((slots, width), bf16 if last else f32),
            near((8, width)),
        ],
        input_output_aliases={8: 0, 9: 1} if begun else {},
        compiler_params=params(11),
        cost_estimate=cost(5 * size),
        name="attention_backward",
    )(scalars, d_attn, d_resid, probs, qkv, source, w_out, w_qkv, *begun)


def qkvo_gradient(core, x, d_qkv, context, d_attn):
    rows, width = x.shape

    def kernel(c_ref, x_ref, dq_ref, ctx_ref, da_ref, send_ref, keep_ref):
        step = pl.program_id(0)
        block = lax.rem(step + 2 * (1 - c_ref[0]), 4)
        cols = pl.ds(pl.multiple_of(jnp.minimum(block, 2) * width, width), width)

        def gradient(to_ref):
            @pl.when(block < 3)
            def _():
                to_ref[...] = mm(x_ref[...], dq_ref[:, cols], TN).astype(bf16)

            @pl.when(block == 3)
            def _():
                to_ref[...] = mm(ctx_ref[...], da_ref[...], TN).astype(bf16)

        @pl.when(step < 2)
        def _():
            gradient(send_ref)

        @pl.when(step >= 2)
        def _():
            gradient(keep_ref)

    return pl.pallas_call(
        kernel,
        grid_spec=pltpu.PrefetchScalarGridSpec(
            num_scalar_prefetch=1,
            grid=(4,),
            in_specs=[VMEM] * 4,
            out_specs=[
                pl.BlockSpec((width, width), lambda i, s: (0, jnp.minimum(i, 1))),
                pl.BlockSpec((width, width), lambda i, s: (0, jnp.maximum(i - 2, 0))),
            ],
        ),
        out_shape=[apart((width, 2 * width), bf16)] * 2,
        compiler_params=params(11),
        cost_estimate=cost(5),
        name="qkvo_gradient",
    )(core, x, d_qkv, context, d_attn)


def region_norm_backward(
    core, returned, target, normed, inv, gain, boxes, w_box_t, sums_forward, sums_ffn, sums_up, sums_attn, groups
):
    rows, width = returned.shape
    half = width // 2
    box = boxes.shape[0]
    share = width // groups
    ff_share = sums_up.shape[1] // groups

    def kernel(
        c_ref, r_ref, t_ref, n_ref, i_ref, g_ref, box_ref, wb_ref, sf_ref, sn_ref, su_ref, sa_ref,
        all_ref, send_ref, keep_ref, small_ref, bg_ref, small,
    ):
        d_region = mm(one_hot(t_ref[...], rows), r_ref[...], TN)
        normed = n_ref[...]
        low = norm_back(d_region, normed, i_ref[:, 0:1], g_ref[...]).astype(bf16)
        all_ref[...] = low
        mine = c_ref[0] == 0
        send_ref[:rows, :] = jnp.where(mine, low[:, half:], low[:, :half])
        keep_ref[...] = jnp.where(mine, low[:, :half], low[:, half:])
        bg_ref[...] = mm(wb_ref[...], low, NT)
        boxes_grad = mm(box_ref[...], low)
        vectors = [
            row_sum(low.astype(f32)),
            row_sum(d_region * normed),
            row_sum(d_region),
            sf_ref[0:1, :],
            sf_ref[1:2, :],
            sf_ref[2:3, :],
            sn_ref[0:1, :],
            sn_ref[1:2, :],
            sn_ref[2:3, :],
        ] + [boxes_grad[at : at + 1] for at in range(box)]
        small[...] = jnp.zeros_like(small)
        lane = lax.broadcasted_iota(jnp.int32, (1, half), 1)
        stats = jnp.zeros((1, half), f32)
        for at in range(4):
            total = jnp.sum(sf_ref[3 + at : 4 + at, :], 1, keepdims=True)
            stats = jnp.where(lane == at, total, stats)
        flat = jnp.concatenate([sa_ref[0:1, :], sa_ref[1:2, :]], 1)
        for group in range(groups):
            small[group, 0:1, 0:ff_share] = su_ref[0:1, group * ff_share : (group + 1) * ff_share]
            small[group, 1:2, 0 : 2 * share] = flat[:, group * 2 * share : (group + 1) * 2 * share]
            for at, value in enumerate(vectors):
                row, col = (1, 2) if at == 0 else (2 + (at - 1) // 3, (at - 1) % 3)
                small[group, row : row + 1, 128 * col : 128 * col + share] = value[
                    :, group * share : (group + 1) * share
                ]
            small[group, 6:7, :] = stats
        small_ref[...] = small[...].astype(bf16)
        for group in range(groups):
            send_ref[rows + 8 * group : rows + 8 * (group + 1), :] = small_ref[group]

    sizes = (sums_forward, sums_ffn, sums_up, sums_attn)
    return pl.pallas_call(
        kernel,
        grid_spec=pltpu.PrefetchScalarGridSpec(
            num_scalar_prefetch=1,
            grid=(1,),
            in_specs=[
                whole((rows, width)),
                whole((1, rows)),
                whole((rows, width)),
                whole((rows, 128)),
                vec(width),
                whole(boxes.shape),
                whole(w_box_t.shape),
            ]
            + [whole(v.shape) for v in sizes],
            out_specs=[VMEM] * 4 + [whole((box, rows))],
            scratch_shapes=[pltpu.VMEM((groups, 8, half), f32)],
        ),
        out_shape=[
            near((rows, width), bf16),
            near((rows + 8 * groups, half), bf16),
            near((rows, half), bf16),
            near((groups, 8, half), bf16),
            shape((box, rows)),
        ],
        compiler_params=params(14),
        cost_estimate=cost(0.1),
        name="region_norm_backward",
    )(core, returned, far(target), far(normed), far(inv), far(gain), far(boxes), w_box_t, *sizes)


def visual_gradient(bits, features, other_features, d_pre, other_d_pre, small, groups):
    rows, feat = features.shape
    half = d_pre.shape[1]
    steps = 4
    part = feat // steps
    quarter = feat // groups // 4
    tall = quarter + 8
    per_step = groups // steps
    high = groups // 2

    def kernel(b_ref, f_ref, o_ref, d_ref, p_ref, s_ref, a_send, a_keep, b_send, b_keep, got):
        step = pl.program_id(0)
        bit2, bit4 = b_ref[1], b_ref[2]
        got[...] = mm(f_ref[...], d_ref[...], TN) + mm(o_ref[...], p_ref[:rows, :], TN)

        def fill(to_ref, at, which, group, x, piece):
            here = pl.ds(pl.multiple_of(((group * 2 + x) * 2 + piece) * quarter, 8), quarter)
            to_ref[at, which, :quarter, :] = got[here, :].astype(bf16)
            number = step * per_step + group
            other = p_ref[pl.ds(pl.multiple_of(rows + 8 * number, 8), 8), :]
            to_ref[at, which, quarter:, :] = add(s_ref[number], other)

        for group in range(per_step):
            y = group % 2
            at = step * (per_step // 2) + group // 2
            fill(a_send, at, y, group, 1 - bit2, 0)
            fill(a_keep, at, y, group, bit2, 0)

            @pl.when(bit4 == y)
            def _():
                for x in range(2):
                    fill(b_keep, at, x, group, x, 1)

            @pl.when(bit4 != y)
            def _():
                for x in range(2):
                    fill(b_send, at, x, group, x, 1)

    return pl.pallas_call(
        kernel,
        grid_spec=pltpu.PrefetchScalarGridSpec(
            num_scalar_prefetch=1,
            grid=(steps,),
            in_specs=[
                pl.BlockSpec((rows, part), lambda i, s: (0, i)),
                pl.BlockSpec((rows, part), lambda i, s: (0, i)),
                VMEM,
                VMEM,
                VMEM,
            ],
            out_specs=[VMEM] * 4,
            scratch_shapes=[pltpu.VMEM((part, half), f32)],
        ),
        out_shape=[near((high, 2, tall, half), bf16)] * 4,
        compiler_params=params(10),
        cost_estimate=cost(0.1),
        name="visual_gradient",
    )(bits, far(features), far(other_features), d_pre, other_d_pre, small)


def feature_gradient(bits, d_pre, w_visual):
    rows, width = d_pre.shape
    feat = w_visual.shape[0]
    steps = 4
    part = feat // steps

    def kernel(b_ref, d_ref, w_ref, o_ref):
        o_ref[...] = mm(d_ref[...], w_ref[...], NT)

    return pl.pallas_call(
        kernel,
        grid_spec=pltpu.PrefetchScalarGridSpec(
            num_scalar_prefetch=1,
            grid=(steps,),
            in_specs=[VMEM, pl.BlockSpec((part, width), lambda i, s: (i, 0))],
            out_specs=pl.BlockSpec((rows, part), lambda i, s: (0, i)),
        ),
        out_shape=shape((rows, feat)),
        compiler_params=params(8),
        cost_estimate=cost(10),
        name="feature_gradient",
    )(bits, d_pre, far(w_visual))


def device_number():
    return lax.axis_index("dp") * lax.axis_size("enc") + lax.axis_index("enc")


def swap(values, bit):
    count = lax.axis_size("dp") * lax.axis_size("enc")
    return lax.ppermute(values, ("dp", "enc"), [(i, i ^ bit) for i in range(count)])


def add(a, b):
    return (a.astype(f32) + b.astype(f32)).astype(bf16)


def scalar_call(kernel, bits, ins, in_specs, outs, out_specs, grid, limit, name, last=False, place=near):
    outs = outs if last else [place(o.shape, o.dtype) for o in outs]
    return pl.pallas_call(
        kernel,
        grid_spec=pltpu.PrefetchScalarGridSpec(
            num_scalar_prefetch=1, grid=(grid,), in_specs=in_specs, out_specs=out_specs
        ),
        out_shape=outs,
        compiler_params=params(limit),
        cost_estimate=cost(1),
        name=name,
    )(bits, *ins)


def first_split(bits, kept, got, groups, place=near):
    tall = kept.ndim == 5
    high = groups // 2
    if tall:
        rows, cols = kept.shape[3:]
        view = (high, 2, 2, 2, rows, cols)
        block = (1, 2, 2, 2, rows, cols)
    else:
        rows, cols = kept.shape[0] // groups, kept.shape[1] // 4
        view = (high, 2, rows, 4 * cols)
        block = (1, 2, rows, 4 * cols)

    def kernel(b_ref, k_ref, r_ref, a_send, a_keep, b_send, b_keep):
        bit2, bit4 = b_ref[1], b_ref[2]

        def total(y, x, piece):
            if tall:
                return add(k_ref[0, y, x, piece], r_ref[0, y, x, piece])
            at = pl.ds(pl.multiple_of((2 * x + piece) * cols, 128), cols)
            return add(k_ref[0, y, :, at], r_ref[0, y, :, at])

        for other in range(2):
            a_send[0, other] = total(other, 1 - bit2, 0)
            a_keep[0, other] = total(other, bit2, 0)
            b_send[0, other] = total(1 - bit4, other, 1)
            b_keep[0, other] = total(bit4, other, 1)

    spec = pl.BlockSpec(block, lambda i, s: (i,) + (0,) * (len(block) - 1))
    out = pl.BlockSpec((1, 2, rows, cols), lambda i, s: (i, 0, 0, 0))
    return scalar_call(
        kernel, bits, (kept.reshape(view), got.reshape(view)), [spec, spec],
        [shape((high, 2, rows, cols), bf16)] * 4, [out] * 4, high, 6, "first_split", place=place,
    )


def second_split(bits, a_kept, a_got, b_kept, b_got):
    high, _, rows, cols = a_kept.shape

    def kernel(b_ref, ak, ar, bk, br, a_send, a_keep, b_send, b_keep):
        bit2, bit4 = b_ref[1], b_ref[2]
        a_send[0] = add(ak[0, 1 - bit4], ar[0, 1 - bit4])
        a_keep[0] = add(ak[0, bit4], ar[0, bit4])
        b_send[0] = add(bk[0, 1 - bit2], br[0, 1 - bit2])
        b_keep[0] = add(bk[0, bit2], br[0, bit2])

    spec = pl.BlockSpec((1, 2, rows, cols), lambda i, s: (i, 0, 0, 0))
    out = pl.BlockSpec((1, rows, cols), lambda i, s: (i, 0, 0))
    return scalar_call(
        kernel, bits, (a_kept, a_got, b_kept, b_got), [spec] * 4,
        [shape((high, rows, cols), bf16)] * 4, [out] * 4, high, 6, "second_split",
    )


def join_split(bits, pairs, place=near):
    high, _, cols = pairs[0][0].shape
    sizes = [kept.shape[1] for kept, _ in pairs]

    def kernel(b_ref, *refs):
        bit = b_ref[3]
        send, keep = refs[-2:]
        at = 0
        for n, size in enumerate(sizes):
            kept, got = refs[2 * n : 2 * n + 2]
            send[0, at : at + size] = add(kept[1 - bit], got[1 - bit])
            keep[0, at : at + size] = add(kept[bit], got[bit])
            at += size

    ins = [value for pair in pairs for value in pair]
    specs = [pl.BlockSpec((2, v.shape[1], cols), lambda i, s: (i, 0, 0)) for v in ins]
    out = pl.BlockSpec((1, sum(sizes), cols), lambda i, s: (i, 0, 0))
    return scalar_call(
        kernel, bits, ins, specs, [shape((high // 2, sum(sizes), cols), bf16)] * 2, [out] * 2,
        high // 2, 6, "join_split", place=place,
    )


def late_split(bits, kept, got, which):
    high, rows, cols = kept.shape

    def kernel(b_ref, k_ref, r_ref, send, keep):
        bit = b_ref[which]
        send[0] = add(k_ref[1 - bit], r_ref[1 - bit])
        keep[0] = add(k_ref[bit], r_ref[bit])

    spec = pl.BlockSpec((2, rows, cols), lambda i, s: (i, 0, 0))
    out = pl.BlockSpec((1, rows, cols), lambda i, s: (i, 0, 0))
    return scalar_call(
        kernel, bits, (kept, got), [spec] * 2, [shape((high // 2, rows, cols), bf16)] * 2, [out] * 2,
        high // 2, 6, "late_split",
    )


def over_two(halves):
    return swap(halves[0], 2), halves[1], swap(halves[2], 4), halves[3]


def over_other_two(halves):
    return swap(halves[0], 4), halves[1], swap(halves[2], 2), halves[3]


def second(bits, moved):
    return second_split(bits, moved[1], moved[0], moved[3], moved[2])


def join(bits, *moved, place=near):
    pairs = []
    for one in moved:
        pairs += [(one[1], one[0]), (one[3], one[2])]
    return join_split(bits, pairs, place)


def after_all(*trees):
    leaves, tree = jax.tree.flatten(trees)
    return jax.tree.unflatten(tree, lax.optimization_barrier(leaves))


def late_first(bits, kept, got):
    if kept.shape[0] == 1:
        return (kept + got,)
    return late_split(bits, kept, got, 4)


def late_move(halves):
    return swap(halves[0], 16) if len(halves) > 1 else None


def late_rest(bits, halves, moved):
    bit, which = 16, 5
    while len(halves) > 1:
        if halves[1].shape[0] == 1:
            halves = (halves[1] + moved,)
        else:
            halves = late_split(bits, halves[1], moved, which)
            bit, which = 2 * bit, which + 1
            moved = swap(halves[0], bit)
    return halves[0][0]


def spread(mine, *late):
    over_x = swap(mine, 2)
    over_core = swap(mine, 1)
    return mine, over_x, over_core, swap(gate(over_x, *late), 1)


def pick(b_ref, pieces, core, x):
    mine, over_x, over_core, over_both = pieces
    same_x = b_ref[1] == x
    return jnp.where(
        b_ref[0] == core, jnp.where(same_x, mine, over_x), jnp.where(same_x, over_core, over_both)
    ).astype(f32)


def finish_ffn(bits, pieces):
    rows, cols = pieces[0].shape
    half = rows // 2
    part = rows // 4

    def kernel(b_ref, p0, p1, p2, p3, down_ref, up_ref):
        for core in range(2):
            for x in range(2):
                got = pick(b_ref, (p0[...], p1[...], p2[...], p3[...]), core, x)
                down_ref[x * half : (x + 1) * half, core * cols : (core + 1) * cols] = got[:half]
                for piece in range(2):
                    at = ((core * 2 + x) * 2 + piece) * cols
                    up_ref[:, at : at + cols] = got[half + piece * part : half + (piece + 1) * part]

    outs = [shape((rows, 2 * cols)), shape((part, 8 * cols))]
    return scalar_call(
        kernel, bits, pieces, [whole((rows, cols))] * 4, outs, [whole(o.shape) for o in outs], 1, 12, "finish_ffn", True
    )


def finish_wide(bits, pieces, sizes):
    rows, cols = pieces[0].shape
    part = rows // 2

    def kernel(b_ref, p0, p1, p2, p3, *out_refs):
        for core in range(2):
            for x in range(2):
                got = pick(b_ref, (p0[...], p1[...], p2[...], p3[...]), core, x)
                for piece in range(2):
                    at = ((core * 2 + x) * 2 + piece) * cols
                    for out_ref, size in zip(out_refs, sizes):
                        if 0 <= at < size:
                            out_ref[:, at : at + cols] = got[piece * part : (piece + 1) * part]
                        at -= size

    outs = [shape((part, size)) for size in sizes]
    return scalar_call(
        kernel, bits, pieces, [whole((rows, cols))] * 4, outs, [whole(o.shape) for o in outs], 1, 8, "finish_wide", True
    )


def finish_visual(bits, pieces, ff_share, share, box):
    rows, cols = pieces[0].shape
    tall = rows // 2
    quarter = tall - 8
    sizes = [share] * 9 + [2 * share, ff_share]

    def kernel(b_ref, p0, p1, p2, p3, vis_ref, box_ref, rms_ref, *small_refs):
        for core in range(2):
            for x in range(2):
                got = pick(b_ref, (p0[...], p1[...], p2[...], p3[...]), core, x)
                for piece in range(2):
                    low = piece * tall
                    vis_ref[(2 * x + piece) * quarter : (2 * x + piece + 1) * quarter, core * cols : (core + 1) * cols] = got[
                        low : low + quarter
                    ]
        small = p0[quarter : quarter + 8, :].astype(f32)
        for at in range(9):
            row, col = (1, 2) if at == 0 else (2 + (at - 1) // 3, (at - 1) % 3)
            small_refs[at][...] = small[row, 128 * col : 128 * col + share]
        small_refs[9][...] = small[1, 0 : 2 * share]
        small_refs[10][...] = small[0, 0:ff_share]
        for at in range(9, 9 + box):
            row, col = 2 + (at - 1) // 3, (at - 1) % 3
            box_ref[at - 9 : at - 8, :] = small[row : row + 1, 128 * col : 128 * col + share]
        stats = small[6, 0:128]
        total = jnp.sum(small[6:7, 3:4])
        rms_ref[...] = jnp.sqrt(stats / total)[:3]

    outs = [shape((4 * quarter, 2 * cols)), shape((box, share)), shape((3,))] + [shape((size,)) for size in sizes]
    specs = [whole(o.shape) for o in outs[:2]] + [vec(3)] + [vec(size) for size in sizes]
    return scalar_call(
        kernel, bits, pieces, [whole((rows, cols))] * 4, outs, specs, 1, 8, "finish_visual", True
    )


def gate(value, *others):
    return lax.optimization_barrier((value, *others))[0]


def on_device(
    text_embed,
    region_features,
    boxes,
    caption_image,
    caption_lengths,
    region_counts,
    region_target,
    region_source,
    w_visual,
    w_box,
    visual_bias,
    visual_gain,
    visual_shift,
    w_qkv,
    qv_bias,
    w_out,
    out_bias,
    attn_gain,
    attn_shift,
    w_up,
    up_bias,
    w_down,
    down_bias,
    ffn_gain,
    ffn_shift,
    out_grad,
):
    width = text_embed.shape[1]
    captions = caption_image.shape[0]
    images = region_counts.shape[0]
    dims = (captions, images)
    axes = ("dp", "enc")
    groups = lax.axis_size("dp")
    count = groups * lax.axis_size("enc")
    me = device_number().astype(jnp.int32)
    places = lax.iota(jnp.int32, 8)
    scalars = jnp.concatenate([(me >> places) & 1, caption_image, caption_lengths, region_counts])
    w_box_t = w_box.T
    row = lambda v: v.reshape(1, -1)
    qv_row = row(qv_bias)

    message, vis_normed, vis_inv = region_forward(
        region_features, boxes, region_target, w_visual, w_box_t, visual_bias, visual_gain, visual_shift
    )
    arrived = lax.all_to_all(message, axes, split_axis=0, concat_axis=0, tiled=True)
    text_low = text_qkv(text_embed, w_qkv, qv_row)
    (
        out_rows, x, qkv, probs, context, attn_normed, attn_inv, hidden_low, slope, d_second, d_ffn,
        sums_forward, w_up_near, w_down_near, down_sent, down_kept,
    ) = forward(
        scalars, text_embed, text_low, arrived, region_source, out_grad, w_qkv, qv_row, w_out,
        out_bias, attn_gain, attn_shift, w_up, row(up_bias), w_down, down_bias, ffn_gain, ffn_shift, dims,
    )
    seq = x.shape[0] // captions
    rest = captions - 1
    bits = core = scalars
    hold = ()
    ffn_ins = (d_ffn, d_second, slope, attn_normed, attn_inv, w_down_near, w_up_near, attn_gain, seq, hold)
    down_view = (groups, 2, 2, w_down.shape[0] // groups // 4, width // 2)
    down_sent, down_kept = down_sent.reshape(down_view), down_kept.reshape(down_view)

    moved = swap(down_sent, 1)
    begun = ffn_backward(core, *ffn_ins, 0, 1, ())

    moved, begun, sc = after_all(moved, begun, scalars)
    down = first_split(sc, down_kept, moved, groups)
    down, begun, sc = after_all(down, begun, sc)
    moved = over_two(down)
    d_upper, d_resid, d_attn, sums_ffn, sums_up = ffn_backward(sc, *ffn_ins, 1, rest, tuple(begun))
    up_sent, up_kept = up_gradient(sc, hidden_low, gate(d_upper, d_attn))

    moved, up_sent, up_kept, d_attn, sc = after_all(moved, up_sent, up_kept, d_attn, sc)
    down = second(sc, moved)
    down, up_sent, up_kept, sc = after_all(down, up_sent, up_kept, sc)
    moved = over_other_two(down), swap(up_sent, 1)
    att_ins = (d_attn, d_resid, probs, qkv, region_source, w_out, w_qkv, dims)
    begun = attention_backward(sc, *att_ins, 0, 1, ())

    moved, up_kept, begun, sc = after_all(moved, up_kept, begun, sc)
    down = moved[0]
    up = first_split(sc, up_kept, moved[1], groups)
    down, up, begun, sc = after_all(down, up, begun, sc)
    moved = over_two(up)
    d_qkv, text_grad, back_message, sums_attn = attention_backward(sc, *att_ins, 1, rest, tuple(begun))

    moved, down, d_qkv, back_message, sc = after_all(moved, down, d_qkv, back_message, sc)
    up = second(sc, moved)
    up, down, sc = after_all(up, down, sc)
    moved = over_other_two(up)
    qkvo_sent, qkvo_kept = qkvo_gradient(sc, x, d_qkv, context, d_attn)

    moved, down, qkvo_sent, qkvo_kept, back_message, sc = after_all(
        moved, down, qkvo_sent, qkvo_kept, back_message, sc
    )
    ffn = join(sc, down, moved, place=apart)
    ffn, qkvo_sent, qkvo_kept, back_message, sc = after_all(ffn, qkvo_sent, qkvo_kept, back_message, sc)
    returned = lax.all_to_all(back_message, axes, split_axis=0, concat_axis=0, tiled=True)
    other_features = swap(gate(region_features, qkvo_kept), 1)
    qkvo = first_split(sc, qkvo_kept, swap(qkvo_sent, 1), groups, apart)
    qkvo_moved = over_two(qkvo)
    ffn_moved = swap(gate(ffn[0], *qkvo), 8)
    returned, sc = after_all(returned, gate(sc, *qkvo))
    d_pre, d_pre_sent, d_pre_kept, small, box_grad = region_norm_backward(
        sc, returned, region_target, vis_normed, vis_inv, visual_gain, boxes, w_box_t,
        sums_forward, sums_ffn, sums_up, sums_attn, groups,
    )
    vis = visual_gradient(
        sc, region_features, other_features, d_pre_kept, swap(d_pre_sent, 1), small, groups
    )
    vis_moved = over_two(vis)
    sc = gate(sc, *vis)
    qkvo = second(sc, qkvo_moved)
    qkvo_moved = over_other_two(qkvo)
    ffn = late_first(gate(sc, *qkvo), ffn[1], ffn_moved)
    ffn_moved = late_move(ffn)
    feature_grad = feature_gradient(gate(sc, *ffn), d_pre, w_visual)

    sc = gate(sc, feature_grad)
    vis = second(sc, vis_moved)
    vis_moved = over_other_two(vis)
    sc = gate(sc, *vis)
    qkvo = join(sc, qkvo_moved)
    qkvo_moved = swap(qkvo[0], 8)
    ffn = late_rest(sc, ffn, gate(ffn_moved, *qkvo))

    vis = join(gate(sc, *qkvo, ffn), vis_moved)
    vis_moved = swap(vis[0], 8)
    sc = gate(sc, *vis)
    qkvo = late_first(sc, qkvo[1], qkvo_moved)
    qkvo_moved = late_move(qkvo)

    vis = late_first(gate(sc, *qkvo), vis[1], vis_moved)
    vis_moved = late_move(vis)
    ffn = spread(ffn, *vis)
    sc = gate(sc, *vis)
    g_down, g_up = finish_ffn(sc, ffn)
    qkvo = late_rest(sc, qkvo, gate(qkvo_moved, *vis))

    vis = late_rest(sc, vis, gate(vis_moved, g_up, qkvo))
    qkvo = spread(qkvo, vis)
    g_qkv, g_out = finish_wide(gate(sc, vis), qkvo, (3 * width, width))
    vis = spread(vis, g_qkv)
    g_visual, g_box_t, rms_values, *small = finish_visual(
        sc, vis, w_up.shape[1] // groups, width // groups, boxes.shape[0]
    )
    return (
        out_rows,
        text_grad,
        feature_grad,
        box_grad,
        rms_values,
        g_visual,
        g_box_t.T,
        small[0],
        small[1],
        small[2],
        g_qkv,
        small[9],
        g_out,
        small[8],
        small[6],
        small[7],
        g_up,
        small[10],
        g_down,
        small[5],
        small[3],
        small[4],
    )


def solution(mesh):
    return jax.shard_map(
        on_device,
        mesh=mesh,
        in_specs=(
            P(("dp", "enc"), None),
            P(("dp", "enc"), None),
            P(None, ("dp", "enc")),
            P(("dp", "enc")),
            P(("dp", "enc")),
            P(("dp", "enc")),
            P(("dp", "enc"), None),
            P(("dp", "enc"), None),
            P(),
            P(),
            P(),
            P(),
            P(),
            P(),
            P(),
            P(),
            P(),
            P(),
            P(),
            P(),
            P(),
            P(),
            P(),
            P(),
            P(),
            P(("dp", "enc"), None),
        ),
        out_specs=(
            P(("dp", "enc"), None),
            P(("dp", "enc"), None),
            P(("dp", "enc"), None),
            P(None, ("dp", "enc")),
            P(),
            P("dp", None),
            P("dp", None),
            P("dp"),
            P("dp"),
            P("dp"),
            P("dp", None),
            P("dp"),
            P("dp", None),
            P("dp"),
            P("dp"),
            P("dp"),
            P("dp", None),
            P("dp"),
            P("dp", None),
            P("dp"),
            P("dp"),
            P("dp"),
        ),
        check_vma=False,
    )
```

```python
import jax
import jax.numpy as jnp
from jax import lax
from jax.experimental import pallas as pl
from jax.experimental.pallas import tpu as pltpu
from jax.sharding import PartitionSpec as P

HEADS = 12
UNROLL = 2
HEAD = 64
epsilon = 1e-12
inv_sqrt_two = 0.7071067811865476
inv_sqrt_tau = 0.3989422804014327
f32 = jnp.float32
bf16 = jnp.bfloat16
NN = (((1,), (0,)), ((), ()))
NT = (((1,), (1,)), ((), ()))
TN = (((0,), (0,)), ((), ()))


def mm(a, b, dims=NN):
    return lax.dot_general(a, b, dims, preferred_element_type=f32)


def cost(us):
    return pl.CostEstimate(flops=int(us * 1e9), bytes_accessed=1 << 20, transcendentals=0)


def params(limit=56):
    return pltpu.CompilerParams(
        dimension_semantics=("arbitrary",), vmem_limit_bytes=limit << 20
    )


def whole(shape):
    return pl.BlockSpec(shape, lambda i, *s: (0,) * len(shape), pipeline_mode=pl.Buffered(1))


def vec(size):
    return pl.BlockSpec((size,), lambda i, *s: (0,))


VMEM = pl.BlockSpec(memory_space=pltpu.VMEM)


def far(value):
    return pltpu.with_memory_space_constraint(value, pltpu.HBM)


def apart(dims, kind=f32):
    return pltpu.HBM(dims, kind)


def near(dims, kind=f32):
    return pltpu.VMEM(dims, kind)


def shape(dims, kind=f32):
    return jax.ShapeDtypeStruct(dims, kind)


def norm_parts(values):
    centre = values - jnp.mean(values, -1, keepdims=True)
    inv_std = lax.rsqrt(jnp.mean(centre * centre, -1, keepdims=True) + epsilon)
    return centre * inv_std, inv_std


def norm_back(grad, normed, inv_std, gain):
    scaled = grad * gain
    return inv_std * (
        scaled
        - jnp.mean(scaled, -1, keepdims=True)
        - normed * jnp.mean(scaled * normed, -1, keepdims=True)
    )


def row_sum(values):
    return jnp.sum(values, 0, keepdims=True)


def one_hot(index_row, count):
    rows = lax.broadcasted_iota(jnp.int32, (count, index_row.shape[1]), 0)
    return jnp.where(rows == index_row, 1.0, 0.0).astype(bf16)


def region_forward(features, boxes, target, w_visual, w_box_t, bias, gain, shift):
    rows, feat = features.shape
    width = w_visual.shape[1]
    steps = 2
    part = feat // steps

    def kernel(f_ref, box_ref, t_ref, wv_ref, wb_ref, b_ref, g_ref, s_ref, m_ref, n_ref, i_ref, acc):
        step = pl.program_id(0)
        partial = mm(f_ref[...], wv_ref[...])

        @pl.when(step == 0)
        def _():
            acc[...] = partial + (mm(box_ref[...], wb_ref[...], TN) + b_ref[...])

        @pl.when(step > 0)
        def _():
            acc[...] += partial

        @pl.when(step == steps - 1)
        def _():
            normed, inv = norm_parts(acc[...])
            n_ref[...] = normed
            i_ref[...] = jnp.broadcast_to(inv, i_ref.shape)
            low = (normed * g_ref[...] + s_ref[...]).astype(bf16)
            m_ref[...] = mm(one_hot(t_ref[...], rows), low).astype(bf16)

    return pl.pallas_call(
        kernel,
        grid=(steps,),
        in_specs=[
            pl.BlockSpec((rows, part), lambda i: (0, i)),
            whole(boxes.shape),
            whole((1, rows)),
            pl.BlockSpec((part, width), lambda i: (i, 0)),
            whole(w_box_t.shape),
            vec(width),
            vec(width),
            vec(width),
        ],
        out_specs=[VMEM, whole((rows, width)), whole((rows, 128))],
        out_shape=[near((rows, width), bf16), apart((rows, width)), apart((rows, 128))],
        scratch_shapes=[pltpu.VMEM((rows, width), f32)],
        compiler_params=params(24),
        cost_estimate=cost(3),
        name="region_forward",
    )(far(features), far(boxes), far(target), far(w_visual), far(w_box_t), far(bias), far(gain), far(shift))


def text_qkv(text, w_qkv, qv_bias):
    rows, width = text.shape

    def kernel(t_ref, w_ref, b_ref, o_ref):
        step = pl.program_id(0)
        bias = b_ref[...] * jnp.where(step == 1, 0.0, 1.0)
        o_ref[...] = (mm(t_ref[...], w_ref[...]) + bias).astype(bf16)

    return pl.pallas_call(
        kernel,
        grid=(3,),
        in_specs=[
            whole((rows, width)),
            pl.BlockSpec((width, width), lambda i: (0, i)),
            pl.BlockSpec((1, width), lambda i: (0, i // 2)),
        ],
        out_specs=pl.BlockSpec((rows, width), lambda i: (0, i)),
        out_shape=apart((rows, 3 * width), bf16),
        compiler_params=params(12),
        cost_estimate=cost(3),
        name="text_qkv",
    )(far(text), far(w_qkv), qv_bias)


def forward(
    scalars, text, text_low, arrived, source, out_grad, w_qkv, qv_bias, w_out, out_bias,
    attn_gain, attn_shift, w_up, up_bias, w_down, down_bias, ffn_gain, ffn_shift, dims,
):
    captions, images = dims
    width = text.shape[1]
    text_len = text.shape[0] // captions
    slots = arrived.shape[0]
    regions = slots // images
    seq = text_len + regions
    rows = captions * seq
    ff = w_up.shape[1]
    half = width // 2
    parts = 4
    part = ff // parts
    grid = captions + parts

    def kernel(
        sc_ref, t_ref, tq_ref, a_ref, src_ref, og_ref, wq_far, qvb_ref, wo_far, ob_ref, ag_ref, as_ref,
        wu_far, ub_ref, wd_far, db_ref, fg_ref, fs_ref,
        out_ref, x_ref, qkv_ref, probs_ref, ctx_ref, an_ref, ai_ref, hid_ref, slope_ref, ds_ref, df_ref,
        sums_ref, wu, wd, send_ref, keep_ref,
        regs, rqkv, act_all, wq, wo, sems,
    ):
        step = pl.program_id(0)

        def third(at):
            cols = slice(at * width, (at + 1) * width)
            return pltpu.make_async_copy(wq_far.at[:, cols], wq.at[:, cols], sems.at[at])

        def load(at):
            source, target = ((wo_far, wo), (wu_far, wu), (wd_far, wd))[at]
            return pltpu.make_async_copy(source, target, sems.at[3 + at])

        @pl.when(step == 0)
        def _():
            for at in range(3):
                third(at).start()
            load(0).start()
            sums_ref[...] = jnp.zeros_like(sums_ref)
            local = mm(one_hot(src_ref[...], slots), a_ref[...], TN).astype(bf16)
            regs[...] = local
            for part_id in range(3):
                at = slice(part_id * width, (part_id + 1) * width)
                third(part_id).wait()
                if part_id == 2:
                    load(1).start()
                    load(2).start()
                got = mm(local, wq[:, at])
                if part_id == 0:
                    got = got + qvb_ref[:, :width]
                if part_id == 2:
                    got = got + qvb_ref[:, width:]
                rqkv[:, at] = got.astype(bf16)

        @pl.when(step < captions)
        def _():
            image = sc_ref[8 + step]
            length = sc_ref[8 + captions + step]
            count = sc_ref[8 + 2 * captions + image]
            at = pl.ds(pl.multiple_of(image * regions, regions), regions)
            here = pl.ds(pl.multiple_of(step * seq, seq), seq)
            x_ref[:text_len, :] = t_ref[...]
            x_ref[text_len:, :] = regs[at, :]
            qkv_ref[:text_len, :] = tq_ref[...]
            qkv_ref[text_len:, :] = rqkv[at, :]
            place = lax.broadcasted_iota(jnp.int32, (seq, 1), 0)
            row_end = jnp.where(place < text_len, length, text_len + count)
            row_mask = jnp.where(place < row_end, 1.0, 0.0)
            key_bias = jnp.where(place < row_end, 0.0, -1e30)
            first = lax.broadcasted_iota(jnp.int32, (1, 2 * HEAD), 1) < HEAD
            scale = [
                jnp.where(first, 0.125, 0.0).astype(bf16),
                jnp.where(first, 0.0, 0.125).astype(bf16),
            ]
            def pair_forward(pair, carry):
                def cols(base):
                    return pl.ds(pl.multiple_of(base + pair * 2 * HEAD, 2 * HEAD), 2 * HEAD)

                q = qkv_ref[:, cols(0)]
                k = qkv_ref[:, cols(width)]
                v = qkv_ref[:, cols(2 * width)]
                scores = mm(k, jnp.concatenate([q * scale[0], q * scale[1]], 0), NT) + key_bias
                raised = jnp.exp(scores - jnp.max(scores, 0, keepdims=True))
                low = (raised * (1.0 / jnp.sum(raised, 0, keepdims=True))).astype(bf16)
                probs_ref[pair] = low
                outs = mm(low, v, TN)
                ctx_ref[:, cols(0)] = jnp.where(first, outs[:seq], outs[seq:]).astype(bf16)
                return carry

            lax.fori_loop(0, HEADS // 2, pair_forward, 0, unroll=3)

            @pl.when(step == 0)
            def _():
                load(0).wait()

            x_wide = x_ref[...].astype(f32)
            attn_out = mm(ctx_ref[...], wo[...]) + ob_ref[...]
            normed, inv = norm_parts(x_wide + attn_out)
            an_ref[here, :] = normed
            ai_ref[here, :] = jnp.broadcast_to(inv, (seq, 128))
            hidden = normed * ag_ref[...] + as_ref[...]
            hidden_low = hidden.astype(bf16)
            hid_ref[here, :] = hidden_low

            @pl.when(step == 0)
            def _():
                load(1).wait()

            for piece in range(parts):
                at = slice(piece * part, (piece + 1) * part)
                upper = mm(hidden_low, wu[:, at]) + ub_ref[:, at]
                phi = 0.5 * (1.0 + lax.erf(upper * inv_sqrt_two))
                act_all[here, at] = (upper * phi).astype(bf16)
                slope = phi + upper * jnp.exp(-0.5 * upper * upper) * inv_sqrt_tau
                slope_ref[here, at] = slope.astype(bf16)
                if piece == 0:

                    @pl.when(step == 0)
                    def _():
                        load(2).wait()

                term = mm(act_all[here, at], wd[at, :])
                ffn_sum = term if piece == 0 else ffn_sum + term

            ffn_out = ffn_sum + db_ref[...]
            ffn_normed, ffn_inv = norm_parts(hidden + ffn_out)
            out_ref[...] = ((ffn_normed * fg_ref[...] + fs_ref[...]) * row_mask).astype(bf16)
            cot = og_ref[...].astype(f32) * row_mask
            second = norm_back(cot, ffn_normed, ffn_inv, fg_ref[...])
            ds_ref[here, :] = second
            low = second.astype(bf16)
            df_ref[here, :] = low
            for at, value in enumerate(
                (
                    cot * ffn_normed,
                    cot,
                    low.astype(f32),
                    row_mask * x_wide * x_wide,
                    row_mask * attn_out * attn_out,
                    row_mask * ffn_out * ffn_out,
                    jnp.broadcast_to(row_mask, (seq, width)),
                )
            ):
                sums_ref[at : at + 1, :] += row_sum(value)

        @pl.when(step >= captions)
        def _():
            acts = pl.ds(pl.multiple_of((step - captions) * part, part), part)
            got = mm(act_all[:, acts], df_ref[...], TN)
            mine = sc_ref[0] == 0
            send_ref[...] = jnp.where(mine, got[:, half:], got[:, :half]).astype(bf16)
            keep_ref[...] = jnp.where(mine, got[:, :half], got[:, half:]).astype(bf16)

    def rowwise(size, cols):
        return pl.BlockSpec((size, cols), lambda i, s: (jnp.minimum(i, captions - 1), 0))

    anywhere = pl.BlockSpec(memory_space=pl.ANY)
    return pl.pallas_call(
        kernel,
        grid_spec=pltpu.PrefetchScalarGridSpec(
            num_scalar_prefetch=1,
            grid=(grid,),
            in_specs=[
                rowwise(text_len, width),
                rowwise(text_len, 3 * width),
                VMEM,
                whole((1, slots)),
                rowwise(seq, width),
                anywhere,
                whole((1, 2 * width)),
                anywhere,
                vec(width),
                vec(width),
                vec(width),
                anywhere,
                whole((1, ff)),
                anywhere,
                vec(width),
                vec(width),
                vec(width),
            ],
            out_specs=[rowwise(seq, width), rowwise(seq, width), rowwise(seq, 3 * width)]
            + [pl.BlockSpec((HEADS // 2, seq, 2 * seq), lambda i, s: (jnp.minimum(i, captions - 1), 0, 0))]
            + [rowwise(seq, width)]
            + [VMEM] * 9
            + [pl.BlockSpec((part, half), lambda i, s: (jnp.maximum(i - captions, 0), 0))] * 2,
            scratch_shapes=[
                pltpu.VMEM((slots, width), bf16),
                pltpu.VMEM((slots, 3 * width), bf16),
                pltpu.VMEM((rows, ff), bf16),
                pltpu.VMEM(w_qkv.shape, bf16),
                pltpu.VMEM(w_out.shape, bf16),
                pltpu.SemaphoreType.DMA((6,)),
            ],
        ),
        out_shape=[
            apart((rows, width), bf16),
            apart((rows, width), bf16),
            apart((rows, 3 * width), bf16),
            apart((captions * HEADS // 2, seq, 2 * seq), bf16),
            apart((rows, width), bf16),
            near((rows, width)),
            near((rows, 128)),
            near((rows, width), bf16),
            near((rows, ff), bf16),
            near((rows, width)),
            near((rows, width), bf16),
            near((8, width)),
            near(w_up.shape, bf16),
            near(w_down.shape, bf16),
            apart((ff, half), bf16),
            apart((ff, half), bf16),
        ],
        compiler_params=params(33),
        cost_estimate=cost(30),
        name="forward",
    )(
        scalars,
        far(text),
        far(text_low),
        arrived,
        *(
            far(v)
            for v in (
                source, out_grad, w_qkv, qv_bias, w_out, out_bias,
                attn_gain, attn_shift, w_up, up_bias, w_down, down_bias, ffn_gain, ffn_shift,
            )
        ),
    )


def ffn_backward(core, d_ffn, d_second, slope, attn_normed, attn_inv, w_down, w_up, attn_gain, seq, hold, first, size, begun):
    rows, width = d_ffn.shape
    ff = w_up.shape[1]
    parts = 4
    part = ff // parts

    def kernel(c_ref, df_ref, ds_ref, sl_ref, an_ref, ai_ref, wd, wu, ag_ref, *rest):
        dup_ref, dr_ref, da_ref, sums_ref, up_ref = rest[len(begun) + len(hold) :]
        step = pl.program_id(0)

        @pl.when(step == 0)
        def _():
            if begun:
                sums_ref[...] = rest[3][...]
                up_ref[...] = rest[4][...]
            else:
                sums_ref[...] = jnp.zeros_like(sums_ref)
                up_ref[...] = jnp.zeros_like(up_ref)

        here = pl.ds(pl.multiple_of((first + step) * seq, seq), seq)
        d_low = df_ref[here, :]
        for piece in range(parts):
            at = slice(piece * part, (piece + 1) * part)
            d_act = mm(d_low, wd[at, :], NT)
            low = (d_act * sl_ref[here, at].astype(f32)).astype(bf16)
            dup_ref[here, at] = low
            up_ref[0:1, at] += row_sum(low.astype(f32))
        d_hidden = ds_ref[here, :] + mm(dup_ref[here, :], wu[...], NT)
        normed = an_ref[here, :]
        resid = norm_back(d_hidden, normed, ai_ref[here, 0:1], ag_ref[...])
        dr_ref[here, :] = resid
        low = resid.astype(bf16)
        da_ref[here, :] = low
        sums_ref[0:1, :] += row_sum(d_hidden * normed)
        sums_ref[1:2, :] += row_sum(d_hidden)
        sums_ref[2:3, :] += row_sum(low.astype(f32))

    return pl.pallas_call(
        kernel,
        grid_spec=pltpu.PrefetchScalarGridSpec(
            num_scalar_prefetch=1,
            grid=(size,),
            in_specs=[VMEM] * 7
            + [vec(width)]
            + [VMEM] * len(begun)
            + [VMEM] * len(hold),
            out_specs=[VMEM] * 5,
        ),
        out_shape=[
            near((rows, ff), bf16),
            near((rows, width)),
            near((rows, width), bf16),
            near((8, width)),
            near((8, ff)),
        ],
        input_output_aliases={9: 0, 10: 1, 11: 2} if begun else {},
        compiler_params=params(6),
        cost_estimate=cost(4 * size),
        name="ffn_backward",
    )(core, d_ffn, d_second, slope, attn_normed, attn_inv, w_down, w_up, attn_gain, *begun, *hold)


def up_gradient(core, hidden_low, d_upper):
    rows, width = hidden_low.shape

    def kernel(c_ref, h_ref, d_ref, send_ref, keep_ref):
        step = pl.program_id(0)
        here = pl.ds(pl.multiple_of(step * width, width), width)
        for to_ref, side in ((send_ref, 1 - c_ref[0]), (keep_ref, c_ref[0])):
            cols = pl.ds(pl.multiple_of((2 * side + step) * width, width), width)
            to_ref[:, here] = mm(h_ref[...], d_ref[:, cols], TN).astype(bf16)

    return pl.pallas_call(
        kernel,
        grid_spec=pltpu.PrefetchScalarGridSpec(
            num_scalar_prefetch=1, grid=(2,), in_specs=[VMEM, VMEM], out_specs=[VMEM, VMEM]
        ),
        out_shape=[near((width, 2 * width), bf16)] * 2,
        compiler_params=params(6),
        cost_estimate=cost(0.1),
        name="up_gradient",
    )(core, hidden_low, d_upper)


def attention_backward(scalars, d_attn, d_resid, probs, qkv, source, w_out, w_qkv, dims, first_caption, size, begun):
    captions, images = dims
    rows, width = d_attn.shape
    seq = rows // captions
    slots = source.shape[1]
    regions = slots // images
    text_len = seq - regions
    last = first_caption + size == captions

    def kernel(
        sc_ref, da_ref, dr_ref, p_ref, qkv_ref, src_ref, wo_ref, wq, *rest,
    ):
        begun_refs = rest[: len(begun)]
        dqkv_ref, text_ref, back_ref, sums_ref, d_img, d_ctx_ref = rest[len(begun) :]
        step = pl.program_id(0)
        here = pl.ds(pl.multiple_of((first_caption + step) * seq, seq), seq)

        @pl.when(step == 0)
        def _():
            if begun:
                sums_ref[...] = begun_refs[3][...]
                d_img[...] = begun_refs[2][...]
            else:
                sums_ref[...] = jnp.zeros_like(sums_ref)
                d_img[...] = jnp.zeros_like(d_img)

        d_ctx_ref[...] = mm(da_ref[here, :], wo_ref[...], NT).astype(bf16)
        first = lax.broadcasted_iota(jnp.int32, (1, 2 * HEAD), 1) < HEAD
        masks = [jnp.where(first, 1.0, 0.0).astype(bf16), jnp.where(first, 0.0, 1.0).astype(bf16)]
        def pair_backward(pair, carry):
            def cols(base):
                return pl.ds(pl.multiple_of(base + pair * 2 * HEAD, 2 * HEAD), 2 * HEAD)

            q = qkv_ref[here, cols(0)]
            k = qkv_ref[here, cols(width)]
            v = qkv_ref[here, cols(2 * width)]
            d_c = d_ctx_ref[:, cols(0)]
            both_c = jnp.concatenate([d_c * masks[0], d_c * masks[1]], 0)
            both_q = jnp.concatenate([q * masks[0], q * masks[1]], 0)
            low = p_ref[pair]
            d_probs = mm(v, both_c, NT)
            wide = low.astype(f32)
            both = wide * d_probs
            inner = jnp.sum(both, 0, keepdims=True)
            d_scores = (both - wide * inner).astype(bf16)
            d_q = mm(d_scores, k, TN) * 0.125
            dqkv_ref[here, cols(0)] = jnp.where(first, d_q[:seq], d_q[seq:]).astype(bf16)
            dqkv_ref[here, cols(width)] = (mm(d_scores, both_q) * 0.125).astype(bf16)
            dqkv_ref[here, cols(2 * width)] = mm(low, both_c).astype(bf16)
            return carry

        lax.fori_loop(0, HEADS // 2, pair_backward, 0, unroll=3)

        sums_ref[0:1, :] += row_sum(dqkv_ref[here, :width].astype(f32))
        sums_ref[1:2, :] += row_sum(dqkv_ref[here, 2 * width :].astype(f32))
        d_x = mm(dqkv_ref[here, :], wq[...], NT) + dr_ref[here, :]
        text_ref[...] = d_x[:text_len]
        at = pl.ds(pl.multiple_of(sc_ref[8 + first_caption + step] * regions, regions), regions)
        d_img[at, :] += d_x[text_len:]

        @pl.when(step == size - 1)
        def _():
            if last:
                back_ref[...] = mm(one_hot(src_ref[...], slots), d_img[...].astype(bf16)).astype(bf16)
            else:
                back_ref[...] = d_img[...]

    return pl.pallas_call(
        kernel,
        grid_spec=pltpu.PrefetchScalarGridSpec(
            num_scalar_prefetch=1,
            grid=(size,),
            in_specs=[VMEM] * 2
            + [pl.BlockSpec((HEADS // 2, seq, 2 * seq), lambda i, s: (i + first_caption, 0, 0)), VMEM]
            + [whole((1, slots)), VMEM, VMEM]
            + ([VMEM, pl.BlockSpec(memory_space=pl.ANY)] + [VMEM, VMEM] if begun else []),
            out_specs=[
                VMEM,
                pl.BlockSpec((text_len, width), lambda i, s: (i + first_caption, 0)),
                VMEM,
                VMEM,
            ],
            scratch_shapes=[
                pltpu.VMEM((slots, width), f32),
                pltpu.VMEM((seq, width), bf16),
            ],
        ),
        out_shape=[
            near((rows, 3 * width), bf16),
            pltpu.HBM((captions * text_len, width), f32),
            near((slots, width), bf16 if last else f32),
            near((8, width)),
        ],
        input_output_aliases={8: 0, 9: 1} if begun else {},
        compiler_params=params(11),
        cost_estimate=cost(5 * size),
        name="attention_backward",
    )(scalars, d_attn, d_resid, far(probs), qkv, source, w_out, w_qkv, *begun)


def qkvo_gradient(core, x, d_qkv, context, d_attn):
    rows, width = x.shape

    def kernel(c_ref, x_ref, dq_ref, ctx_ref, da_ref, send_ref, keep_ref):
        step = pl.program_id(0)

        def store(low_block, high_block):
            low, high = low_block.astype(bf16), high_block.astype(bf16)

            @pl.when(c_ref[0] == 0)
            def _():
                keep_ref[...] = low
                send_ref[...] = high

            @pl.when(c_ref[0] != 0)
            def _():
                send_ref[...] = low
                keep_ref[...] = high

        @pl.when(step == 0)
        def _():
            store(mm(x_ref[...], dq_ref[:, :width], TN), mm(x_ref[...], dq_ref[:, 2 * width :], TN))

        @pl.when(step == 1)
        def _():
            store(mm(x_ref[...], dq_ref[:, width : 2 * width], TN), mm(ctx_ref[...], da_ref[...], TN))

    out = pl.BlockSpec((width, width), lambda i, s: (0, i))
    return pl.pallas_call(
        kernel,
        grid_spec=pltpu.PrefetchScalarGridSpec(
            num_scalar_prefetch=1, grid=(2,), in_specs=[VMEM] * 4, out_specs=[out, out]
        ),
        out_shape=[apart((width, 2 * width), bf16)] * 2,
        compiler_params=params(14),
        cost_estimate=cost(5),
        name="qkvo_gradient",
    )(core, x, d_qkv, context, d_attn)


def region_norm_backward(
    core, returned, target, normed, inv, gain, boxes, w_box_t, sums_forward, sums_ffn, sums_up, sums_attn, groups
):
    rows, width = returned.shape
    half = width // 2
    box = boxes.shape[0]
    share = width // groups
    ff_share = sums_up.shape[1] // groups

    def kernel(
        c_ref, r_ref, t_ref, n_ref, i_ref, g_ref, box_ref, wb_ref, sf_ref, sn_ref, su_ref, sa_ref,
        all_ref, send_ref, keep_ref, small_ref, bg_ref, small,
    ):
        d_region = mm(one_hot(t_ref[...], rows), r_ref[...], TN)
        normed = n_ref[...]
        low = norm_back(d_region, normed, i_ref[:, 0:1], g_ref[...]).astype(bf16)
        all_ref[...] = low
        mine = c_ref[0] == 0
        send_ref[:rows, :] = jnp.where(mine, low[:, half:], low[:, :half])
        keep_ref[...] = jnp.where(mine, low[:, :half], low[:, half:])
        bg_ref[...] = mm(wb_ref[...], low, NT)
        boxes_grad = mm(box_ref[...], low)
        vectors = [
            row_sum(low.astype(f32)),
            row_sum(d_region * normed),
            row_sum(d_region),
            sf_ref[0:1, :],
            sf_ref[1:2, :],
            sf_ref[2:3, :],
            sn_ref[0:1, :],
            sn_ref[1:2, :],
            sn_ref[2:3, :],
        ] + [boxes_grad[at : at + 1] for at in range(box)]
        small[...] = jnp.zeros_like(small)
        lane = lax.broadcasted_iota(jnp.int32, (1, half), 1)
        stats = jnp.zeros((1, half), f32)
        for at in range(4):
            total = jnp.sum(sf_ref[3 + at : 4 + at, :], 1, keepdims=True)
            stats = jnp.where(lane == at, total, stats)
        flat = jnp.concatenate([sa_ref[0:1, :], sa_ref[1:2, :]], 1)
        for group in range(groups):
            small[group, 0:1, 0:ff_share] = su_ref[0:1, group * ff_share : (group + 1) * ff_share]
            small[group, 1:2, 0 : 2 * share] = flat[:, group * 2 * share : (group + 1) * 2 * share]
            for at, value in enumerate(vectors):
                row, col = (1, 2) if at == 0 else (2 + (at - 1) // 3, (at - 1) % 3)
                small[group, row : row + 1, 128 * col : 128 * col + share] = value[
                    :, group * share : (group + 1) * share
                ]
            small[group, 6:7, :] = stats
        small_ref[...] = small[...].astype(bf16)
        for group in range(groups):
            send_ref[rows + 8 * group : rows + 8 * (group + 1), :] = small_ref[group]

    sizes = (sums_forward, sums_ffn, sums_up, sums_attn)
    return pl.pallas_call(
        kernel,
        grid_spec=pltpu.PrefetchScalarGridSpec(
            num_scalar_prefetch=1,
            grid=(1,),
            in_specs=[
                whole((rows, width)),
                whole((1, rows)),
                whole((rows, width)),
                whole((rows, 128)),
                vec(width),
                whole(boxes.shape),
                whole(w_box_t.shape),
            ]
            + [whole(v.shape) for v in sizes],
            out_specs=[VMEM] * 4 + [whole((box, rows))],
            scratch_shapes=[pltpu.VMEM((groups, 8, half), f32)],
        ),
        out_shape=[
            near((rows, width), bf16),
            near((rows + 8 * groups, half), bf16),
            near((rows, half), bf16),
            near((groups, 8, half), bf16),
            shape((box, rows)),
        ],
        compiler_params=params(14),
        cost_estimate=cost(0.1),
        name="region_norm_backward",
    )(core, returned, far(target), far(normed), far(inv), far(gain), far(boxes), far(w_box_t), *sizes)


def visual_gradient(bits, features, other_features, d_pre, other_d_pre, small, groups):
    rows, feat = features.shape
    half = d_pre.shape[1]
    steps = 4
    part = feat // steps
    quarter = feat // groups // 4
    tall = quarter + 8
    per_step = groups // steps
    high = groups // 2

    def kernel(b_ref, f_ref, o_ref, d_ref, p_ref, s_ref, a_send, a_keep, b_send, b_keep, got):
        step = pl.program_id(0)
        bit2, bit4 = b_ref[1], b_ref[2]
        got[...] = mm(f_ref[...], d_ref[...], TN) + mm(o_ref[...], p_ref[:rows, :], TN)

        def fill(to_ref, at, which, group, x, piece):
            here = pl.ds(pl.multiple_of(((group * 2 + x) * 2 + piece) * quarter, 8), quarter)
            to_ref[at, which, :quarter, :] = got[here, :].astype(bf16)
            number = step * per_step + group
            other = p_ref[pl.ds(pl.multiple_of(rows + 8 * number, 8), 8), :]
            to_ref[at, which, quarter:, :] = add(s_ref[number], other)

        for group in range(per_step):
            y = group % 2
            at = step * (per_step // 2) + group // 2
            fill(a_send, at, y, group, 1 - bit2, 0)
            fill(a_keep, at, y, group, bit2, 0)

            @pl.when(bit4 == y)
            def _():
                for x in range(2):
                    fill(b_keep, at, x, group, x, 1)

            @pl.when(bit4 != y)
            def _():
                for x in range(2):
                    fill(b_send, at, x, group, x, 1)

    return pl.pallas_call(
        kernel,
        grid_spec=pltpu.PrefetchScalarGridSpec(
            num_scalar_prefetch=1,
            grid=(steps,),
            in_specs=[
                pl.BlockSpec((rows, part), lambda i, s: (0, i)),
                pl.BlockSpec((rows, part), lambda i, s: (0, i)),
                VMEM,
                VMEM,
                VMEM,
            ],
            out_specs=[VMEM] * 4,
            scratch_shapes=[pltpu.VMEM((part, half), f32)],
        ),
        out_shape=[near((high, 2, tall, half), bf16)] * 4,
        compiler_params=params(10),
        cost_estimate=cost(0.1),
        name="visual_gradient",
    )(bits, far(features), far(other_features), d_pre, other_d_pre, small)


def feature_gradient(bits, d_pre, w_visual):
    rows, width = d_pre.shape
    feat = w_visual.shape[0]
    steps = 4
    part = feat // steps

    def kernel(b_ref, d_ref, w_ref, o_ref):
        o_ref[...] = mm(d_ref[...], w_ref[...], NT)

    return pl.pallas_call(
        kernel,
        grid_spec=pltpu.PrefetchScalarGridSpec(
            num_scalar_prefetch=1,
            grid=(steps,),
            in_specs=[VMEM, pl.BlockSpec((part, width), lambda i, s: (i, 0))],
            out_specs=pl.BlockSpec((rows, part), lambda i, s: (0, i)),
        ),
        out_shape=shape((rows, feat)),
        compiler_params=params(8),
        cost_estimate=cost(10),
        name="feature_gradient",
    )(bits, d_pre, far(w_visual))


def device_number():
    return lax.axis_index("dp") * lax.axis_size("enc") + lax.axis_index("enc")


def swap(values, bit):
    count = lax.axis_size("dp") * lax.axis_size("enc")
    return lax.ppermute(values, ("dp", "enc"), [(i, i ^ bit) for i in range(count)])


def add(a, b):
    return (a.astype(f32) + b.astype(f32)).astype(bf16)


def scalar_call(kernel, bits, ins, in_specs, outs, out_specs, grid, limit, name, last=False, place=near):
    outs = outs if last else [place(o.shape, o.dtype) for o in outs]
    return pl.pallas_call(
        kernel,
        grid_spec=pltpu.PrefetchScalarGridSpec(
            num_scalar_prefetch=1, grid=(grid,), in_specs=in_specs, out_specs=out_specs
        ),
        out_shape=outs,
        compiler_params=params(limit),
        cost_estimate=cost(1),
        name=name,
    )(bits, *ins)


def first_split(bits, kept, got, groups, place=near):
    tall = kept.ndim == 5
    high = groups // 2
    if tall:
        rows, cols = kept.shape[3:]
        view = (high, 2, 2, 2, rows, cols)
        block = (1, 2, 2, 2, rows, cols)
    else:
        rows, cols = kept.shape[0] // groups, kept.shape[1] // 4
        view = (high, 2, rows, 4 * cols)
        block = (1, 2, rows, 4 * cols)

    def kernel(b_ref, k_ref, r_ref, a_send, a_keep, b_send, b_keep):
        bit2, bit4 = b_ref[1], b_ref[2]

        def total(y, x, piece):
            if tall:
                return add(k_ref[0, y, x, piece], r_ref[0, y, x, piece])
            at = pl.ds(pl.multiple_of((2 * x + piece) * cols, 128), cols)
            return add(k_ref[0, y, :, at], r_ref[0, y, :, at])

        for other in range(2):
            a_send[0, other] = total(other, 1 - bit2, 0)
            a_keep[0, other] = total(other, bit2, 0)
            b_send[0, other] = total(1 - bit4, other, 1)
            b_keep[0, other] = total(bit4, other, 1)

    spec = pl.BlockSpec(block, lambda i, s: (i,) + (0,) * (len(block) - 1))
    out = pl.BlockSpec((1, 2, rows, cols), lambda i, s: (i, 0, 0, 0))
    return scalar_call(
        kernel, bits, (kept.reshape(view), got.reshape(view)), [spec, spec],
        [shape((high, 2, rows, cols), bf16)] * 4, [out] * 4, high, 6, "first_split", place=place,
    )


def second_split(bits, a_kept, a_got, b_kept, b_got):
    high, _, rows, cols = a_kept.shape

    def kernel(b_ref, ak, ar, bk, br, a_send, a_keep, b_send, b_keep):
        bit2, bit4 = b_ref[1], b_ref[2]
        a_send[0] = add(ak[0, 1 - bit4], ar[0, 1 - bit4])
        a_keep[0] = add(ak[0, bit4], ar[0, bit4])
        b_send[0] = add(bk[0, 1 - bit2], br[0, 1 - bit2])
        b_keep[0] = add(bk[0, bit2], br[0, bit2])

    spec = pl.BlockSpec((1, 2, rows, cols), lambda i, s: (i, 0, 0, 0))
    out = pl.BlockSpec((1, rows, cols), lambda i, s: (i, 0, 0))
    return scalar_call(
        kernel, bits, (a_kept, a_got, b_kept, b_got), [spec] * 4,
        [shape((high, rows, cols), bf16)] * 4, [out] * 4, high, 6, "second_split",
    )


def join_split(bits, pairs, place=near):
    high, _, cols = pairs[0][0].shape
    sizes = [kept.shape[1] for kept, _ in pairs]

    def kernel(b_ref, *refs):
        bit = b_ref[3]
        send, keep = refs[-2:]
        at = 0
        for n, size in enumerate(sizes):
            kept, got = refs[2 * n : 2 * n + 2]
            send[0, at : at + size] = add(kept[1 - bit], got[1 - bit])
            keep[0, at : at + size] = add(kept[bit], got[bit])
            at += size

    ins = [value for pair in pairs for value in pair]
    specs = [pl.BlockSpec((2, v.shape[1], cols), lambda i, s: (i, 0, 0)) for v in ins]
    out = pl.BlockSpec((1, sum(sizes), cols), lambda i, s: (i, 0, 0))
    return scalar_call(
        kernel, bits, ins, specs, [shape((high // 2, sum(sizes), cols), bf16)] * 2, [out] * 2,
        high // 2, 6, "join_split", place=place,
    )


def late_split(bits, kept, got, which):
    high, rows, cols = kept.shape

    def kernel(b_ref, k_ref, r_ref, send, keep):
        bit = b_ref[which]
        send[0] = add(k_ref[1 - bit], r_ref[1 - bit])
        keep[0] = add(k_ref[bit], r_ref[bit])

    spec = pl.BlockSpec((2, rows, cols), lambda i, s: (i, 0, 0))
    out = pl.BlockSpec((1, rows, cols), lambda i, s: (i, 0, 0))
    return scalar_call(
        kernel, bits, (kept, got), [spec] * 2, [shape((high // 2, rows, cols), bf16)] * 2, [out] * 2,
        high // 2, 6, "late_split",
    )


def over_two(halves):
    return swap(halves[0], 2), halves[1], swap(halves[2], 4), halves[3]


def over_other_two(halves):
    return swap(halves[0], 4), halves[1], swap(halves[2], 2), halves[3]


def second(bits, moved):
    return second_split(bits, moved[1], moved[0], moved[3], moved[2])


def join(bits, *moved, place=near):
    pairs = []
    for one in moved:
        pairs += [(one[1], one[0]), (one[3], one[2])]
    return join_split(bits, pairs, place)


def after_all(*trees):
    leaves, tree = jax.tree.flatten(trees)
    return jax.tree.unflatten(tree, lax.optimization_barrier(leaves))


def late_first(bits, kept, got):
    if kept.shape[0] == 1:
        return (kept + got,)
    return late_split(bits, kept, got, 4)


def late_move(halves):
    return swap(halves[0], 16) if len(halves) > 1 else None


def late_rest(bits, halves, moved):
    bit, which = 16, 5
    while len(halves) > 1:
        if halves[1].shape[0] == 1:
            halves = (halves[1] + moved,)
        else:
            halves = late_split(bits, halves[1], moved, which)
            bit, which = 2 * bit, which + 1
            moved = swap(halves[0], bit)
    return halves[0][0]


def spread(mine, *late):
    over_x = swap(mine, 2)
    over_core = swap(mine, 1)
    return mine, over_x, over_core, swap(gate(over_x, *late), 1)


def pick(b_ref, pieces, core, x):
    mine, over_x, over_core, over_both = pieces
    same_x = b_ref[1] == x
    return jnp.where(
        b_ref[0] == core, jnp.where(same_x, mine, over_x), jnp.where(same_x, over_core, over_both)
    ).astype(f32)


def finish_ffn(bits, pieces):
    rows, cols = pieces[0].shape
    half = rows // 2
    part = rows // 4

    def kernel(b_ref, p0, p1, p2, p3, down_ref, up_ref):
        for core in range(2):
            for x in range(2):
                got = pick(b_ref, (p0[...], p1[...], p2[...], p3[...]), core, x)
                down_ref[x * half : (x + 1) * half, core * cols : (core + 1) * cols] = got[:half]
                for piece in range(2):
                    at = ((core * 2 + x) * 2 + piece) * cols
                    up_ref[:, at : at + cols] = got[half + piece * part : half + (piece + 1) * part]

    outs = [shape((rows, 2 * cols)), shape((part, 8 * cols))]
    return scalar_call(
        kernel, bits, pieces, [whole((rows, cols))] * 4, outs, [whole(o.shape) for o in outs], 1, 12, "finish_ffn", True
    )


def finish_wide(bits, pieces, sizes):
    rows, cols = pieces[0].shape
    part = rows // 2

    def kernel(b_ref, p0, p1, p2, p3, *out_refs):
        for core in range(2):
            for x in range(2):
                got = pick(b_ref, (p0[...], p1[...], p2[...], p3[...]), core, x)
                for piece in range(2):
                    at = ((core * 2 + x) * 2 + piece) * cols
                    for out_ref, size in zip(out_refs, sizes):
                        if 0 <= at < size:
                            out_ref[:, at : at + cols] = got[piece * part : (piece + 1) * part]
                        at -= size

    outs = [shape((part, size)) for size in sizes]
    return scalar_call(
        kernel, bits, pieces, [whole((rows, cols))] * 4, outs, [whole(o.shape) for o in outs], 1, 8, "finish_wide", True
    )


def finish_visual(bits, pieces, ff_share, share, box):
    rows, cols = pieces[0].shape
    tall = rows // 2
    quarter = tall - 8
    sizes = [share] * 9 + [2 * share, ff_share]

    def kernel(b_ref, p0, p1, p2, p3, vis_ref, box_ref, rms_ref, *small_refs):
        for core in range(2):
            for x in range(2):
                got = pick(b_ref, (p0[...], p1[...], p2[...], p3[...]), core, x)
                for piece in range(2):
                    low = piece * tall
                    vis_ref[(2 * x + piece) * quarter : (2 * x + piece + 1) * quarter, core * cols : (core + 1) * cols] = got[
                        low : low + quarter
                    ]
        small = p0[quarter : quarter + 8, :].astype(f32)
        for at in range(9):
            row, col = (1, 2) if at == 0 else (2 + (at - 1) // 3, (at - 1) % 3)
            small_refs[at][...] = small[row, 128 * col : 128 * col + share]
        small_refs[9][...] = small[1, 0 : 2 * share]
        small_refs[10][...] = small[0, 0:ff_share]
        for at in range(9, 9 + box):
            row, col = 2 + (at - 1) // 3, (at - 1) % 3
            box_ref[at - 9 : at - 8, :] = small[row : row + 1, 128 * col : 128 * col + share]
        stats = small[6, 0:128]
        total = jnp.sum(small[6:7, 3:4])
        rms_ref[...] = jnp.sqrt(stats / total)[:3]

    outs = [shape((4 * quarter, 2 * cols)), shape((box, share)), shape((3,))] + [shape((size,)) for size in sizes]
    specs = [whole(o.shape) for o in outs[:2]] + [vec(3)] + [vec(size) for size in sizes]
    return scalar_call(
        kernel, bits, pieces, [whole((rows, cols))] * 4, outs, specs, 1, 8, "finish_visual", True
    )


def gate(value, *others):
    return lax.optimization_barrier((value, *others))[0]


def on_device(
    text_embed,
    region_features,
    boxes,
    caption_image,
    caption_lengths,
    region_counts,
    region_target,
    region_source,
    w_visual,
    w_box,
    visual_bias,
    visual_gain,
    visual_shift,
    w_qkv,
    qv_bias,
    w_out,
    out_bias,
    attn_gain,
    attn_shift,
    w_up,
    up_bias,
    w_down,
    down_bias,
    ffn_gain,
    ffn_shift,
    out_grad,
):
    width = text_embed.shape[1]
    captions = caption_image.shape[0]
    images = region_counts.shape[0]
    dims = (captions, images)
    axes = ("dp", "enc")
    groups = lax.axis_size("dp")
    count = groups * lax.axis_size("enc")
    me = device_number().astype(jnp.int32)
    places = lax.iota(jnp.int32, 8)
    scalars = jnp.concatenate([(me >> places) & 1, caption_image, caption_lengths, region_counts])
    w_box_t = w_box.T
    row = lambda v: v.reshape(1, -1)
    qv_row = row(qv_bias)

    message, vis_normed, vis_inv = region_forward(
        region_features, boxes, region_target, w_visual, w_box_t, visual_bias, visual_gain, visual_shift
    )
    arrived = lax.all_to_all(message, axes, split_axis=0, concat_axis=0, tiled=True)
    text_low = text_qkv(text_embed, w_qkv, qv_row)
    (
        out_rows, x, qkv, probs, context, attn_normed, attn_inv, hidden_low, slope, d_second, d_ffn,
        sums_forward, w_up_near, w_down_near, down_sent, down_kept,
    ) = forward(
        scalars, text_embed, text_low, arrived, region_source, out_grad, w_qkv, qv_row, w_out,
        out_bias, attn_gain, attn_shift, w_up, row(up_bias), w_down, down_bias, ffn_gain, ffn_shift, dims,
    )
    seq = x.shape[0] // captions
    rest = captions - 1
    bits = core = scalars
    hold = ()
    ffn_ins = (d_ffn, d_second, slope, attn_normed, attn_inv, w_down_near, w_up_near, attn_gain, seq, hold)
    down_view = (groups, 2, 2, w_down.shape[0] // groups // 4, width // 2)
    down_sent, down_kept = down_sent.reshape(down_view), down_kept.reshape(down_view)

    moved = swap(down_sent, 1)
    begun = ffn_backward(core, *ffn_ins, 0, 1, ())

    moved, begun, sc = after_all(moved, begun, scalars)
    down = first_split(sc, down_kept, moved, groups)
    down, begun, sc = after_all(down, begun, sc)
    moved = over_two(down)
    d_upper, d_resid, d_attn, sums_ffn, sums_up = ffn_backward(sc, *ffn_ins, 1, rest, tuple(begun))
    up_sent, up_kept = up_gradient(sc, hidden_low, gate(d_upper, d_attn))

    moved, up_sent, up_kept, d_attn, sc = after_all(moved, up_sent, up_kept, d_attn, sc)
    down = second(sc, moved)
    down, up_sent, up_kept, sc = after_all(down, up_sent, up_kept, sc)
    moved = over_other_two(down), swap(up_sent, 1)
    att_ins = (d_attn, d_resid, probs, qkv, region_source, w_out, w_qkv, dims)
    begun = attention_backward(sc, *att_ins, 0, 1, ())

    moved, up_kept, begun, sc = after_all(moved, up_kept, begun, sc)
    down = moved[0]
    up = first_split(sc, up_kept, moved[1], groups)
    down, up, begun, sc = after_all(down, up, begun, sc)
    moved = over_two(up)
    d_qkv, text_grad, back_message, sums_attn = attention_backward(sc, *att_ins, 1, rest, tuple(begun))

    moved, down, d_qkv, back_message, sc = after_all(moved, down, d_qkv, back_message, sc)
    up = second(sc, moved)
    up, down, sc = after_all(up, down, sc)
    moved = over_other_two(up)
    qkvo_sent, qkvo_kept = qkvo_gradient(sc, x, d_qkv, context, d_attn)

    moved, down, qkvo_sent, qkvo_kept, back_message, sc = after_all(
        moved, down, qkvo_sent, qkvo_kept, back_message, sc
    )
    ffn = join(sc, down, moved, place=apart)
    ffn, qkvo_sent, qkvo_kept, back_message, sc = after_all(ffn, qkvo_sent, qkvo_kept, back_message, sc)
    returned = lax.all_to_all(back_message, axes, split_axis=0, concat_axis=0, tiled=True)
    other_features = swap(gate(region_features, qkvo_kept), 1)
    qkvo = first_split(sc, qkvo_kept, swap(qkvo_sent, 1), groups, apart)
    qkvo_moved = over_two(qkvo)
    ffn_moved = swap(gate(ffn[0], *qkvo), 8)
    returned, sc = after_all(returned, gate(sc, *qkvo))
    d_pre, d_pre_sent, d_pre_kept, small, box_grad = region_norm_backward(
        sc, returned, region_target, vis_normed, vis_inv, visual_gain, boxes, w_box_t,
        sums_forward, sums_ffn, sums_up, sums_attn, groups,
    )
    vis = visual_gradient(
        sc, region_features, other_features, d_pre_kept, swap(d_pre_sent, 1), small, groups
    )
    vis_moved = over_two(vis)
    sc = gate(sc, *vis)
    qkvo = second(sc, qkvo_moved)
    qkvo_moved = over_other_two(qkvo)
    ffn = late_first(gate(sc, *qkvo), ffn[1], ffn_moved)
    ffn_moved = late_move(ffn)
    feature_grad = feature_gradient(gate(sc, *ffn), d_pre, w_visual)

    sc = gate(sc, feature_grad)
    vis = second(sc, vis_moved)
    vis_moved = over_other_two(vis)
    sc = gate(sc, *vis)
    qkvo = join(sc, qkvo_moved)
    qkvo_moved = swap(qkvo[0], 8)
    ffn = late_rest(sc, ffn, gate(ffn_moved, *qkvo))

    vis = join(gate(sc, *qkvo, ffn), vis_moved)
    vis_moved = swap(vis[0], 8)
    sc = gate(sc, *vis)
    qkvo = late_first(sc, qkvo[1], qkvo_moved)
    qkvo_moved = late_move(qkvo)

    vis = late_first(gate(sc, *qkvo), vis[1], vis_moved)
    vis_moved = late_move(vis)
    ffn = spread(ffn, *vis)
    sc = gate(sc, *vis)
    g_down, g_up = finish_ffn(sc, ffn)
    qkvo = late_rest(sc, qkvo, gate(qkvo_moved, *vis))

    vis = late_rest(sc, vis, gate(vis_moved, g_up, qkvo))
    qkvo = spread(qkvo, vis)
    g_qkv, g_out = finish_wide(gate(sc, vis), qkvo, (3 * width, width))
    vis = spread(vis, g_qkv)
    g_visual, g_box_t, rms_values, *small = finish_visual(
        sc, vis, w_up.shape[1] // groups, width // groups, boxes.shape[0]
    )
    return (
        out_rows,
        text_grad,
        feature_grad,
        box_grad,
        rms_values,
        g_visual,
        g_box_t.T,
        small[0],
        small[1],
        small[2],
        g_qkv,
        small[9],
        g_out,
        small[8],
        small[6],
        small[7],
        g_up,
        small[10],
        g_down,
        small[5],
        small[3],
        small[4],
    )


def solution(mesh):
    return jax.shard_map(
        on_device,
        mesh=mesh,
        in_specs=(
            P(("dp", "enc"), None),
            P(("dp", "enc"), None),
            P(None, ("dp", "enc")),
            P(("dp", "enc")),
            P(("dp", "enc")),
            P(("dp", "enc")),
            P(("dp", "enc"), None),
            P(("dp", "enc"), None),
            P(),
            P(),
            P(),
            P(),
            P(),
            P(),
            P(),
            P(),
            P(),
            P(),
            P(),
            P(),
            P(),
            P(),
            P(),
            P(),
            P(),
            P(("dp", "enc"), None),
        ),
        out_specs=(
            P(("dp", "enc"), None),
            P(("dp", "enc"), None),
            P(("dp", "enc"), None),
            P(None, ("dp", "enc")),
            P(),
            P("dp", None),
            P("dp", None),
            P("dp"),
            P("dp"),
            P("dp"),
            P("dp", None),
            P("dp"),
            P("dp", None),
            P("dp"),
            P("dp"),
            P("dp"),
            P("dp", None),
            P("dp"),
            P("dp", None),
            P("dp"),
            P("dp"),
            P("dp"),
        ),
        check_vma=False,
    )
```

```python
import jax
import jax.numpy as jnp
from jax import lax
from jax.experimental import pallas as pl
from jax.experimental.pallas import tpu as pltpu
from jax.sharding import PartitionSpec as P

HEADS = 12
UNROLL = 2
HEAD = 64
epsilon = 1e-12
inv_sqrt_two = 0.7071067811865476
inv_sqrt_tau = 0.3989422804014327
f32 = jnp.float32
bf16 = jnp.bfloat16
NN = (((1,), (0,)), ((), ()))
NT = (((1,), (1,)), ((), ()))
TN = (((0,), (0,)), ((), ()))


def mm(a, b, dims=NN):
    return lax.dot_general(a, b, dims, preferred_element_type=f32)


def cost(us):
    return pl.CostEstimate(flops=int(us * 1e9), bytes_accessed=1 << 20, transcendentals=0)


def params(limit=56):
    return pltpu.CompilerParams(
        dimension_semantics=("arbitrary",), vmem_limit_bytes=limit << 20
    )


def whole(shape):
    return pl.BlockSpec(shape, lambda i, *s: (0,) * len(shape), pipeline_mode=pl.Buffered(1))


def vec(size):
    return pl.BlockSpec((size,), lambda i, *s: (0,))


VMEM = pl.BlockSpec(memory_space=pltpu.VMEM)


def far(value):
    return pltpu.with_memory_space_constraint(value, pltpu.HBM)


def apart(dims, kind=f32):
    return pltpu.HBM(dims, kind)


def near(dims, kind=f32):
    return pltpu.VMEM(dims, kind)


def shape(dims, kind=f32):
    return jax.ShapeDtypeStruct(dims, kind)


def norm_parts(values):
    centre = values - jnp.mean(values, -1, keepdims=True)
    inv_std = lax.rsqrt(jnp.mean(centre * centre, -1, keepdims=True) + epsilon)
    return centre * inv_std, inv_std


def norm_back(grad, normed, inv_std, gain):
    scaled = grad * gain
    return inv_std * (
        scaled
        - jnp.mean(scaled, -1, keepdims=True)
        - normed * jnp.mean(scaled * normed, -1, keepdims=True)
    )


def row_sum(values):
    return jnp.sum(values, 0, keepdims=True)


def one_hot(index_row, count):
    rows = lax.broadcasted_iota(jnp.int32, (count, index_row.shape[1]), 0)
    return jnp.where(rows == index_row, 1.0, 0.0).astype(bf16)


def region_forward(features, boxes, target, w_visual, w_box_t, bias, gain, shift):
    rows, feat = features.shape
    width = w_visual.shape[1]
    steps = 2
    part = feat // steps

    def kernel(f_ref, box_ref, t_ref, wv_ref, wb_ref, b_ref, g_ref, s_ref, m_ref, n_ref, i_ref, acc):
        step = pl.program_id(0)
        partial = mm(f_ref[...], wv_ref[...])

        @pl.when(step == 0)
        def _():
            acc[...] = partial + (mm(box_ref[...], wb_ref[...], TN) + b_ref[...])

        @pl.when(step > 0)
        def _():
            acc[...] += partial

        @pl.when(step == steps - 1)
        def _():
            normed, inv = norm_parts(acc[...])
            n_ref[...] = normed
            i_ref[...] = jnp.broadcast_to(inv, i_ref.shape)
            low = (normed * g_ref[...] + s_ref[...]).astype(bf16)
            m_ref[...] = mm(one_hot(t_ref[...], rows), low).astype(bf16)

    return pl.pallas_call(
        kernel,
        grid=(steps,),
        in_specs=[
            pl.BlockSpec((rows, part), lambda i: (0, i)),
            whole(boxes.shape),
            whole((1, rows)),
            pl.BlockSpec((part, width), lambda i: (i, 0)),
            whole(w_box_t.shape),
            vec(width),
            vec(width),
            vec(width),
        ],
        out_specs=[VMEM, whole((rows, width)), whole((rows, 128))],
        out_shape=[near((rows, width), bf16), apart((rows, width)), apart((rows, 128))],
        scratch_shapes=[pltpu.VMEM((rows, width), f32)],
        compiler_params=params(24),
        cost_estimate=cost(3),
        name="region_forward",
    )(far(features), far(boxes), far(target), far(w_visual), far(w_box_t), far(bias), far(gain), far(shift))


def text_qkv(text, w_qkv, qv_bias):
    rows, width = text.shape

    def kernel(t_ref, w_ref, b_ref, o_ref):
        step = pl.program_id(0)
        bias = b_ref[...] * jnp.where(step == 1, 0.0, 1.0)
        o_ref[...] = (mm(t_ref[...], w_ref[...]) + bias).astype(bf16)

    return pl.pallas_call(
        kernel,
        grid=(3,),
        in_specs=[
            whole((rows, width)),
            pl.BlockSpec((width, width), lambda i: (0, i)),
            pl.BlockSpec((1, width), lambda i: (0, i // 2)),
        ],
        out_specs=pl.BlockSpec((rows, width), lambda i: (0, i)),
        out_shape=apart((rows, 3 * width), bf16),
        compiler_params=params(12),
        cost_estimate=cost(3),
        name="text_qkv",
    )(far(text), far(w_qkv), qv_bias)


def forward(
    scalars, text, text_low, arrived, source, out_grad, w_qkv, qv_bias, w_out, out_bias,
    attn_gain, attn_shift, w_up, up_bias, w_down, down_bias, ffn_gain, ffn_shift, dims,
):
    captions, images = dims
    width = text.shape[1]
    text_len = text.shape[0] // captions
    slots = arrived.shape[0]
    regions = slots // images
    seq = text_len + regions
    rows = captions * seq
    ff = w_up.shape[1]
    half = width // 2
    parts = 4
    part = ff // parts
    grid = captions + parts

    def kernel(
        sc_ref, t_ref, tq_ref, a_ref, src_ref, og_ref, wq_far, qvb_ref, wo_far, ob_ref, ag_ref, as_ref,
        wu_far, ub_ref, wd_far, db_ref, fg_ref, fs_ref,
        out_ref, x_ref, qkv_ref, probs_ref, ctx_ref, an_ref, ai_ref, hid_ref, slope_ref, ds_ref, df_ref,
        sums_ref, wu, wd, send_ref, keep_ref,
        regs, rqkv, act_all, wq, wo, sems,
    ):
        step = pl.program_id(0)

        def third(at):
            cols = slice(at * width, (at + 1) * width)
            return pltpu.make_async_copy(wq_far.at[:, cols], wq.at[:, cols], sems.at[at])

        def load(at):
            source, target = ((wo_far, wo), (wu_far, wu), (wd_far, wd))[at]
            return pltpu.make_async_copy(source, target, sems.at[3 + at])

        @pl.when(step == 0)
        def _():
            for at in range(3):
                third(at).start()
            load(0).start()
            sums_ref[...] = jnp.zeros_like(sums_ref)
            local = mm(one_hot(src_ref[...], slots), a_ref[...], TN).astype(bf16)
            regs[...] = local
            for part_id in range(3):
                at = slice(part_id * width, (part_id + 1) * width)
                third(part_id).wait()
                if part_id == 2:
                    load(1).start()
                    load(2).start()
                got = mm(local, wq[:, at])
                if part_id == 0:
                    got = got + qvb_ref[:, :width]
                if part_id == 2:
                    got = got + qvb_ref[:, width:]
                rqkv[:, at] = got.astype(bf16)

        @pl.when(step < captions)
        def _():
            image = sc_ref[8 + step]
            length = sc_ref[8 + captions + step]
            count = sc_ref[8 + 2 * captions + image]
            at = pl.ds(pl.multiple_of(image * regions, regions), regions)
            here = pl.ds(pl.multiple_of(step * seq, seq), seq)
            x_ref[:text_len, :] = t_ref[...]
            x_ref[text_len:, :] = regs[at, :]
            qkv_ref[:text_len, :] = tq_ref[...]
            qkv_ref[text_len:, :] = rqkv[at, :]
            place = lax.broadcasted_iota(jnp.int32, (seq, 1), 0)
            row_end = jnp.where(place < text_len, length, text_len + count)
            row_mask = jnp.where(place < row_end, 1.0, 0.0)
            key_bias = jnp.where(place < row_end, 0.0, -1e30)
            first = lax.broadcasted_iota(jnp.int32, (1, 2 * HEAD), 1) < HEAD
            scale = [
                jnp.where(first, 0.125, 0.0).astype(bf16),
                jnp.where(first, 0.0, 0.125).astype(bf16),
            ]
            def pair_forward(pair, carry):
                def cols(base):
                    return pl.ds(pl.multiple_of(base + pair * 2 * HEAD, 2 * HEAD), 2 * HEAD)

                q = qkv_ref[:, cols(0)]
                k = qkv_ref[:, cols(width)]
                v = qkv_ref[:, cols(2 * width)]
                scores = mm(k, jnp.concatenate([q * scale[0], q * scale[1]], 0), NT) + key_bias
                raised = jnp.exp(scores - jnp.max(scores, 0, keepdims=True))
                low = (raised * (1.0 / jnp.sum(raised, 0, keepdims=True))).astype(bf16)
                probs_ref[pair] = low
                outs = mm(low, v, TN)
                ctx_ref[:, cols(0)] = jnp.where(first, outs[:seq], outs[seq:]).astype(bf16)
                return carry

            lax.fori_loop(0, HEADS // 2, pair_forward, 0, unroll=3)

            @pl.when(step == 0)
            def _():
                load(0).wait()

            x_wide = x_ref[...].astype(f32)
            attn_out = mm(ctx_ref[...], wo[...]) + ob_ref[...]
            normed, inv = norm_parts(x_wide + attn_out)
            an_ref[here, :] = normed
            ai_ref[here, :] = jnp.broadcast_to(inv, (seq, 128))
            hidden = normed * ag_ref[...] + as_ref[...]
            hidden_low = hidden.astype(bf16)
            hid_ref[here, :] = hidden_low

            @pl.when(step == 0)
            def _():
                load(1).wait()

            for piece in range(parts):
                at = slice(piece * part, (piece + 1) * part)
                upper = mm(hidden_low, wu[:, at]) + ub_ref[:, at]
                phi = 0.5 * (1.0 + lax.erf(upper * inv_sqrt_two))
                act_all[here, at] = (upper * phi).astype(bf16)
                slope = phi + upper * jnp.exp(-0.5 * upper * upper) * inv_sqrt_tau
                slope_ref[here, at] = slope.astype(bf16)
                if piece == 0:

                    @pl.when(step == 0)
                    def _():
                        load(2).wait()

                term = mm(act_all[here, at], wd[at, :])
                ffn_sum = term if piece == 0 else ffn_sum + term

            ffn_out = ffn_sum + db_ref[...]
            ffn_normed, ffn_inv = norm_parts(hidden + ffn_out)
            out_ref[...] = ((ffn_normed * fg_ref[...] + fs_ref[...]) * row_mask).astype(bf16)
            cot = og_ref[...].astype(f32) * row_mask
            second = norm_back(cot, ffn_normed, ffn_inv, fg_ref[...])
            ds_ref[here, :] = second
            low = second.astype(bf16)
            df_ref[here, :] = low
            for at, value in enumerate(
                (
                    cot * ffn_normed,
                    cot,
                    low.astype(f32),
                    row_mask * x_wide * x_wide,
                    row_mask * attn_out * attn_out,
                    row_mask * ffn_out * ffn_out,
                )
            ):
                sums_ref[at : at + 1, :] += row_sum(value)
            lane = lax.broadcasted_iota(jnp.int32, (1, width), 1)
            slots_here = ((length + count) * width).astype(f32)
            sums_ref[6:7, :] += jnp.where(lane == 0, slots_here, 0.0)

        @pl.when(step >= captions)
        def _():
            acts = pl.ds(pl.multiple_of((step - captions) * part, part), part)
            got = mm(act_all[:, acts], df_ref[...], TN)
            mine = sc_ref[0] == 0
            send_ref[...] = jnp.where(mine, got[:, half:], got[:, :half]).astype(bf16)
            keep_ref[...] = jnp.where(mine, got[:, :half], got[:, half:]).astype(bf16)

    def rowwise(size, cols):
        return pl.BlockSpec((size, cols), lambda i, s: (jnp.minimum(i, captions - 1), 0))

    anywhere = pl.BlockSpec(memory_space=pl.ANY)
    return pl.pallas_call(
        kernel,
        grid_spec=pltpu.PrefetchScalarGridSpec(
            num_scalar_prefetch=1,
            grid=(grid,),
            in_specs=[
                rowwise(text_len, width),
                rowwise(text_len, 3 * width),
                VMEM,
                whole((1, slots)),
                rowwise(seq, width),
                anywhere,
                whole((1, 2 * width)),
                anywhere,
                vec(width),
                vec(width),
                vec(width),
                anywhere,
                whole((1, ff)),
                anywhere,
                vec(width),
                vec(width),
                vec(width),
            ],
            out_specs=[rowwise(seq, width), rowwise(seq, width), rowwise(seq, 3 * width)]
            + [pl.BlockSpec((HEADS // 2, seq, 2 * seq), lambda i, s: (jnp.minimum(i, captions - 1), 0, 0))]
            + [rowwise(seq, width)]
            + [VMEM] * 9
            + [pl.BlockSpec((part, half), lambda i, s: (jnp.maximum(i - captions, 0), 0))] * 2,
            scratch_shapes=[
                pltpu.VMEM((slots, width), bf16),
                pltpu.VMEM((slots, 3 * width), bf16),
                pltpu.VMEM((rows, ff), bf16),
                pltpu.VMEM(w_qkv.shape, bf16),
                pltpu.VMEM(w_out.shape, bf16),
                pltpu.SemaphoreType.DMA((6,)),
            ],
        ),
        out_shape=[
            apart((rows, width), bf16),
            apart((rows, width), bf16),
            apart((rows, 3 * width), bf16),
            apart((captions * HEADS // 2, seq, 2 * seq), bf16),
            apart((rows, width), bf16),
            near((rows, width)),
            near((rows, 128)),
            near((rows, width), bf16),
            near((rows, ff), bf16),
            near((rows, width)),
            near((rows, width), bf16),
            near((8, width)),
            near(w_up.shape, bf16),
            near(w_down.shape, bf16),
            apart((ff, half), bf16),
            apart((ff, half), bf16),
        ],
        compiler_params=params(33),
        cost_estimate=cost(30),
        name="forward",
    )(
        scalars,
        far(text),
        far(text_low),
        arrived,
        *(
            far(v)
            for v in (
                source, out_grad, w_qkv, qv_bias, w_out, out_bias,
                attn_gain, attn_shift, w_up, up_bias, w_down, down_bias, ffn_gain, ffn_shift,
            )
        ),
    )


def ffn_backward(core, d_ffn, d_second, slope, attn_normed, attn_inv, w_down, w_up, attn_gain, seq, hold, first, size, begun):
    rows, width = d_ffn.shape
    ff = w_up.shape[1]
    parts = 4
    part = ff // parts

    def kernel(c_ref, df_ref, ds_ref, sl_ref, an_ref, ai_ref, wd, wu, ag_ref, *rest):
        dup_ref, dr_ref, da_ref, sums_ref, up_ref = rest[len(begun) + len(hold) :]
        step = pl.program_id(0)

        @pl.when(step == 0)
        def _():
            if begun:
                sums_ref[...] = rest[3][...]
                up_ref[...] = rest[4][...]
            else:
                sums_ref[...] = jnp.zeros_like(sums_ref)
                up_ref[...] = jnp.zeros_like(up_ref)

        here = pl.ds(pl.multiple_of((first + step) * seq, seq), seq)
        d_low = df_ref[here, :]
        for piece in range(parts):
            at = slice(piece * part, (piece + 1) * part)
            d_act = mm(d_low, wd[at, :], NT)
            low = (d_act * sl_ref[here, at].astype(f32)).astype(bf16)
            dup_ref[here, at] = low
            up_ref[0:1, at] += row_sum(low.astype(f32))
        d_hidden = ds_ref[here, :] + mm(dup_ref[here, :], wu[...], NT)
        normed = an_ref[here, :]
        resid = norm_back(d_hidden, normed, ai_ref[here, 0:1], ag_ref[...])
        dr_ref[here, :] = resid
        low = resid.astype(bf16)
        da_ref[here, :] = low
        sums_ref[0:1, :] += row_sum(d_hidden * normed)
        sums_ref[1:2, :] += row_sum(d_hidden)
        sums_ref[2:3, :] += row_sum(low.astype(f32))

    return pl.pallas_call(
        kernel,
        grid_spec=pltpu.PrefetchScalarGridSpec(
            num_scalar_prefetch=1,
            grid=(size,),
            in_specs=[VMEM] * 7
            + [vec(width)]
            + [VMEM] * len(begun)
            + [VMEM] * len(hold),
            out_specs=[VMEM] * 5,
        ),
        out_shape=[
            near((rows, ff), bf16),
            near((rows, width)),
            near((rows, width), bf16),
            near((8, width)),
            near((8, ff)),
        ],
        input_output_aliases={9: 0, 10: 1, 11: 2} if begun else {},
        compiler_params=params(6),
        cost_estimate=cost(4 * size),
        name="ffn_backward",
    )(core, d_ffn, d_second, slope, attn_normed, attn_inv, w_down, w_up, attn_gain, *begun, *hold)


def up_gradient(core, hidden_low, d_upper):
    rows, width = hidden_low.shape

    def kernel(c_ref, h_ref, d_ref, send_ref, keep_ref):
        step = pl.program_id(0)
        here = pl.ds(pl.multiple_of(step * width, width), width)
        for to_ref, side in ((send_ref, 1 - c_ref[0]), (keep_ref, c_ref[0])):
            cols = pl.ds(pl.multiple_of((2 * side + step) * width, width), width)
            to_ref[:, here] = mm(h_ref[...], d_ref[:, cols], TN).astype(bf16)

    return pl.pallas_call(
        kernel,
        grid_spec=pltpu.PrefetchScalarGridSpec(
            num_scalar_prefetch=1, grid=(2,), in_specs=[VMEM, VMEM], out_specs=[VMEM, VMEM]
        ),
        out_shape=[near((width, 2 * width), bf16)] * 2,
        compiler_params=params(6),
        cost_estimate=cost(0.1),
        name="up_gradient",
    )(core, hidden_low, d_upper)


def attention_backward(scalars, d_attn, d_resid, probs, qkv, source, w_out, w_qkv, dims, first_caption, size, begun):
    captions, images = dims
    rows, width = d_attn.shape
    seq = rows // captions
    slots = source.shape[1]
    regions = slots // images
    text_len = seq - regions
    last = first_caption + size == captions

    def kernel(
        sc_ref, da_ref, dr_ref, p_ref, qkv_ref, src_ref, wo_ref, wq, *rest,
    ):
        begun_refs = rest[: len(begun)]
        dqkv_ref, text_ref, back_ref, sums_ref, d_img, d_ctx_ref = rest[len(begun) :]
        step = pl.program_id(0)
        here = pl.ds(pl.multiple_of((first_caption + step) * seq, seq), seq)

        @pl.when(step == 0)
        def _():
            if begun:
                sums_ref[...] = begun_refs[3][...]
                d_img[...] = begun_refs[2][...]
            else:
                sums_ref[...] = jnp.zeros_like(sums_ref)
                d_img[...] = jnp.zeros_like(d_img)

        d_ctx_ref[...] = mm(da_ref[here, :], wo_ref[...], NT).astype(bf16)
        first = lax.broadcasted_iota(jnp.int32, (1, 2 * HEAD), 1) < HEAD
        masks = [jnp.where(first, 1.0, 0.0).astype(bf16), jnp.where(first, 0.0, 1.0).astype(bf16)]
        def pair_backward(pair, carry):
            def cols(base):
                return pl.ds(pl.multiple_of(base + pair * 2 * HEAD, 2 * HEAD), 2 * HEAD)

            q = qkv_ref[here, cols(0)]
            k = qkv_ref[here, cols(width)]
            v = qkv_ref[here, cols(2 * width)]
            d_c = d_ctx_ref[:, cols(0)]
            both_c = jnp.concatenate([d_c * masks[0], d_c * masks[1]], 0)
            both_q = jnp.concatenate([q * masks[0], q * masks[1]], 0)
            low = p_ref[pair]
            d_probs = mm(v, both_c, NT)
            wide = low.astype(f32)
            both = wide * d_probs
            inner = jnp.sum(both, 0, keepdims=True)
            d_scores = (both - wide * inner).astype(bf16)
            d_q = mm(d_scores, k, TN) * 0.125
            dqkv_ref[here, cols(0)] = jnp.where(first, d_q[:seq], d_q[seq:]).astype(bf16)
            dqkv_ref[here, cols(width)] = (mm(d_scores, both_q) * 0.125).astype(bf16)
            dqkv_ref[here, cols(2 * width)] = mm(low, both_c).astype(bf16)
            return carry

        lax.fori_loop(0, HEADS // 2, pair_backward, 0, unroll=3)

        sums_ref[0:1, :] += row_sum(dqkv_ref[here, :width].astype(f32))
        sums_ref[1:2, :] += row_sum(dqkv_ref[here, 2 * width :].astype(f32))
        d_x = mm(dqkv_ref[here, :], wq[...], NT) + dr_ref[here, :]
        text_ref[...] = d_x[:text_len]
        at = pl.ds(pl.multiple_of(sc_ref[8 + first_caption + step] * regions, regions), regions)
        d_img[at, :] += d_x[text_len:]

        @pl.when(step == size - 1)
        def _():
            if last:
                back_ref[...] = mm(one_hot(src_ref[...], slots), d_img[...].astype(bf16)).astype(bf16)
            else:
                back_ref[...] = d_img[...]

    return pl.pallas_call(
        kernel,
        grid_spec=pltpu.PrefetchScalarGridSpec(
            num_scalar_prefetch=1,
            grid=(size,),
            in_specs=[VMEM] * 2
            + [pl.BlockSpec((HEADS // 2, seq, 2 * seq), lambda i, s: (i + first_caption, 0, 0)), VMEM]
            + [whole((1, slots)), VMEM, VMEM]
            + ([VMEM, pl.BlockSpec(memory_space=pl.ANY)] + [VMEM, VMEM] if begun else []),
            out_specs=[
                VMEM,
                pl.BlockSpec((text_len, width), lambda i, s: (i + first_caption, 0)),
                VMEM,
                VMEM,
            ],
            scratch_shapes=[
                pltpu.VMEM((slots, width), f32),
                pltpu.VMEM((seq, width), bf16),
            ],
        ),
        out_shape=[
            near((rows, 3 * width), bf16),
            pltpu.HBM((captions * text_len, width), f32),
            near((slots, width), bf16 if last else f32),
            near((8, width)),
        ],
        input_output_aliases={8: 0, 9: 1} if begun else {},
        compiler_params=params(15),
        cost_estimate=cost(5 * size),
        name="attention_backward",
    )(scalars, d_attn, d_resid, far(probs), qkv, source, w_out, w_qkv, *begun)


def qkvo_gradient(core, x, d_qkv, context, d_attn):
    rows, width = x.shape

    def kernel(c_ref, x_ref, dq_ref, ctx_ref, da_ref, send_ref, keep_ref):
        step = pl.program_id(0)

        def store(low_block, high_block):
            low, high = low_block.astype(bf16), high_block.astype(bf16)

            @pl.when(c_ref[0] == 0)
            def _():
                keep_ref[...] = low
                send_ref[...] = high

            @pl.when(c_ref[0] != 0)
            def _():
                send_ref[...] = low
                keep_ref[...] = high

        @pl.when(step == 0)
        def _():
            store(mm(x_ref[...], dq_ref[:, :width], TN), mm(x_ref[...], dq_ref[:, 2 * width :], TN))

        @pl.when(step == 1)
        def _():
            store(mm(x_ref[...], dq_ref[:, width : 2 * width], TN), mm(ctx_ref[...], da_ref[...], TN))

    out = pl.BlockSpec((width, width), lambda i, s: (0, i))
    return pl.pallas_call(
        kernel,
        grid_spec=pltpu.PrefetchScalarGridSpec(
            num_scalar_prefetch=1, grid=(2,), in_specs=[VMEM] * 4, out_specs=[out, out]
        ),
        out_shape=[apart((width, 2 * width), bf16)] * 2,
        compiler_params=params(14),
        cost_estimate=cost(5),
        name="qkvo_gradient",
    )(core, x, d_qkv, context, d_attn)


def region_norm_backward(
    core, returned, target, normed, inv, gain, boxes, w_box_t, sums_forward, sums_ffn, sums_up, sums_attn, groups
):
    rows, width = returned.shape
    half = width // 2
    box = boxes.shape[0]
    share = width // groups
    ff_share = sums_up.shape[1] // groups

    def kernel(
        c_ref, r_ref, t_ref, n_ref, i_ref, g_ref, box_ref, wb_ref, sf_ref, sn_ref, su_ref, sa_ref,
        all_ref, send_ref, keep_ref, small_ref, bg_ref, small,
    ):
        d_region = mm(one_hot(t_ref[...], rows), r_ref[...], TN)
        normed = n_ref[...]
        low = norm_back(d_region, normed, i_ref[:, 0:1], g_ref[...]).astype(bf16)
        all_ref[...] = low
        mine = c_ref[0] == 0
        send_ref[:rows, :] = jnp.where(mine, low[:, half:], low[:, :half])
        keep_ref[...] = jnp.where(mine, low[:, :half], low[:, half:])
        bg_ref[...] = mm(wb_ref[...], low, NT)
        boxes_grad = mm(box_ref[...], low)
        vectors = [
            row_sum(low.astype(f32)),
            row_sum(d_region * normed),
            row_sum(d_region),
            sf_ref[0:1, :],
            sf_ref[1:2, :],
            sf_ref[2:3, :],
            sn_ref[0:1, :],
            sn_ref[1:2, :],
            sn_ref[2:3, :],
        ] + [boxes_grad[at : at + 1] for at in range(box)]
        small[...] = jnp.zeros_like(small)
        lane = lax.broadcasted_iota(jnp.int32, (1, half), 1)
        stats = jnp.zeros((1, half), f32)
        for at in range(4):
            total = jnp.sum(sf_ref[3 + at : 4 + at, :], 1, keepdims=True)
            stats = jnp.where(lane == at, total, stats)
        flat = jnp.concatenate([sa_ref[0:1, :], sa_ref[1:2, :]], 1)
        for group in range(groups):
            small[group, 0:1, 0:ff_share] = su_ref[0:1, group * ff_share : (group + 1) * ff_share]
            small[group, 1:2, 0 : 2 * share] = flat[:, group * 2 * share : (group + 1) * 2 * share]
            for at, value in enumerate(vectors):
                row, col = (1, 2) if at == 0 else (2 + (at - 1) // 3, (at - 1) % 3)
                small[group, row : row + 1, 128 * col : 128 * col + share] = value[
                    :, group * share : (group + 1) * share
                ]
            small[group, 6:7, :] = stats
        small_ref[...] = small[...].astype(bf16)
        for group in range(groups):
            send_ref[rows + 8 * group : rows + 8 * (group + 1), :] = small_ref[group]

    sizes = (sums_forward, sums_ffn, sums_up, sums_attn)
    return pl.pallas_call(
        kernel,
        grid_spec=pltpu.PrefetchScalarGridSpec(
            num_scalar_prefetch=1,
            grid=(1,),
            in_specs=[
                whole((rows, width)),
                whole((1, rows)),
                whole((rows, width)),
                whole((rows, 128)),
                vec(width),
                whole(boxes.shape),
                whole(w_box_t.shape),
            ]
            + [whole(v.shape) for v in sizes],
            out_specs=[VMEM] * 4 + [whole((box, rows))],
            scratch_shapes=[pltpu.VMEM((groups, 8, half), f32)],
        ),
        out_shape=[
            near((rows, width), bf16),
            near((rows + 8 * groups, half), bf16),
            near((rows, half), bf16),
            near((groups, 8, half), bf16),
            shape((box, rows)),
        ],
        compiler_params=params(14),
        cost_estimate=cost(0.1),
        name="region_norm_backward",
    )(core, returned, far(target), far(normed), far(inv), far(gain), far(boxes), far(w_box_t), *sizes)


def visual_gradient(bits, features, other_features, d_pre, other_d_pre, small, groups):
    rows, feat = features.shape
    half = d_pre.shape[1]
    steps = 2
    part = feat // steps
    quarter = feat // groups // 4
    tall = quarter + 8
    per_step = groups // steps
    high = groups // 2

    def kernel(b_ref, f_ref, o_ref, d_ref, p_ref, s_ref, a_send, a_keep, b_send, b_keep, got):
        step = pl.program_id(0)
        bit2, bit4 = b_ref[1], b_ref[2]
        got[...] = mm(f_ref[...], d_ref[...], TN) + mm(o_ref[...], p_ref[:rows, :], TN)

        def fill(to_ref, at, which, group, x, piece):
            here = pl.ds(pl.multiple_of(((group * 2 + x) * 2 + piece) * quarter, 8), quarter)
            to_ref[at, which, :quarter, :] = got[here, :].astype(bf16)
            number = step * per_step + group
            other = p_ref[pl.ds(pl.multiple_of(rows + 8 * number, 8), 8), :]
            to_ref[at, which, quarter:, :] = add(s_ref[number], other)

        for group in range(per_step):
            y = group % 2
            at = step * (per_step // 2) + group // 2
            fill(a_send, at, y, group, 1 - bit2, 0)
            fill(a_keep, at, y, group, bit2, 0)

            @pl.when(bit4 == y)
            def _():
                for x in range(2):
                    fill(b_keep, at, x, group, x, 1)

            @pl.when(bit4 != y)
            def _():
                for x in range(2):
                    fill(b_send, at, x, group, x, 1)

    return pl.pallas_call(
        kernel,
        grid_spec=pltpu.PrefetchScalarGridSpec(
            num_scalar_prefetch=1,
            grid=(steps,),
            in_specs=[
                pl.BlockSpec((rows, part), lambda i, s: (0, i)),
                pl.BlockSpec((rows, part), lambda i, s: (0, i)),
                VMEM,
                VMEM,
                VMEM,
            ],
            out_specs=[VMEM] * 4,
            scratch_shapes=[pltpu.VMEM((part, half), f32)],
        ),
        out_shape=[near((high, 2, tall, half), bf16)] * 4,
        compiler_params=params(14),
        cost_estimate=cost(0.1),
        name="visual_gradient",
    )(bits, far(features), far(other_features), d_pre, other_d_pre, small)


def feature_gradient(bits, d_pre, w_visual):
    rows, width = d_pre.shape
    feat = w_visual.shape[0]
    steps = 4
    part = feat // steps

    def kernel(b_ref, d_ref, w_ref, o_ref):
        o_ref[...] = mm(d_ref[...], w_ref[...], NT)

    return pl.pallas_call(
        kernel,
        grid_spec=pltpu.PrefetchScalarGridSpec(
            num_scalar_prefetch=1,
            grid=(steps,),
            in_specs=[VMEM, pl.BlockSpec((part, width), lambda i, s: (i, 0))],
            out_specs=pl.BlockSpec((rows, part), lambda i, s: (0, i)),
        ),
        out_shape=shape((rows, feat)),
        compiler_params=params(8),
        cost_estimate=cost(10),
        name="feature_gradient",
    )(bits, d_pre, far(w_visual))


def device_number():
    return lax.axis_index("dp") * lax.axis_size("enc") + lax.axis_index("enc")


def swap(values, bit):
    count = lax.axis_size("dp") * lax.axis_size("enc")
    return lax.ppermute(values, ("dp", "enc"), [(i, i ^ bit) for i in range(count)])


def add(a, b):
    return (a.astype(f32) + b.astype(f32)).astype(bf16)


def scalar_call(kernel, bits, ins, in_specs, outs, out_specs, grid, limit, name, last=False, place=near):
    outs = outs if last else [place(o.shape, o.dtype) for o in outs]
    return pl.pallas_call(
        kernel,
        grid_spec=pltpu.PrefetchScalarGridSpec(
            num_scalar_prefetch=1, grid=(grid,), in_specs=in_specs, out_specs=out_specs
        ),
        out_shape=outs,
        compiler_params=params(limit),
        cost_estimate=cost(1),
        name=name,
    )(bits, *ins)


def first_split(bits, kept, got, groups, place=near):
    tall = kept.ndim == 5
    high = groups // 2
    if tall:
        rows, cols = kept.shape[3:]
        view = (high, 2, 2, 2, rows, cols)
        block = (1, 2, 2, 2, rows, cols)
    else:
        rows, cols = kept.shape[0] // groups, kept.shape[1] // 4
        view = (high, 2, rows, 4 * cols)
        block = (1, 2, rows, 4 * cols)

    def kernel(b_ref, k_ref, r_ref, a_send, a_keep, b_send, b_keep):
        bit2, bit4 = b_ref[1], b_ref[2]

        def total(y, x, piece):
            if tall:
                return add(k_ref[0, y, x, piece], r_ref[0, y, x, piece])
            at = pl.ds(pl.multiple_of((2 * x + piece) * cols, 128), cols)
            return add(k_ref[0, y, :, at], r_ref[0, y, :, at])

        for other in range(2):
            a_send[0, other] = total(other, 1 - bit2, 0)
            a_keep[0, other] = total(other, bit2, 0)
            b_send[0, other] = total(1 - bit4, other, 1)
            b_keep[0, other] = total(bit4, other, 1)

    spec = pl.BlockSpec(block, lambda i, s: (i,) + (0,) * (len(block) - 1))
    out = pl.BlockSpec((1, 2, rows, cols), lambda i, s: (i, 0, 0, 0))
    return scalar_call(
        kernel, bits, (kept.reshape(view), got.reshape(view)), [spec, spec],
        [shape((high, 2, rows, cols), bf16)] * 4, [out] * 4, high, 6, "first_split", place=place,
    )


def second_split(bits, a_kept, a_got, b_kept, b_got):
    high, _, rows, cols = a_kept.shape

    def kernel(b_ref, ak, ar, bk, br, a_send, a_keep, b_send, b_keep):
        bit2, bit4 = b_ref[1], b_ref[2]
        a_send[0] = add(ak[0, 1 - bit4], ar[0, 1 - bit4])
        a_keep[0] = add(ak[0, bit4], ar[0, bit4])
        b_send[0] = add(bk[0, 1 - bit2], br[0, 1 - bit2])
        b_keep[0] = add(bk[0, bit2], br[0, bit2])

    spec = pl.BlockSpec((1, 2, rows, cols), lambda i, s: (i, 0, 0, 0))
    out = pl.BlockSpec((1, rows, cols), lambda i, s: (i, 0, 0))
    return scalar_call(
        kernel, bits, (a_kept, a_got, b_kept, b_got), [spec] * 4,
        [shape((high, rows, cols), bf16)] * 4, [out] * 4, high, 6, "second_split",
    )


def join_split(bits, pairs, place=near):
    high, _, cols = pairs[0][0].shape
    sizes = [kept.shape[1] for kept, _ in pairs]

    def kernel(b_ref, *refs):
        bit = b_ref[3]
        send, keep = refs[-2:]
        at = 0
        for n, size in enumerate(sizes):
            kept, got = refs[2 * n : 2 * n + 2]
            send[0, at : at + size] = add(kept[1 - bit], got[1 - bit])
            keep[0, at : at + size] = add(kept[bit], got[bit])
            at += size

    ins = [value for pair in pairs for value in pair]
    specs = [pl.BlockSpec((2, v.shape[1], cols), lambda i, s: (i, 0, 0)) for v in ins]
    out = pl.BlockSpec((1, sum(sizes), cols), lambda i, s: (i, 0, 0))
    return scalar_call(
        kernel, bits, ins, specs, [shape((high // 2, sum(sizes), cols), bf16)] * 2, [out] * 2,
        high // 2, 6, "join_split", place=place,
    )


def late_split(bits, kept, got, which):
    high, rows, cols = kept.shape

    def kernel(b_ref, k_ref, r_ref, send, keep):
        bit = b_ref[which]
        send[0] = add(k_ref[1 - bit], r_ref[1 - bit])
        keep[0] = add(k_ref[bit], r_ref[bit])

    spec = pl.BlockSpec((2, rows, cols), lambda i, s: (i, 0, 0))
    out = pl.BlockSpec((1, rows, cols), lambda i, s: (i, 0, 0))
    return scalar_call(
        kernel, bits, (kept, got), [spec] * 2, [shape((high // 2, rows, cols), bf16)] * 2, [out] * 2,
        high // 2, 6, "late_split",
    )


def over_two(halves):
    return swap(halves[0], 2), halves[1], swap(halves[2], 4), halves[3]


def over_other_two(halves):
    return swap(halves[0], 4), halves[1], swap(halves[2], 2), halves[3]


def second(bits, moved):
    return second_split(bits, moved[1], moved[0], moved[3], moved[2])


def join(bits, *moved, place=near):
    pairs = []
    for one in moved:
        pairs += [(one[1], one[0]), (one[3], one[2])]
    return join_split(bits, pairs, place)


def after_all(*trees):
    leaves, tree = jax.tree.flatten(trees)
    return jax.tree.unflatten(tree, lax.optimization_barrier(leaves))


def late_first(bits, kept, got):
    if kept.shape[0] == 1:
        return (kept + got,)
    return late_split(bits, kept, got, 4)


def late_move(halves):
    return swap(halves[0], 16) if len(halves) > 1 else None


def late_rest(bits, halves, moved):
    bit, which = 16, 5
    while len(halves) > 1:
        if halves[1].shape[0] == 1:
            halves = (halves[1] + moved,)
        else:
            halves = late_split(bits, halves[1], moved, which)
            bit, which = 2 * bit, which + 1
            moved = swap(halves[0], bit)
    return halves[0][0]


def spread(mine, *late):
    over_x = swap(mine, 2)
    over_core = swap(mine, 1)
    return mine, over_x, over_core, swap(gate(over_x, *late), 1)


def pick(b_ref, pieces, core, x):
    mine, over_x, over_core, over_both = pieces
    same_x = b_ref[1] == x
    return jnp.where(
        b_ref[0] == core, jnp.where(same_x, mine, over_x), jnp.where(same_x, over_core, over_both)
    ).astype(f32)


def finish_ffn(bits, pieces):
    rows, cols = pieces[0].shape
    half = rows // 2
    part = rows // 4

    def kernel(b_ref, p0, p1, p2, p3, down_ref, up_ref):
        for core in range(2):
            for x in range(2):
                got = pick(b_ref, (p0[...], p1[...], p2[...], p3[...]), core, x)
                down_ref[x * half : (x + 1) * half, core * cols : (core + 1) * cols] = got[:half]
                for piece in range(2):
                    at = ((core * 2 + x) * 2 + piece) * cols
                    up_ref[:, at : at + cols] = got[half + piece * part : half + (piece + 1) * part]

    outs = [shape((rows, 2 * cols)), shape((part, 8 * cols))]
    return scalar_call(
        kernel, bits, pieces, [whole((rows, cols))] * 4, outs, [whole(o.shape) for o in outs], 1, 12, "finish_ffn", True
    )


def finish_wide(bits, pieces, sizes):
    rows, cols = pieces[0].shape
    part = rows // 2

    def kernel(b_ref, p0, p1, p2, p3, *out_refs):
        for core in range(2):
            for x in range(2):
                got = pick(b_ref, (p0[...], p1[...], p2[...], p3[...]), core, x)
                for piece in range(2):
                    at = ((core * 2 + x) * 2 + piece) * cols
                    for out_ref, size in zip(out_refs, sizes):
                        if 0 <= at < size:
                            out_ref[:, at : at + cols] = got[piece * part : (piece + 1) * part]
                        at -= size

    outs = [shape((part, size)) for size in sizes]
    return scalar_call(
        kernel, bits, pieces, [whole((rows, cols))] * 4, outs, [whole(o.shape) for o in outs], 1, 8, "finish_wide", True
    )


def finish_visual(bits, pieces, ff_share, share, box):
    rows, cols = pieces[0].shape
    tall = rows // 2
    quarter = tall - 8
    sizes = [share] * 9 + [2 * share, ff_share]

    def kernel(b_ref, p0, p1, p2, p3, vis_ref, box_ref, rms_ref, *small_refs):
        for core in range(2):
            for x in range(2):
                got = pick(b_ref, (p0[...], p1[...], p2[...], p3[...]), core, x)
                for piece in range(2):
                    low = piece * tall
                    vis_ref[(2 * x + piece) * quarter : (2 * x + piece + 1) * quarter, core * cols : (core + 1) * cols] = got[
                        low : low + quarter
                    ]
        small = p0[quarter : quarter + 8, :].astype(f32)
        for at in range(9):
            row, col = (1, 2) if at == 0 else (2 + (at - 1) // 3, (at - 1) % 3)
            small_refs[at][...] = small[row, 128 * col : 128 * col + share]
        small_refs[9][...] = small[1, 0 : 2 * share]
        small_refs[10][...] = small[0, 0:ff_share]
        for at in range(9, 9 + box):
            row, col = 2 + (at - 1) // 3, (at - 1) % 3
            box_ref[at - 9 : at - 8, :] = small[row : row + 1, 128 * col : 128 * col + share]
        stats = small[6, 0:128]
        total = jnp.sum(small[6:7, 3:4])
        rms_ref[...] = jnp.sqrt(stats / total)[:3]

    outs = [shape((4 * quarter, 2 * cols)), shape((box, share)), shape((3,))] + [shape((size,)) for size in sizes]
    specs = [whole(o.shape) for o in outs[:2]] + [vec(3)] + [vec(size) for size in sizes]
    return scalar_call(
        kernel, bits, pieces, [whole((rows, cols))] * 4, outs, specs, 1, 8, "finish_visual", True
    )


def gate(value, *others):
    return lax.optimization_barrier((value, *others))[0]


def on_device(
    text_embed,
    region_features,
    boxes,
    caption_image,
    caption_lengths,
    region_counts,
    region_target,
    region_source,
    w_visual,
    w_box,
    visual_bias,
    visual_gain,
    visual_shift,
    w_qkv,
    qv_bias,
    w_out,
    out_bias,
    attn_gain,
    attn_shift,
    w_up,
    up_bias,
    w_down,
    down_bias,
    ffn_gain,
    ffn_shift,
    out_grad,
):
    width = text_embed.shape[1]
    captions = caption_image.shape[0]
    images = region_counts.shape[0]
    dims = (captions, images)
    axes = ("dp", "enc")
    groups = lax.axis_size("dp")
    count = groups * lax.axis_size("enc")
    me = device_number().astype(jnp.int32)
    places = lax.iota(jnp.int32, 8)
    scalars = jnp.concatenate([(me >> places) & 1, caption_image, caption_lengths, region_counts])
    w_box_t = w_box.T
    row = lambda v: v.reshape(1, -1)
    qv_row = row(qv_bias)

    message, vis_normed, vis_inv = region_forward(
        region_features, boxes, region_target, w_visual, w_box_t, visual_bias, visual_gain, visual_shift
    )
    arrived = lax.all_to_all(message, axes, split_axis=0, concat_axis=0, tiled=True)
    text_low = text_qkv(text_embed, w_qkv, qv_row)
    (
        out_rows, x, qkv, probs, context, attn_normed, attn_inv, hidden_low, slope, d_second, d_ffn,
        sums_forward, w_up_near, w_down_near, down_sent, down_kept,
    ) = forward(
        scalars, text_embed, text_low, arrived, region_source, out_grad, w_qkv, qv_row, w_out,
        out_bias, attn_gain, attn_shift, w_up, row(up_bias), w_down, down_bias, ffn_gain, ffn_shift, dims,
    )
    seq = x.shape[0] // captions
    rest = captions - 1
    bits = core = scalars
    hold = ()
    ffn_ins = (d_ffn, d_second, slope, attn_normed, attn_inv, w_down_near, w_up_near, attn_gain, seq, hold)
    down_view = (groups, 2, 2, w_down.shape[0] // groups // 4, width // 2)
    down_sent, down_kept = down_sent.reshape(down_view), down_kept.reshape(down_view)

    moved = swap(down_sent, 1)
    begun = ffn_backward(core, *ffn_ins, 0, 1, ())

    moved, begun, sc = after_all(moved, begun, scalars)
    down = first_split(sc, down_kept, moved, groups)
    down, begun, sc = after_all(down, begun, sc)
    moved = over_two(down)
    d_upper, d_resid, d_attn, sums_ffn, sums_up = ffn_backward(sc, *ffn_ins, 1, rest, tuple(begun))
    up_sent, up_kept = up_gradient(sc, hidden_low, gate(d_upper, d_attn))

    moved, up_sent, up_kept, d_attn, sc = after_all(moved, up_sent, up_kept, d_attn, sc)
    down = second(sc, moved)
    down, up_sent, up_kept, sc = after_all(down, up_sent, up_kept, sc)
    moved = over_other_two(down), swap(up_sent, 1)
    att_ins = (d_attn, d_resid, probs, qkv, region_source, w_out, w_qkv, dims)
    begun = attention_backward(sc, *att_ins, 0, 1, ())

    moved, up_kept, begun, sc = after_all(moved, up_kept, begun, sc)
    down = moved[0]
    up = first_split(sc, up_kept, moved[1], groups)
    down, up, begun, sc = after_all(down, up, begun, sc)
    moved = over_two(up)
    d_qkv, text_grad, back_message, sums_attn = attention_backward(sc, *att_ins, 1, rest, tuple(begun))

    moved, down, d_qkv, back_message, sc = after_all(moved, down, d_qkv, back_message, sc)
    up = second(sc, moved)
    up, down, sc = after_all(up, down, sc)
    moved = over_other_two(up)
    qkvo_sent, qkvo_kept = qkvo_gradient(sc, x, d_qkv, context, d_attn)

    moved, down, qkvo_sent, qkvo_kept, back_message, sc = after_all(
        moved, down, qkvo_sent, qkvo_kept, back_message, sc
    )
    ffn = join(sc, down, moved, place=apart)
    ffn, qkvo_sent, qkvo_kept, back_message, sc = after_all(ffn, qkvo_sent, qkvo_kept, back_message, sc)
    returned = lax.all_to_all(back_message, axes, split_axis=0, concat_axis=0, tiled=True)
    other_features = swap(gate(region_features, qkvo_kept), 1)
    qkvo = first_split(sc, qkvo_kept, swap(qkvo_sent, 1), groups, apart)
    qkvo_moved = over_two(qkvo)
    ffn_moved = swap(gate(ffn[0], *qkvo), 8)
    returned, sc = after_all(returned, gate(sc, *qkvo))
    d_pre, d_pre_sent, d_pre_kept, small, box_grad = region_norm_backward(
        sc, returned, region_target, vis_normed, vis_inv, visual_gain, boxes, w_box_t,
        sums_forward, sums_ffn, sums_up, sums_attn, groups,
    )
    vis = visual_gradient(
        sc, region_features, other_features, d_pre_kept, swap(d_pre_sent, 1), small, groups
    )
    vis_moved = over_two(vis)
    sc = gate(sc, *vis)
    qkvo = second(sc, qkvo_moved)
    qkvo_moved = over_other_two(qkvo)
    ffn = late_first(gate(sc, *qkvo), ffn[1], ffn_moved)
    ffn_moved = late_move(ffn)
    feature_grad = feature_gradient(gate(sc, *ffn), d_pre, w_visual)

    sc = gate(sc, feature_grad)
    vis = second(sc, vis_moved)
    vis_moved = over_other_two(vis)
    sc = gate(sc, *vis)
    qkvo = join(sc, qkvo_moved)
    qkvo_moved = swap(qkvo[0], 8)
    ffn = late_rest(sc, ffn, gate(ffn_moved, *qkvo))

    vis = join(gate(sc, *qkvo, ffn), vis_moved)
    vis_moved = swap(vis[0], 8)
    sc = gate(sc, *vis)
    qkvo = late_first(sc, qkvo[1], qkvo_moved)
    qkvo_moved = late_move(qkvo)

    vis = late_first(gate(sc, *qkvo), vis[1], vis_moved)
    vis_moved = late_move(vis)
    ffn = spread(ffn, *vis)
    sc = gate(sc, *vis)
    g_down, g_up = finish_ffn(sc, ffn)
    qkvo = late_rest(sc, qkvo, gate(qkvo_moved, *vis))

    vis = late_rest(sc, vis, gate(vis_moved, g_up, qkvo))
    qkvo = spread(qkvo, vis)
    g_qkv, g_out = finish_wide(gate(sc, vis), qkvo, (3 * width, width))
    vis = spread(vis, g_qkv)
    g_visual, g_box_t, rms_values, *small = finish_visual(
        sc, vis, w_up.shape[1] // groups, width // groups, boxes.shape[0]
    )
    return (
        out_rows,
        text_grad,
        feature_grad,
        box_grad,
        rms_values,
        g_visual,
        g_box_t.T,
        small[0],
        small[1],
        small[2],
        g_qkv,
        small[9],
        g_out,
        small[8],
        small[6],
        small[7],
        g_up,
        small[10],
        g_down,
        small[5],
        small[3],
        small[4],
    )


def solution(mesh):
    return jax.shard_map(
        on_device,
        mesh=mesh,
        in_specs=(
            P(("dp", "enc"), None),
            P(("dp", "enc"), None),
            P(None, ("dp", "enc")),
            P(("dp", "enc")),
            P(("dp", "enc")),
            P(("dp", "enc")),
            P(("dp", "enc"), None),
            P(("dp", "enc"), None),
            P(),
            P(),
            P(),
            P(),
            P(),
            P(),
            P(),
            P(),
            P(),
            P(),
            P(),
            P(),
            P(),
            P(),
            P(),
            P(),
            P(),
            P(("dp", "enc"), None),
        ),
        out_specs=(
            P(("dp", "enc"), None),
            P(("dp", "enc"), None),
            P(("dp", "enc"), None),
            P(None, ("dp", "enc")),
            P(),
            P("dp", None),
            P("dp", None),
            P("dp"),
            P("dp"),
            P("dp"),
            P("dp", None),
            P("dp"),
            P("dp", None),
            P("dp"),
            P("dp"),
            P("dp"),
            P("dp", None),
            P("dp"),
            P("dp", None),
            P("dp"),
            P("dp"),
            P("dp"),
        ),
        check_vma=False,
    )
```

```python
import jax
import jax.numpy as jnp
from jax import lax
from jax.experimental import pallas as pl
from jax.experimental.pallas import tpu as pltpu
from jax.sharding import PartitionSpec as P

HEADS = 12
UNROLL = 2
HEAD = 64
epsilon = 1e-12
inv_sqrt_two = 0.7071067811865476
inv_sqrt_tau = 0.3989422804014327
f32 = jnp.float32
bf16 = jnp.bfloat16
NN = (((1,), (0,)), ((), ()))
NT = (((1,), (1,)), ((), ()))
TN = (((0,), (0,)), ((), ()))


def mm(a, b, dims=NN):
    return lax.dot_general(a, b, dims, preferred_element_type=f32)


def cost(us):
    return pl.CostEstimate(flops=int(us * 1e9), bytes_accessed=1 << 20, transcendentals=0)


def params(limit=56):
    return pltpu.CompilerParams(
        dimension_semantics=("arbitrary",), vmem_limit_bytes=limit << 20
    )


def whole(shape):
    return pl.BlockSpec(shape, lambda i, *s: (0,) * len(shape), pipeline_mode=pl.Buffered(1))


def vec(size):
    return pl.BlockSpec((size,), lambda i, *s: (0,))


VMEM = pl.BlockSpec(memory_space=pltpu.VMEM)


def far(value):
    return pltpu.with_memory_space_constraint(value, pltpu.HBM)


def apart(dims, kind=f32):
    return pltpu.HBM(dims, kind)


def near(dims, kind=f32):
    return pltpu.VMEM(dims, kind)


def shape(dims, kind=f32):
    return jax.ShapeDtypeStruct(dims, kind)


def norm_parts(values):
    centre = values - jnp.mean(values, -1, keepdims=True)
    inv_std = lax.rsqrt(jnp.mean(centre * centre, -1, keepdims=True) + epsilon)
    return centre * inv_std, inv_std


def norm_back(grad, normed, inv_std, gain):
    scaled = grad * gain
    return inv_std * (
        scaled
        - jnp.mean(scaled, -1, keepdims=True)
        - normed * jnp.mean(scaled * normed, -1, keepdims=True)
    )


def row_sum(values):
    return jnp.sum(values, 0, keepdims=True)


def one_hot(index_row, count):
    rows = lax.broadcasted_iota(jnp.int32, (count, index_row.shape[1]), 0)
    return jnp.where(rows == index_row, 1.0, 0.0).astype(bf16)


def region_forward(features, boxes, target, w_visual, w_box_t, bias, gain, shift):
    rows, feat = features.shape
    width = w_visual.shape[1]
    steps = 2
    part = feat // steps

    def kernel(f_ref, box_ref, t_ref, wv_ref, wb_ref, b_ref, g_ref, s_ref, m_ref, n_ref, i_ref, acc):
        step = pl.program_id(0)
        partial = mm(f_ref[...], wv_ref[...])

        @pl.when(step == 0)
        def _():
            acc[...] = partial + (mm(box_ref[...], wb_ref[...], TN) + b_ref[...])

        @pl.when(step > 0)
        def _():
            acc[...] += partial

        @pl.when(step == steps - 1)
        def _():
            normed, inv = norm_parts(acc[...])
            n_ref[...] = normed
            i_ref[...] = jnp.broadcast_to(inv, i_ref.shape)
            low = (normed * g_ref[...] + s_ref[...]).astype(bf16)
            m_ref[...] = mm(one_hot(t_ref[...], rows), low).astype(bf16)

    return pl.pallas_call(
        kernel,
        grid=(steps,),
        in_specs=[
            pl.BlockSpec((rows, part), lambda i: (0, i)),
            whole(boxes.shape),
            whole((1, rows)),
            pl.BlockSpec((part, width), lambda i: (i, 0)),
            whole(w_box_t.shape),
            vec(width),
            vec(width),
            vec(width),
        ],
        out_specs=[VMEM, whole((rows, width)), whole((rows, 128))],
        out_shape=[near((rows, width), bf16), apart((rows, width)), apart((rows, 128))],
        scratch_shapes=[pltpu.VMEM((rows, width), f32)],
        compiler_params=params(24),
        cost_estimate=cost(3),
        name="region_forward",
    )(far(features), far(boxes), far(target), far(w_visual), far(w_box_t), far(bias), far(gain), far(shift))


def text_qkv(text, w_qkv, qv_bias):
    rows, width = text.shape

    def kernel(t_ref, w_ref, b_ref, o_ref):
        step = pl.program_id(0)
        bias = b_ref[...] * jnp.where(step == 1, 0.0, 1.0)
        o_ref[...] = (mm(t_ref[...], w_ref[...]) + bias).astype(bf16)

    return pl.pallas_call(
        kernel,
        grid=(3,),
        in_specs=[
            whole((rows, width)),
            pl.BlockSpec((width, width), lambda i: (0, i)),
            pl.BlockSpec((1, width), lambda i: (0, i // 2)),
        ],
        out_specs=pl.BlockSpec((rows, width), lambda i: (0, i)),
        out_shape=apart((rows, 3 * width), bf16),
        compiler_params=params(12),
        cost_estimate=cost(3),
        name="text_qkv",
    )(far(text), far(w_qkv), qv_bias)


def forward(
    scalars, text, text_low, arrived, source, out_grad, w_qkv, qv_bias, w_out, out_bias,
    attn_gain, attn_shift, w_up, up_bias, w_down, down_bias, ffn_gain, ffn_shift, dims,
):
    captions, images = dims
    width = text.shape[1]
    text_len = text.shape[0] // captions
    slots = arrived.shape[0]
    regions = slots // images
    seq = text_len + regions
    rows = captions * seq
    ff = w_up.shape[1]
    half = width // 2
    parts = 4
    part = ff // parts
    grid = captions + parts

    def kernel(
        sc_ref, t_ref, tq_ref, a_ref, src_ref, og_ref, wq_far, qvb_ref, wo_far, ob_ref, ag_ref, as_ref,
        wu_far, ub_ref, wd_far, db_ref, fg_ref, fs_ref,
        out_ref, x_ref, qkv_ref, probs_ref, ctx_ref, an_ref, ai_ref, hid_ref, slope_ref, ds_ref, df_ref,
        sums_ref, wu, wd, send_ref, keep_ref,
        regs, rqkv, act_all, wq, wo, sems,
    ):
        step = pl.program_id(0)

        def third(at):
            cols = slice(at * width, (at + 1) * width)
            return pltpu.make_async_copy(wq_far.at[:, cols], wq.at[:, cols], sems.at[at])

        def load(at):
            source, target = ((wo_far, wo), (wu_far, wu), (wd_far, wd))[at]
            return pltpu.make_async_copy(source, target, sems.at[3 + at])

        @pl.when(step == 0)
        def _():
            for at in range(3):
                third(at).start()
            load(0).start()
            sums_ref[...] = jnp.zeros_like(sums_ref)
            local = mm(one_hot(src_ref[...], slots), a_ref[...], TN).astype(bf16)
            regs[...] = local
            for part_id in range(3):
                at = slice(part_id * width, (part_id + 1) * width)
                third(part_id).wait()
                if part_id == 2:
                    load(1).start()
                    load(2).start()
                got = mm(local, wq[:, at])
                if part_id == 0:
                    got = got + qvb_ref[:, :width]
                if part_id == 2:
                    got = got + qvb_ref[:, width:]
                rqkv[:, at] = got.astype(bf16)

        @pl.when(step < captions)
        def _():
            image = sc_ref[8 + step]
            length = sc_ref[8 + captions + step]
            count = sc_ref[8 + 2 * captions + image]
            at = pl.ds(pl.multiple_of(image * regions, regions), regions)
            here = pl.ds(pl.multiple_of(step * seq, seq), seq)
            x_ref[:text_len, :] = t_ref[...]
            x_ref[text_len:, :] = regs[at, :]
            qkv_ref[:text_len, :] = tq_ref[...]
            qkv_ref[text_len:, :] = rqkv[at, :]
            place = lax.broadcasted_iota(jnp.int32, (seq, 1), 0)
            row_end = jnp.where(place < text_len, length, text_len + count)
            row_mask = jnp.where(place < row_end, 1.0, 0.0)
            key_mask = jnp.broadcast_to(row_mask, (seq, 2 * seq)) > 0.5
            first = lax.broadcasted_iota(jnp.int32, (1, 2 * HEAD), 1) < HEAD
            scale = [
                jnp.where(first, 0.125, 0.0).astype(bf16),
                jnp.where(first, 0.0, 0.125).astype(bf16),
            ]
            def pair_forward(pair, carry):
                def cols(base):
                    return pl.ds(pl.multiple_of(base + pair * 2 * HEAD, 2 * HEAD), 2 * HEAD)

                q = qkv_ref[:, cols(0)]
                k = qkv_ref[:, cols(width)]
                v = qkv_ref[:, cols(2 * width)]
                scores = mm(k, jnp.concatenate([q * scale[0], q * scale[1]], 0), NT)
                scores = jnp.where(key_mask, scores, -1e30)
                raised = jnp.exp(scores - jnp.max(scores, 0, keepdims=True))
                low = (raised * (1.0 / jnp.sum(raised, 0, keepdims=True))).astype(bf16)
                probs_ref[pair] = low
                outs = mm(low, v, TN)
                ctx_ref[:, cols(0)] = jnp.where(first, outs[:seq], outs[seq:]).astype(bf16)
                return carry

            lax.fori_loop(0, HEADS // 2, pair_forward, 0, unroll=3)

            @pl.when(step == 0)
            def _():
                load(0).wait()

            x_wide = x_ref[...].astype(f32)
            attn_out = mm(ctx_ref[...], wo[...]) + ob_ref[...]
            normed, inv = norm_parts(x_wide + attn_out)
            an_ref[here, :] = normed
            ai_ref[here, :] = jnp.broadcast_to(inv, (seq, 128))
            hidden = normed * ag_ref[...] + as_ref[...]
            hidden_low = hidden.astype(bf16)
            hid_ref[here, :] = hidden_low

            @pl.when(step == 0)
            def _():
                load(1).wait()

            for piece in range(parts):
                at = slice(piece * part, (piece + 1) * part)
                upper = mm(hidden_low, wu[:, at]) + ub_ref[:, at]
                phi = 0.5 * (1.0 + lax.erf(upper * inv_sqrt_two))
                act_all[here, at] = (upper * phi).astype(bf16)
                slope = phi + upper * jnp.exp(-0.5 * upper * upper) * inv_sqrt_tau
                slope_ref[here, at] = slope.astype(bf16)
                if piece == 0:

                    @pl.when(step == 0)
                    def _():
                        load(2).wait()

                term = mm(act_all[here, at], wd[at, :])
                ffn_sum = term if piece == 0 else ffn_sum + term

            ffn_out = ffn_sum + db_ref[...]
            ffn_normed, ffn_inv = norm_parts(hidden + ffn_out)
            out_ref[...] = ((ffn_normed * fg_ref[...] + fs_ref[...]) * row_mask).astype(bf16)
            cot = og_ref[...].astype(f32) * row_mask
            second = norm_back(cot, ffn_normed, ffn_inv, fg_ref[...])
            ds_ref[here, :] = second
            low = second.astype(bf16)
            df_ref[here, :] = low
            for at, value in enumerate(
                (
                    cot * ffn_normed,
                    cot,
                    low.astype(f32),
                    row_mask * x_wide * x_wide,
                    row_mask * attn_out * attn_out,
                    row_mask * ffn_out * ffn_out,
                )
            ):
                sums_ref[at : at + 1, :] += row_sum(value)
            lane = lax.broadcasted_iota(jnp.int32, (1, width), 1)
            slots_here = ((length + count) * width).astype(f32)
            sums_ref[6:7, :] += jnp.where(lane == 0, slots_here, 0.0)

        @pl.when(step >= captions)
        def _():
            acts = pl.ds(pl.multiple_of((step - captions) * part, part), part)
            got = mm(act_all[:, acts], df_ref[...], TN)
            mine = sc_ref[0] == 0
            send_ref[...] = jnp.where(mine, got[:, half:], got[:, :half]).astype(bf16)
            keep_ref[...] = jnp.where(mine, got[:, :half], got[:, half:]).astype(bf16)

    def rowwise(size, cols):
        return pl.BlockSpec((size, cols), lambda i, s: (jnp.minimum(i, captions - 1), 0))

    anywhere = pl.BlockSpec(memory_space=pl.ANY)
    return pl.pallas_call(
        kernel,
        grid_spec=pltpu.PrefetchScalarGridSpec(
            num_scalar_prefetch=1,
            grid=(grid,),
            in_specs=[
                rowwise(text_len, width),
                rowwise(text_len, 3 * width),
                VMEM,
                whole((1, slots)),
                rowwise(seq, width),
                anywhere,
                whole((1, 2 * width)),
                anywhere,
                vec(width),
                vec(width),
                vec(width),
                anywhere,
                whole((1, ff)),
                anywhere,
                vec(width),
                vec(width),
                vec(width),
            ],
            out_specs=[rowwise(seq, width), rowwise(seq, width), rowwise(seq, 3 * width)]
            + [pl.BlockSpec((HEADS // 2, seq, 2 * seq), lambda i, s: (jnp.minimum(i, captions - 1), 0, 0))]
            + [rowwise(seq, width)]
            + [VMEM] * 9
            + [pl.BlockSpec((part, half), lambda i, s: (jnp.maximum(i - captions, 0), 0))] * 2,
            scratch_shapes=[
                pltpu.VMEM((slots, width), bf16),
                pltpu.VMEM((slots, 3 * width), bf16),
                pltpu.VMEM((rows, ff), bf16),
                pltpu.VMEM(w_qkv.shape, bf16),
                pltpu.VMEM(w_out.shape, bf16),
                pltpu.SemaphoreType.DMA((6,)),
            ],
        ),
        out_shape=[
            apart((rows, width), bf16),
            apart((rows, width), bf16),
            apart((rows, 3 * width), bf16),
            apart((captions * HEADS // 2, seq, 2 * seq), bf16),
            apart((rows, width), bf16),
            near((rows, width)),
            near((rows, 128)),
            near((rows, width), bf16),
            near((rows, ff), bf16),
            near((rows, width)),
            near((rows, width), bf16),
            near((8, width)),
            near(w_up.shape, bf16),
            near(w_down.shape, bf16),
            apart((ff, half), bf16),
            apart((ff, half), bf16),
        ],
        compiler_params=params(33),
        cost_estimate=cost(30),
        name="forward",
    )(
        scalars,
        far(text),
        far(text_low),
        arrived,
        *(
            far(v)
            for v in (
                source, out_grad, w_qkv, qv_bias, w_out, out_bias,
                attn_gain, attn_shift, w_up, up_bias, w_down, down_bias, ffn_gain, ffn_shift,
            )
        ),
    )


def ffn_backward(core, d_ffn, d_second, slope, attn_normed, attn_inv, w_down, w_up, attn_gain, seq, hold, first, size, begun):
    rows, width = d_ffn.shape
    ff = w_up.shape[1]
    parts = 4
    part = ff // parts

    def kernel(c_ref, df_ref, ds_ref, sl_ref, an_ref, ai_ref, wd, wu, ag_ref, *rest):
        dup_ref, dr_ref, da_ref, sums_ref, up_ref = rest[len(begun) + len(hold) :]
        step = pl.program_id(0)

        @pl.when(step == 0)
        def _():
            if begun:
                sums_ref[...] = rest[3][...]
                up_ref[...] = rest[4][...]
            else:
                sums_ref[...] = jnp.zeros_like(sums_ref)
                up_ref[...] = jnp.zeros_like(up_ref)

        here = pl.ds(pl.multiple_of((first + step) * seq, seq), seq)
        d_low = df_ref[here, :]
        for piece in range(parts):
            at = slice(piece * part, (piece + 1) * part)
            d_act = mm(d_low, wd[at, :], NT)
            low = (d_act * sl_ref[here, at].astype(f32)).astype(bf16)
            dup_ref[here, at] = low
            up_ref[0:1, at] += row_sum(low.astype(f32))
        d_hidden = ds_ref[here, :] + mm(dup_ref[here, :], wu[...], NT)
        normed = an_ref[here, :]
        resid = norm_back(d_hidden, normed, ai_ref[here, 0:1], ag_ref[...])
        dr_ref[here, :] = resid
        low = resid.astype(bf16)
        da_ref[here, :] = low
        sums_ref[0:1, :] += row_sum(d_hidden * normed)
        sums_ref[1:2, :] += row_sum(d_hidden)
        sums_ref[2:3, :] += row_sum(low.astype(f32))

    return pl.pallas_call(
        kernel,
        grid_spec=pltpu.PrefetchScalarGridSpec(
            num_scalar_prefetch=1,
            grid=(size,),
            in_specs=[VMEM] * 7
            + [vec(width)]
            + [VMEM] * len(begun)
            + [VMEM] * len(hold),
            out_specs=[VMEM] * 5,
        ),
        out_shape=[
            near((rows, ff), bf16),
            near((rows, width)),
            near((rows, width), bf16),
            near((8, width)),
            near((8, ff)),
        ],
        input_output_aliases={9: 0, 10: 1, 11: 2} if begun else {},
        compiler_params=params(6),
        cost_estimate=cost(4 * size),
        name="ffn_backward",
    )(core, d_ffn, d_second, slope, attn_normed, attn_inv, w_down, w_up, attn_gain, *begun, *hold)


def up_gradient(core, hidden_low, d_upper):
    rows, width = hidden_low.shape

    def kernel(c_ref, h_ref, d_ref, send_ref, keep_ref):
        step = pl.program_id(0)
        here = pl.ds(pl.multiple_of(step * width, width), width)
        for to_ref, side in ((send_ref, 1 - c_ref[0]), (keep_ref, c_ref[0])):
            cols = pl.ds(pl.multiple_of((2 * side + step) * width, width), width)
            to_ref[:, here] = mm(h_ref[...], d_ref[:, cols], TN).astype(bf16)

    return pl.pallas_call(
        kernel,
        grid_spec=pltpu.PrefetchScalarGridSpec(
            num_scalar_prefetch=1, grid=(2,), in_specs=[VMEM, VMEM], out_specs=[VMEM, VMEM]
        ),
        out_shape=[near((width, 2 * width), bf16)] * 2,
        compiler_params=params(6),
        cost_estimate=cost(0.1),
        name="up_gradient",
    )(core, hidden_low, d_upper)


def attention_backward(scalars, d_attn, d_resid, probs, qkv, source, w_out, w_qkv, dims, first_caption, size, begun):
    captions, images = dims
    rows, width = d_attn.shape
    seq = rows // captions
    slots = source.shape[1]
    regions = slots // images
    text_len = seq - regions
    last = first_caption + size == captions

    def kernel(
        sc_ref, da_ref, dr_ref, p_ref, qkv_ref, src_ref, wo_ref, wq, *rest,
    ):
        begun_refs = rest[: len(begun)]
        dqkv_ref, text_ref, back_ref, sums_ref, d_img, d_ctx_ref = rest[len(begun) :]
        step = pl.program_id(0)
        here = pl.ds(pl.multiple_of((first_caption + step) * seq, seq), seq)

        @pl.when(step == 0)
        def _():
            if begun:
                sums_ref[...] = begun_refs[3][...]
                d_img[...] = begun_refs[2][...]
            else:
                sums_ref[...] = jnp.zeros_like(sums_ref)
                d_img[...] = jnp.zeros_like(d_img)

        d_ctx_ref[...] = mm(da_ref[here, :], wo_ref[...], NT).astype(bf16)
        first = lax.broadcasted_iota(jnp.int32, (1, 2 * HEAD), 1) < HEAD
        masks = [jnp.where(first, 1.0, 0.0).astype(bf16), jnp.where(first, 0.0, 1.0).astype(bf16)]
        def pair_backward(pair, carry):
            def cols(base):
                return pl.ds(pl.multiple_of(base + pair * 2 * HEAD, 2 * HEAD), 2 * HEAD)

            q = qkv_ref[here, cols(0)]
            k = qkv_ref[here, cols(width)]
            v = qkv_ref[here, cols(2 * width)]
            d_c = d_ctx_ref[:, cols(0)]
            both_c = jnp.concatenate([d_c * masks[0], d_c * masks[1]], 0)
            both_q = jnp.concatenate([q * masks[0], q * masks[1]], 0)
            low = p_ref[pair]
            d_probs = mm(v, both_c, NT)
            wide = low.astype(f32)
            both = wide * d_probs
            inner = jnp.sum(both, 0, keepdims=True)
            d_scores = (both - wide * inner).astype(bf16)
            d_q = mm(d_scores, k, TN) * 0.125
            dqkv_ref[here, cols(0)] = jnp.where(first, d_q[:seq], d_q[seq:]).astype(bf16)
            dqkv_ref[here, cols(width)] = (mm(d_scores, both_q) * 0.125).astype(bf16)
            dqkv_ref[here, cols(2 * width)] = mm(low, both_c).astype(bf16)
            return carry

        lax.fori_loop(0, HEADS // 2, pair_backward, 0, unroll=3)

        sums_ref[0:1, :] += row_sum(dqkv_ref[here, :width].astype(f32))
        sums_ref[1:2, :] += row_sum(dqkv_ref[here, 2 * width :].astype(f32))
        d_x = mm(dqkv_ref[here, :], wq[...], NT) + dr_ref[here, :]
        text_ref[...] = d_x[:text_len]
        at = pl.ds(pl.multiple_of(sc_ref[8 + first_caption + step] * regions, regions), regions)
        d_img[at, :] += d_x[text_len:]

        @pl.when(step == size - 1)
        def _():
            if last:
                back_ref[...] = mm(one_hot(src_ref[...], slots), d_img[...].astype(bf16)).astype(bf16)
            else:
                back_ref[...] = d_img[...]

    return pl.pallas_call(
        kernel,
        grid_spec=pltpu.PrefetchScalarGridSpec(
            num_scalar_prefetch=1,
            grid=(size,),
            in_specs=[VMEM] * 2
            + [pl.BlockSpec((HEADS // 2, seq, 2 * seq), lambda i, s: (i + first_caption, 0, 0)), VMEM]
            + [whole((1, slots)), VMEM, VMEM]
            + ([VMEM, pl.BlockSpec(memory_space=pl.ANY)] + [VMEM, VMEM] if begun else []),
            out_specs=[
                VMEM,
                pl.BlockSpec((text_len, width), lambda i, s: (i + first_caption, 0)),
                VMEM,
                VMEM,
            ],
            scratch_shapes=[
                pltpu.VMEM((slots, width), f32),
                pltpu.VMEM((seq, width), bf16),
            ],
        ),
        out_shape=[
            near((rows, 3 * width), bf16),
            pltpu.HBM((captions * text_len, width), f32),
            near((slots, width), bf16 if last else f32),
            near((8, width)),
        ],
        input_output_aliases={8: 0, 9: 1} if begun else {},
        compiler_params=params(15),
        cost_estimate=cost(5 * size),
        name="attention_backward",
    )(scalars, d_attn, d_resid, far(probs), qkv, source, w_out, w_qkv, *begun)


def qkvo_gradient(core, x, d_qkv, context, d_attn):
    rows, width = x.shape

    def kernel(c_ref, x_ref, dq_ref, ctx_ref, da_ref, send_ref, keep_ref):
        step = pl.program_id(0)

        def store(low_block, high_block):
            low, high = low_block.astype(bf16), high_block.astype(bf16)

            @pl.when(c_ref[0] == 0)
            def _():
                keep_ref[...] = low
                send_ref[...] = high

            @pl.when(c_ref[0] != 0)
            def _():
                send_ref[...] = low
                keep_ref[...] = high

        @pl.when(step == 0)
        def _():
            store(mm(x_ref[...], dq_ref[:, :width], TN), mm(x_ref[...], dq_ref[:, 2 * width :], TN))

        @pl.when(step == 1)
        def _():
            store(mm(x_ref[...], dq_ref[:, width : 2 * width], TN), mm(ctx_ref[...], da_ref[...], TN))

    out = pl.BlockSpec((width, width), lambda i, s: (0, i))
    return pl.pallas_call(
        kernel,
        grid_spec=pltpu.PrefetchScalarGridSpec(
            num_scalar_prefetch=1, grid=(2,), in_specs=[VMEM] * 4, out_specs=[out, out]
        ),
        out_shape=[apart((width, 2 * width), bf16)] * 2,
        compiler_params=params(14),
        cost_estimate=cost(5),
        name="qkvo_gradient",
    )(core, x, d_qkv, context, d_attn)


def region_norm_backward(
    core, returned, target, normed, inv, gain, boxes, w_box_t, sums_forward, sums_ffn, sums_up, sums_attn, groups
):
    rows, width = returned.shape
    half = width // 2
    box = boxes.shape[0]
    share = width // groups
    ff_share = sums_up.shape[1] // groups

    def kernel(
        c_ref, r_ref, t_ref, n_ref, i_ref, g_ref, box_ref, wb_ref, sf_ref, sn_ref, su_ref, sa_ref,
        all_ref, send_ref, keep_ref, small_ref, bg_ref, small,
    ):
        d_region = mm(one_hot(t_ref[...], rows), r_ref[...], TN)
        normed = n_ref[...]
        low = norm_back(d_region, normed, i_ref[:, 0:1], g_ref[...]).astype(bf16)
        all_ref[...] = low
        mine = c_ref[0] == 0
        send_ref[:rows, :] = jnp.where(mine, low[:, half:], low[:, :half])
        keep_ref[...] = jnp.where(mine, low[:, :half], low[:, half:])
        bg_ref[...] = mm(wb_ref[...], low, NT)
        boxes_grad = mm(box_ref[...], low)
        vectors = [
            row_sum(low.astype(f32)),
            row_sum(d_region * normed),
            row_sum(d_region),
            sf_ref[0:1, :],
            sf_ref[1:2, :],
            sf_ref[2:3, :],
            sn_ref[0:1, :],
            sn_ref[1:2, :],
            sn_ref[2:3, :],
        ] + [boxes_grad[at : at + 1] for at in range(box)]
        small[...] = jnp.zeros_like(small)
        lane = lax.broadcasted_iota(jnp.int32, (1, half), 1)
        stats = jnp.zeros((1, half), f32)
        for at in range(4):
            total = jnp.sum(sf_ref[3 + at : 4 + at, :], 1, keepdims=True)
            stats = jnp.where(lane == at, total, stats)
        flat = jnp.concatenate([sa_ref[0:1, :], sa_ref[1:2, :]], 1)
        for group in range(groups):
            small[group, 0:1, 0:ff_share] = su_ref[0:1, group * ff_share : (group + 1) * ff_share]
            small[group, 1:2, 0 : 2 * share] = flat[:, group * 2 * share : (group + 1) * 2 * share]
            for at, value in enumerate(vectors):
                row, col = (1, 2) if at == 0 else (2 + (at - 1) // 3, (at - 1) % 3)
                small[group, row : row + 1, 128 * col : 128 * col + share] = value[
                    :, group * share : (group + 1) * share
                ]
            small[group, 6:7, :] = stats
        small_ref[...] = small[...].astype(bf16)
        for group in range(groups):
            send_ref[rows + 8 * group : rows + 8 * (group + 1), :] = small_ref[group]

    sizes = (sums_forward, sums_ffn, sums_up, sums_attn)
    return pl.pallas_call(
        kernel,
        grid_spec=pltpu.PrefetchScalarGridSpec(
            num_scalar_prefetch=1,
            grid=(1,),
            in_specs=[
                whole((rows, width)),
                whole((1, rows)),
                whole((rows, width)),
                whole((rows, 128)),
                vec(width),
                whole(boxes.shape),
                whole(w_box_t.shape),
            ]
            + [whole(v.shape) for v in sizes],
            out_specs=[VMEM] * 4 + [whole((box, rows))],
            scratch_shapes=[pltpu.VMEM((groups, 8, half), f32)],
        ),
        out_shape=[
            near((rows, width), bf16),
            near((rows + 8 * groups, half), bf16),
            near((rows, half), bf16),
            near((groups, 8, half), bf16),
            shape((box, rows)),
        ],
        compiler_params=params(14),
        cost_estimate=cost(0.1),
        name="region_norm_backward",
    )(core, returned, far(target), far(normed), far(inv), far(gain), far(boxes), far(w_box_t), *sizes)


def visual_gradient(bits, features, other_features, d_pre, other_d_pre, small, groups):
    rows, feat = features.shape
    half = d_pre.shape[1]
    steps = 2
    part = feat // steps
    quarter = feat // groups // 4
    tall = quarter + 8
    per_step = groups // steps
    high = groups // 2

    def kernel(b_ref, f_ref, o_ref, d_ref, p_ref, s_ref, a_send, a_keep, b_send, b_keep, got):
        step = pl.program_id(0)
        bit2, bit4 = b_ref[1], b_ref[2]
        got[...] = mm(f_ref[...], d_ref[...], TN) + mm(o_ref[...], p_ref[:rows, :], TN)

        def fill(to_ref, at, which, group, x, piece):
            here = pl.ds(pl.multiple_of(((group * 2 + x) * 2 + piece) * quarter, 8), quarter)
            to_ref[at, which, :quarter, :] = got[here, :].astype(bf16)
            number = step * per_step + group
            other = p_ref[pl.ds(pl.multiple_of(rows + 8 * number, 8), 8), :]
            to_ref[at, which, quarter:, :] = add(s_ref[number], other)

        for group in range(per_step):
            y = group % 2
            at = step * (per_step // 2) + group // 2
            fill(a_send, at, y, group, 1 - bit2, 0)
            fill(a_keep, at, y, group, bit2, 0)

            @pl.when(bit4 == y)
            def _():
                for x in range(2):
                    fill(b_keep, at, x, group, x, 1)

            @pl.when(bit4 != y)
            def _():
                for x in range(2):
                    fill(b_send, at, x, group, x, 1)

    return pl.pallas_call(
        kernel,
        grid_spec=pltpu.PrefetchScalarGridSpec(
            num_scalar_prefetch=1,
            grid=(steps,),
            in_specs=[
                pl.BlockSpec((rows, part), lambda i, s: (0, i)),
                pl.BlockSpec((rows, part), lambda i, s: (0, i)),
                VMEM,
                VMEM,
                VMEM,
            ],
            out_specs=[VMEM] * 4,
            scratch_shapes=[pltpu.VMEM((part, half), f32)],
        ),
        out_shape=[near((high, 2, tall, half), bf16)] * 4,
        compiler_params=params(14),
        cost_estimate=cost(0.1),
        name="visual_gradient",
    )(bits, far(features), far(other_features), d_pre, other_d_pre, small)


def feature_gradient(bits, d_pre, w_visual):
    rows, width = d_pre.shape
    feat = w_visual.shape[0]
    steps = 4
    part = feat // steps

    def kernel(b_ref, d_ref, w_ref, o_ref):
        o_ref[...] = mm(d_ref[...], w_ref[...], NT)

    return pl.pallas_call(
        kernel,
        grid_spec=pltpu.PrefetchScalarGridSpec(
            num_scalar_prefetch=1,
            grid=(steps,),
            in_specs=[VMEM, pl.BlockSpec((part, width), lambda i, s: (i, 0))],
            out_specs=pl.BlockSpec((rows, part), lambda i, s: (0, i)),
        ),
        out_shape=shape((rows, feat)),
        compiler_params=params(8),
        cost_estimate=cost(10),
        name="feature_gradient",
    )(bits, d_pre, far(w_visual))


def device_number():
    return lax.axis_index("dp") * lax.axis_size("enc") + lax.axis_index("enc")


def swap(values, bit):
    count = lax.axis_size("dp") * lax.axis_size("enc")
    return lax.ppermute(values, ("dp", "enc"), [(i, i ^ bit) for i in range(count)])


def add(a, b):
    return (a.astype(f32) + b.astype(f32)).astype(bf16)


def scalar_call(kernel, bits, ins, in_specs, outs, out_specs, grid, limit, name, last=False, place=near):
    outs = outs if last else [place(o.shape, o.dtype) for o in outs]
    return pl.pallas_call(
        kernel,
        grid_spec=pltpu.PrefetchScalarGridSpec(
            num_scalar_prefetch=1, grid=(grid,), in_specs=in_specs, out_specs=out_specs
        ),
        out_shape=outs,
        compiler_params=params(limit),
        cost_estimate=cost(1),
        name=name,
    )(bits, *ins)


def first_split(bits, kept, got, groups, place=near):
    tall = kept.ndim == 5
    high = groups // 2
    if tall:
        rows, cols = kept.shape[3:]
        view = (high, 2, 2, 2, rows, cols)
        block = (1, 2, 2, 2, rows, cols)
    else:
        rows, cols = kept.shape[0] // groups, kept.shape[1] // 4
        view = (high, 2, rows, 4 * cols)
        block = (1, 2, rows, 4 * cols)

    def kernel(b_ref, k_ref, r_ref, a_send, a_keep, b_send, b_keep):
        bit2, bit4 = b_ref[1], b_ref[2]

        def total(y, x, piece):
            if tall:
                return add(k_ref[0, y, x, piece], r_ref[0, y, x, piece])
            at = pl.ds(pl.multiple_of((2 * x + piece) * cols, 128), cols)
            return add(k_ref[0, y, :, at], r_ref[0, y, :, at])

        for other in range(2):
            a_send[0, other] = total(other, 1 - bit2, 0)
            a_keep[0, other] = total(other, bit2, 0)
            b_send[0, other] = total(1 - bit4, other, 1)
            b_keep[0, other] = total(bit4, other, 1)

    spec = pl.BlockSpec(block, lambda i, s: (i,) + (0,) * (len(block) - 1))
    out = pl.BlockSpec((1, 2, rows, cols), lambda i, s: (i, 0, 0, 0))
    return scalar_call(
        kernel, bits, (kept.reshape(view), got.reshape(view)), [spec, spec],
        [shape((high, 2, rows, cols), bf16)] * 4, [out] * 4, high, 6, "first_split", place=place,
    )


def second_split(bits, a_kept, a_got, b_kept, b_got):
    high, _, rows, cols = a_kept.shape

    def kernel(b_ref, ak, ar, bk, br, a_send, a_keep, b_send, b_keep):
        bit2, bit4 = b_ref[1], b_ref[2]
        a_send[0] = add(ak[0, 1 - bit4], ar[0, 1 - bit4])
        a_keep[0] = add(ak[0, bit4], ar[0, bit4])
        b_send[0] = add(bk[0, 1 - bit2], br[0, 1 - bit2])
        b_keep[0] = add(bk[0, bit2], br[0, bit2])

    spec = pl.BlockSpec((1, 2, rows, cols), lambda i, s: (i, 0, 0, 0))
    out = pl.BlockSpec((1, rows, cols), lambda i, s: (i, 0, 0))
    return scalar_call(
        kernel, bits, (a_kept, a_got, b_kept, b_got), [spec] * 4,
        [shape((high, rows, cols), bf16)] * 4, [out] * 4, high, 6, "second_split",
    )


def join_split(bits, pairs, place=near):
    high, _, cols = pairs[0][0].shape
    sizes = [kept.shape[1] for kept, _ in pairs]

    def kernel(b_ref, *refs):
        bit = b_ref[3]
        send, keep = refs[-2:]
        at = 0
        for n, size in enumerate(sizes):
            kept, got = refs[2 * n : 2 * n + 2]
            send[0, at : at + size] = add(kept[1 - bit], got[1 - bit])
            keep[0, at : at + size] = add(kept[bit], got[bit])
            at += size

    ins = [value for pair in pairs for value in pair]
    specs = [pl.BlockSpec((2, v.shape[1], cols), lambda i, s: (i, 0, 0)) for v in ins]
    out = pl.BlockSpec((1, sum(sizes), cols), lambda i, s: (i, 0, 0))
    return scalar_call(
        kernel, bits, ins, specs, [shape((high // 2, sum(sizes), cols), bf16)] * 2, [out] * 2,
        high // 2, 6, "join_split", place=place,
    )


def late_split(bits, kept, got, which):
    high, rows, cols = kept.shape

    def kernel(b_ref, k_ref, r_ref, send, keep):
        bit = b_ref[which]
        send[0] = add(k_ref[1 - bit], r_ref[1 - bit])
        keep[0] = add(k_ref[bit], r_ref[bit])

    spec = pl.BlockSpec((2, rows, cols), lambda i, s: (i, 0, 0))
    out = pl.BlockSpec((1, rows, cols), lambda i, s: (i, 0, 0))
    return scalar_call(
        kernel, bits, (kept, got), [spec] * 2, [shape((high // 2, rows, cols), bf16)] * 2, [out] * 2,
        high // 2, 6, "late_split",
    )


def over_two(halves):
    return swap(halves[0], 2), halves[1], swap(halves[2], 4), halves[3]


def over_other_two(halves):
    return swap(halves[0], 4), halves[1], swap(halves[2], 2), halves[3]


def second(bits, moved):
    return second_split(bits, moved[1], moved[0], moved[3], moved[2])


def join(bits, *moved, place=near):
    pairs = []
    for one in moved:
        pairs += [(one[1], one[0]), (one[3], one[2])]
    return join_split(bits, pairs, place)


def after_all(*trees):
    leaves, tree = jax.tree.flatten(trees)
    return jax.tree.unflatten(tree, lax.optimization_barrier(leaves))


def late_first(bits, kept, got):
    if kept.shape[0] == 1:
        return (kept + got,)
    return late_split(bits, kept, got, 4)


def late_move(halves):
    return swap(halves[0], 16) if len(halves) > 1 else None


def late_rest(bits, halves, moved):
    bit, which = 16, 5
    while len(halves) > 1:
        if halves[1].shape[0] == 1:
            halves = (halves[1] + moved,)
        else:
            halves = late_split(bits, halves[1], moved, which)
            bit, which = 2 * bit, which + 1
            moved = swap(halves[0], bit)
    return halves[0][0]


def spread(mine, *late):
    over_x = swap(mine, 2)
    over_core = swap(mine, 1)
    return mine, over_x, over_core, swap(gate(over_x, *late), 1)


def pick(b_ref, pieces, core, x):
    mine, over_x, over_core, over_both = pieces
    same_x = b_ref[1] == x
    return jnp.where(
        b_ref[0] == core, jnp.where(same_x, mine, over_x), jnp.where(same_x, over_core, over_both)
    ).astype(f32)


def finish_ffn(bits, pieces):
    rows, cols = pieces[0].shape
    half = rows // 2
    part = rows // 4

    def kernel(b_ref, p0, p1, p2, p3, down_ref, up_ref):
        for core in range(2):
            for x in range(2):
                got = pick(b_ref, (p0[...], p1[...], p2[...], p3[...]), core, x)
                down_ref[x * half : (x + 1) * half, core * cols : (core + 1) * cols] = got[:half]
                for piece in range(2):
                    at = ((core * 2 + x) * 2 + piece) * cols
                    up_ref[:, at : at + cols] = got[half + piece * part : half + (piece + 1) * part]

    outs = [shape((rows, 2 * cols)), shape((part, 8 * cols))]
    return scalar_call(
        kernel, bits, pieces, [whole((rows, cols))] * 4, outs, [whole(o.shape) for o in outs], 1, 12, "finish_ffn", True
    )


def finish_wide(bits, pieces, sizes):
    rows, cols = pieces[0].shape
    part = rows // 2

    def kernel(b_ref, p0, p1, p2, p3, *out_refs):
        for core in range(2):
            for x in range(2):
                got = pick(b_ref, (p0[...], p1[...], p2[...], p3[...]), core, x)
                for piece in range(2):
                    at = ((core * 2 + x) * 2 + piece) * cols
                    for out_ref, size in zip(out_refs, sizes):
                        if 0 <= at < size:
                            out_ref[:, at : at + cols] = got[piece * part : (piece + 1) * part]
                        at -= size

    outs = [shape((part, size)) for size in sizes]
    return scalar_call(
        kernel, bits, pieces, [whole((rows, cols))] * 4, outs, [whole(o.shape) for o in outs], 1, 8, "finish_wide", True
    )


def finish_visual(bits, pieces, ff_share, share, box):
    rows, cols = pieces[0].shape
    tall = rows // 2
    quarter = tall - 8
    sizes = [share] * 9 + [2 * share, ff_share]

    def kernel(b_ref, p0, p1, p2, p3, vis_ref, box_ref, rms_ref, *small_refs):
        for core in range(2):
            for x in range(2):
                got = pick(b_ref, (p0[...], p1[...], p2[...], p3[...]), core, x)
                for piece in range(2):
                    low = piece * tall
                    vis_ref[(2 * x + piece) * quarter : (2 * x + piece + 1) * quarter, core * cols : (core + 1) * cols] = got[
                        low : low + quarter
                    ]
        small = p0[quarter : quarter + 8, :].astype(f32)
        for at in range(9):
            row, col = (1, 2) if at == 0 else (2 + (at - 1) // 3, (at - 1) % 3)
            small_refs[at][...] = small[row, 128 * col : 128 * col + share]
        small_refs[9][...] = small[1, 0 : 2 * share]
        small_refs[10][...] = small[0, 0:ff_share]
        for at in range(9, 9 + box):
            row, col = 2 + (at - 1) // 3, (at - 1) % 3
            box_ref[at - 9 : at - 8, :] = small[row : row + 1, 128 * col : 128 * col + share]
        stats = small[6, 0:128]
        total = jnp.sum(small[6:7, 3:4])
        rms_ref[...] = jnp.sqrt(stats / total)[:3]

    outs = [shape((4 * quarter, 2 * cols)), shape((box, share)), shape((3,))] + [shape((size,)) for size in sizes]
    specs = [whole(o.shape) for o in outs[:2]] + [vec(3)] + [vec(size) for size in sizes]
    return scalar_call(
        kernel, bits, pieces, [whole((rows, cols))] * 4, outs, specs, 1, 8, "finish_visual", True
    )


def gate(value, *others):
    return lax.optimization_barrier((value, *others))[0]


def on_device(
    text_embed,
    region_features,
    boxes,
    caption_image,
    caption_lengths,
    region_counts,
    region_target,
    region_source,
    w_visual,
    w_box,
    visual_bias,
    visual_gain,
    visual_shift,
    w_qkv,
    qv_bias,
    w_out,
    out_bias,
    attn_gain,
    attn_shift,
    w_up,
    up_bias,
    w_down,
    down_bias,
    ffn_gain,
    ffn_shift,
    out_grad,
):
    width = text_embed.shape[1]
    captions = caption_image.shape[0]
    images = region_counts.shape[0]
    dims = (captions, images)
    axes = ("dp", "enc")
    groups = lax.axis_size("dp")
    count = groups * lax.axis_size("enc")
    me = device_number().astype(jnp.int32)
    places = lax.iota(jnp.int32, 8)
    scalars = jnp.concatenate([(me >> places) & 1, caption_image, caption_lengths, region_counts])
    w_box_t = w_box.T
    row = lambda v: v.reshape(1, -1)
    qv_row = row(qv_bias)

    message, vis_normed, vis_inv = region_forward(
        region_features, boxes, region_target, w_visual, w_box_t, visual_bias, visual_gain, visual_shift
    )
    arrived = lax.all_to_all(message, axes, split_axis=0, concat_axis=0, tiled=True)
    text_low = text_qkv(text_embed, w_qkv, qv_row)
    (
        out_rows, x, qkv, probs, context, attn_normed, attn_inv, hidden_low, slope, d_second, d_ffn,
        sums_forward, w_up_near, w_down_near, down_sent, down_kept,
    ) = forward(
        scalars, text_embed, text_low, arrived, region_source, out_grad, w_qkv, qv_row, w_out,
        out_bias, attn_gain, attn_shift, w_up, row(up_bias), w_down, down_bias, ffn_gain, ffn_shift, dims,
    )
    seq = x.shape[0] // captions
    rest = captions - 1
    bits = core = scalars
    hold = ()
    ffn_ins = (d_ffn, d_second, slope, attn_normed, attn_inv, w_down_near, w_up_near, attn_gain, seq, hold)
    down_view = (groups, 2, 2, w_down.shape[0] // groups // 4, width // 2)
    down_sent, down_kept = down_sent.reshape(down_view), down_kept.reshape(down_view)

    moved = swap(down_sent, 1)
    begun = ffn_backward(core, *ffn_ins, 0, 1, ())

    moved, begun, sc = after_all(moved, begun, scalars)
    down = first_split(sc, down_kept, moved, groups)
    down, begun, sc = after_all(down, begun, sc)
    moved = over_two(down)
    d_upper, d_resid, d_attn, sums_ffn, sums_up = ffn_backward(sc, *ffn_ins, 1, rest, tuple(begun))
    up_sent, up_kept = up_gradient(sc, hidden_low, gate(d_upper, d_attn))

    moved, up_sent, up_kept, d_attn, sc = after_all(moved, up_sent, up_kept, d_attn, sc)
    down = second(sc, moved)
    down, up_sent, up_kept, sc = after_all(down, up_sent, up_kept, sc)
    moved = over_other_two(down), swap(up_sent, 1)
    att_ins = (d_attn, d_resid, probs, qkv, region_source, w_out, w_qkv, dims)
    begun = attention_backward(sc, *att_ins, 0, 1, ())

    moved, up_kept, begun, sc = after_all(moved, up_kept, begun, sc)
    down = moved[0]
    up = first_split(sc, up_kept, moved[1], groups)
    down, up, begun, sc = after_all(down, up, begun, sc)
    moved = over_two(up)
    d_qkv, text_grad, back_message, sums_attn = attention_backward(sc, *att_ins, 1, rest, tuple(begun))

    moved, down, d_qkv, back_message, sc = after_all(moved, down, d_qkv, back_message, sc)
    up = second(sc, moved)
    up, down, sc = after_all(up, down, sc)
    moved = over_other_two(up)
    qkvo_sent, qkvo_kept = qkvo_gradient(sc, x, d_qkv, context, d_attn)

    moved, down, qkvo_sent, qkvo_kept, back_message, sc = after_all(
        moved, down, qkvo_sent, qkvo_kept, back_message, sc
    )
    ffn = join(sc, down, moved, place=apart)
    ffn, qkvo_sent, qkvo_kept, back_message, sc = after_all(ffn, qkvo_sent, qkvo_kept, back_message, sc)
    returned = lax.all_to_all(back_message, axes, split_axis=0, concat_axis=0, tiled=True)
    other_features = swap(gate(region_features, qkvo_kept), 1)
    qkvo = first_split(sc, qkvo_kept, swap(qkvo_sent, 1), groups, apart)
    qkvo_moved = over_two(qkvo)
    ffn_moved = swap(gate(ffn[0], *qkvo), 8)
    returned, sc = after_all(returned, gate(sc, *qkvo))
    d_pre, d_pre_sent, d_pre_kept, small, box_grad = region_norm_backward(
        sc, returned, region_target, vis_normed, vis_inv, visual_gain, boxes, w_box_t,
        sums_forward, sums_ffn, sums_up, sums_attn, groups,
    )
    vis = visual_gradient(
        sc, region_features, other_features, d_pre_kept, swap(d_pre_sent, 1), small, groups
    )
    vis_moved = over_two(vis)
    sc = gate(sc, *vis)
    qkvo = second(sc, qkvo_moved)
    qkvo_moved = over_other_two(qkvo)
    ffn = late_first(gate(sc, *qkvo), ffn[1], ffn_moved)
    ffn_moved = late_move(ffn)
    feature_grad = feature_gradient(gate(sc, *ffn), d_pre, w_visual)

    sc = gate(sc, feature_grad)
    vis = second(sc, vis_moved)
    vis_moved = over_other_two(vis)
    sc = gate(sc, *vis)
    qkvo = join(sc, qkvo_moved)
    qkvo_moved = swap(qkvo[0], 8)
    ffn = late_rest(sc, ffn, gate(ffn_moved, *qkvo))

    vis = join(gate(sc, *qkvo, ffn), vis_moved)
    vis_moved = swap(vis[0], 8)
    sc = gate(sc, *vis)
    qkvo = late_first(sc, qkvo[1], qkvo_moved)
    qkvo_moved = late_move(qkvo)

    vis = late_first(gate(sc, *qkvo), vis[1], vis_moved)
    vis_moved = late_move(vis)
    ffn = spread(ffn, *vis)
    sc = gate(sc, *vis)
    g_down, g_up = finish_ffn(sc, ffn)
    qkvo = late_rest(sc, qkvo, gate(qkvo_moved, *vis))

    vis = late_rest(sc, vis, gate(vis_moved, g_up, qkvo))
    qkvo = spread(qkvo, vis)
    g_qkv, g_out = finish_wide(gate(sc, vis), qkvo, (3 * width, width))
    vis = spread(vis, g_qkv)
    g_visual, g_box_t, rms_values, *small = finish_visual(
        sc, vis, w_up.shape[1] // groups, width // groups, boxes.shape[0]
    )
    return (
        out_rows,
        text_grad,
        feature_grad,
        box_grad,
        rms_values,
        g_visual,
        g_box_t.T,
        small[0],
        small[1],
        small[2],
        g_qkv,
        small[9],
        g_out,
        small[8],
        small[6],
        small[7],
        g_up,
        small[10],
        g_down,
        small[5],
        small[3],
        small[4],
    )


def solution(mesh):
    return jax.shard_map(
        on_device,
        mesh=mesh,
        in_specs=(
            P(("dp", "enc"), None),
            P(("dp", "enc"), None),
            P(None, ("dp", "enc")),
            P(("dp", "enc")),
            P(("dp", "enc")),
            P(("dp", "enc")),
            P(("dp", "enc"), None),
            P(("dp", "enc"), None),
            P(),
            P(),
            P(),
            P(),
            P(),
            P(),
            P(),
            P(),
            P(),
            P(),
            P(),
            P(),
            P(),
            P(),
            P(),
            P(),
            P(),
            P(("dp", "enc"), None),
        ),
        out_specs=(
            P(("dp", "enc"), None),
            P(("dp", "enc"), None),
            P(("dp", "enc"), None),
            P(None, ("dp", "enc")),
            P(),
            P("dp", None),
            P("dp", None),
            P("dp"),
            P("dp"),
            P("dp"),
            P("dp", None),
            P("dp"),
            P("dp", None),
            P("dp"),
            P("dp"),
            P("dp"),
            P("dp", None),
            P("dp"),
            P("dp", None),
            P("dp"),
            P("dp"),
            P("dp"),
        ),
        check_vma=False,
    )
```

```python
import jax
import jax.numpy as jnp
from jax import lax
from jax.experimental import pallas as pl
from jax.experimental.pallas import tpu as pltpu
from jax.sharding import PartitionSpec as P

HEADS = 12
UNROLL = 2
HEAD = 64
epsilon = 1e-12
inv_sqrt_two = 0.7071067811865476
inv_sqrt_tau = 0.3989422804014327
f32 = jnp.float32
bf16 = jnp.bfloat16
NN = (((1,), (0,)), ((), ()))
NT = (((1,), (1,)), ((), ()))
TN = (((0,), (0,)), ((), ()))


def mm(a, b, dims=NN):
    return lax.dot_general(a, b, dims, preferred_element_type=f32)


def cost(us):
    return pl.CostEstimate(flops=int(us * 1e9), bytes_accessed=1 << 20, transcendentals=0)


def params(limit=56):
    return pltpu.CompilerParams(
        dimension_semantics=("arbitrary",), vmem_limit_bytes=limit << 20
    )


def whole(shape):
    return pl.BlockSpec(shape, lambda i, *s: (0,) * len(shape), pipeline_mode=pl.Buffered(1))


def vec(size):
    return pl.BlockSpec((size,), lambda i, *s: (0,))


VMEM = pl.BlockSpec(memory_space=pltpu.VMEM)


def far(value):
    return pltpu.with_memory_space_constraint(value, pltpu.HBM)


def apart(dims, kind=f32):
    return pltpu.HBM(dims, kind)


def near(dims, kind=f32):
    return pltpu.VMEM(dims, kind)


def shape(dims, kind=f32):
    return jax.ShapeDtypeStruct(dims, kind)


def norm_parts(values):
    centre = values - jnp.mean(values, -1, keepdims=True)
    inv_std = lax.rsqrt(jnp.mean(centre * centre, -1, keepdims=True) + epsilon)
    return centre * inv_std, inv_std


def norm_back(grad, normed, inv_std, gain):
    scaled = grad * gain
    return inv_std * (
        scaled
        - jnp.mean(scaled, -1, keepdims=True)
        - normed * jnp.mean(scaled * normed, -1, keepdims=True)
    )


def row_sum(values):
    return jnp.sum(values, 0, keepdims=True)


def one_hot(index_row, count):
    rows = lax.broadcasted_iota(jnp.int32, (count, index_row.shape[1]), 0)
    return jnp.where(rows == index_row, 1.0, 0.0).astype(bf16)


def region_forward(features, boxes, target, w_visual, w_box_t, bias, gain, shift):
    rows, feat = features.shape
    width = w_visual.shape[1]
    steps = 2
    part = feat // steps

    def kernel(f_ref, box_ref, t_ref, wv_ref, wb_ref, b_ref, g_ref, s_ref, m_ref, n_ref, i_ref, acc):
        step = pl.program_id(0)
        partial = mm(f_ref[...], wv_ref[...])

        @pl.when(step == 0)
        def _():
            acc[...] = partial + (mm(box_ref[...], wb_ref[...], TN) + b_ref[...])

        @pl.when(step > 0)
        def _():
            acc[...] += partial

        @pl.when(step == steps - 1)
        def _():
            normed, inv = norm_parts(acc[...])
            n_ref[...] = normed
            i_ref[...] = jnp.broadcast_to(inv, i_ref.shape)
            low = (normed * g_ref[...] + s_ref[...]).astype(bf16)
            m_ref[...] = mm(one_hot(t_ref[...], rows), low).astype(bf16)

    return pl.pallas_call(
        kernel,
        grid=(steps,),
        in_specs=[
            pl.BlockSpec((rows, part), lambda i: (0, i)),
            whole(boxes.shape),
            whole((1, rows)),
            pl.BlockSpec((part, width), lambda i: (i, 0)),
            whole(w_box_t.shape),
            vec(width),
            vec(width),
            vec(width),
        ],
        out_specs=[VMEM, whole((rows, width)), whole((rows, 128))],
        out_shape=[near((rows, width), bf16), apart((rows, width)), apart((rows, 128))],
        scratch_shapes=[pltpu.VMEM((rows, width), f32)],
        compiler_params=params(24),
        cost_estimate=cost(3),
        name="region_forward",
    )(far(features), far(boxes), far(target), far(w_visual), far(w_box_t), far(bias), far(gain), far(shift))


def text_qkv(text, w_qkv, qv_bias):
    rows, width = text.shape

    def kernel(t_ref, w_ref, b_ref, o_ref):
        step = pl.program_id(0)
        bias = b_ref[...] * jnp.where(step == 1, 0.0, 1.0)
        o_ref[...] = (mm(t_ref[...], w_ref[...]) + bias).astype(bf16)

    return pl.pallas_call(
        kernel,
        grid=(3,),
        in_specs=[
            whole((rows, width)),
            pl.BlockSpec((width, width), lambda i: (0, i)),
            pl.BlockSpec((1, width), lambda i: (0, i // 2)),
        ],
        out_specs=pl.BlockSpec((rows, width), lambda i: (0, i)),
        out_shape=apart((rows, 3 * width), bf16),
        compiler_params=params(12),
        cost_estimate=cost(3),
        name="text_qkv",
    )(far(text), far(w_qkv), qv_bias)


def forward(
    scalars, text, text_low, arrived, source, out_grad, w_qkv, qv_bias, w_out, out_bias,
    attn_gain, attn_shift, w_up, up_bias, w_down, down_bias, ffn_gain, ffn_shift, dims,
):
    captions, images = dims
    width = text.shape[1]
    text_len = text.shape[0] // captions
    slots = arrived.shape[0]
    regions = slots // images
    seq = text_len + regions
    rows = captions * seq
    ff = w_up.shape[1]
    half = width // 2
    parts = 4
    part = ff // parts
    grid = captions + parts

    def kernel(
        sc_ref, t_ref, tq_ref, a_ref, src_ref, og_ref, wq_far, qvb_ref, wo_far, ob_ref, ag_ref, as_ref,
        wu_far, ub_ref, wd_far, db_ref, fg_ref, fs_ref,
        out_ref, x_ref, qkv_ref, probs_ref, ctx_ref, an_ref, ai_ref, hid_ref, slope_ref, ds_ref, df_ref,
        sums_ref, wu, wd, send_ref, keep_ref,
        regs, rqkv, act_all, wq, wo, sems,
    ):
        step = pl.program_id(0)

        def third(at):
            cols = slice(at * width, (at + 1) * width)
            return pltpu.make_async_copy(wq_far.at[:, cols], wq.at[:, cols], sems.at[at])

        def load(at):
            source, target = ((wo_far, wo), (wu_far, wu), (wd_far, wd))[at]
            return pltpu.make_async_copy(source, target, sems.at[3 + at])

        @pl.when(step == 0)
        def _():
            for at in range(3):
                third(at).start()
            load(0).start()
            sums_ref[...] = jnp.zeros_like(sums_ref)
            local = mm(one_hot(src_ref[...], slots), a_ref[...], TN).astype(bf16)
            regs[...] = local
            for part_id in range(3):
                at = slice(part_id * width, (part_id + 1) * width)
                third(part_id).wait()
                if part_id == 2:
                    load(1).start()
                    load(2).start()
                got = mm(local, wq[:, at])
                if part_id == 0:
                    got = got + qvb_ref[:, :width]
                if part_id == 2:
                    got = got + qvb_ref[:, width:]
                rqkv[:, at] = got.astype(bf16)

        @pl.when(step < captions)
        def _():
            image = sc_ref[8 + step]
            length = sc_ref[8 + captions + step]
            count = sc_ref[8 + 2 * captions + image]
            at = pl.ds(pl.multiple_of(image * regions, regions), regions)
            here = pl.ds(pl.multiple_of(step * seq, seq), seq)
            x_ref[:text_len, :] = t_ref[...]
            x_ref[text_len:, :] = regs[at, :]
            qkv_ref[:text_len, :] = tq_ref[...]
            qkv_ref[text_len:, :] = rqkv[at, :]
            place = lax.broadcasted_iota(jnp.int32, (seq, 1), 0)
            row_end = jnp.where(place < text_len, length, text_len + count)
            row_mask = jnp.where(place < row_end, 1.0, 0.0)
            key_mask = jnp.broadcast_to(row_mask, (seq, 2 * seq)) > 0.5
            first = lax.broadcasted_iota(jnp.int32, (1, 2 * HEAD), 1) < HEAD
            scale = [
                jnp.where(first, 0.125, 0.0).astype(bf16),
                jnp.where(first, 0.0, 0.125).astype(bf16),
            ]
            def pair_forward(pair, carry):
                def cols(base):
                    return pl.ds(pl.multiple_of(base + pair * 2 * HEAD, 2 * HEAD), 2 * HEAD)

                q = qkv_ref[:, cols(0)]
                k = qkv_ref[:, cols(width)]
                v = qkv_ref[:, cols(2 * width)]
                scores = mm(k, jnp.concatenate([q * scale[0], q * scale[1]], 0), NT)
                scores = jnp.where(key_mask, scores, -1e30)
                raised = jnp.exp(scores - jnp.max(scores, 0, keepdims=True))
                low = (raised * (1.0 / jnp.sum(raised, 0, keepdims=True))).astype(bf16)
                probs_ref[pair] = low
                outs = mm(low, v, TN)
                ctx_ref[:, cols(0)] = jnp.where(first, outs[:seq], outs[seq:]).astype(bf16)
                return carry

            lax.fori_loop(0, HEADS // 2, pair_forward, 0, unroll=3)

            @pl.when(step == 0)
            def _():
                load(0).wait()

            x_wide = x_ref[...].astype(f32)
            attn_out = mm(ctx_ref[...], wo[...]) + ob_ref[...]
            normed, inv = norm_parts(x_wide + attn_out)
            an_ref[here, :] = normed
            ai_ref[here, :] = jnp.broadcast_to(inv, (seq, 128))
            hidden = normed * ag_ref[...] + as_ref[...]
            hidden_low = hidden.astype(bf16)
            hid_ref[here, :] = hidden_low

            @pl.when(step == 0)
            def _():
                load(1).wait()

            for piece in range(parts):
                at = slice(piece * part, (piece + 1) * part)
                upper = mm(hidden_low, wu[:, at]) + ub_ref[:, at]
                phi = 0.5 * (1.0 + lax.erf(upper * inv_sqrt_two))
                act_all[here, at] = (upper * phi).astype(bf16)
                slope = phi + upper * jnp.exp(-0.5 * upper * upper) * inv_sqrt_tau
                slope_ref[here, at] = slope.astype(bf16)
                if piece == 0:

                    @pl.when(step == 0)
                    def _():
                        load(2).wait()

                term = mm(act_all[here, at], wd[at, :])
                ffn_sum = term if piece == 0 else ffn_sum + term

            ffn_out = ffn_sum + db_ref[...]
            ffn_normed, ffn_inv = norm_parts(hidden + ffn_out)
            out_ref[...] = ((ffn_normed * fg_ref[...] + fs_ref[...]) * row_mask).astype(bf16)
            cot = og_ref[...].astype(f32) * row_mask
            second = norm_back(cot, ffn_normed, ffn_inv, fg_ref[...])
            ds_ref[here, :] = second
            low = second.astype(bf16)
            df_ref[here, :] = low
            for at, value in enumerate(
                (
                    cot * ffn_normed,
                    cot,
                    low.astype(f32),
                    row_mask * x_wide * x_wide,
                    row_mask * attn_out * attn_out,
                    row_mask * ffn_out * ffn_out,
                )
            ):
                sums_ref[at : at + 1, :] += row_sum(value)
            lane = lax.broadcasted_iota(jnp.int32, (1, width), 1)
            slots_here = ((length + count) * width).astype(f32)
            sums_ref[6:7, :] += jnp.where(lane == 0, slots_here, 0.0)

        @pl.when(step >= captions)
        def _():
            acts = pl.ds(pl.multiple_of((step - captions) * part, part), part)
            got = mm(act_all[:, acts], df_ref[...], TN)
            mine = sc_ref[0] == 0
            send_ref[...] = jnp.where(mine, got[:, half:], got[:, :half]).astype(bf16)
            keep_ref[...] = jnp.where(mine, got[:, :half], got[:, half:]).astype(bf16)

    def rowwise(size, cols):
        return pl.BlockSpec((size, cols), lambda i, s: (jnp.minimum(i, captions - 1), 0))

    anywhere = pl.BlockSpec(memory_space=pl.ANY)
    return pl.pallas_call(
        kernel,
        grid_spec=pltpu.PrefetchScalarGridSpec(
            num_scalar_prefetch=1,
            grid=(grid,),
            in_specs=[
                rowwise(text_len, width),
                rowwise(text_len, 3 * width),
                VMEM,
                whole((1, slots)),
                rowwise(seq, width),
                anywhere,
                whole((1, 2 * width)),
                anywhere,
                vec(width),
                vec(width),
                vec(width),
                anywhere,
                whole((1, ff)),
                anywhere,
                vec(width),
                vec(width),
                vec(width),
            ],
            out_specs=[rowwise(seq, width), rowwise(seq, width), rowwise(seq, 3 * width)]
            + [pl.BlockSpec((HEADS // 2, seq, 2 * seq), lambda i, s: (jnp.minimum(i, captions - 1), 0, 0))]
            + [rowwise(seq, width)]
            + [VMEM] * 9
            + [pl.BlockSpec((part, half), lambda i, s: (jnp.maximum(i - captions, 0), 0))] * 2,
            scratch_shapes=[
                pltpu.VMEM((slots, width), bf16),
                pltpu.VMEM((slots, 3 * width), bf16),
                pltpu.VMEM((rows, ff), bf16),
                pltpu.VMEM(w_qkv.shape, bf16),
                pltpu.VMEM(w_out.shape, bf16),
                pltpu.SemaphoreType.DMA((6,)),
            ],
        ),
        out_shape=[
            apart((rows, width), bf16),
            apart((rows, width), bf16),
            apart((rows, 3 * width), bf16),
            apart((captions * HEADS // 2, seq, 2 * seq), bf16),
            apart((rows, width), bf16),
            near((rows, width)),
            near((rows, 128)),
            near((rows, width), bf16),
            near((rows, ff), bf16),
            near((rows, width)),
            near((rows, width), bf16),
            near((8, width)),
            near(w_up.shape, bf16),
            near(w_down.shape, bf16),
            apart((ff, half), bf16),
            apart((ff, half), bf16),
        ],
        compiler_params=params(33),
        cost_estimate=cost(30),
        name="forward",
    )(
        scalars,
        far(text),
        far(text_low),
        arrived,
        *(
            far(v)
            for v in (
                source, out_grad, w_qkv, qv_bias, w_out, out_bias,
                attn_gain, attn_shift, w_up, up_bias, w_down, down_bias, ffn_gain, ffn_shift,
            )
        ),
    )


def ffn_backward(core, d_ffn, d_second, slope, attn_normed, attn_inv, w_down, w_up, attn_gain, seq, hold, first, size, begun):
    rows, width = d_ffn.shape
    ff = w_up.shape[1]
    parts = 4
    part = ff // parts

    def kernel(c_ref, df_ref, ds_ref, sl_ref, an_ref, ai_ref, wd, wu, ag_ref, *rest):
        dup_ref, dr_ref, da_ref, sums_ref, up_ref = rest[len(begun) + len(hold) :]
        step = pl.program_id(0)

        @pl.when(step == 0)
        def _():
            if begun:
                sums_ref[...] = rest[3][...]
                up_ref[...] = rest[4][...]
            else:
                sums_ref[...] = jnp.zeros_like(sums_ref)
                up_ref[...] = jnp.zeros_like(up_ref)

        here = pl.ds(pl.multiple_of((first + step) * seq, seq), seq)
        d_low = df_ref[here, :]
        for piece in range(parts):
            at = slice(piece * part, (piece + 1) * part)
            d_act = mm(d_low, wd[at, :], NT)
            low = (d_act * sl_ref[here, at].astype(f32)).astype(bf16)
            dup_ref[here, at] = low
            up_ref[0:1, at] += row_sum(low.astype(f32))
            term = mm(low, wu[:, at], NT)
            through = term if piece == 0 else through + term
        d_hidden = ds_ref[here, :] + through
        normed = an_ref[here, :]
        resid = norm_back(d_hidden, normed, ai_ref[here, 0:1], ag_ref[...])
        dr_ref[here, :] = resid
        low = resid.astype(bf16)
        da_ref[here, :] = low
        sums_ref[0:1, :] += row_sum(d_hidden * normed)
        sums_ref[1:2, :] += row_sum(d_hidden)
        sums_ref[2:3, :] += row_sum(low.astype(f32))

    return pl.pallas_call(
        kernel,
        grid_spec=pltpu.PrefetchScalarGridSpec(
            num_scalar_prefetch=1,
            grid=(size,),
            in_specs=[VMEM] * 7
            + [vec(width)]
            + [VMEM] * len(begun)
            + [VMEM] * len(hold),
            out_specs=[VMEM] * 5,
        ),
        out_shape=[
            near((rows, ff), bf16),
            near((rows, width)),
            near((rows, width), bf16),
            near((8, width)),
            near((8, ff)),
        ],
        input_output_aliases={9: 0, 10: 1, 11: 2} if begun else {},
        compiler_params=params(6),
        cost_estimate=cost(4 * size),
        name="ffn_backward",
    )(core, d_ffn, d_second, slope, attn_normed, attn_inv, w_down, w_up, attn_gain, *begun, *hold)


def up_gradient(core, hidden_low, d_upper):
    rows, width = hidden_low.shape

    def kernel(c_ref, h_ref, d_ref, send_ref, keep_ref):
        step = pl.program_id(0)
        here = pl.ds(pl.multiple_of(step * width, width), width)
        for to_ref, side in ((send_ref, 1 - c_ref[0]), (keep_ref, c_ref[0])):
            cols = pl.ds(pl.multiple_of((2 * side + step) * width, width), width)
            to_ref[:, here] = mm(h_ref[...], d_ref[:, cols], TN).astype(bf16)

    return pl.pallas_call(
        kernel,
        grid_spec=pltpu.PrefetchScalarGridSpec(
            num_scalar_prefetch=1, grid=(2,), in_specs=[VMEM, VMEM], out_specs=[VMEM, VMEM]
        ),
        out_shape=[near((width, 2 * width), bf16)] * 2,
        compiler_params=params(6),
        cost_estimate=cost(0.1),
        name="up_gradient",
    )(core, hidden_low, d_upper)


def attention_backward(scalars, d_attn, d_resid, probs, qkv, source, w_out, w_qkv, dims, first_caption, size, begun):
    captions, images = dims
    rows, width = d_attn.shape
    seq = rows // captions
    slots = source.shape[1]
    regions = slots // images
    text_len = seq - regions
    last = first_caption + size == captions

    def kernel(
        sc_ref, da_ref, dr_ref, p_ref, qkv_ref, src_ref, wo_ref, wq, *rest,
    ):
        begun_refs = rest[: len(begun)]
        dqkv_ref, text_ref, back_ref, sums_ref, d_img, d_ctx_ref = rest[len(begun) :]
        step = pl.program_id(0)
        here = pl.ds(pl.multiple_of((first_caption + step) * seq, seq), seq)

        @pl.when(step == 0)
        def _():
            if begun:
                sums_ref[...] = begun_refs[3][...]
                d_img[...] = begun_refs[2][...]
            else:
                sums_ref[...] = jnp.zeros_like(sums_ref)
                d_img[...] = jnp.zeros_like(d_img)

        d_ctx_ref[...] = mm(da_ref[here, :], wo_ref[...], NT).astype(bf16)
        first = lax.broadcasted_iota(jnp.int32, (1, 2 * HEAD), 1) < HEAD
        masks = [jnp.where(first, 1.0, 0.0).astype(bf16), jnp.where(first, 0.0, 1.0).astype(bf16)]
        def pair_backward(pair, carry):
            def cols(base):
                return pl.ds(pl.multiple_of(base + pair * 2 * HEAD, 2 * HEAD), 2 * HEAD)

            q = qkv_ref[here, cols(0)]
            k = qkv_ref[here, cols(width)]
            v = qkv_ref[here, cols(2 * width)]
            d_c = d_ctx_ref[:, cols(0)]
            both_c = jnp.concatenate([d_c * masks[0], d_c * masks[1]], 0)
            both_q = jnp.concatenate([q * masks[0], q * masks[1]], 0)
            low = p_ref[pair]
            d_probs = mm(v, both_c, NT)
            wide = low.astype(f32)
            both = wide * d_probs
            inner = jnp.sum(both, 0, keepdims=True)
            d_scores = (both - wide * inner).astype(bf16)
            d_q = mm(d_scores, k, TN) * 0.125
            dqkv_ref[here, cols(0)] = jnp.where(first, d_q[:seq], d_q[seq:]).astype(bf16)
            dqkv_ref[here, cols(width)] = (mm(d_scores, both_q) * 0.125).astype(bf16)
            dqkv_ref[here, cols(2 * width)] = mm(low, both_c).astype(bf16)
            return carry

        lax.fori_loop(0, HEADS // 2, pair_backward, 0, unroll=3)

        sums_ref[0:1, :] += row_sum(dqkv_ref[here, :width].astype(f32))
        sums_ref[1:2, :] += row_sum(dqkv_ref[here, 2 * width :].astype(f32))
        d_x = mm(dqkv_ref[here, :], wq[...], NT) + dr_ref[here, :]
        text_ref[...] = d_x[:text_len]
        at = pl.ds(pl.multiple_of(sc_ref[8 + first_caption + step] * regions, regions), regions)
        d_img[at, :] += d_x[text_len:]

        @pl.when(step == size - 1)
        def _():
            if last:
                back_ref[...] = mm(one_hot(src_ref[...], slots), d_img[...].astype(bf16)).astype(bf16)
            else:
                back_ref[...] = d_img[...]

    return pl.pallas_call(
        kernel,
        grid_spec=pltpu.PrefetchScalarGridSpec(
            num_scalar_prefetch=1,
            grid=(size,),
            in_specs=[VMEM] * 2
            + [pl.BlockSpec((HEADS // 2, seq, 2 * seq), lambda i, s: (i + first_caption, 0, 0)), VMEM]
            + [whole((1, slots)), VMEM, VMEM]
            + ([VMEM, pl.BlockSpec(memory_space=pl.ANY)] + [VMEM, VMEM] if begun else []),
            out_specs=[
                VMEM,
                pl.BlockSpec((text_len, width), lambda i, s: (i + first_caption, 0)),
                VMEM,
                VMEM,
            ],
            scratch_shapes=[
                pltpu.VMEM((slots, width), f32),
                pltpu.VMEM((seq, width), bf16),
            ],
        ),
        out_shape=[
            near((rows, 3 * width), bf16),
            pltpu.HBM((captions * text_len, width), f32),
            near((slots, width), bf16 if last else f32),
            near((8, width)),
        ],
        input_output_aliases={8: 0, 9: 1} if begun else {},
        compiler_params=params(15),
        cost_estimate=cost(5 * size),
        name="attention_backward",
    )(scalars, d_attn, d_resid, far(probs), qkv, source, w_out, w_qkv, *begun)


def qkvo_gradient(core, x, d_qkv, context, d_attn):
    rows, width = x.shape

    def kernel(c_ref, x_ref, dq_ref, ctx_ref, da_ref, send_ref, keep_ref):
        step = pl.program_id(0)

        def store(low_block, high_block):
            low, high = low_block.astype(bf16), high_block.astype(bf16)

            @pl.when(c_ref[0] == 0)
            def _():
                keep_ref[...] = low
                send_ref[...] = high

            @pl.when(c_ref[0] != 0)
            def _():
                send_ref[...] = low
                keep_ref[...] = high

        @pl.when(step == 0)
        def _():
            store(mm(x_ref[...], dq_ref[:, :width], TN), mm(x_ref[...], dq_ref[:, 2 * width :], TN))

        @pl.when(step == 1)
        def _():
            store(mm(x_ref[...], dq_ref[:, width : 2 * width], TN), mm(ctx_ref[...], da_ref[...], TN))

    out = pl.BlockSpec((width, width), lambda i, s: (0, i))
    return pl.pallas_call(
        kernel,
        grid_spec=pltpu.PrefetchScalarGridSpec(
            num_scalar_prefetch=1, grid=(2,), in_specs=[VMEM] * 4, out_specs=[out, out]
        ),
        out_shape=[apart((width, 2 * width), bf16)] * 2,
        compiler_params=params(14),
        cost_estimate=cost(5),
        name="qkvo_gradient",
    )(core, x, d_qkv, context, d_attn)


def region_norm_backward(
    core, returned, target, normed, inv, gain, boxes, w_box_t, sums_forward, sums_ffn, sums_up, sums_attn, groups
):
    rows, width = returned.shape
    half = width // 2
    box = boxes.shape[0]
    share = width // groups
    ff_share = sums_up.shape[1] // groups

    def kernel(
        c_ref, r_ref, t_ref, n_ref, i_ref, g_ref, box_ref, wb_ref, sf_ref, sn_ref, su_ref, sa_ref,
        all_ref, send_ref, keep_ref, small_ref, bg_ref, small,
    ):
        d_region = mm(one_hot(t_ref[...], rows), r_ref[...], TN)
        normed = n_ref[...]
        low = norm_back(d_region, normed, i_ref[:, 0:1], g_ref[...]).astype(bf16)
        all_ref[...] = low
        mine = c_ref[0] == 0
        send_ref[:rows, :] = jnp.where(mine, low[:, half:], low[:, :half])
        keep_ref[...] = jnp.where(mine, low[:, :half], low[:, half:])
        bg_ref[...] = mm(wb_ref[...], low, NT)
        boxes_grad = mm(box_ref[...], low)
        vectors = [
            row_sum(low.astype(f32)),
            row_sum(d_region * normed),
            row_sum(d_region),
            sf_ref[0:1, :],
            sf_ref[1:2, :],
            sf_ref[2:3, :],
            sn_ref[0:1, :],
            sn_ref[1:2, :],
            sn_ref[2:3, :],
        ] + [boxes_grad[at : at + 1] for at in range(box)]
        small[...] = jnp.zeros_like(small)
        lane = lax.broadcasted_iota(jnp.int32, (1, half), 1)
        stats = jnp.zeros((1, half), f32)
        for at in range(4):
            total = jnp.sum(sf_ref[3 + at : 4 + at, :], 1, keepdims=True)
            stats = jnp.where(lane == at, total, stats)
        flat = jnp.concatenate([sa_ref[0:1, :], sa_ref[1:2, :]], 1)
        for group in range(groups):
            small[group, 0:1, 0:ff_share] = su_ref[0:1, group * ff_share : (group + 1) * ff_share]
            small[group, 1:2, 0 : 2 * share] = flat[:, group * 2 * share : (group + 1) * 2 * share]
            for at, value in enumerate(vectors):
                row, col = (1, 2) if at == 0 else (2 + (at - 1) // 3, (at - 1) % 3)
                small[group, row : row + 1, 128 * col : 128 * col + share] = value[
                    :, group * share : (group + 1) * share
                ]
            small[group, 6:7, :] = stats
        small_ref[...] = small[...].astype(bf16)
        for group in range(groups):
            send_ref[rows + 8 * group : rows + 8 * (group + 1), :] = small_ref[group]

    sizes = (sums_forward, sums_ffn, sums_up, sums_attn)
    return pl.pallas_call(
        kernel,
        grid_spec=pltpu.PrefetchScalarGridSpec(
            num_scalar_prefetch=1,
            grid=(1,),
            in_specs=[
                whole((rows, width)),
                whole((1, rows)),
                whole((rows, width)),
                whole((rows, 128)),
                vec(width),
                whole(boxes.shape),
                whole(w_box_t.shape),
            ]
            + [whole(v.shape) for v in sizes],
            out_specs=[VMEM] * 4 + [whole((box, rows))],
            scratch_shapes=[pltpu.VMEM((groups, 8, half), f32)],
        ),
        out_shape=[
            near((rows, width), bf16),
            near((rows + 8 * groups, half), bf16),
            near((rows, half), bf16),
            near((groups, 8, half), bf16),
            shape((box, rows)),
        ],
        compiler_params=params(14),
        cost_estimate=cost(0.1),
        name="region_norm_backward",
    )(core, returned, far(target), far(normed), far(inv), far(gain), far(boxes), far(w_box_t), *sizes)


def visual_gradient(bits, features, other_features, d_pre, other_d_pre, small, groups):
    rows, feat = features.shape
    half = d_pre.shape[1]
    steps = 2
    part = feat // steps
    quarter = feat // groups // 4
    tall = quarter + 8
    per_step = groups // steps
    high = groups // 2

    def kernel(b_ref, f_ref, o_ref, d_ref, p_ref, s_ref, a_send, a_keep, b_send, b_keep, got):
        step = pl.program_id(0)
        bit2, bit4 = b_ref[1], b_ref[2]
        got[...] = mm(f_ref[...], d_ref[...], TN) + mm(o_ref[...], p_ref[:rows, :], TN)

        def fill(to_ref, at, which, group, x, piece):
            here = pl.ds(pl.multiple_of(((group * 2 + x) * 2 + piece) * quarter, 8), quarter)
            to_ref[at, which, :quarter, :] = got[here, :].astype(bf16)
            number = step * per_step + group
            other = p_ref[pl.ds(pl.multiple_of(rows + 8 * number, 8), 8), :]
            to_ref[at, which, quarter:, :] = add(s_ref[number], other)

        for group in range(per_step):
            y = group % 2
            at = step * (per_step // 2) + group // 2
            fill(a_send, at, y, group, 1 - bit2, 0)
            fill(a_keep, at, y, group, bit2, 0)

            @pl.when(bit4 == y)
            def _():
                for x in range(2):
                    fill(b_keep, at, x, group, x, 1)

            @pl.when(bit4 != y)
            def _():
                for x in range(2):
                    fill(b_send, at, x, group, x, 1)

    return pl.pallas_call(
        kernel,
        grid_spec=pltpu.PrefetchScalarGridSpec(
            num_scalar_prefetch=1,
            grid=(steps,),
            in_specs=[
                pl.BlockSpec((rows, part), lambda i, s: (0, i)),
                pl.BlockSpec((rows, part), lambda i, s: (0, i)),
                VMEM,
                VMEM,
                VMEM,
            ],
            out_specs=[VMEM] * 4,
            scratch_shapes=[pltpu.VMEM((part, half), f32)],
        ),
        out_shape=[near((high, 2, tall, half), bf16)] * 4,
        compiler_params=params(14),
        cost_estimate=cost(0.1),
        name="visual_gradient",
    )(bits, far(features), far(other_features), d_pre, other_d_pre, small)


def feature_gradient(bits, d_pre, w_visual):
    rows, width = d_pre.shape
    feat = w_visual.shape[0]
    steps = 4
    part = feat // steps

    def kernel(b_ref, d_ref, w_ref, o_ref):
        o_ref[...] = mm(d_ref[...], w_ref[...], NT)

    return pl.pallas_call(
        kernel,
        grid_spec=pltpu.PrefetchScalarGridSpec(
            num_scalar_prefetch=1,
            grid=(steps,),
            in_specs=[VMEM, pl.BlockSpec((part, width), lambda i, s: (i, 0))],
            out_specs=pl.BlockSpec((rows, part), lambda i, s: (0, i)),
        ),
        out_shape=shape((rows, feat)),
        compiler_params=params(8),
        cost_estimate=cost(10),
        name="feature_gradient",
    )(bits, d_pre, far(w_visual))


def device_number():
    return lax.axis_index("dp") * lax.axis_size("enc") + lax.axis_index("enc")


def swap(values, bit):
    count = lax.axis_size("dp") * lax.axis_size("enc")
    return lax.ppermute(values, ("dp", "enc"), [(i, i ^ bit) for i in range(count)])


def add(a, b):
    return (a.astype(f32) + b.astype(f32)).astype(bf16)


def scalar_call(kernel, bits, ins, in_specs, outs, out_specs, grid, limit, name, last=False, place=near):
    outs = outs if last else [place(o.shape, o.dtype) for o in outs]
    return pl.pallas_call(
        kernel,
        grid_spec=pltpu.PrefetchScalarGridSpec(
            num_scalar_prefetch=1, grid=(grid,), in_specs=in_specs, out_specs=out_specs
        ),
        out_shape=outs,
        compiler_params=params(limit),
        cost_estimate=cost(1),
        name=name,
    )(bits, *ins)


def first_split(bits, kept, got, groups, place=near):
    tall = kept.ndim == 5
    high = groups // 2
    if tall:
        rows, cols = kept.shape[3:]
        view = (high, 2, 2, 2, rows, cols)
        block = (1, 2, 2, 2, rows, cols)
    else:
        rows, cols = kept.shape[0] // groups, kept.shape[1] // 4
        view = (high, 2, rows, 4 * cols)
        block = (1, 2, rows, 4 * cols)

    def kernel(b_ref, k_ref, r_ref, a_send, a_keep, b_send, b_keep):
        bit2, bit4 = b_ref[1], b_ref[2]

        def total(y, x, piece):
            if tall:
                return add(k_ref[0, y, x, piece], r_ref[0, y, x, piece])
            at = pl.ds(pl.multiple_of((2 * x + piece) * cols, 128), cols)
            return add(k_ref[0, y, :, at], r_ref[0, y, :, at])

        for other in range(2):
            a_send[0, other] = total(other, 1 - bit2, 0)
            a_keep[0, other] = total(other, bit2, 0)
            b_send[0, other] = total(1 - bit4, other, 1)
            b_keep[0, other] = total(bit4, other, 1)

    spec = pl.BlockSpec(block, lambda i, s: (i,) + (0,) * (len(block) - 1))
    out = pl.BlockSpec((1, 2, rows, cols), lambda i, s: (i, 0, 0, 0))
    return scalar_call(
        kernel, bits, (kept.reshape(view), got.reshape(view)), [spec, spec],
        [shape((high, 2, rows, cols), bf16)] * 4, [out] * 4, high, 6, "first_split", place=place,
    )


def second_split(bits, a_kept, a_got, b_kept, b_got):
    high, _, rows, cols = a_kept.shape

    def kernel(b_ref, ak, ar, bk, br, a_send, a_keep, b_send, b_keep):
        bit2, bit4 = b_ref[1], b_ref[2]
        a_send[0] = add(ak[0, 1 - bit4], ar[0, 1 - bit4])
        a_keep[0] = add(ak[0, bit4], ar[0, bit4])
        b_send[0] = add(bk[0, 1 - bit2], br[0, 1 - bit2])
        b_keep[0] = add(bk[0, bit2], br[0, bit2])

    spec = pl.BlockSpec((1, 2, rows, cols), lambda i, s: (i, 0, 0, 0))
    out = pl.BlockSpec((1, rows, cols), lambda i, s: (i, 0, 0))
    return scalar_call(
        kernel, bits, (a_kept, a_got, b_kept, b_got), [spec] * 4,
        [shape((high, rows, cols), bf16)] * 4, [out] * 4, high, 6, "second_split",
    )


def join_split(bits, pairs, place=near):
    high, _, cols = pairs[0][0].shape
    sizes = [kept.shape[1] for kept, _ in pairs]

    def kernel(b_ref, *refs):
        bit = b_ref[3]
        send, keep = refs[-2:]
        at = 0
        for n, size in enumerate(sizes):
            kept, got = refs[2 * n : 2 * n + 2]
            send[0, at : at + size] = add(kept[1 - bit], got[1 - bit])
            keep[0, at : at + size] = add(kept[bit], got[bit])
            at += size

    ins = [value for pair in pairs for value in pair]
    specs = [pl.BlockSpec((2, v.shape[1], cols), lambda i, s: (i, 0, 0)) for v in ins]
    out = pl.BlockSpec((1, sum(sizes), cols), lambda i, s: (i, 0, 0))
    return scalar_call(
        kernel, bits, ins, specs, [shape((high // 2, sum(sizes), cols), bf16)] * 2, [out] * 2,
        high // 2, 6, "join_split", place=place,
    )


def late_split(bits, kept, got, which):
    high, rows, cols = kept.shape

    def kernel(b_ref, k_ref, r_ref, send, keep):
        bit = b_ref[which]
        send[0] = add(k_ref[1 - bit], r_ref[1 - bit])
        keep[0] = add(k_ref[bit], r_ref[bit])

    spec = pl.BlockSpec((2, rows, cols), lambda i, s: (i, 0, 0))
    out = pl.BlockSpec((1, rows, cols), lambda i, s: (i, 0, 0))
    return scalar_call(
        kernel, bits, (kept, got), [spec] * 2, [shape((high // 2, rows, cols), bf16)] * 2, [out] * 2,
        high // 2, 6, "late_split",
    )


def over_two(halves):
    return swap(halves[0], 2), halves[1], swap(halves[2], 4), halves[3]


def over_other_two(halves):
    return swap(halves[0], 4), halves[1], swap(halves[2], 2), halves[3]


def second(bits, moved):
    return second_split(bits, moved[1], moved[0], moved[3], moved[2])


def join(bits, *moved, place=near):
    pairs = []
    for one in moved:
        pairs += [(one[1], one[0]), (one[3], one[2])]
    return join_split(bits, pairs, place)


def after_all(*trees):
    leaves, tree = jax.tree.flatten(trees)
    return jax.tree.unflatten(tree, lax.optimization_barrier(leaves))


def late_first(bits, kept, got):
    if kept.shape[0] == 1:
        return (kept + got,)
    return late_split(bits, kept, got, 4)


def late_move(halves):
    return swap(halves[0], 16) if len(halves) > 1 else None


def late_rest(bits, halves, moved):
    bit, which = 16, 5
    while len(halves) > 1:
        if halves[1].shape[0] == 1:
            halves = (halves[1] + moved,)
        else:
            halves = late_split(bits, halves[1], moved, which)
            bit, which = 2 * bit, which + 1
            moved = swap(halves[0], bit)
    return halves[0][0]


def spread(mine, *late):
    over_x = swap(mine, 2)
    over_core = swap(mine, 1)
    return mine, over_x, over_core, swap(gate(over_x, *late), 1)


def pick(b_ref, pieces, core, x):
    mine, over_x, over_core, over_both = pieces
    same_x = b_ref[1] == x
    return jnp.where(
        b_ref[0] == core, jnp.where(same_x, mine, over_x), jnp.where(same_x, over_core, over_both)
    ).astype(f32)


def finish_ffn(bits, pieces):
    rows, cols = pieces[0].shape
    half = rows // 2
    part = rows // 4

    def kernel(b_ref, p0, p1, p2, p3, down_ref, up_ref):
        for core in range(2):
            for x in range(2):
                got = pick(b_ref, (p0[...], p1[...], p2[...], p3[...]), core, x)
                down_ref[x * half : (x + 1) * half, core * cols : (core + 1) * cols] = got[:half]
                for piece in range(2):
                    at = ((core * 2 + x) * 2 + piece) * cols
                    up_ref[:, at : at + cols] = got[half + piece * part : half + (piece + 1) * part]

    outs = [shape((rows, 2 * cols)), shape((part, 8 * cols))]
    return scalar_call(
        kernel, bits, pieces, [whole((rows, cols))] * 4, outs, [whole(o.shape) for o in outs], 1, 12, "finish_ffn", True
    )


def finish_wide(bits, pieces, sizes):
    rows, cols = pieces[0].shape
    part = rows // 2

    def kernel(b_ref, p0, p1, p2, p3, *out_refs):
        for core in range(2):
            for x in range(2):
                got = pick(b_ref, (p0[...], p1[...], p2[...], p3[...]), core, x)
                for piece in range(2):
                    at = ((core * 2 + x) * 2 + piece) * cols
                    for out_ref, size in zip(out_refs, sizes):
                        if 0 <= at < size:
                            out_ref[:, at : at + cols] = got[piece * part : (piece + 1) * part]
                        at -= size

    outs = [shape((part, size)) for size in sizes]
    return scalar_call(
        kernel, bits, pieces, [whole((rows, cols))] * 4, outs, [whole(o.shape) for o in outs], 1, 8, "finish_wide", True
    )


def finish_visual(bits, pieces, ff_share, share, box):
    rows, cols = pieces[0].shape
    tall = rows // 2
    quarter = tall - 8
    sizes = [share] * 9 + [2 * share, ff_share]

    def kernel(b_ref, p0, p1, p2, p3, vis_ref, box_ref, rms_ref, *small_refs):
        for core in range(2):
            for x in range(2):
                got = pick(b_ref, (p0[...], p1[...], p2[...], p3[...]), core, x)
                for piece in range(2):
                    low = piece * tall
                    vis_ref[(2 * x + piece) * quarter : (2 * x + piece + 1) * quarter, core * cols : (core + 1) * cols] = got[
                        low : low + quarter
                    ]
        small = p0[quarter : quarter + 8, :].astype(f32)
        for at in range(9):
            row, col = (1, 2) if at == 0 else (2 + (at - 1) // 3, (at - 1) % 3)
            small_refs[at][...] = small[row, 128 * col : 128 * col + share]
        small_refs[9][...] = small[1, 0 : 2 * share]
        small_refs[10][...] = small[0, 0:ff_share]
        for at in range(9, 9 + box):
            row, col = 2 + (at - 1) // 3, (at - 1) % 3
            box_ref[at - 9 : at - 8, :] = small[row : row + 1, 128 * col : 128 * col + share]
        stats = small[6, 0:128]
        total = jnp.sum(small[6:7, 3:4])
        rms_ref[...] = jnp.sqrt(stats / total)[:3]

    outs = [shape((4 * quarter, 2 * cols)), shape((box, share)), shape((3,))] + [shape((size,)) for size in sizes]
    specs = [whole(o.shape) for o in outs[:2]] + [vec(3)] + [vec(size) for size in sizes]
    return scalar_call(
        kernel, bits, pieces, [whole((rows, cols))] * 4, outs, specs, 1, 8, "finish_visual", True
    )


def gate(value, *others):
    return lax.optimization_barrier((value, *others))[0]


def on_device(
    text_embed,
    region_features,
    boxes,
    caption_image,
    caption_lengths,
    region_counts,
    region_target,
    region_source,
    w_visual,
    w_box,
    visual_bias,
    visual_gain,
    visual_shift,
    w_qkv,
    qv_bias,
    w_out,
    out_bias,
    attn_gain,
    attn_shift,
    w_up,
    up_bias,
    w_down,
    down_bias,
    ffn_gain,
    ffn_shift,
    out_grad,
):
    width = text_embed.shape[1]
    captions = caption_image.shape[0]
    images = region_counts.shape[0]
    dims = (captions, images)
    axes = ("dp", "enc")
    groups = lax.axis_size("dp")
    count = groups * lax.axis_size("enc")
    me = device_number().astype(jnp.int32)
    places = lax.iota(jnp.int32, 8)
    scalars = jnp.concatenate([(me >> places) & 1, caption_image, caption_lengths, region_counts])
    w_box_t = w_box.T
    row = lambda v: v.reshape(1, -1)
    qv_row = row(qv_bias)

    message, vis_normed, vis_inv = region_forward(
        region_features, boxes, region_target, w_visual, w_box_t, visual_bias, visual_gain, visual_shift
    )
    arrived = lax.all_to_all(message, axes, split_axis=0, concat_axis=0, tiled=True)
    text_low = text_qkv(text_embed, w_qkv, qv_row)
    (
        out_rows, x, qkv, probs, context, attn_normed, attn_inv, hidden_low, slope, d_second, d_ffn,
        sums_forward, w_up_near, w_down_near, down_sent, down_kept,
    ) = forward(
        scalars, text_embed, text_low, arrived, region_source, out_grad, w_qkv, qv_row, w_out,
        out_bias, attn_gain, attn_shift, w_up, row(up_bias), w_down, down_bias, ffn_gain, ffn_shift, dims,
    )
    seq = x.shape[0] // captions
    rest = captions - 1
    bits = core = scalars
    hold = ()
    ffn_ins = (d_ffn, d_second, slope, attn_normed, attn_inv, w_down_near, w_up_near, attn_gain, seq, hold)
    down_view = (groups, 2, 2, w_down.shape[0] // groups // 4, width // 2)
    down_sent, down_kept = down_sent.reshape(down_view), down_kept.reshape(down_view)

    moved = swap(down_sent, 1)
    begun = ffn_backward(core, *ffn_ins, 0, 1, ())

    moved, begun, sc = after_all(moved, begun, scalars)
    down = first_split(sc, down_kept, moved, groups)
    down, begun, sc = after_all(down, begun, sc)
    moved = over_two(down)
    d_upper, d_resid, d_attn, sums_ffn, sums_up = ffn_backward(sc, *ffn_ins, 1, rest, tuple(begun))
    up_sent, up_kept = up_gradient(sc, hidden_low, gate(d_upper, d_attn))

    moved, up_sent, up_kept, d_attn, sc = after_all(moved, up_sent, up_kept, d_attn, sc)
    down = second(sc, moved)
    down, up_sent, up_kept, sc = after_all(down, up_sent, up_kept, sc)
    moved = over_other_two(down), swap(up_sent, 1)
    att_ins = (d_attn, d_resid, probs, qkv, region_source, w_out, w_qkv, dims)
    begun = attention_backward(sc, *att_ins, 0, 1, ())

    moved, up_kept, begun, sc = after_all(moved, up_kept, begun, sc)
    down = moved[0]
    up = first_split(sc, up_kept, moved[1], groups)
    down, up, begun, sc = after_all(down, up, begun, sc)
    moved = over_two(up)
    d_qkv, text_grad, back_message, sums_attn = attention_backward(sc, *att_ins, 1, rest, tuple(begun))

    moved, down, d_qkv, back_message, sc = after_all(moved, down, d_qkv, back_message, sc)
    up = second(sc, moved)
    up, down, sc = after_all(up, down, sc)
    moved = over_other_two(up)
    qkvo_sent, qkvo_kept = qkvo_gradient(sc, x, d_qkv, context, d_attn)

    moved, down, qkvo_sent, qkvo_kept, back_message, sc = after_all(
        moved, down, qkvo_sent, qkvo_kept, back_message, sc
    )
    ffn = join(sc, down, moved, place=apart)
    ffn, qkvo_sent, qkvo_kept, back_message, sc = after_all(ffn, qkvo_sent, qkvo_kept, back_message, sc)
    returned = lax.all_to_all(back_message, axes, split_axis=0, concat_axis=0, tiled=True)
    other_features = swap(gate(region_features, qkvo_kept), 1)
    qkvo = first_split(sc, qkvo_kept, swap(qkvo_sent, 1), groups, apart)
    qkvo_moved = over_two(qkvo)
    ffn_moved = swap(gate(ffn[0], *qkvo), 8)
    returned, sc = after_all(returned, gate(sc, *qkvo))
    d_pre, d_pre_sent, d_pre_kept, small, box_grad = region_norm_backward(
        sc, returned, region_target, vis_normed, vis_inv, visual_gain, boxes, w_box_t,
        sums_forward, sums_ffn, sums_up, sums_attn, groups,
    )
    vis = visual_gradient(
        sc, region_features, other_features, d_pre_kept, swap(d_pre_sent, 1), small, groups
    )
    vis_moved = over_two(vis)
    sc = gate(sc, *vis)
    qkvo = second(sc, qkvo_moved)
    qkvo_moved = over_other_two(qkvo)
    ffn = late_first(gate(sc, *qkvo), ffn[1], ffn_moved)
    ffn_moved = late_move(ffn)
    feature_grad = feature_gradient(gate(sc, *ffn), d_pre, w_visual)

    sc = gate(sc, feature_grad)
    vis = second(sc, vis_moved)
    vis_moved = over_other_two(vis)
    sc = gate(sc, *vis)
    qkvo = join(sc, qkvo_moved)
    qkvo_moved = swap(qkvo[0], 8)
    ffn = late_rest(sc, ffn, gate(ffn_moved, *qkvo))

    vis = join(gate(sc, *qkvo, ffn), vis_moved)
    vis_moved = swap(vis[0], 8)
    sc = gate(sc, *vis)
    qkvo = late_first(sc, qkvo[1], qkvo_moved)
    qkvo_moved = late_move(qkvo)

    vis = late_first(gate(sc, *qkvo), vis[1], vis_moved)
    vis_moved = late_move(vis)
    ffn = spread(ffn, *vis)
    sc = gate(sc, *vis)
    g_down, g_up = finish_ffn(sc, ffn)
    qkvo = late_rest(sc, qkvo, gate(qkvo_moved, *vis))

    vis = late_rest(sc, vis, gate(vis_moved, g_up, qkvo))
    qkvo = spread(qkvo, vis)
    g_qkv, g_out = finish_wide(gate(sc, vis), qkvo, (3 * width, width))
    vis = spread(vis, g_qkv)
    g_visual, g_box_t, rms_values, *small = finish_visual(
        sc, vis, w_up.shape[1] // groups, width // groups, boxes.shape[0]
    )
    return (
        out_rows,
        text_grad,
        feature_grad,
        box_grad,
        rms_values,
        g_visual,
        g_box_t.T,
        small[0],
        small[1],
        small[2],
        g_qkv,
        small[9],
        g_out,
        small[8],
        small[6],
        small[7],
        g_up,
        small[10],
        g_down,
        small[5],
        small[3],
        small[4],
    )


def solution(mesh):
    return jax.shard_map(
        on_device,
        mesh=mesh,
        in_specs=(
            P(("dp", "enc"), None),
            P(("dp", "enc"), None),
            P(None, ("dp", "enc")),
            P(("dp", "enc")),
            P(("dp", "enc")),
            P(("dp", "enc")),
            P(("dp", "enc"), None),
            P(("dp", "enc"), None),
            P(),
            P(),
            P(),
            P(),
            P(),
            P(),
            P(),
            P(),
            P(),
            P(),
            P(),
            P(),
            P(),
            P(),
            P(),
            P(),
            P(),
            P(("dp", "enc"), None),
        ),
        out_specs=(
            P(("dp", "enc"), None),
            P(("dp", "enc"), None),
            P(("dp", "enc"), None),
            P(None, ("dp", "enc")),
            P(),
            P("dp", None),
            P("dp", None),
            P("dp"),
            P("dp"),
            P("dp"),
            P("dp", None),
            P("dp"),
            P("dp", None),
            P("dp"),
            P("dp"),
            P("dp"),
            P("dp", None),
            P("dp"),
            P("dp", None),
            P("dp"),
            P("dp"),
            P("dp"),
        ),
        check_vma=False,
    )
```
